32 devices in a mesh: dp: 8 (over z, y), mp: 4 (over x, core).
Axes of the slice: x: 2, y: 2, z: 4, core: 2. Of those that a mesh axis runs over, the one named last changes fastest.
Arguments:
- tokens: bfloat16 [19200, 768], P(('dp', 'mp')), may hold values from -48 to 48
- token_mask: int32 [96, 200], P('dp'), may hold values from 0 to 1, as said below
- gain_one: bfloat16 [768], P('dp'), may hold values from 0.25 to 1.75
- w_qkv: bfloat16 [768, 3, 768], P('dp', None, 'mp'), may hold values from -0.21875 to 0.21875
- w_out: bfloat16 [768, 768], P('mp', 'dp'), may hold values from -1.75 to 1.75
- gain_two: bfloat16 [768], P('dp'), may hold values from 0.25 to 1.75
- router: bfloat16 [768, 8], P('dp'), may hold values from -0.109375 to 0.109375
- w_in: bfloat16 [8, 768, 3072], P('dp', None, 'mp'), may hold values from -2.5 to 2.5
- w_back: bfloat16 [8, 3072, 768], P('dp', 'mp'), may hold values from -1 to 1
- cotangent: bfloat16 [19200, 768], P(('dp', 'mp')), may hold values from -6 to 6
Outputs:
- out: bfloat16 [19200, 768], P(('dp', 'mp'))
- grad_tokens: float32 [19200, 768], P(('dp', 'mp'))
- grad_gain_one: float32 [768], P('dp')
- grad_w_qkv: float32 [768, 3, 768], P('dp', None, 'mp')
- grad_w_out: float32 [768, 768], P('mp', 'dp')
- grad_gain_two: float32 [768], P('dp')
- grad_router: float32 [768, 8], P('dp')
- grad_w_in: float32 [8, 768, 3072], P('dp', None, 'mp')
- grad_w_back: float32 [8, 3072, 768], P('dp', 'mp')
- root_squares: float32 [3, 96], P(None, 'dp')
The draws below stay inside these ranges and needn't reach their ends.
Inputs may be any that keep to these rules, and one draw needn't show every extreme that they name: `token_mask`: for each image the positions with 1 form a prefix of 98 to 197 positions; some image has 197; positions 197 and beyond are 0.
All inputs are finite; a program needn't handle non-finite values.
Results may differ from the reference program's by a relative error of at most 0.02.
Values may be sent and summed in bfloat16 or wider, within the bound.
No kernel may reach another device: no remote copies, remote signals or barrier semaphores. Data moves between devices by JAX's collectives and lax.ppermute only.
A program may use at most 192 MiB of HBM per device.

```python
import math
from functools import partial
import jax
import jax.numpy as jnp
from jax import lax

D = 768
HEADS = 12
HEAD_DIM = 64
FF = 3072
IMG_DEV = 12
SEQ = 200
VALID = 197
EXPERTS = 8
IMAGES = 96
TOKENS = 19200


def draw_tokens(key, part):
    key_base, key_rows, key_cols = jax.random.split(key, 3)
    row_scale = jnp.exp(jax.random.uniform(key_rows, (TOKENS, 1), jnp.float32, math.log(0.3), math.log(3.0)))
    col_scale = jnp.exp(jax.random.uniform(key_cols, (1, D), jnp.float32, math.log(0.3), math.log(3.0)))
    base_draw = jax.random.truncated_normal(key_base, -4.0, 4.0, (TOKENS, D), jnp.float32)
    return (base_draw * row_scale * col_scale).astype(jnp.bfloat16)


def draw_token_mask(key, part):
    key_lengths, key_chosen = jax.random.split(key, 2)
    lengths = jax.random.randint(key_lengths, (IMAGES,), VALID // 2, VALID + 1)
    chosen = jax.random.randint(key_chosen, (), 0, IMAGES)
    lengths = jnp.where(jnp.arange(IMAGES) == chosen, VALID, lengths)
    positions = jnp.arange(SEQ)
    return (positions[None, :] < lengths[:, None]).astype(jnp.int32)


def spiked(values, own_key, source, target, blocks, factor):
    def block_of(axis_at):
        return (jnp.arange(values.shape[axis_at]) // (values.shape[axis_at] // blocks)).reshape((-1,) + (1,) * (values.ndim - 1 - axis_at))

    one_side = jax.random.permutation(own_key, blocks)[block_of(target)]
    other_side = (block_of(target) + blocks // 2) % blocks
    return jnp.where((block_of(source) == one_side) | (block_of(source) == other_side), factor * values, values)


def block_scale(key, extent, cuts, smallest, largest):
    loudness, own = 1.0, jax.random.fold_in(key, 6)
    for dim, blocks in cuts:
        steps = jnp.exp(jax.random.uniform(jax.random.fold_in(own, dim), (blocks,), jnp.float32, smallest / len(cuts), largest / len(cuts)))
        loudness = loudness * jnp.repeat(steps, extent[dim] // blocks).reshape([-1 if axis == dim else 1 for axis in range(len(extent))])
    return loudness


def gaussian(stream_key, extent, spread, most, shards=(), kind=jnp.bfloat16):
    gain = block_scale(stream_key, extent, shards, -0.22, 0.18) if shards else 1.0
    array = jax.random.normal(stream_key, extent, jnp.float32) * spread * gain
    return jnp.minimum(jnp.maximum(array, -most), most).astype(kind)


def noise_with(own_key, shape, scale, most, cuts, heavy, dtype=jnp.bfloat16):
    array = scale * jax.random.normal(own_key, shape, jnp.float32)
    if cuts:
        array = array * block_scale(own_key, shape, cuts, -0.22, 0.18)
    return jnp.clip(spiked(array, jax.random.fold_in(own_key, 3), *heavy), -most, most).astype(dtype)


def setup_inputs(seed: int = 0) -> dict:
    streams_of = jax.random.split(jax.random.key(seed), 11)
    tokens = draw_tokens(jax.random.fold_in(streams_of[10], 71), 0)
    token_mask = draw_token_mask(jax.random.fold_in(streams_of[10], 71), 0)
    gain_one = jnp.clip(1.0 + 0.15 * jax.random.normal(streams_of[2], (D,), jnp.float32), 0.25, 1.75).astype(jnp.bfloat16)
    w_qkv = gaussian(streams_of[3], (D, 3, D), D ** -0.5, 0.21875, ((0, 8), (2, 4)))
    w_out = gaussian(streams_of[4], (D, D), (max(D // 64, 1)) ** -0.5, 1.75, ((0, 4), (1, 8)))
    gain_two = jnp.clip(1.0 + 0.15 * jax.random.normal(streams_of[5], (D,), jnp.float32), 0.25, 1.75).astype(jnp.bfloat16)
    router = gaussian(streams_of[6], (D, EXPERTS), (4 * D) ** -0.5, 0.109375, ((0, 8),))
    w_in = gaussian(streams_of[7], (EXPERTS, D, FF), (max(D // 128, 1)) ** -0.5, 2.5, ((0, 8), (2, 4)))
    w_back = gaussian(streams_of[8], (EXPERTS, FF, D), (max(FF // 96, 1)) ** -0.5, 1.0, ((0, 8), (1, 4)))
    cotangent = noise_with(streams_of[9], (TOKENS, D), 1.0, 6.0, ((0, 32),), (0, 1, 32, 2.75))
    return {"tokens": tokens, "token_mask": token_mask, "gain_one": gain_one, "w_qkv": w_qkv, "w_out": w_out, "gain_two": gain_two, "router": router, "w_in": w_in, "w_back": w_back, "cotangent": cotangent}


epsilon = 1e-06
highest = lax.Precision.HIGHEST

@jax.custom_vjp
def low(v):
    return lax.optimization_barrier(v.astype(jnp.bfloat16)).astype(jnp.float32)

@jax.custom_vjp
def low_back(v):
    return v

def low_keep(v):
    return (low(v), None)

def low_pass(kept, grad):
    return (grad,)

def back_keep(v):
    return (v, None)

def back_low(kept, grad):
    return (low(grad),)
low.defvjp(low_keep, low_pass)
low_back.defvjp(back_keep, back_low)

def layer_norm(array_in, gain_vec):
    mean_row = lax.optimization_barrier(jnp.mean(array_in, axis=-1, keepdims=True))
    centered = array_in - mean_row
    variance = lax.optimization_barrier(jnp.mean(centered * centered, axis=-1, keepdims=True))
    return centered * lax.rsqrt(variance + epsilon) * gain_vec

def softmax_over(array_in, axis_index):
    shifted = array_in - lax.optimization_barrier(jnp.max(array_in, axis=axis_index, keepdims=True))
    exp_terms = jnp.exp(shifted)
    return exp_terms / lax.optimization_barrier(jnp.sum(exp_terms, axis=axis_index, keepdims=True))

def gelu_tanh(array_in):
    tanh_arg = 0.7978845608028654 * (array_in + 0.044715 * array_in * array_in * array_in)
    return 0.5 * array_in * (1.0 + jnp.tanh(tanh_arg))

def attend_block(block_args, gain_one, w_qkv, w_out):
    block_rows, present = block_args
    image_count = present.shape[0]
    h_one = low(layer_norm(block_rows, gain_one))
    joined_qkv = low_back(low(jnp.einsum('td,dcf->tcf', h_one, w_qkv, precision=highest)))
    joined_qkv = joined_qkv.reshape(image_count, SEQ, 3, HEADS, HEAD_DIM)
    queries = joined_qkv[:, :, 0]
    key_rows = joined_qkv[:, :, 1]
    values = joined_qkv[:, :, 2]
    raw_scores = jnp.einsum('bqhe,bkhe->bhqk', queries, key_rows, precision=highest) * HEAD_DIM ** (-0.5)
    raw_scores = low_back(raw_scores)
    raw_scores = jnp.where(present[:, None, None, :] > 0, raw_scores, -1e+30)
    attention = low(softmax_over(raw_scores, 3))
    heads_out = jnp.einsum('bhqk,bkhe->bqhe', attention, values, precision=highest)
    heads_out = low_back(low(heads_out.reshape(image_count * SEQ, D)))
    return low_back(jnp.dot(heads_out, w_out, precision=highest))

def expert_block(block_args):
    slot_rows, first_w, second_w = block_args
    pre_gelu = low_back(jnp.dot(slot_rows, first_w, precision=highest))
    hidden = low(gelu_tanh(pre_gelu))
    return jnp.dot(hidden, second_w, precision=highest)

def forward(tokens, token_mask, gain_one, w_qkv, w_out, gain_two, router, w_in, w_back):
    images = token_mask.shape[0]
    blocks = images // IMG_DEV
    block_rows = tokens.reshape(blocks, IMG_DEV * SEQ, D)
    present = token_mask.reshape(blocks, IMG_DEV, SEQ)
    attend_fn = jax.checkpoint(partial(attend_block, gain_one=gain_one, w_qkv=w_qkv, w_out=w_out))
    branch = lax.map(attend_fn, (block_rows, present)).reshape(images * SEQ, D)
    resid = tokens + branch
    h_two = low(layer_norm(resid, gain_two))
    logits = low_back(jnp.dot(h_two, router, precision=highest)).reshape(images, SEQ, EXPERTS)
    dispatch = low(softmax_over(jnp.where(token_mask[:, :, None] > 0, logits, -1e+30), 1))
    combine = low(softmax_over(logits, 2))
    slots_in = jnp.einsum('bse,bsd->ebd', dispatch, h_two.reshape(images, SEQ, D), precision=highest)
    slots_in = low_back(low(slots_in))
    slots_out = low_back(low(lax.map(jax.checkpoint(expert_block), (slots_in, w_in, w_back))))
    mixed_rows = jnp.einsum('bse,ebd->bsd', combine, slots_out, precision=highest).reshape(images * SEQ, D)
    return (resid + mixed_rows, (branch, mixed_rows))

def root_mean(array_in, token_mask):
    images = token_mask.shape[0]
    weight_rows = token_mask.astype(jnp.float32)
    shaped = array_in.reshape(images, SEQ, D)
    squares = lax.optimization_barrier(jnp.sum(shaped * shaped, axis=-1))
    counted = lax.optimization_barrier(jnp.sum(weight_rows, axis=1)) * D
    return jnp.sqrt(lax.optimization_barrier(jnp.sum(squares * weight_rows, axis=1)) / counted)

def reference(tokens, token_mask, gain_one, w_qkv, w_out, gain_two, router, w_in, w_back, cotangent):
    floats = [array_in.astype(jnp.float32) for array_in in (tokens, gain_one, w_qkv, w_out, gain_two, router, w_in, w_back)]

    def closed(tokens_f, first_gain, qkv_weight, out_weight, second_gain, route_weight, in_weight, back_weight):
        return forward(tokens_f, token_mask, first_gain, qkv_weight, out_weight, second_gain, route_weight, in_weight, back_weight)
    result, pullback, extras = jax.vjp(closed, *floats, has_aux=True)
    gradients = pullback(cotangent.astype(jnp.float32))
    branch, mixed_rows = extras
    root_squares = jnp.stack([root_mean(result, token_mask), root_mean(branch, token_mask), root_mean(mixed_rows, token_mask)])
    return (result.astype(jnp.bfloat16), gradients[0], gradients[1], gradients[2], gradients[3], gradients[4], gradients[5], gradients[6], gradients[7], root_squares)
```

```python
import jax
import jax.numpy as jnp
from jax import lax
from jax.sharding import PartitionSpec as P

HEAD_DIM = 64


epsilon = 1e-06
bf16 = jnp.bfloat16
f32 = jnp.float32


def softmax_over(array_in, axis_index):
    shifted = array_in - jnp.max(array_in, axis=axis_index, keepdims=True)
    exp_terms = jnp.exp(shifted)
    return exp_terms / jnp.sum(exp_terms, axis=axis_index, keepdims=True)


def gelu_tanh(array_in):
    tanh_arg = 0.7978845608028654 * (array_in + 0.044715 * array_in * array_in * array_in)
    return 0.5 * array_in * (1.0 + jnp.tanh(tanh_arg))


def normalize(array_in, gain_vec):
    mean_row = jnp.mean(array_in, axis=-1, keepdims=True)
    centered = array_in - mean_row
    variance = jnp.mean(centered * centered, axis=-1, keepdims=True)
    inverse = lax.rsqrt(variance + epsilon)
    unit_rows = centered * inverse
    return (unit_rows * gain_vec, unit_rows, inverse)


def norm_back(grad_rows, unit_rows, inverse, gain_vec):
    scaled = grad_rows * gain_vec
    mean_grad = jnp.mean(scaled, axis=-1, keepdims=True)
    mean_proj = jnp.mean(scaled * unit_rows, axis=-1, keepdims=True)
    return (
        inverse * (scaled - mean_grad - unit_rows * mean_proj),
        jnp.sum(grad_rows * unit_rows, axis=0),
    )


def root_mean(array_in, token_mask):
    images, seq_len = token_mask.shape
    weight_rows = token_mask.astype(jnp.float32)
    shaped = array_in.reshape(images, seq_len, -1)
    squares = jnp.sum(shaped * shaped, axis=-1)
    counted = jnp.sum(weight_rows, axis=1) * shaped.shape[2]
    return jnp.sqrt(jnp.sum(squares * weight_rows, axis=1) / counted)


def swap(array_in, axis_name, size, bit):
    return lax.ppermute(array_in, axis_name, [(i, i ^ bit) for i in range(size)])


def bits_of(size):
    return [1 << k for k in range(size.bit_length() - 1)]


def gather_dp(block, dp):
    index = lax.axis_index("dp")
    held = block[None]
    for bit in bits_of(dp):
        other = swap(held, "dp", dp, bit)
        upper = (index & bit) > 0
        held = jnp.where(
            upper, jnp.concatenate([other, held], 0), jnp.concatenate([held, other], 0)
        )
    return held


def gather_mp(block, mp):
    held = block[None]
    for bit in reversed(bits_of(mp)):
        other = swap(held, "mp", mp, bit)
        held = jnp.stack([held, other], 1).reshape((-1,) + block.shape)
    return held


def scatter_mp(held, mp):
    for bit in bits_of(mp):
        pairs = held.reshape((-1, 2) + held.shape[1:])
        other = swap(pairs[:, 1], "mp", mp, bit)
        held = (pairs[:, 0].astype(f32) + other.astype(f32)).astype(bf16)
    return held[0]


def scatter_dp(held, dp):
    index = lax.axis_index("dp")
    for bit in reversed(bits_of(dp)):
        half = held.shape[0] // 2
        upper = (index & bit) > 0
        low, high = held[:half], held[half:]
        other = swap(jnp.where(upper, low, high), "dp", dp, bit)
        held = (jnp.where(upper, high, low).astype(f32) + other.astype(f32)).astype(bf16)
    return held[0]


def make(mesh):
    dp, mp = mesh.shape["dp"], mesh.shape["mp"]

    def per_device(
        tokens, token_mask, gain_one, w_qkv, w_out, gain_two, router, w_in, w_back, cotangent
    ):
        rows = tokens.shape[0]
        width = tokens.shape[1]
        seq_len = token_mask.shape[1]
        images = rows // seq_len
        experts = router.shape[1]
        part = w_qkv.shape[2]
        heads = part // HEAD_DIM
        d_rows = w_qkv.shape[0]
        score_scale = HEAD_DIM ** (-0.5)
        mask = lax.dynamic_slice_in_dim(token_mask, lax.axis_index("mp") * images, images, 0)
        present = mask > 0
        key_keep = present[:, None, None, :]
        packed = jnp.concatenate([w_qkv.reshape(d_rows, 3 * part), w_out.T], axis=1)
        extra = jnp.concatenate([gain_one[:, None], gain_two[:, None], router], axis=1)
        extra = gather_dp(extra, dp).reshape(width, experts + 2)
        gain_a_f = extra[:, 0].astype(f32)
        gain_b_f = extra[:, 1].astype(f32)
        route_w = extra[:, 2:]
        weights = gather_mp(gather_dp(packed, dp).reshape(width, 4 * part), mp)
        qkv_w = weights[:, :, : 3 * part]
        out_w = weights[:, :, 3 * part :]

        tokens_f = tokens.astype(f32)
        h_one_f, unit_one, inv_one = normalize(tokens_f, gain_a_f)
        h_one = h_one_f.astype(bf16)
        joined = jnp.einsum("td,jdf->jtf", h_one, qkv_w, preferred_element_type=f32).astype(bf16)
        joined = joined.reshape(mp, images, seq_len, 3, heads, HEAD_DIM)
        queries, key_rows, values = joined[:, :, :, 0], joined[:, :, :, 1], joined[:, :, :, 2]
        raw = jnp.einsum("jbqhe,jbkhe->jbhqk", queries, key_rows, preferred_element_type=f32)
        scores = jnp.where(key_keep, raw * score_scale, -1e30)
        soft = softmax_over(scores, 4)
        attention = soft.astype(bf16)
        heads_out = jnp.einsum("jbhqk,jbkhe->jbqhe", attention, values, preferred_element_type=f32)
        heads_out = heads_out.astype(bf16).reshape(mp, rows, part)
        branch = jnp.einsum("jtf,jdf->td", heads_out, out_w, preferred_element_type=f32)
        resid = tokens_f + branch
        h_two_f, unit_two, inv_two = normalize(resid, gain_b_f)
        h_two = h_two_f.astype(bf16)
        logits = jnp.dot(h_two, route_w, preferred_element_type=f32)
        logits = logits.reshape(images, seq_len, experts)
        dispatch_f = softmax_over(jnp.where(present[:, :, None], logits, -1e30), 1)
        combine_f = softmax_over(logits, 2)
        dispatch = dispatch_f.astype(bf16)
        combine = combine_f.astype(bf16)
        h_two_img = h_two.reshape(images, seq_len, width)
        cot_img = cotangent.reshape(images, seq_len, width)
        slot_rows = jnp.einsum("bse,bsd->ebd", dispatch, h_two_img, preferred_element_type=f32)
        grad_slot = jnp.einsum("bse,bsd->ebd", combine, cot_img, preferred_element_type=f32)
        sent = jnp.stack([slot_rows, grad_slot], 1).astype(bf16)
        got = lax.all_to_all(sent, "dp", split_axis=0, concat_axis=0, tiled=True)
        got = gather_mp(got, mp)
        slot_in = got[:, :, 0].reshape(-1, width)
        grad_expert = got[:, :, 1].reshape(-1, width)
        first_w, second_w = w_in[0], w_back[0]
        pre_gelu = jnp.dot(slot_in, first_w, preferred_element_type=f32)
        hidden_f, gelu_pull = jax.vjp(gelu_tanh, pre_gelu)
        hidden = hidden_f.astype(bf16)
        partial_out = jnp.dot(hidden, second_w, preferred_element_type=f32)
        grad_hidden = jnp.einsum("nd,fd->nf", grad_expert, second_w, preferred_element_type=f32)
        grad_w_back = jnp.einsum("nf,nd->fd", hidden, grad_expert, preferred_element_type=f32)
        grad_pre = gelu_pull(grad_hidden)[0].astype(bf16)
        grad_w_in = jnp.einsum("nd,nf->df", slot_in, grad_pre, preferred_element_type=f32)
        grad_part = jnp.einsum("nf,df->nd", grad_pre, first_w, preferred_element_type=f32)
        shape = got[:, :, 0].shape
        back = jnp.stack([partial_out.reshape(shape), grad_part.reshape(shape)], 2).astype(bf16)
        back = scatter_mp(back, mp)
        back = lax.all_to_all(back, "dp", split_axis=0, concat_axis=0, tiled=True)
        returned, grad_slots = back[:, 0], back[:, 1]

        mixed = jnp.einsum("bse,ebd->bsd", combine, returned, preferred_element_type=f32)
        mixed = mixed.reshape(rows, width)
        stream = resid + mixed
        out_rows = stream.astype(bf16)
        squares = jnp.stack(
            [root_mean(stream, mask), root_mean(branch, mask), root_mean(mixed, mask)]
        )
        root_squares = lax.all_gather(squares, "mp", axis=1, tiled=True)
        grad_combine = jnp.einsum("bsd,ebd->bse", cot_img, returned, preferred_element_type=f32)
        grad_logit_c = combine_f * (
            grad_combine - jnp.sum(grad_combine * combine_f, axis=2, keepdims=True)
        )
        grad_dispatch = jnp.einsum("bsd,ebd->bse", h_two_img, grad_slots, preferred_element_type=f32)
        grad_logit_d = dispatch_f * (
            grad_dispatch - jnp.sum(grad_dispatch * dispatch_f, axis=1, keepdims=True)
        )
        grad_logits = (grad_logit_d + grad_logit_c).reshape(rows, experts).astype(bf16)
        grad_h_two = jnp.einsum(
            "bse,ebd->bsd", dispatch, grad_slots, preferred_element_type=f32
        ).reshape(rows, width)
        grad_h_two = grad_h_two + jnp.einsum(
            "te,de->td", grad_logits, route_w, preferred_element_type=f32
        )
        grad_router = jnp.einsum("td,te->de", h_two, grad_logits, preferred_element_type=f32)
        grad_norm_two, grad_gain_two = norm_back(grad_h_two, unit_two, inv_two, gain_b_f)
        grad_resid = cotangent.astype(f32) + grad_norm_two
        grad_branch = grad_resid.astype(bf16)
        grad_w_out = jnp.einsum("td,jtf->jdf", grad_branch, heads_out, preferred_element_type=f32)
        grad_heads = jnp.einsum("td,jdf->jtf", grad_branch, out_w, preferred_element_type=f32)
        grad_heads = grad_heads.astype(bf16).reshape(mp, images, seq_len, heads, HEAD_DIM)
        grad_values = jnp.einsum(
            "jbhqk,jbqhe->jbkhe", attention, grad_heads, preferred_element_type=f32
        )
        grad_soft = jnp.einsum(
            "jbqhe,jbkhe->jbhqk", grad_heads, values, preferred_element_type=f32
        )
        grad_scores = (
            soft * (grad_soft - jnp.sum(grad_soft * soft, axis=-1, keepdims=True))
        ).astype(bf16)
        grad_queries = score_scale * jnp.einsum(
            "jbhqk,jbkhe->jbqhe", grad_scores, key_rows, preferred_element_type=f32
        )
        grad_keys = score_scale * jnp.einsum(
            "jbhqk,jbqhe->jbkhe", grad_scores, queries, preferred_element_type=f32
        )
        grad_joined = jnp.stack([grad_queries, grad_keys, grad_values], axis=3).astype(bf16)
        grad_joined = grad_joined.reshape(mp, rows, 3 * part)
        grad_w_qkv = jnp.einsum("td,jtf->jdf", h_one, grad_joined, preferred_element_type=f32)
        grad_h_one = jnp.einsum("jtf,jdf->td", grad_joined, qkv_w, preferred_element_type=f32)
        grad_norm_one, grad_gain_one = norm_back(grad_h_one, unit_one, inv_one, gain_a_f)
        grad_tokens = grad_resid + grad_norm_one

        grads = jnp.concatenate([grad_w_qkv, grad_w_out], axis=2).astype(bf16)
        summed = scatter_mp(grads, mp).reshape(dp, d_rows, 4 * part)
        summed = scatter_dp(summed, dp).astype(f32)
        small = jnp.concatenate(
            [grad_gain_one[:, None], grad_gain_two[:, None], grad_router], axis=1
        )
        small = lax.psum(small, ("dp", "mp"))
        small = lax.dynamic_slice_in_dim(small, lax.axis_index("dp") * d_rows, d_rows, 0)
        return (
            out_rows,
            grad_tokens,
            small[:, 0],
            summed[:, : 3 * part].reshape(d_rows, 3, part),
            summed[:, 3 * part :].T,
            small[:, 1],
            small[:, 2:],
            grad_w_in[None],
            grad_w_back[None],
            root_squares,
        )

    return per_device


def solution(mesh):
    in_specs = (
        P(("dp", "mp"), None),
        P("dp", None),
        P("dp"),
        P("dp", None, "mp"),
        P("mp", "dp"),
        P("dp"),
        P("dp", None),
        P("dp", None, "mp"),
        P("dp", "mp", None),
        P(("dp", "mp"), None),
    )
    out_specs = (
        P(("dp", "mp"), None),
        P(("dp", "mp"), None),
        P("dp"),
        P("dp", None, "mp"),
        P("mp", "dp"),
        P("dp"),
        P("dp", None),
        P("dp", None, "mp"),
        P("dp", "mp", None),
        P(None, "dp"),
    )
    return jax.shard_map(
        make(mesh), mesh=mesh, in_specs=in_specs, out_specs=out_specs, check_vma=False
    )
```

```python
import functools
import math

import jax
import jax.numpy as jnp
from jax import lax
from jax.experimental import pallas as pl
from jax.experimental.pallas import tpu as pltpu
from jax.sharding import PartitionSpec as P

HEAD_DIM = 64


epsilon = 1e-06
bf16 = jnp.bfloat16
f32 = jnp.float32


def swap(array_in, axis_name, size, bit):
    return lax.ppermute(array_in, axis_name, [(i, i ^ bit) for i in range(size)])


def bits_of(size):
    return [1 << k for k in reversed(range(size.bit_length() - 1))]


def gather_pair(block, dp, mp, late):
    held = block
    depth = 0
    bits = bits_of(dp)
    for bit in bits[:-1] if late else bits:
        held = jnp.stack([held, swap(held, "dp", dp, bit)], depth)
        depth += 1
    held = jnp.stack([held, swap(held, "mp", mp, 2)], 0)
    if late:
        held = jnp.stack([held, swap(held, "dp", dp, bits[-1])], depth + 1)
    held = held.reshape((mp // 2, dp) + block.shape)
    return held, swap(held, "mp", mp, 1)


def gather_mp(block, mp):
    held = block[None]
    for bit in bits_of(mp):
        other = swap(held, "mp", mp, bit)
        held = jnp.stack([held, other], 1).reshape((-1,) + block.shape)
    return held


def scatter(held, axis_name, size, bits):
    left = sorted(bits)
    for bit in bits:
        inner = 1 << left.index(bit)
        left.remove(bit)
        pairs = held.reshape((held.shape[0] // (2 * inner), 2, inner) + held.shape[1:])
        other = swap(pairs[:, 1], axis_name, size, bit)
        held = pairs[:, 0].astype(f32) + other.astype(f32)
        held = held.astype(bf16).reshape((-1,) + held.shape[2:])
    return held[0]


def mm(a, b):
    return lax.dot_general(a, b, (((1,), (0,)), ((), ())), preferred_element_type=f32)


def mm_nt(a, b):
    return lax.dot_general(a, b, (((1,), (1,)), ((), ())), preferred_element_type=f32)


def mm_tn(a, b):
    return lax.dot_general(a, b, (((0,), (0,)), ((), ())), preferred_element_type=f32)


def unit_of(rows_f):
    mean_row = jnp.mean(rows_f, axis=-1, keepdims=True)
    centered = rows_f - mean_row
    variance = jnp.mean(centered * centered, axis=-1, keepdims=True)
    inverse = lax.rsqrt(variance + epsilon)
    return centered * inverse, inverse


def padded(value, pad):
    return jnp.concatenate([value, jnp.zeros((pad, value.shape[1]), value.dtype)], 0)


def low_lanes(rows):
    return lax.broadcasted_iota(jnp.int32, (rows, 128), 1) < HEAD_DIM


JOINED = 640


def front_kernel(
    x_ref, bias_ref, gain_ref, w_ref, h_ref, qkv_ref, p_ref, ho_ref, br_ref, *, images, seq, tall
):
    groups = w_ref.shape[0]
    scale = HEAD_DIM ** (-0.5)
    for b in range(images):
        unit, _ = unit_of(x_ref[b].astype(f32))
        h_ref[pl.ds(b * tall, tall), :] = padded((unit * gain_ref[...]).astype(bf16), tall - seq)
    br_ref[...] = jnp.zeros_like(br_ref)
    low = low_lanes(tall)

    def group(j, carry):
        qkv_ref[j] = mm(h_ref[...], w_ref[j, :, :JOINED]).astype(bf16)

        def image(b, inner):
            at = pl.ds(pl.multiple_of(b * tall, 16), tall)
            joined = qkv_ref[j, at, :]
            q_pair, k_pair, v_pair = joined[:, :128], joined[:, 128:256], joined[:, 256:384]
            qk_last, v_last = joined[:, 384:512], joined[:, 512:640]
            k_last = pltpu.roll(qk_last.astype(f32), HEAD_DIM, 1).astype(bf16)
            none = jnp.zeros_like(q_pair)
            bias = bias_ref[b]
            outs = []
            for head, (q, k, v) in enumerate(
                (
                    (jnp.where(low, q_pair, none), k_pair, v_pair),
                    (jnp.where(low, none, q_pair), k_pair, v_pair),
                    (jnp.where(low, qk_last, none), k_last, v_last),
                )
            ):
                scores = mm_nt(q, k) * scale + bias
                terms = jnp.exp(scores - jnp.max(scores, axis=-1, keepdims=True))
                probs = (terms * (1.0 / jnp.sum(terms, axis=-1, keepdims=True))).astype(bf16)
                p_ref[j, b, head] = probs
                outs.append(mm(probs, v))
            last = jnp.where(low, 0.0, pltpu.roll(outs[2], HEAD_DIM, 1))
            pair = jnp.where(low, outs[0], outs[1])
            ho_ref[j, at, :] = jnp.concatenate([last, pair], 1).astype(bf16)
            return inner

        lax.fori_loop(0, images, image, 0, unroll=True)
        br_ref[...] += mm_nt(ho_ref[j], w_ref[j, :, 512:])
        return carry

    lax.fori_loop(0, groups, group, 0)


def route_kernel(
    x_ref, br_ref, cot_ref, mask_ref, column_ref, gain_ref, router_ref,
    res_ref, h_ref, soft_ref, sent_ref, sq_ref, *, images, seq, tall
):
    for b in range(images):
        at = pl.ds(b * tall, tall)
        branch = br_ref[at, :]
        resid = padded(x_ref[b].astype(f32), tall - seq) + branch
        res_ref[at, :] = resid
        unit, _ = unit_of(resid)
        h_two = (unit * gain_ref[...]).astype(bf16)
        h_ref[at, :] = h_two
        logits = mm_nt(router_ref[...], h_two)
        seen = mask_ref[b] > 0
        held = jnp.where(seen, logits, -1e30)
        terms = jnp.exp(held - jnp.max(held, axis=1, keepdims=True))
        dispatch = terms / jnp.sum(terms, axis=1, keepdims=True)
        terms = jnp.exp(logits - jnp.max(logits, axis=0, keepdims=True))
        combine = terms / jnp.sum(terms, axis=0, keepdims=True)
        soft_ref[0, b] = dispatch
        soft_ref[1, b] = combine
        cot = padded(cot_ref[b], tall - seq)
        sent_ref[0, b] = mm(dispatch.astype(bf16), h_two).astype(bf16)
        sent_ref[1, b] = mm(combine.astype(bf16), cot).astype(bf16)
        squares = jnp.sum(branch * branch, axis=1, keepdims=True)
        sq_ref[b] = jnp.broadcast_to(
            jnp.sum(squares * column_ref[b], axis=0, keepdims=True), (1, 128)
        )


def expert_kernel(slot_ref, grad_ref, first_ref, second_ref, hid_ref, pre_ref, back_ref):
    slots, grads = slot_ref[...], grad_ref[...]
    u = mm(slots, first_ref[...])
    cubic = 0.7978845608028654 * (u + 0.044715 * u * u * u)
    t = jnp.tanh(cubic)
    hidden = (0.5 * u * (1.0 + t)).astype(bf16)
    hid_ref[...] = hidden
    back_ref[0] = mm(hidden, second_ref[...]).astype(bf16)
    slope = 0.5 * (1.0 + t) + 0.5 * u * (1.0 - t * t) * 0.7978845608028654 * (
        1.0 + 3.0 * 0.044715 * u * u
    )
    grad_pre = (mm_nt(grads, second_ref[...]) * slope).astype(bf16)
    pre_ref[...] = grad_pre
    back_ref[1] = mm_nt(grad_pre, first_ref[...]).astype(bf16)


def mix_kernel(
    res_ref, h_ref, soft_ref, cot_ref, column_ref, gain_ref, router_ref, back_ref,
    out_ref, gres_ref, grouter_ref, ggain_ref, sq_ref, *, images, seq, tall
):
    grouter_ref[...] = jnp.zeros_like(grouter_ref)
    ggain_ref[...] = jnp.zeros_like(ggain_ref)
    for b in range(images):
        at = pl.ds(b * tall, tall)
        resid, h_two = res_ref[at, :], h_ref[at, :]
        dispatch, combine = soft_ref[0, b], soft_ref[1, b]
        dispatch_low, combine_low = dispatch.astype(bf16), combine.astype(bf16)
        returned, grad_slots = back_ref[0, b], back_ref[1, b]
        cot = padded(cot_ref[b], tall - seq)
        mixed = mm_tn(combine_low, returned)
        stream = resid + mixed
        out_ref[b] = stream[:seq].astype(bf16)
        column = column_ref[b]
        for k, value in enumerate((stream, mixed)):
            squares = jnp.sum(value * value, axis=1, keepdims=True)
            sq_ref[k, b] = jnp.broadcast_to(
                jnp.sum(squares * column, axis=0, keepdims=True), (1, 128)
            )
        grad_c = mm_nt(returned, cot)
        grad_c = combine * (grad_c - jnp.sum(grad_c * combine, axis=0, keepdims=True))
        grad_d = mm_nt(grad_slots, h_two)
        grad_d = dispatch * (grad_d - jnp.sum(grad_d * dispatch, axis=1, keepdims=True))
        grad_logits = (grad_d + grad_c).astype(bf16)
        grad_h = mm_tn(dispatch_low, grad_slots) + mm_tn(grad_logits, router_ref[...])
        grouter_ref[...] += mm(grad_logits, h_two)
        unit, inverse = unit_of(resid)
        ggain_ref[...] += jnp.sum(grad_h * unit, axis=0, keepdims=True)
        scaled = grad_h * gain_ref[...]
        mean_grad = jnp.mean(scaled, axis=-1, keepdims=True)
        mean_proj = jnp.mean(scaled * unit, axis=-1, keepdims=True)
        gres_ref[at, :] = cot.astype(f32) + inverse * (scaled - mean_grad - unit * mean_proj)


def back_kernel(
    gres_ref, h_ref, qkv_ref, p_ref, ho_ref, w_ref,
    gw_ref, gh_ref, gb_ref, gj_ref, dho_ref, gbt_ref, ht_ref, *, images, seq, tall
):
    groups = w_ref.shape[0]
    scale = HEAD_DIM ** (-0.5)
    gb_ref[...] = gres_ref[...].astype(bf16)
    gbt_ref[...] = gres_ref[...].T.astype(bf16)
    ht_ref[...] = h_ref[...].T
    gh_ref[...] = jnp.zeros_like(gh_ref)
    low = low_lanes(tall)

    def group(j, carry):
        dho_ref[...] = mm(gb_ref[...], w_ref[j, :, 512:])

        def image(b, inner):
            at = pl.ds(pl.multiple_of(b * tall, 16), tall)
            joined = qkv_ref[j, at, :]
            q_pair, k_pair, v_pair = joined[:, :128], joined[:, 128:256], joined[:, 256:384]
            qk_last, v_last = joined[:, 384:512], joined[:, 512:640]
            heads = ho_ref[j, at, :].astype(f32)
            grad = dho_ref[at, :].astype(bf16).astype(f32)
            product = grad * heads
            pair = product[:, 128:]
            dots = (
                jnp.sum(jnp.where(low, pair, 0.0), axis=1, keepdims=True),
                jnp.sum(jnp.where(low, 0.0, pair), axis=1, keepdims=True),
                jnp.sum(product[:, :128], axis=1, keepdims=True),
            )
            grad_pair = grad[:, 128:]
            grad_last = jnp.where(low, pltpu.roll(grad[:, :128], HEAD_DIM, 1), 0.0).astype(bf16)
            gq, gk, gv = [], [], []
            for head, (g, v, q, k) in enumerate(
                (
                    (jnp.where(low, grad_pair, 0.0).astype(bf16), v_pair, q_pair, k_pair),
                    (jnp.where(low, 0.0, grad_pair).astype(bf16), v_pair, q_pair, k_pair),
                    (grad_last, v_last, qk_last, qk_last),
                )
            ):
                probs = p_ref[j, b, head]
                grad_p = mm_nt(g, v)
                grad_s = (probs.astype(f32) * (grad_p - dots[head])).astype(bf16)
                gq.append(mm(grad_s, k))
                gk.append(mm_tn(grad_s, q))
                gv.append(mm_tn(probs, g))
            last = pltpu.roll(jnp.where(low, gk[2], gq[2]), HEAD_DIM, 1)
            gj_ref[at, :] = jnp.concatenate(
                [
                    jnp.where(low, gq[0], gq[1]) * scale,
                    jnp.where(low, gk[0], gk[1]) * scale,
                    gv[0] + gv[1],
                    last * scale,
                    gv[2],
                ],
                1,
            ).astype(bf16)
            return inner

        lax.fori_loop(0, images, image, 0, unroll=True)
        grad_out = mm(gbt_ref[...], ho_ref[j])
        grad_in = mm(ht_ref[...], gj_ref[...])
        gw_ref[j, :, :512] = grad_in[:, :512].astype(bf16)
        gw_ref[j, :, 512:640] = (grad_in[:, 512:] + grad_out[:, :128]).astype(bf16)
        gw_ref[j, :, 640:] = grad_out[:, 128:].astype(bf16)
        gh_ref[...] += mm_nt(gj_ref[...], w_ref[j, :, :JOINED])
        return carry

    lax.fori_loop(0, groups, group, 0)


def last_kernel(x_ref, gres_ref, gh_ref, gain_ref, gt_ref, ggain_ref, *, images, seq, tall):
    total = jnp.zeros(ggain_ref.shape, f32)
    for b in range(images):
        at = pl.ds(b * tall, seq)
        unit, inverse = unit_of(x_ref[b].astype(f32))
        grad_h = gh_ref[at, :]
        total += jnp.sum(grad_h * unit, axis=0, keepdims=True)
        scaled = grad_h * gain_ref[...]
        mean_grad = jnp.mean(scaled, axis=-1, keepdims=True)
        mean_proj = jnp.mean(scaled * unit, axis=-1, keepdims=True)
        gt_ref[b] = gres_ref[at, :] + inverse * (scaled - mean_grad - unit * mean_proj)
    ggain_ref[...] = total


def call(kernel, outs, args, scratch=(), flops=0, name=None, **static):
    spec = pl.BlockSpec(memory_space=pltpu.VMEM)
    moved = sum(math.prod(a.shape) * a.dtype.itemsize for a in args)
    return pl.pallas_call(
        functools.partial(kernel, **static),
        out_shape=[jax.ShapeDtypeStruct(s, d) for s, d in outs],
        in_specs=[spec] * len(args),
        out_specs=[spec] * len(outs),
        scratch_shapes=list(scratch),
        compiler_params=pltpu.CompilerParams(vmem_limit_bytes=60 << 20),
        cost_estimate=pl.CostEstimate(flops=flops, bytes_accessed=moved, transcendentals=0),
        name=name,
    )(*args)


def assemble_kernel(me_ref, a_ref, a_other_ref, b_ref, b_other_ref, w_ref):
    me = me_ref[0]
    half_groups, dp, half = a_ref.shape[0], a_ref.shape[1], a_ref.shape[2]
    for d in range(dp):
        r = jnp.bitwise_xor(me, d)
        for g in range(half_groups):
            for core, (first, second) in enumerate(((a_ref, b_ref), (a_other_ref, b_other_ref))):
                for part, ref in enumerate((first, second)):
                    at = (2 * d + part) * half
                    w_ref[2 * g + core, at : at + half, :] = ref[g, r]


def spread_kernel(me_ref, gw_ref, out_ref):
    me = me_ref[0]
    groups, dp, rows = out_ref.shape[0], out_ref.shape[1], out_ref.shape[2]
    for d in range(dp):
        r = jnp.bitwise_xor(me, d)
        for j in range(groups):
            out_ref[j, r] = gw_ref[j, d * rows : (d + 1) * rows, :]


def make(mesh):
    dp, mp = mesh.shape["dp"], mesh.shape["mp"]

    def per_device(
        tokens, token_mask, gain_one, w_qkv, w_out, gain_two, router, w_in, w_back, cotangent
    ):
        rows, width = tokens.shape
        seq = token_mask.shape[1]
        tall = -(-seq // 16) * 16
        images = rows // seq
        experts = router.shape[1]
        d_rows, _, part = w_qkv.shape
        half = d_rows // 2
        count = images * tall
        static = {"images": images, "seq": seq, "tall": tall}
        me = lax.axis_index("dp")
        at_mp = lax.axis_index("mp")
        me_word = me.astype(jnp.int32).reshape(1)

        low_dim, mid = 2 * HEAD_DIM, part
        wo = w_out.T
        packed = jnp.concatenate(
            [w_qkv[:, c, :low_dim] for c in range(3)]
            + [w_qkv[:, c, low_dim:mid] for c in range(3)]
            + [wo[:, low_dim:mid], wo[:, :low_dim]],
            axis=1,
        )
        extra = jnp.concatenate([gain_one[None], gain_two[None], router.T], axis=0)
        held = extra
        for depth, bit in enumerate(bits_of(dp)):
            other = swap(held, "dp", dp, bit)
            held = jnp.stack([held, other], depth)
        extra = held.reshape((dp,) + extra.shape)
        for bit in bits_of(dp):
            pairs = extra.reshape((dp // (2 * bit), 2, bit) + extra.shape[1:])
            extra = jnp.where((me & bit) > 0, pairs[:, ::-1], pairs).reshape(extra.shape)
        extra = extra.transpose(1, 0, 2).reshape(experts + 2, width)
        gain_a, gain_b = extra[:1].astype(f32), extra[1:2].astype(f32)
        route_w = extra[2:]

        first, first_other = gather_pair(packed[:half], dp, mp, False)
        second, second_other = gather_pair(packed[half:], dp, mp, True)
        spec = pl.BlockSpec(memory_space=pltpu.VMEM)
        weights = pl.pallas_call(
            assemble_kernel,
            out_shape=jax.ShapeDtypeStruct((mp, width, 4 * part), bf16),
            in_specs=[pl.BlockSpec(memory_space=pltpu.SMEM)] + [spec] * 4,
            out_specs=spec,
            name="assemble",
        )(me_word, first, first_other, second, second_other)

        mask = lax.dynamic_slice_in_dim(token_mask, at_mp * images, images, 0)
        mask = jnp.pad(mask, ((0, 0), (0, tall - seq))).astype(f32)
        bias = jnp.where(mask > 0, 0.0, -1e30)[:, None, :]
        column = mask[:, :, None]
        mask_row = mask[:, None, :]
        valid = jnp.sum(mask, axis=1) * width
        x3 = tokens.reshape(images, seq, width)
        cot3 = cotangent.reshape(images, seq, width)

        h_one, joined, probs, heads_out, branch = call(
            front_kernel,
            [
                ((count, width), bf16),
                ((mp, count, JOINED), bf16),
                ((mp, images, part // HEAD_DIM, tall, tall), bf16),
                ((mp, count, 256), bf16),
                ((count, width), f32),
            ],
            (x3, bias, gain_a, weights),
            flops=4_000_000_000,
            name="front",
            **static,
        )
        resid, h_two, soft, sent, sq_branch = call(
            route_kernel,
            [
                ((count, width), f32),
                ((count, width), bf16),
                ((2, images, experts, tall), f32),
                ((2, images, experts, width), bf16),
                ((images, 1, 128), f32),
            ],
            (x3, branch, cot3, mask_row, column, gain_b, route_w),
            flops=100_000_000,
            name="route",
            **static,
        )
        got = sent.transpose(2, 0, 1, 3)
        got = lax.all_to_all(got, "dp", split_axis=0, concat_axis=0, tiled=True)
        got = gather_mp(got, mp).transpose(2, 0, 1, 3, 4).reshape(2, -1, width)
        slot_in, grad_expert = got[0], got[1]
        hidden, grad_pre, back = call(
            expert_kernel,
            [
                (slot_in.shape[:1] + w_in.shape[2:], bf16),
                (slot_in.shape[:1] + w_in.shape[2:], bf16),
                ((2,) + slot_in.shape, bf16),
            ],
            (slot_in, grad_expert, w_in[0], w_back[0]),
            flops=500_000_000,
            name="expert",
        )
        back = back.reshape(2, mp, dp, images, width).transpose(1, 2, 0, 3, 4)
        back = scatter(back, "mp", mp, [1, 2])
        back = lax.all_to_all(back, "dp", split_axis=0, concat_axis=0, tiled=True)
        back = back.transpose(1, 2, 0, 3)
        grad_w_back = mm_tn(hidden, grad_expert)
        grad_w_in = mm_tn(slot_in, grad_pre)

        out_rows, grad_resid, grad_router, grad_gain_two, sq_rest = call(
            mix_kernel,
            [
                ((images, seq, width), bf16),
                ((count, width), f32),
                ((experts, width), f32),
                ((1, width), f32),
                ((2, images, 1, 128), f32),
            ],
            (resid, h_two, soft, cot3, column, gain_b, route_w, back),
            flops=100_000_000,
            name="mix",
            **static,
        )
        grads, grad_h = call(
            back_kernel,
            [((mp, width, 4 * part), bf16), ((count, width), f32)],
            (grad_resid, h_one, joined, probs, heads_out, weights),
            [
                pltpu.VMEM((count, width), bf16),
                pltpu.VMEM((count, JOINED), bf16),
                pltpu.VMEM((count, 256), f32),
                pltpu.VMEM((width, count), bf16),
                pltpu.VMEM((width, count), bf16),
            ],
            flops=8_000_000_000,
            name="back",
            **static,
        )
        grad_tokens, grad_gain_one = call(
            last_kernel,
            [((images, seq, width), f32), ((1, width), f32)],
            (x3, grad_resid, grad_h, gain_a),
            flops=10_000_000,
            name="last",
            **static,
        )
        grads = pl.pallas_call(
            spread_kernel,
            out_shape=jax.ShapeDtypeStruct((mp, dp, d_rows, 4 * part), bf16),
            in_specs=[pl.BlockSpec(memory_space=pltpu.SMEM), spec],
            out_specs=spec,
            name="spread",
        )(me_word, grads)
        summed = scatter(grads, "mp", mp, [1, 2])
        summed = scatter(summed, "dp", dp, bits_of(dp)[-1:] + bits_of(dp)[:-1]).astype(f32)

        squares = jnp.concatenate([sq_rest[:1, :, 0, 0], sq_branch[None, :, 0, 0], sq_rest[1:, :, 0, 0]])
        squares = jnp.sqrt(squares / valid[None])
        own = lax.broadcasted_iota(jnp.int32, (1, mp, 1), 1) == at_mp
        squares = jnp.where(own, squares[:, None, :], 0.0).reshape(1, -1)
        squares = jnp.pad(squares, ((0, 0), (0, width - squares.shape[1])))
        small = jnp.concatenate([grad_gain_one, grad_gain_two, grad_router, squares], axis=0)
        for bit in bits_of(mp)[::-1]:
            small = small + swap(small, "mp", mp, bit)
        root_squares = small[-1, : 3 * mp * images].reshape(3, mp * images)
        for bit in bits_of(dp)[::-1]:
            small = small + swap(small, "dp", dp, bit)
        small = lax.dynamic_slice_in_dim(small, me * d_rows, d_rows, 1)
        grad_qkv = jnp.stack(
            [
                jnp.concatenate(
                    [
                        summed[:, c * low_dim : (c + 1) * low_dim],
                        summed[:, 3 * low_dim + c * HEAD_DIM : 3 * low_dim + (c + 1) * HEAD_DIM],
                    ],
                    axis=1,
                )
                for c in range(3)
            ],
            axis=1,
        )
        grad_out = jnp.concatenate([summed[:, 640:], summed[:, 576:640]], axis=1).T
        return (
            out_rows.reshape(rows, width),
            grad_tokens.reshape(rows, width),
            small[0],
            grad_qkv,
            grad_out,
            small[1],
            small[2:-1].T,
            grad_w_in[None],
            grad_w_back[None],
            root_squares,
        )

    return per_device


def solution(mesh):
    in_specs = (
        P(("dp", "mp"), None),
        P("dp", None),
        P("dp"),
        P("dp", None, "mp"),
        P("mp", "dp"),
        P("dp"),
        P("dp", None),
        P("dp", None, "mp"),
        P("dp", "mp", None),
        P(("dp", "mp"), None),
    )
    out_specs = (
        P(("dp", "mp"), None),
        P(("dp", "mp"), None),
        P("dp"),
        P("dp", None, "mp"),
        P("mp", "dp"),
        P("dp"),
        P("dp", None),
        P("dp", None, "mp"),
        P("dp", "mp", None),
        P(None, "dp"),
    )
    return jax.shard_map(
        make(mesh), mesh=mesh, in_specs=in_specs, out_specs=out_specs, check_vma=False
    )
```

```python
import functools
import math

import jax
import jax.numpy as jnp
from jax import lax
from jax.experimental import pallas as pl
from jax.experimental.pallas import tpu as pltpu
from jax.sharding import PartitionSpec as P

HEAD_DIM = 64


epsilon = 1e-06
bf16 = jnp.bfloat16
f32 = jnp.float32


def swap(array_in, axis_name, size, bit):
    return lax.ppermute(array_in, axis_name, [(i, i ^ bit) for i in range(size)])


def bits_of(size):
    return [1 << k for k in reversed(range(size.bit_length() - 1))]


def gather_pair(block, dp, mp, late):
    held = block
    depth = 0
    bits = bits_of(dp)
    for bit in bits[:-1] if late else bits:
        held = jnp.stack([held, swap(held, "dp", dp, bit)], depth)
        depth += 1
    held = jnp.stack([held, swap(held, "mp", mp, 2)], 0)
    if late:
        held = jnp.stack([held, swap(held, "dp", dp, bits[-1])], depth + 1)
    held = held.reshape((mp // 2, dp) + block.shape)
    return held, swap(held, "mp", mp, 1)


def gather_mp(block, mp):
    held = block[None]
    for bit in bits_of(mp):
        other = swap(held, "mp", mp, bit)
        held = jnp.stack([held, other], 1).reshape((-1,) + block.shape)
    return held


def scatter(held, axis_name, size, bits):
    left = sorted(bits)
    for bit in bits:
        inner = 1 << left.index(bit)
        left.remove(bit)
        pairs = held.reshape((held.shape[0] // (2 * inner), 2, inner) + held.shape[1:])
        other = swap(pairs[:, 1], axis_name, size, bit)
        held = pairs[:, 0].astype(f32) + other.astype(f32)
        held = held.astype(bf16).reshape((-1,) + held.shape[2:])
    return held[0]


def mm(a, b):
    return lax.dot_general(a, b, (((1,), (0,)), ((), ())), preferred_element_type=f32)


def mm_nt(a, b):
    return lax.dot_general(a, b, (((1,), (1,)), ((), ())), preferred_element_type=f32)


def mm_tn(a, b):
    return lax.dot_general(a, b, (((0,), (0,)), ((), ())), preferred_element_type=f32)


def unit_of(rows_f):
    mean_row = jnp.mean(rows_f, axis=-1, keepdims=True)
    centered = rows_f - mean_row
    variance = jnp.mean(centered * centered, axis=-1, keepdims=True)
    inverse = lax.rsqrt(variance + epsilon)
    return centered * inverse, inverse


def padded(value, pad):
    return jnp.concatenate([value, jnp.zeros((pad, value.shape[1]), value.dtype)], 0)


def low_lanes(rows):
    return lax.broadcasted_iota(jnp.int32, (rows, 128), 1) < HEAD_DIM


JOINED = 640


def front_kernel(
    x_ref, bias_ref, gain_ref, w_ref, h_ref, qkv_ref, p_ref, ho_ref, br_ref, *, images, seq, tall
):
    groups = w_ref.shape[0]
    scale = HEAD_DIM ** (-0.5)
    for b in range(images):
        unit, _ = unit_of(x_ref[b].astype(f32))
        h_ref[pl.ds(b * tall, tall), :] = padded((unit * gain_ref[...]).astype(bf16), tall - seq)
    br_ref[...] = jnp.zeros_like(br_ref)
    low = low_lanes(tall)

    def group(j, carry):
        qkv_ref[j] = mm(h_ref[...], w_ref[j, :, :JOINED]).astype(bf16)

        def image(b, inner):
            at = pl.ds(pl.multiple_of(b * tall, 16), tall)
            joined = qkv_ref[j, at, :]
            q_pair, k_pair, v_pair = joined[:, :128], joined[:, 128:256], joined[:, 256:384]
            qk_last, v_last = joined[:, 384:512], joined[:, 512:640]
            k_last = pltpu.roll(qk_last.astype(f32), HEAD_DIM, 1).astype(bf16)
            none = jnp.zeros_like(q_pair)
            bias = bias_ref[b]
            outs = []
            for head, (q, k, v) in enumerate(
                (
                    (jnp.where(low, q_pair, none), k_pair, v_pair),
                    (jnp.where(low, none, q_pair), k_pair, v_pair),
                    (jnp.where(low, qk_last, none), k_last, v_last),
                )
            ):
                scores = mm_nt(q, k) * scale + bias
                terms = jnp.exp(scores - jnp.max(scores, axis=-1, keepdims=True))
                probs = (terms * (1.0 / jnp.sum(terms, axis=-1, keepdims=True))).astype(bf16)
                p_ref[j, b, head] = probs
                outs.append(mm(probs, v))
            last = jnp.where(low, 0.0, pltpu.roll(outs[2], HEAD_DIM, 1))
            pair = jnp.where(low, outs[0], outs[1])
            ho_ref[j, at, :] = jnp.concatenate([last, pair], 1).astype(bf16)
            return inner

        lax.fori_loop(0, images, image, 0, unroll=True)
        br_ref[...] += mm_nt(ho_ref[j], w_ref[j, :, 512:])
        return carry

    lax.fori_loop(0, groups, group, 0)


def route_kernel(
    x_ref, br_ref, cot_ref, mask_ref, column_ref, gain_ref, router_ref,
    res_ref, h_ref, soft_ref, sent_ref, sq_ref, *, images, seq, tall
):
    for b in range(images):
        at = pl.ds(b * tall, tall)
        branch = br_ref[at, :]
        resid = padded(x_ref[b].astype(f32), tall - seq) + branch
        res_ref[at, :] = resid
        unit, _ = unit_of(resid)
        h_two = (unit * gain_ref[...]).astype(bf16)
        h_ref[at, :] = h_two
        logits = mm_nt(router_ref[...], h_two)
        seen = mask_ref[b] > 0
        held = jnp.where(seen, logits, -1e30)
        terms = jnp.exp(held - jnp.max(held, axis=1, keepdims=True))
        dispatch = terms / jnp.sum(terms, axis=1, keepdims=True)
        terms = jnp.exp(logits - jnp.max(logits, axis=0, keepdims=True))
        combine = terms / jnp.sum(terms, axis=0, keepdims=True)
        soft_ref[0, b] = dispatch
        soft_ref[1, b] = combine
        cot = padded(cot_ref[b], tall - seq)
        sent_ref[0, b] = mm(dispatch.astype(bf16), h_two).astype(bf16)
        sent_ref[1, b] = mm(combine.astype(bf16), cot).astype(bf16)
        squares = jnp.sum(branch * branch, axis=1, keepdims=True)
        sq_ref[b] = jnp.broadcast_to(
            jnp.sum(squares * column_ref[b], axis=0, keepdims=True), (1, 128)
        )


def expert_kernel(slot_ref, grad_ref, first_ref, second_ref, hid_ref, pre_ref, back_ref):
    slots, grads = slot_ref[...], grad_ref[...]
    u = mm(slots, first_ref[...])
    cubic = 0.7978845608028654 * (u + 0.044715 * u * u * u)
    t = jnp.tanh(cubic)
    hidden = (0.5 * u * (1.0 + t)).astype(bf16)
    hid_ref[...] = hidden
    back_ref[0] = mm(hidden, second_ref[...]).astype(bf16)
    slope = 0.5 * (1.0 + t) + 0.5 * u * (1.0 - t * t) * 0.7978845608028654 * (
        1.0 + 3.0 * 0.044715 * u * u
    )
    grad_pre = (mm_nt(grads, second_ref[...]) * slope).astype(bf16)
    pre_ref[...] = grad_pre
    back_ref[1] = mm_nt(grad_pre, first_ref[...]).astype(bf16)


def mix_kernel(
    res_ref, h_ref, soft_ref, cot_ref, column_ref, gain_ref, router_ref, back_ref,
    out_ref, gres_ref, grouter_ref, ggain_ref, sq_ref, *, images, seq, tall
):
    grouter_ref[...] = jnp.zeros_like(grouter_ref)
    ggain_ref[...] = jnp.zeros_like(ggain_ref)
    for b in range(images):
        at = pl.ds(b * tall, tall)
        resid, h_two = res_ref[at, :], h_ref[at, :]
        dispatch, combine = soft_ref[0, b], soft_ref[1, b]
        dispatch_low, combine_low = dispatch.astype(bf16), combine.astype(bf16)
        returned, grad_slots = back_ref[0, b], back_ref[1, b]
        cot = padded(cot_ref[b], tall - seq)
        mixed = mm_tn(combine_low, returned)
        stream = resid + mixed
        out_ref[b] = stream[:seq].astype(bf16)
        column = column_ref[b]
        for k, value in enumerate((stream, mixed)):
            squares = jnp.sum(value * value, axis=1, keepdims=True)
            sq_ref[k, b] = jnp.broadcast_to(
                jnp.sum(squares * column, axis=0, keepdims=True), (1, 128)
            )
        grad_c = mm_nt(returned, cot)
        grad_c = combine * (grad_c - jnp.sum(grad_c * combine, axis=0, keepdims=True))
        grad_d = mm_nt(grad_slots, h_two)
        grad_d = dispatch * (grad_d - jnp.sum(grad_d * dispatch, axis=1, keepdims=True))
        grad_logits = (grad_d + grad_c).astype(bf16)
        grad_h = mm_tn(dispatch_low, grad_slots) + mm_tn(grad_logits, router_ref[...])
        grouter_ref[...] += mm(grad_logits, h_two)
        unit, inverse = unit_of(resid)
        ggain_ref[...] += jnp.sum(grad_h * unit, axis=0, keepdims=True)
        scaled = grad_h * gain_ref[...]
        mean_grad = jnp.mean(scaled, axis=-1, keepdims=True)
        mean_proj = jnp.mean(scaled * unit, axis=-1, keepdims=True)
        gres_ref[at, :] = cot.astype(f32) + inverse * (scaled - mean_grad - unit * mean_proj)


def back_kernel(
    gres_ref, h_ref, qkv_ref, p_ref, ho_ref, w_ref,
    gw_ref, gh_ref, gb_ref, gj_ref, dho_ref, gbt_ref, ht_ref, *, images, seq, tall
):
    groups = w_ref.shape[0]
    scale = HEAD_DIM ** (-0.5)
    gb_ref[...] = gres_ref[...].astype(bf16)
    gbt_ref[...] = gres_ref[...].T.astype(bf16)
    ht_ref[...] = h_ref[...].T
    gh_ref[...] = jnp.zeros_like(gh_ref)
    low = low_lanes(tall)

    def group(j, carry):
        dho_ref[...] = mm(gb_ref[...], w_ref[j, :, 512:])

        def image(b, inner):
            at = pl.ds(pl.multiple_of(b * tall, 16), tall)
            joined = qkv_ref[j, at, :]
            q_pair, k_pair, v_pair = joined[:, :128], joined[:, 128:256], joined[:, 256:384]
            qk_last, v_last = joined[:, 384:512], joined[:, 512:640]
            heads = ho_ref[j, at, :].astype(f32)
            grad = dho_ref[at, :].astype(bf16).astype(f32)
            product = grad * heads
            pair = product[:, 128:]
            dots = (
                jnp.sum(jnp.where(low, pair, 0.0), axis=1, keepdims=True),
                jnp.sum(jnp.where(low, 0.0, pair), axis=1, keepdims=True),
                jnp.sum(product[:, :128], axis=1, keepdims=True),
            )
            grad_pair = grad[:, 128:]
            grad_last = jnp.where(low, pltpu.roll(grad[:, :128], HEAD_DIM, 1), 0.0).astype(bf16)
            gq, gk, gv = [], [], []
            for head, (g, v, q, k) in enumerate(
                (
                    (jnp.where(low, grad_pair, 0.0).astype(bf16), v_pair, q_pair, k_pair),
                    (jnp.where(low, 0.0, grad_pair).astype(bf16), v_pair, q_pair, k_pair),
                    (grad_last, v_last, qk_last, qk_last),
                )
            ):
                probs = p_ref[j, b, head]
                grad_p = mm_nt(g, v)
                grad_s = (probs.astype(f32) * (grad_p - dots[head])).astype(bf16)
                gq.append(mm(grad_s, k))
                gk.append(mm_tn(grad_s, q))
                gv.append(mm_tn(probs, g))
            last = pltpu.roll(jnp.where(low, gk[2], gq[2]), HEAD_DIM, 1)
            gj_ref[at, :] = jnp.concatenate(
                [
                    jnp.where(low, gq[0], gq[1]) * scale,
                    jnp.where(low, gk[0], gk[1]) * scale,
                    gv[0] + gv[1],
                    last * scale,
                    gv[2],
                ],
                1,
            ).astype(bf16)
            return inner

        lax.fori_loop(0, images, image, 0, unroll=True)
        grad_out = mm(gbt_ref[...], ho_ref[j])
        grad_in = mm(ht_ref[...], gj_ref[...])
        gw_ref[j, :, :512] = grad_in[:, :512].astype(bf16)
        gw_ref[j, :, 512:640] = (grad_in[:, 512:] + grad_out[:, :128]).astype(bf16)
        gw_ref[j, :, 640:] = grad_out[:, 128:].astype(bf16)
        gh_ref[...] += mm_nt(gj_ref[...], w_ref[j, :, :JOINED])
        return carry

    lax.fori_loop(0, groups, group, 0)


def last_kernel(x_ref, gres_ref, gh_ref, gain_ref, gt_ref, ggain_ref, *, images, seq, tall):
    total = jnp.zeros(ggain_ref.shape, f32)
    for b in range(images):
        at = pl.ds(b * tall, seq)
        unit, inverse = unit_of(x_ref[b].astype(f32))
        grad_h = gh_ref[at, :]
        total += jnp.sum(grad_h * unit, axis=0, keepdims=True)
        scaled = grad_h * gain_ref[...]
        mean_grad = jnp.mean(scaled, axis=-1, keepdims=True)
        mean_proj = jnp.mean(scaled * unit, axis=-1, keepdims=True)
        gt_ref[b] = gres_ref[at, :] + inverse * (scaled - mean_grad - unit * mean_proj)
    ggain_ref[...] = total


def static_limit(name):
    return {'front':26<<20,'route':14<<20,'expert':10<<20,'mix':16<<20,'back':34<<20,'last':14<<20}[name]


def call(kernel, outs, args, scratch=(), flops=0, name=None, **static):
    spec = pl.BlockSpec(memory_space=pltpu.VMEM)
    moved = sum(math.prod(a.shape) * a.dtype.itemsize for a in args)
    return pl.pallas_call(
        functools.partial(kernel, **static),
        out_shape=[jax.ShapeDtypeStruct(s, d) for s, d in outs],
        in_specs=[spec] * len(args),
        out_specs=[spec] * len(outs),
        scratch_shapes=list(scratch),
        compiler_params=pltpu.CompilerParams(vmem_limit_bytes=static_limit(name)),
        cost_estimate=pl.CostEstimate(flops=flops, bytes_accessed=moved, transcendentals=0),
        name=name,
    )(*args)


def assemble_kernel(me_ref, a_ref, a_other_ref, b_ref, b_other_ref, w_ref):
    me = me_ref[0]
    half_groups, dp, half = a_ref.shape[0], a_ref.shape[1], a_ref.shape[2]
    for d in range(dp):
        r = jnp.bitwise_xor(me, d)
        for g in range(half_groups):
            for core, (first, second) in enumerate(((a_ref, b_ref), (a_other_ref, b_other_ref))):
                for part, ref in enumerate((first, second)):
                    at = (2 * d + part) * half
                    w_ref[2 * g + core, at : at + half, :] = ref[g, r]


def spread_kernel(me_ref, gw_ref, out_ref):
    me = me_ref[0]
    groups, dp, rows = out_ref.shape[0], out_ref.shape[1], out_ref.shape[2]
    for d in range(dp):
        r = jnp.bitwise_xor(me, d)
        for j in range(groups):
            out_ref[j, r] = gw_ref[j, d * rows : (d + 1) * rows, :]


def make(mesh):
    dp, mp = mesh.shape["dp"], mesh.shape["mp"]

    def per_device(
        tokens, token_mask, gain_one, w_qkv, w_out, gain_two, router, w_in, w_back, cotangent
    ):
        rows, width = tokens.shape
        seq = token_mask.shape[1]
        tall = -(-seq // 16) * 16
        images = rows // seq
        experts = router.shape[1]
        d_rows, _, part = w_qkv.shape
        half = d_rows // 2
        count = images * tall
        static = {"images": images, "seq": seq, "tall": tall}
        me = lax.axis_index("dp")
        at_mp = lax.axis_index("mp")
        me_word = me.astype(jnp.int32).reshape(1)

        low_dim, mid = 2 * HEAD_DIM, part
        wo = w_out.T
        packed = jnp.concatenate(
            [w_qkv[:, c, :low_dim] for c in range(3)]
            + [w_qkv[:, c, low_dim:mid] for c in range(3)]
            + [wo[:, low_dim:mid], wo[:, :low_dim]],
            axis=1,
        )
        extra = jnp.concatenate([gain_one[None], gain_two[None], router.T], axis=0)
        held = extra
        for depth, bit in enumerate(bits_of(dp)):
            other = swap(held, "dp", dp, bit)
            held = jnp.stack([held, other], depth)
        extra = held.reshape((dp,) + extra.shape)
        for bit in bits_of(dp):
            pairs = extra.reshape((dp // (2 * bit), 2, bit) + extra.shape[1:])
            extra = jnp.where((me & bit) > 0, pairs[:, ::-1], pairs).reshape(extra.shape)
        extra = extra.transpose(1, 0, 2).reshape(experts + 2, width)
        gain_a, gain_b = extra[:1].astype(f32), extra[1:2].astype(f32)
        route_w = extra[2:]

        first, first_other = gather_pair(packed[:half], dp, mp, False)
        second, second_other = gather_pair(packed[half:], dp, mp, True)
        spec = pl.BlockSpec(memory_space=pltpu.VMEM)
        weights = pl.pallas_call(
            assemble_kernel,
            out_shape=jax.ShapeDtypeStruct((mp, width, 4 * part), bf16),
            in_specs=[pl.BlockSpec(memory_space=pltpu.SMEM)] + [spec] * 4,
            out_specs=spec,
            name="assemble",
        )(me_word, first, first_other, second, second_other)

        mask = lax.dynamic_slice_in_dim(token_mask, at_mp * images, images, 0)
        mask = jnp.pad(mask, ((0, 0), (0, tall - seq))).astype(f32)
        bias = jnp.where(mask > 0, 0.0, -1e30)[:, None, :]
        column = mask[:, :, None]
        mask_row = mask[:, None, :]
        valid = jnp.sum(mask, axis=1) * width
        x3 = tokens.reshape(images, seq, width)
        cot3 = cotangent.reshape(images, seq, width)

        h_one, joined, probs, heads_out, branch = call(
            front_kernel,
            [
                ((count, width), bf16),
                ((mp, count, JOINED), bf16),
                ((mp, images, part // HEAD_DIM, tall, tall), bf16),
                ((mp, count, 256), bf16),
                ((count, width), f32),
            ],
            (x3, bias, gain_a, weights),
            flops=4_000_000_000,
            name="front",
            **static,
        )
        resid, h_two, soft, sent, sq_branch = call(
            route_kernel,
            [
                ((count, width), f32),
                ((count, width), bf16),
                ((2, images, experts, tall), f32),
                ((2, images, experts, width), bf16),
                ((images, 1, 128), f32),
            ],
            (x3, branch, cot3, mask_row, column, gain_b, route_w),
            flops=100_000_000,
            name="route",
            **static,
        )
        got = sent.transpose(2, 0, 1, 3)
        got = lax.all_to_all(got, "dp", split_axis=0, concat_axis=0, tiled=True)
        got = gather_mp(got, mp).transpose(2, 0, 1, 3, 4).reshape(2, -1, width)
        slot_in, grad_expert = got[0], got[1]
        hidden, grad_pre, back = call(
            expert_kernel,
            [
                (slot_in.shape[:1] + w_in.shape[2:], bf16),
                (slot_in.shape[:1] + w_in.shape[2:], bf16),
                ((2,) + slot_in.shape, bf16),
            ],
            (slot_in, grad_expert, w_in[0], w_back[0]),
            flops=500_000_000,
            name="expert",
        )
        back = back.reshape(2, mp, dp, images, width).transpose(1, 2, 0, 3, 4)
        back = scatter(back, "mp", mp, [1, 2])
        back = lax.all_to_all(back, "dp", split_axis=0, concat_axis=0, tiled=True)
        back = back.transpose(1, 2, 0, 3)
        grad_w_back = mm_tn(hidden, grad_expert)
        grad_w_in = mm_tn(slot_in, grad_pre)

        out_rows, grad_resid, grad_router, grad_gain_two, sq_rest = call(
            mix_kernel,
            [
                ((images, seq, width), bf16),
                ((count, width), f32),
                ((experts, width), f32),
                ((1, width), f32),
                ((2, images, 1, 128), f32),
            ],
            (resid, h_two, soft, cot3, column, gain_b, route_w, back),
            flops=100_000_000,
            name="mix",
            **static,
        )
        grads, grad_h = call(
            back_kernel,
            [((mp, width, 4 * part), bf16), ((count, width), f32)],
            (grad_resid, h_one, joined, probs, heads_out, weights),
            [
                pltpu.VMEM((count, width), bf16),
                pltpu.VMEM((count, JOINED), bf16),
                pltpu.VMEM((count, 256), f32),
                pltpu.VMEM((width, count), bf16),
                pltpu.VMEM((width, count), bf16),
            ],
            flops=8_000_000_000,
            name="back",
            **static,
        )
        grad_tokens, grad_gain_one = call(
            last_kernel,
            [((images, seq, width), f32), ((1, width), f32)],
            (x3, grad_resid, grad_h, gain_a),
            flops=10_000_000,
            name="last",
            **static,
        )
        grads = pl.pallas_call(
            spread_kernel,
            out_shape=jax.ShapeDtypeStruct((mp, dp, d_rows, 4 * part), bf16),
            in_specs=[pl.BlockSpec(memory_space=pltpu.SMEM), spec],
            out_specs=spec,
            name="spread",
        )(me_word, grads)
        summed = scatter(grads, "mp", mp, [1, 2])
        summed = scatter(summed, "dp", dp, bits_of(dp)[-1:] + bits_of(dp)[:-1]).astype(f32)

        squares = jnp.concatenate([sq_rest[:1, :, 0, 0], sq_branch[None, :, 0, 0], sq_rest[1:, :, 0, 0]])
        squares = jnp.sqrt(squares / valid[None])
        own = lax.broadcasted_iota(jnp.int32, (1, mp, 1), 1) == at_mp
        squares = jnp.where(own, squares[:, None, :], 0.0).reshape(1, -1)
        squares = jnp.pad(squares, ((0, 0), (0, width - squares.shape[1])))
        small = jnp.concatenate([grad_gain_one, grad_gain_two, grad_router, squares], axis=0)
        for bit in bits_of(mp)[::-1]:
            small = small + swap(small, "mp", mp, bit)
        root_squares = small[-1, : 3 * mp * images].reshape(3, mp * images)
        for bit in bits_of(dp)[::-1]:
            small = small + swap(small, "dp", dp, bit)
        small = lax.dynamic_slice_in_dim(small, me * d_rows, d_rows, 1)
        grad_qkv = jnp.stack(
            [
                jnp.concatenate(
                    [
                        summed[:, c * low_dim : (c + 1) * low_dim],
                        summed[:, 3 * low_dim + c * HEAD_DIM : 3 * low_dim + (c + 1) * HEAD_DIM],
                    ],
                    axis=1,
                )
                for c in range(3)
            ],
            axis=1,
        )
        grad_out = jnp.concatenate([summed[:, 640:], summed[:, 576:640]], axis=1).T
        return (
            out_rows.reshape(rows, width),
            grad_tokens.reshape(rows, width),
            small[0],
            grad_qkv,
            grad_out,
            small[1],
            small[2:-1].T,
            grad_w_in[None],
            grad_w_back[None],
            root_squares,
        )

    return per_device


def solution(mesh):
    in_specs = (
        P(("dp", "mp"), None),
        P("dp", None),
        P("dp"),
        P("dp", None, "mp"),
        P("mp", "dp"),
        P("dp"),
        P("dp", None),
        P("dp", None, "mp"),
        P("dp", "mp", None),
        P(("dp", "mp"), None),
    )
    out_specs = (
        P(("dp", "mp"), None),
        P(("dp", "mp"), None),
        P("dp"),
        P("dp", None, "mp"),
        P("mp", "dp"),
        P("dp"),
        P("dp", None),
        P("dp", None, "mp"),
        P("dp", "mp", None),
        P(None, "dp"),
    )
    return jax.shard_map(
        make(mesh), mesh=mesh, in_specs=in_specs, out_specs=out_specs, check_vma=False
    )
```

```python
import functools
import math

import jax
import jax.numpy as jnp
from jax import lax
from jax.experimental import pallas as pl
from jax.experimental.pallas import tpu as pltpu
from jax.sharding import PartitionSpec as P

HEAD_DIM = 64


epsilon = 1e-06
bf16 = jnp.bfloat16
f32 = jnp.float32


def bits_of(size):
    return [1 << k for k in reversed(range(size.bit_length() - 1))]


def swap(array_in, axis_name, size, bit):
    return lax.ppermute(array_in, axis_name, [(i, i ^ bit) for i in range(size)])


def swap_both(array_in, dp, mp, even, odd):
    pairs = []
    for d in range(dp):
        for m in range(mp):
            flip = odd if m & 1 else even
            pairs.append((d * mp + m, (d ^ flip[0]) * mp + (m ^ flip[1])))
    return lax.ppermute(array_in, ("dp", "mp"), pairs)


def gather_mp(block, mp):
    held = block[None]
    for bit in bits_of(mp):
        other = swap(held, "mp", mp, bit)
        held = jnp.stack([held, other], 1).reshape((-1,) + block.shape)
    return held


def scatter(held, axis_name, size, bits, unit=1):
    left = sorted(bits)
    for bit in bits:
        inner = 1 << left.index(bit)
        left.remove(bit)
        pairs = held.reshape((held.shape[0] // (2 * inner), 2, inner) + held.shape[1:])
        other = swap(pairs[:, 1], axis_name, size, bit * unit)
        held = pairs[:, 0].astype(f32) + other.astype(f32)
        held = held.astype(bf16).reshape((-1,) + held.shape[2:])
    return held[0]


def scatter_open(held, axis_name, size, bits, unit):
    held = held.reshape((-1,) + held.shape[-2:])
    last = bits[-1]
    for bit in bits[:-1]:
        half = held.shape[0] // 2
        other = swap(held[half:], axis_name, size, bit * unit)
        held = plus(held[:half], other)
    return held[0], swap(held[1], axis_name, size, last * unit)


def plus(*terms):
    total = terms[0].astype(f32)
    for term in terms[1:]:
        total = total + term.astype(f32)
    return total.astype(bf16)


def reorder(blocks, me):
    size = blocks.shape[0]
    for bit in bits_of(size):
        pairs = blocks.reshape((size // (2 * bit), 2, bit) + blocks.shape[1:])
        blocks = jnp.where((me & bit) > 0, pairs[:, ::-1], pairs).reshape(blocks.shape)
    return blocks


def mm(a, b):
    return lax.dot_general(a, b, (((1,), (0,)), ((), ())), preferred_element_type=f32)


def mm_nt(a, b):
    return lax.dot_general(a, b, (((1,), (1,)), ((), ())), preferred_element_type=f32)


def mm_tn(a, b):
    return lax.dot_general(a, b, (((0,), (0,)), ((), ())), preferred_element_type=f32)


def unit_of(rows_f):
    mean_row = jnp.mean(rows_f, axis=-1, keepdims=True)
    centered = rows_f - mean_row
    variance = jnp.mean(centered * centered, axis=-1, keepdims=True)
    inverse = lax.rsqrt(variance + epsilon)
    return centered * inverse, inverse


def padded(value, pad):
    return jnp.concatenate([value, jnp.zeros((pad, value.shape[1]), value.dtype)], 0)


def low_lanes(rows):
    return lax.broadcasted_iota(jnp.int32, (rows, 128), 1) < HEAD_DIM


JOINED = 640


def pack_kernel(qkv_ref, out_ref, one_ref, two_ref, router_ref, packed_ref, extra_ref):
    low, mid = 2 * HEAD_DIM, qkv_ref.shape[2]
    out = out_ref[...].astype(f32).T.astype(bf16)
    packed_ref[...] = jnp.concatenate(
        [qkv_ref[c, :, :low] for c in range(3)]
        + [qkv_ref[c, :, low:mid] for c in range(3)]
        + [out[:, low:mid], out[:, :low]],
        axis=1,
    )
    rows = one_ref.shape[1]
    columns = [one_ref[...], two_ref[...], router_ref[...]]
    columns = [value.astype(f32) for value in columns]
    filled = sum(value.shape[0] for value in columns)
    columns.append(jnp.zeros((extra_ref.shape[1] - filled, rows), f32))
    extra_ref[...] = jnp.concatenate(columns, 0).T.astype(bf16)


def unpack_kernel(own_ref, other_ref, qkv_ref, out_ref):
    low, mid = 2 * HEAD_DIM, qkv_ref.shape[2]
    summed = own_ref[...].astype(f32) + other_ref[...].astype(f32)
    for c in range(3):
        qkv_ref[c, :, :low] = summed[:, c * low : (c + 1) * low]
        start = 3 * low + c * HEAD_DIM
        qkv_ref[c, :, low:mid] = summed[:, start : start + HEAD_DIM]
    out_ref[...] = jnp.concatenate([summed[:, 640:], summed[:, 576:640]], axis=1).T


def length_of(mask_ref, me_ref, b, images):
    row = mask_ref[pl.ds(me_ref[2] * images + b, 1), :]
    return jnp.sum(row.astype(f32), axis=1, keepdims=True)


def seen_row(length, tall):
    return lax.broadcasted_iota(jnp.int32, (1, tall), 1).astype(f32) < length


def seen_column(length, tall):
    return lax.broadcasted_iota(jnp.int32, (tall, 1), 0).astype(f32) < length


def prep_kernel(me_ref, x_ref, extra_ref, h_ref, ht_ref, small_ref, *, images, seq, tall):
    blocks, rows = extra_ref.shape[0], extra_ref.shape[1]
    me = me_ref[0]
    parts = [extra_ref[jnp.bitwise_xor(me, d) if blocks > 1 else 0] for d in range(blocks)]
    small_ref[...] = jnp.concatenate(parts, 0).astype(f32).T
    gain = small_ref[0:1, :]
    for b in range(images):
        unit, _ = unit_of(x_ref[b].astype(f32))
        h_ref[pl.ds(b * tall, tall), :] = padded((unit * gain).astype(bf16), tall - seq)
    ht_ref[...] = h_ref[...].T


def fetch_group(me_ref, w_ref, slot, x, core, near, far, other_near, other_far):
    me, at_core = me_ref[0], me_ref[1]
    rows = near.shape[2]
    blocks = 2 * near.shape[1]

    def block(d, carry):
        r = jnp.bitwise_xor(me, d)
        low, high = jnp.bitwise_and(r, 1), jnp.right_shift(r, 1)
        at = pl.ds(pl.multiple_of(d * rows, 16), rows)
        for mine, first, second in ((True, near, far), (False, other_near, other_far)):
            ours = at_core == core if mine else at_core != core
            if core == 0:

                @pl.when(ours)
                def _(first=first, second=second):
                    w_ref[slot, at, :] = (second if x else first)[low, high]

            else:

                @pl.when(jnp.logical_and(ours, low == 0))
                def _(first=first):
                    w_ref[slot, at, :] = first[x, high]

                @pl.when(jnp.logical_and(ours, low == 1))
                def _(second=second):
                    w_ref[slot, at, :] = second[x, high]

        return carry

    lax.fori_loop(0, blocks, block, 0)


def front_group(j, h_ref, mask_ref, me_ref, w_ref, qkv_ref, p_ref, ho_ref, br_ref, images, tall):
    scale = HEAD_DIM ** (-0.5)
    low = low_lanes(tall)
    qkv_ref[j] = mm(h_ref[...], w_ref[j, :, :JOINED]).astype(bf16)
    for b in range(images):
        at = pl.ds(b * tall, tall)
        joined = qkv_ref[j, at, :]
        q_pair, k_pair, v_pair = joined[:, :128], joined[:, 128:256], joined[:, 256:384]
        qk_last, v_last = joined[:, 384:512], joined[:, 512:640]
        k_last = pltpu.roll(qk_last.astype(f32), HEAD_DIM, 1).astype(bf16)
        none = jnp.zeros_like(q_pair)
        bias = jnp.where(seen_row(length_of(mask_ref, me_ref, b, images), tall), 0.0, -1e30)
        outs = []
        for head, (q, k, v) in enumerate(
            (
                (jnp.where(low, q_pair, none), k_pair, v_pair),
                (jnp.where(low, none, q_pair), k_pair, v_pair),
                (jnp.where(low, qk_last, none), k_last, v_last),
            )
        ):
            scores = mm_nt(q, k) * scale + bias
            terms = jnp.exp(scores - jnp.max(scores, axis=-1, keepdims=True))
            probs = (terms * (1.0 / jnp.sum(terms, axis=-1, keepdims=True))).astype(bf16)
            p_ref[j, b, head] = probs
            outs.append(mm(probs, v))
        last = jnp.where(low, 0.0, pltpu.roll(outs[2], HEAD_DIM, 1))
        pair = jnp.where(low, outs[0], outs[1])
        ho_ref[j, at, :] = jnp.concatenate([last, pair], 1).astype(bf16)
    br_ref[...] += mm_nt(ho_ref[j], w_ref[j, :, 512:])


def front_first_kernel(me_ref, h_ref, mask_ref, *refs, images, tall, ready):
    if ready:
        (source,), outs = refs[:1], refs[1:]
    else:
        (near, other_near), outs = refs[:2], refs[2:]
    w_ref, qkv_ref, p_ref, ho_ref, br_ref = outs
    if ready:
        w_ref[0] = source[...]
    else:
        fetch_group(me_ref, w_ref, 0, 0, 0, near, None, other_near, None)
    br_ref[...] = jnp.zeros_like(br_ref)
    front_group(0, h_ref, mask_ref, me_ref, w_ref, qkv_ref, p_ref, ho_ref, br_ref, images, tall)


def front_rest_kernel(me_ref, h_ref, mask_ref, first_ref, *refs, images, tall, ready):
    outs = refs[-5:]
    w_ref, qkv_ref, p_ref, ho_ref, br_ref = outs
    order = ((1, 0), (0, 1), (1, 1))
    for slot, (x, core) in enumerate(order):
        if ready:
            w_ref[slot] = refs[slot][...]
        else:
            fetch_group(me_ref, w_ref, slot, x, core, *refs[:4])
    br_ref[...] = first_ref[...]

    def group(j, carry):
        front_group(j, h_ref, mask_ref, me_ref, w_ref, qkv_ref, p_ref, ho_ref, br_ref, images, tall)
        return carry

    lax.fori_loop(0, len(order), group, 0)


def spot(rows, b, start, experts):
    each = rows // experts
    at_row = lax.broadcasted_iota(jnp.int32, (rows, experts), 0)
    at_column = lax.broadcasted_iota(jnp.int32, (rows, experts), 1)
    return jnp.where(at_row == at_column * each + (start + b), 1.0, 0.0).astype(bf16)


def route_kernel(
    me_ref, x_ref, br_ref, cot_ref, mask_ref, ex_ref,
    res_ref, h_ref, soft_ref, sent_ref, sq_ref, *, images, seq, tall, experts
):
    rows = sent_ref.shape[0]
    half = rows // experts // 2
    router = ex_ref[2 : 2 + experts, :].astype(bf16)
    gain = ex_ref[1:2, :]
    total = jnp.zeros(sent_ref.shape, f32)
    for b in range(images):
        at = pl.ds(b * tall, tall)
        length = length_of(mask_ref, me_ref, b, images)
        branch = br_ref[at, :]
        resid = padded(x_ref[b].astype(f32), tall - seq) + branch
        res_ref[at, :] = resid
        unit, _ = unit_of(resid)
        h_two = (unit * gain).astype(bf16)
        h_ref[at, :] = h_two
        logits = mm_nt(router, h_two)
        held = jnp.where(seen_row(length, tall), logits, -1e30)
        terms = jnp.exp(held - jnp.max(held, axis=1, keepdims=True))
        dispatch = terms / jnp.sum(terms, axis=1, keepdims=True)
        terms = jnp.exp(logits - jnp.max(logits, axis=0, keepdims=True))
        combine = terms / jnp.sum(terms, axis=0, keepdims=True)
        soft_ref[0, b] = dispatch
        soft_ref[1, b] = combine
        cot = padded(cot_ref[b], tall - seq)
        wide_d = mm(spot(rows, b, 0, experts), dispatch.astype(bf16)).astype(bf16)
        wide_c = mm(spot(rows, b, half, experts), combine.astype(bf16)).astype(bf16)
        total += mm(wide_d, h_two) + mm(wide_c, cot)
        squares = jnp.sum(branch * branch, axis=1, keepdims=True)
        squares = jnp.sum(jnp.where(seen_column(length, tall), squares, 0.0), axis=0, keepdims=True)
        sq_ref[b] = jnp.broadcast_to(squares, (1, 128))
    sent_ref[...] = total.astype(bf16)


def expert_kernel(got_ref, first_ref, second_ref, hid_ref, pre_ref, grad_ref, back_ref, *, each):
    rows = got_ref.shape[0]
    half = each // 2
    got = got_ref[...]
    own = jnp.bitwise_and(lax.broadcasted_iota(jnp.int32, (rows, 1), 0), each - 1) < half
    grads = jnp.where(own, pltpu.roll(got.astype(f32), rows - half, 0), 0.0).astype(bf16)
    grad_ref[...] = grads
    u = mm(got, first_ref[...])
    cubic = 0.7978845608028654 * (u + 0.044715 * u * u * u)
    t = jnp.tanh(cubic)
    hidden = jnp.where(own, 0.5 * u * (1.0 + t), 0.0).astype(bf16)
    hid_ref[...] = hidden
    slope = 0.5 * (1.0 + t) + 0.5 * u * (1.0 - t * t) * 0.7978845608028654 * (
        1.0 + 3.0 * 0.044715 * u * u
    )
    grad_pre = (mm_nt(grads, second_ref[...]) * slope).astype(bf16)
    pre_ref[...] = grad_pre
    out = mm(hidden, second_ref[...])
    grad_in = mm_nt(grad_pre, first_ref[...])
    back_ref[...] = jnp.where(own, out, pltpu.roll(grad_in, half, 0)).astype(bf16)


def mix_kernel(
    me_ref, res_ref, h_ref, soft_ref, cot_ref, mask_ref, ex_ref, back_ref, sq_ref,
    out_ref, gres_ref, small_ref, *, images, seq, tall, experts, groups
):
    small_ref[...] = jnp.zeros_like(small_ref)
    router = ex_ref[2 : 2 + experts, :].astype(bf16)
    gain = ex_ref[1:2, :]
    width = out_ref.shape[2]
    lanes = lax.broadcasted_iota(jnp.int32, (1, width), 1)
    roots = jnp.zeros((1, width), f32)
    for b in range(images):
        at = pl.ds(b * tall, tall)
        length = length_of(mask_ref, me_ref, b, images)
        resid, h_two = res_ref[at, :], h_ref[at, :]
        dispatch, combine = soft_ref[0, b], soft_ref[1, b]
        dispatch_low, combine_low = dispatch.astype(bf16), combine.astype(bf16)
        returned, grad_slots = back_ref[0, b], back_ref[1, b]
        cot = padded(cot_ref[b], tall - seq)
        mixed = mm_tn(combine_low, returned)
        stream = resid + mixed
        out_ref[b] = stream[:seq].astype(bf16)
        column = seen_column(length, tall)
        sums = []
        for value in (stream, mixed):
            squares = jnp.sum(value * value, axis=1, keepdims=True)
            sums.append(jnp.sum(jnp.where(column, squares, 0.0), axis=0, keepdims=True))
        sums.insert(1, sq_ref[b, :, 0:1])
        for k, value in enumerate(sums):
            root = jnp.sqrt(value / (length * width))
            mine = lanes == k * (groups * images) + me_ref[2] * images + b
            roots += jnp.where(mine, root, 0.0)
        grad_c = mm_nt(returned, cot)
        grad_c = combine * (grad_c - jnp.sum(grad_c * combine, axis=0, keepdims=True))
        grad_d = mm_nt(grad_slots, h_two)
        grad_d = dispatch * (grad_d - jnp.sum(grad_d * dispatch, axis=1, keepdims=True))
        grad_logits = (grad_d + grad_c).astype(bf16)
        grad_h = mm_tn(dispatch_low, grad_slots) + mm_tn(grad_logits, router)
        small_ref[0:experts, :] += mm(grad_logits, h_two)
        unit, inverse = unit_of(resid)
        small_ref[experts + 1 : experts + 2, :] += jnp.sum(grad_h * unit, axis=0, keepdims=True)
        scaled = grad_h * gain
        mean_grad = jnp.mean(scaled, axis=-1, keepdims=True)
        mean_proj = jnp.mean(scaled * unit, axis=-1, keepdims=True)
        gres_ref[at, :] = cot.astype(f32) + inverse * (scaled - mean_grad - unit * mean_proj)
    small_ref[experts + 2 : experts + 3, :] = roots


def back_group(
    core, source, me_ref, gb_ref, gbt_ref, ht_ref, gw_ref, gh_ref, gj_ref, dho_ref, images, tall
):
    qkv_ref, p_ref, ho_ref, w_ref, j = source
    scale = HEAD_DIM ** (-0.5)
    low = low_lanes(tall)
    dho_ref[...] = mm(gb_ref[...], w_ref[j, :, 512:])
    for b in range(images):
        at = pl.ds(b * tall, tall)
        joined = qkv_ref[j, at, :]
        q_pair, k_pair, v_pair = joined[:, :128], joined[:, 128:256], joined[:, 256:384]
        qk_last, v_last = joined[:, 384:512], joined[:, 512:640]
        heads = ho_ref[j, at, :].astype(f32)
        grad = dho_ref[at, :].astype(bf16).astype(f32)
        product = grad * heads
        pair = product[:, 128:]
        dots = (
            jnp.sum(jnp.where(low, pair, 0.0), axis=1, keepdims=True),
            jnp.sum(jnp.where(low, 0.0, pair), axis=1, keepdims=True),
            jnp.sum(product[:, :128], axis=1, keepdims=True),
        )
        grad_pair = grad[:, 128:]
        grad_last = jnp.where(low, pltpu.roll(grad[:, :128], HEAD_DIM, 1), 0.0).astype(bf16)
        gq, gk, gv = [], [], []
        for head, (g, v, q, k) in enumerate(
            (
                (jnp.where(low, grad_pair, 0.0).astype(bf16), v_pair, q_pair, k_pair),
                (jnp.where(low, 0.0, grad_pair).astype(bf16), v_pair, q_pair, k_pair),
                (grad_last, v_last, qk_last, qk_last),
            )
        ):
            probs = p_ref[j, b, head]
            grad_p = mm_nt(g, v)
            grad_s = (probs.astype(f32) * (grad_p - dots[head])).astype(bf16)
            gq.append(mm(grad_s, k))
            gk.append(mm_tn(grad_s, q))
            gv.append(mm_tn(probs, g))
        last = pltpu.roll(jnp.where(low, gk[2], gq[2]), HEAD_DIM, 1)
        gj_ref[at, :] = jnp.concatenate(
            [
                jnp.where(low, gq[0], gq[1]) * scale,
                jnp.where(low, gk[0], gk[1]) * scale,
                gv[0] + gv[1],
                last * scale,
                gv[2],
            ],
            1,
        ).astype(bf16)
    grad_out = mm(gbt_ref[...], ho_ref[j])
    grad_in = mm(ht_ref[...], gj_ref[...])
    slot = jnp.bitwise_xor(me_ref[1], core)
    halves, blocks, rows = gw_ref.shape[1:4]
    for d in range(halves * blocks):
        r = jnp.bitwise_xor(me_ref[0], d) if halves > 1 else 0
        entry = (slot, jnp.bitwise_and(r, 1), jnp.right_shift(r, 1)) if halves > 1 else (slot, 0, 0)
        at = slice(d * rows, (d + 1) * rows)
        gw_ref[entry + (slice(None), slice(0, 512))] = grad_in[at, :512].astype(bf16)
        gw_ref[entry + (slice(None), slice(512, 640))] = (
            grad_in[at, 512:] + grad_out[at, :128]
        ).astype(bf16)
        gw_ref[entry + (slice(None), slice(640, 768))] = grad_out[at, 128:].astype(bf16)
    gh_ref[...] += mm_nt(gj_ref[...], w_ref[j, :, :JOINED])


def back_far_kernel(
    me_ref, gres_ref, ht_ref, qkv_ref, p_ref, ho_ref, w_ref,
    gw_ref, gh_ref, gb_ref, gbt_ref, gj_ref, dho_ref, *, images, tall
):
    gb_ref[...] = gres_ref[...].astype(bf16)
    gbt_ref[...] = gres_ref[...].T.astype(bf16)
    gh_ref[...] = jnp.zeros_like(gh_ref)

    def group(core, carry):
        source = (qkv_ref, p_ref, ho_ref, w_ref, 2 * core)
        back_group(
            core, source, me_ref, gb_ref, gbt_ref, ht_ref, gw_ref, gh_ref, gj_ref, dho_ref, images, tall
        )
        return carry

    lax.fori_loop(0, 2, group, 0)


def back_near_kernel(
    me_ref, gb_ref, gbt_ref, ht_ref, far_ref, qkv_a, p_a, ho_a, w_a, qkv_b, p_b, ho_b, w_b,
    gw_ref, gh_ref, gj_ref, dho_ref, *, images, tall
):
    gh_ref[...] = far_ref[...]
    for core, source in enumerate(((qkv_a, p_a, ho_a, w_a, 0), (qkv_b, p_b, ho_b, w_b, 1))):
        back_group(
            core, source, me_ref, gb_ref, gbt_ref, ht_ref, gw_ref, gh_ref, gj_ref, dho_ref, images, tall
        )


def last_kernel(
    x_ref, gres_ref, gh_ref, ex_ref, part_ref, gt_ref, small_ref, *, images, seq, tall, experts
):
    total = jnp.zeros((1, x_ref.shape[2]), f32)
    gain = ex_ref[0:1, :]
    for b in range(images):
        at = pl.ds(b * tall, seq)
        unit, inverse = unit_of(x_ref[b].astype(f32))
        grad_h = gh_ref[at, :]
        total += jnp.sum(grad_h * unit, axis=0, keepdims=True)
        scaled = grad_h * gain
        mean_grad = jnp.mean(scaled, axis=-1, keepdims=True)
        mean_proj = jnp.mean(scaled * unit, axis=-1, keepdims=True)
        gt_ref[b] = gres_ref[at, :] + inverse * (scaled - mean_grad - unit * mean_proj)
    small_ref[...] = part_ref[...]
    small_ref[experts : experts + 1, :] = total


def cost(microseconds):
    return int(microseconds * 1.1e9)


def call(kernel, outs, args, scratch=(), flops=0, name=None, scalars=1, grant=16, **static):
    spec = pl.BlockSpec(memory_space=pltpu.VMEM)
    word = pl.BlockSpec(memory_space=pltpu.SMEM)
    moved = sum(math.prod(a.shape) * a.dtype.itemsize for a in args)
    return pl.pallas_call(
        functools.partial(kernel, **static),
        out_shape=[jax.ShapeDtypeStruct(s, d) for s, d in outs],
        in_specs=[word] * scalars + [spec] * (len(args) - scalars),
        out_specs=[spec] * len(outs),
        scratch_shapes=list(scratch),
        compiler_params=pltpu.CompilerParams(vmem_limit_bytes=grant << 20),
        cost_estimate=pl.CostEstimate(flops=flops, bytes_accessed=moved, transcendentals=0),
        name=name,
    )(*args)


def make(mesh):
    dp, mp = mesh.shape["dp"], mesh.shape["mp"]

    def per_device(
        tokens, token_mask, gain_one, w_qkv, w_out, gain_two, router, w_in, w_back, cotangent
    ):
        rows, width = tokens.shape
        seq = token_mask.shape[1]
        tall = -(-seq // 16) * 16
        images = rows // seq
        experts = router.shape[1]
        d_rows, _, part = w_qkv.shape
        count = images * tall
        high = dp // 2
        heads = part // HEAD_DIM
        ready = d_rows % 16 != 0
        each = 2 * (1 << (images - 1).bit_length())
        me = lax.axis_index("dp")
        at_mp = lax.axis_index("mp")
        core = at_mp & 1
        words = jnp.stack([me, core, at_mp]).astype(jnp.int32)
        static = {"images": images, "tall": tall}
        exact = {"images": images, "seq": seq, "tall": tall}

        columns = experts + 2
        packed, extra = call(
            pack_kernel,
            [((d_rows, 4 * part), bf16), ((d_rows, columns + -columns % 128), bf16)],
            (w_qkv.transpose(1, 0, 2), w_out, gain_one[None], gain_two[None], router.T),
            flops=cost(1),
            name="pack",
            scalars=0,
            grant=4,
        )

        held, held_extra = packed, extra
        for depth, bit in enumerate(bits_of(dp)[:-1]):
            other, other_extra = lax.optimization_barrier(
                (swap(held, "dp", dp, bit), swap(held_extra, "dp", dp, bit))
            )
            held = jnp.stack([held, other], depth)
            held_extra = jnp.stack([held_extra, other_extra], depth)
        held = held.reshape((high,) + packed.shape)
        other, other_extra = lax.optimization_barrier(
            (swap_both(held, dp, mp, (1, 0), (0, 2)), swap(held_extra, "dp", dp, 1))
        )
        near = jnp.stack([held, other])
        held_extra = jnp.stack([held_extra, other_extra], len(bits_of(dp)) - 1)
        held_extra = held_extra.reshape((dp,) + extra.shape)
        far = swap_both(near, dp, mp, (0, 2), (1, 0))
        other_near = swap(near, "mp", mp, 1)
        other_far = swap(far, "mp", mp, 1)
        if ready:
            held_extra = reorder(held_extra, me).reshape(1, width, -1)

            def whole(x, of_core):
                mine = core == of_core
                first = jnp.where(mine, near, other_near)
                second = jnp.where(mine, far, other_far)
                blocks = jnp.stack([first[x], second[x]]) if of_core else (second if x else first)
                blocks = blocks.transpose(1, 0, 2, 3).reshape((dp,) + packed.shape)
                return reorder(blocks, me).reshape(width, 4 * part)

            first_weights = (whole(0, 0),)
            rest_weights = (whole(1, 0), whole(0, 1), whole(1, 1))
        else:
            first_weights = (near, other_near)
            rest_weights = (near, far, other_near, other_far)

        x3 = tokens.reshape(images, seq, width)
        cot3 = cotangent.reshape(images, seq, width)
        h_one, h_turned, ex = call(
            prep_kernel,
            [((count, width), bf16), ((width, count), bf16), ((held_extra.shape[2], width), f32)],
            (words, x3, held_extra),
            flops=cost(2),
            name="prep",
            grant=4,
            **exact,
        )

        def saved(groups):
            return [
                ((groups, width, 4 * part), bf16),
                ((groups, count, JOINED), bf16),
                ((groups, images, heads, tall, tall), bf16),
                ((groups, count, 256), bf16),
                ((count, width), f32),
            ]

        w_a, qkv_a, p_a, ho_a, branch = call(
            front_first_kernel,
            saved(1),
            (words, h_one, token_mask) + first_weights,
            flops=cost(5),
            name="front_first",
            grant=6,
            ready=ready,
            **static,
        )
        w_b, qkv_b, p_b, ho_b, branch = call(
            front_rest_kernel,
            saved(3),
            (words, h_one, token_mask, branch) + rest_weights,
            flops=cost(12),
            name="front_rest",
            grant=10,
            ready=ready,
            **static,
        )
        resid, h_two, soft, sent, sq_branch = call(
            route_kernel,
            [
                ((count, width), f32),
                ((count, width), bf16),
                ((2, images, experts, tall), f32),
                ((experts * each, width), bf16),
                ((images, 1, 128), f32),
            ],
            (words, x3, branch, cot3, token_mask, ex),
            flops=cost(2),
            name="route",
            grant=6,
            experts=experts,
            **exact,
        )
        got = sent.reshape(dp, each, width)
        got = lax.all_to_all(got, "dp", split_axis=0, concat_axis=0, tiled=True)
        got = gather_mp(got, mp).reshape(-1, width)
        everyone = got.shape[0]
        hidden, grad_pre, grad_expert, back = call(
            expert_kernel,
            [
                ((everyone, w_in.shape[2]), bf16),
                ((everyone, w_in.shape[2]), bf16),
                ((everyone, width), bf16),
                ((everyone, width), bf16),
            ],
            (got, w_in[0], w_back[0]),
            flops=cost(2),
            name="expert",
            scalars=0,
            grant=12 if dp <= 8 else 56,
            each=each,
        )
        back = back.reshape(mp, dp, each, width)
        back = scatter(back, "mp", mp, [1, 2])
        back = lax.all_to_all(back, "dp", split_axis=0, concat_axis=0, tiled=True)
        back = back.reshape(dp, 2, each // 2, width)[:, :, :images].transpose(1, 2, 0, 3)
        grad_w_back = mm_tn(hidden, grad_expert)
        grad_w_in = mm_tn(got, grad_pre)

        out_rows, grad_resid, small = call(
            mix_kernel,
            [
                ((images, seq, width), bf16),
                ((count, width), f32),
                ((experts + 3, width), f32),
            ],
            (words, resid, h_two, soft, cot3, token_mask, ex, back, sq_branch),
            flops=cost(4),
            name="mix",
            grant=6,
            experts=experts,
            groups=mp,
            **exact,
        )
        shape = (2, 1, 1, width, 4 * part) if ready else (2, 2, high, d_rows, 4 * part)
        scratch = [pltpu.VMEM((count, JOINED), bf16), pltpu.VMEM((count, 256), f32)]
        far_grads, grad_h, grad_low, grad_turned = call(
            back_far_kernel,
            [
                (shape, bf16),
                ((count, width), f32),
                ((count, width), bf16),
                ((width, count), bf16),
            ],
            (words, grad_resid, h_turned, qkv_b, p_b, ho_b, w_b),
            scratch,
            flops=cost(12),
            name="back_far",
            grant=10,
            **static,
        )
        if ready:

            def spread(grads):
                grads = grads.reshape(2, dp, d_rows, 4 * part)
                grads = jnp.stack([reorder(grads[0], me), reorder(grads[1], me)])
                return grads.reshape(2, high, 2, d_rows, 4 * part).transpose(0, 2, 1, 3, 4)

        else:

            def spread(grads):
                return grads

        far_grads = spread(far_grads)
        far_sum = plus(far_grads[0], swap(far_grads[1], "mp", mp, 1))
        far_sum, grad_low = lax.optimization_barrier((far_sum, grad_low))
        early = swap_both(far_sum[1], dp, mp, (0, 2), (1, 0))
        near_grads, grad_h = call(
            back_near_kernel,
            [(shape, bf16), ((count, width), f32)],
            (words, grad_low, grad_turned, h_turned, grad_h)
            + (qkv_a, p_a, ho_a, w_a, qkv_b, p_b, ho_b, w_b),
            scratch,
            flops=cost(12),
            name="back_near",
            grant=10,
            **static,
        )
        grad_tokens, small = call(
            last_kernel,
            [((images, seq, width), f32), ((experts + 3, width), f32)],
            (x3, grad_resid, grad_h, ex, small),
            flops=cost(3),
            name="last",
            scalars=0,
            grant=6,
            experts=experts,
            **exact,
        )
        near_grads = spread(near_grads)
        near_sum = plus(near_grads[0], swap(near_grads[1], "mp", mp, 1))
        second = jnp.where(core == 0, far_sum[0], near_sum[1])
        third = plus(jnp.where(core == 0, near_sum[1], far_sum[0]), early)
        second = swap_both(second, dp, mp, (0, 2), (1, 0))
        third = swap_both(third, dp, mp, (1, 0), (0, 2))
        summed = plus(near_sum[0], second, third)
        own, other = scatter_open(summed, "dp", dp, bits_of(high), 2)
        grad_qkv, grad_out = call(
            unpack_kernel,
            [((3, d_rows, part), f32), ((part, d_rows), f32)],
            (own, other),
            flops=cost(1),
            name="unpack",
            scalars=0,
            grant=6,
        )

        for bit in bits_of(mp)[::-1]:
            small = small + swap(small, "mp", mp, bit)
        root_squares = small[-1, : 3 * mp * images].reshape(3, mp * images)
        for bit in bits_of(dp)[::-1]:
            small = small + swap(small, "dp", dp, bit)
        small = lax.dynamic_slice_in_dim(small, me * d_rows, d_rows, 1)
        return (
            out_rows.reshape(rows, width),
            grad_tokens.reshape(rows, width),
            small[experts],
            grad_qkv.transpose(1, 0, 2),
            grad_out,
            small[experts + 1],
            small[:experts].T,
            grad_w_in[None],
            grad_w_back[None],
            root_squares,
        )

    return per_device


def solution(mesh):
    in_specs = (
        P(("dp", "mp"), None),
        P("dp", None),
        P("dp"),
        P("dp", None, "mp"),
        P("mp", "dp"),
        P("dp"),
        P("dp", None),
        P("dp", None, "mp"),
        P("dp", "mp", None),
        P(("dp", "mp"), None),
    )
    out_specs = (
        P(("dp", "mp"), None),
        P(("dp", "mp"), None),
        P("dp"),
        P("dp", None, "mp"),
        P("mp", "dp"),
        P("dp"),
        P("dp", None),
        P("dp", None, "mp"),
        P("dp", "mp", None),
        P(None, "dp"),
    )
    return jax.shard_map(
        make(mesh), mesh=mesh, in_specs=in_specs, out_specs=out_specs, check_vma=False
    )
```

```python
import functools
import math

import jax
import jax.numpy as jnp
from jax import lax
from jax.experimental import pallas as pl
from jax.experimental.pallas import tpu as pltpu
from jax.sharding import PartitionSpec as P

HEAD_DIM = 64


epsilon = 1e-06
bf16 = jnp.bfloat16
f32 = jnp.float32


def bits_of(size):
    return [1 << k for k in reversed(range(size.bit_length() - 1))]


def swap(array_in, axis_name, size, bit):
    return lax.ppermute(array_in, axis_name, [(i, i ^ bit) for i in range(size)])


def swap_both(array_in, dp, mp, even, odd):
    pairs = []
    for d in range(dp):
        for m in range(mp):
            flip = odd if m & 1 else even
            pairs.append((d * mp + m, (d ^ flip[0]) * mp + (m ^ flip[1])))
    return lax.ppermute(array_in, ("dp", "mp"), pairs)


def gather_mp(block, mp):
    held = block[None]
    for bit in bits_of(mp):
        other = swap(held, "mp", mp, bit)
        held = jnp.stack([held, other], 1).reshape((-1,) + block.shape)
    return held


def scatter(held, axis_name, size, bits, unit=1):
    left = sorted(bits)
    for bit in bits:
        inner = 1 << left.index(bit)
        left.remove(bit)
        pairs = held.reshape((held.shape[0] // (2 * inner), 2, inner) + held.shape[1:])
        other = swap(pairs[:, 1], axis_name, size, bit * unit)
        held = pairs[:, 0].astype(f32) + other.astype(f32)
        held = held.astype(bf16).reshape((-1,) + held.shape[2:])
    return held[0]


def scatter_open(held, axis_name, size, bits, unit):
    held = held.reshape((2,) * len(bits) + held.shape[-2:])
    for bit in bits[:0:-1]:
        depth = held.ndim - 3
        kept, left = (lax.index_in_dim(held, k, depth, keepdims=False) for k in (0, 1))
        held = plus(kept, swap(left, axis_name, size, bit * unit))
    return held[0], swap(held[1], axis_name, size, bits[0] * unit)


def plus(*terms):
    total = terms[0].astype(f32)
    for term in terms[1:]:
        total = total + term.astype(f32)
    return total.astype(bf16)


def reorder(blocks, me):
    size = blocks.shape[0]
    for bit in bits_of(size):
        pairs = blocks.reshape((size // (2 * bit), 2, bit) + blocks.shape[1:])
        blocks = jnp.where((me & bit) > 0, pairs[:, ::-1], pairs).reshape(blocks.shape)
    return blocks


def mm(a, b):
    return lax.dot_general(a, b, (((1,), (0,)), ((), ())), preferred_element_type=f32)


def mm_nt(a, b):
    return lax.dot_general(a, b, (((1,), (1,)), ((), ())), preferred_element_type=f32)


def mm_tn(a, b):
    return lax.dot_general(a, b, (((0,), (0,)), ((), ())), preferred_element_type=f32)


def unit_of(rows_f):
    mean_row = jnp.mean(rows_f, axis=-1, keepdims=True)
    centered = rows_f - mean_row
    variance = jnp.mean(centered * centered, axis=-1, keepdims=True)
    inverse = lax.rsqrt(variance + epsilon)
    return centered * inverse, inverse


def padded(value, pad):
    return jnp.concatenate([value, jnp.zeros((pad, value.shape[1]), value.dtype)], 0)


def low_lanes(rows):
    return lax.broadcasted_iota(jnp.int32, (rows, 128), 1) < HEAD_DIM


JOINED = 640


def pack_kernel(qkv_ref, out_ref, one_ref, two_ref, router_ref, packed_ref, extra_ref):
    low, mid = 2 * HEAD_DIM, qkv_ref.shape[2]
    out = out_ref[...].astype(f32).T.astype(bf16)
    packed_ref[...] = jnp.concatenate(
        [qkv_ref[c, :, :low] for c in range(3)]
        + [qkv_ref[c, :, low:mid] for c in range(3)]
        + [out[:, low:mid], out[:, :low]],
        axis=1,
    )
    rows = one_ref.shape[1]
    columns = [one_ref[...], two_ref[...], router_ref[...]]
    columns = [value.astype(f32) for value in columns]
    filled = sum(value.shape[0] for value in columns)
    columns.append(jnp.zeros((extra_ref.shape[1] - filled, rows), f32))
    extra_ref[...] = jnp.concatenate(columns, 0).T.astype(bf16)


def unpack_kernel(own_ref, other_ref, qkv_ref, out_ref):
    low, mid = 2 * HEAD_DIM, qkv_ref.shape[2]
    summed = own_ref[...].astype(f32) + other_ref[...].astype(f32)
    for c in range(3):
        qkv_ref[c, :, :low] = summed[:, c * low : (c + 1) * low]
        start = 3 * low + c * HEAD_DIM
        qkv_ref[c, :, low:mid] = summed[:, start : start + HEAD_DIM]
    out_ref[...] = jnp.concatenate([summed[:, 640:], summed[:, 576:640]], axis=1).T


def length_of(mask_ref, me_ref, b, images):
    row = mask_ref[pl.ds(me_ref[2] * images + b, 1), :]
    return jnp.sum(row.astype(f32), axis=1, keepdims=True)


def seen_row(length, tall):
    return lax.broadcasted_iota(jnp.int32, (1, tall), 1).astype(f32) < length


def seen_column(length, tall):
    return lax.broadcasted_iota(jnp.int32, (tall, 1), 0).astype(f32) < length


def prep_kernel(me_ref, x_ref, extra_ref, h_ref, ht_ref, small_ref, *, images, seq, tall):
    blocks, rows = extra_ref.shape[0], extra_ref.shape[1]
    me = me_ref[0]
    parts = [extra_ref[jnp.bitwise_xor(me, d) if blocks > 1 else 0] for d in range(blocks)]
    small_ref[...] = jnp.concatenate(parts, 0).astype(f32).T
    gain = small_ref[0:1, :]
    for b in range(images):
        unit, _ = unit_of(x_ref[b].astype(f32))
        h_ref[pl.ds(b * tall, tall), :] = padded((unit * gain).astype(bf16), tall - seq)
    ht_ref[...] = h_ref[...].T


def fetch_group(me_ref, w_ref, slot, x, core, near, far, other_near, other_far):
    me, at_core = me_ref[0], me_ref[1]
    rows = near.shape[2]
    blocks = 2 * near.shape[1]

    def block(d, carry):
        r = jnp.bitwise_xor(me, d)
        low, high = jnp.bitwise_and(r, 1), jnp.right_shift(r, 1)
        at = pl.ds(pl.multiple_of(d * rows, 16), rows)
        for mine, first, second in ((True, near, far), (False, other_near, other_far)):
            ours = at_core == core if mine else at_core != core
            if core == 0:

                @pl.when(ours)
                def _(first=first, second=second):
                    w_ref[slot, at, :] = (second if x else first)[low, high]

            else:

                @pl.when(jnp.logical_and(ours, low == 0))
                def _(first=first):
                    w_ref[slot, at, :] = first[x, high]

                @pl.when(jnp.logical_and(ours, low == 1))
                def _(second=second):
                    w_ref[slot, at, :] = second[x, high]

        return carry

    lax.fori_loop(0, blocks, block, 0)


def attend(q, k, v, bias):
    scores = mm_nt(q, k) * HEAD_DIM ** (-0.5) + bias
    terms = jnp.exp(scores - jnp.max(scores, axis=-1, keepdims=True))
    probs = (terms * (1.0 / jnp.sum(terms, axis=-1, keepdims=True))).astype(bf16)
    return probs, mm(probs, v)


def bias_of(mask_ref, me_ref, b, images, tall):
    return jnp.where(seen_row(length_of(mask_ref, me_ref, b, images), tall), 0.0, -1e30)


def fetch_all(me_ref, w_ref, refs, ready):
    for slot in range(w_ref.shape[0]):
        if ready:
            w_ref[slot] = refs[slot][...]
        else:
            fetch_group(me_ref, w_ref, slot, slot & 1, slot >> 1, *refs)


def front_pair_kernel(me_ref, h_ref, mask_ref, *refs, images, tall, ready):
    w_ref, qkv_ref, p_ref, ho_ref = refs[4:]
    fetch_all(me_ref, w_ref, refs[:4], ready)
    low = low_lanes(tall)

    def group(j, carry):
        qkv_ref[j] = mm(h_ref[...], w_ref[j]).astype(bf16)
        for b in range(images):
            at = pl.ds(b * tall, tall)
            joined = qkv_ref[j, at, :]
            q, k, v = joined[:, :128], joined[:, 128:256], joined[:, 256:384]
            none = jnp.zeros_like(q)
            bias = bias_of(mask_ref, me_ref, b, images, tall)
            p_ref[j, b, 0], first = attend(jnp.where(low, q, none), k, v, bias)
            p_ref[j, b, 1], second = attend(jnp.where(low, none, q), k, v, bias)
            ho_ref[j, at, :] = jnp.where(low, first, second).astype(bf16)
        return carry

    lax.fori_loop(0, w_ref.shape[0], group, 0)


def front_last_kernel(me_ref, h_ref, mask_ref, pair_ref, *refs, images, tall, ready):
    w_ref, qkv_ref, p_ref, ho_ref, br_ref = refs[4:]
    fetch_all(me_ref, w_ref, refs[:4], ready)
    low = low_lanes(tall)
    br_ref[...] = jnp.zeros_like(br_ref)

    def group(j, carry):
        qkv_ref[j] = mm(h_ref[...], w_ref[j, :, :256]).astype(bf16)
        for b in range(images):
            at = pl.ds(b * tall, tall)
            joined = qkv_ref[j, at, :]
            qk, v = joined[:, :128], joined[:, 128:256]
            k = pltpu.roll(qk.astype(f32), HEAD_DIM, 1).astype(bf16)
            bias = bias_of(mask_ref, me_ref, b, images, tall)
            p_ref[j, b], out = attend(jnp.where(low, qk, jnp.zeros_like(qk)), k, v, bias)
            ho_ref[j, at, :] = jnp.where(low, 0.0, pltpu.roll(out, HEAD_DIM, 1)).astype(bf16)
        heads = jnp.concatenate([ho_ref[j], pair_ref[j]], 1)
        br_ref[...] += mm_nt(heads, w_ref[j, :, 128:])
        return carry

    lax.fori_loop(0, w_ref.shape[0], group, 0)


def spot(rows, b, start, experts):
    each = rows // experts
    at_row = lax.broadcasted_iota(jnp.int32, (rows, experts), 0)
    at_column = lax.broadcasted_iota(jnp.int32, (rows, experts), 1)
    return jnp.where(at_row == at_column * each + (start + b), 1.0, 0.0).astype(bf16)


def route_kernel(
    me_ref, x_ref, br_ref, cot_ref, mask_ref, ex_ref,
    res_ref, h_ref, soft_ref, sent_ref, sq_ref, *, images, seq, tall, experts
):
    rows = sent_ref.shape[0]
    half = rows // experts // 2
    router = ex_ref[2 : 2 + experts, :].astype(bf16)
    gain = ex_ref[1:2, :]
    total = jnp.zeros(sent_ref.shape, f32)
    for b in range(images):
        at = pl.ds(b * tall, tall)
        length = length_of(mask_ref, me_ref, b, images)
        branch = br_ref[at, :]
        resid = padded(x_ref[b].astype(f32), tall - seq) + branch
        res_ref[at, :] = resid
        unit, _ = unit_of(resid)
        h_two = (unit * gain).astype(bf16)
        h_ref[at, :] = h_two
        logits = mm_nt(router, h_two)
        held = jnp.where(seen_row(length, tall), logits, -1e30)
        terms = jnp.exp(held - jnp.max(held, axis=1, keepdims=True))
        dispatch = terms / jnp.sum(terms, axis=1, keepdims=True)
        terms = jnp.exp(logits - jnp.max(logits, axis=0, keepdims=True))
        combine = terms / jnp.sum(terms, axis=0, keepdims=True)
        soft_ref[0, b] = dispatch
        soft_ref[1, b] = combine
        cot = padded(cot_ref[b], tall - seq)
        wide_d = mm(spot(rows, b, 0, experts), dispatch.astype(bf16)).astype(bf16)
        wide_c = mm(spot(rows, b, half, experts), combine.astype(bf16)).astype(bf16)
        total += mm(wide_d, h_two) + mm(wide_c, cot)
        squares = jnp.sum(branch * branch, axis=1, keepdims=True)
        squares = jnp.sum(jnp.where(seen_column(length, tall), squares, 0.0), axis=0, keepdims=True)
        sq_ref[b] = jnp.broadcast_to(squares, (1, 128))
    sent_ref[...] = total.astype(bf16)


def expert_kernel(got_ref, first_ref, second_ref, hid_ref, pre_ref, grad_ref, back_ref, *, each):
    rows = got_ref.shape[0]
    half = each // 2
    got = got_ref[...]
    own = jnp.bitwise_and(lax.broadcasted_iota(jnp.int32, (rows, 1), 0), each - 1) < half
    grads = jnp.where(own, pltpu.roll(got.astype(f32), rows - half, 0), 0.0).astype(bf16)
    grad_ref[...] = grads
    u = mm(got, first_ref[...])
    cubic = 0.7978845608028654 * (u + 0.044715 * u * u * u)
    t = jnp.tanh(cubic)
    hidden = jnp.where(own, 0.5 * u * (1.0 + t), 0.0).astype(bf16)
    hid_ref[...] = hidden
    slope = 0.5 * (1.0 + t) + 0.5 * u * (1.0 - t * t) * 0.7978845608028654 * (
        1.0 + 3.0 * 0.044715 * u * u
    )
    grad_pre = (mm_nt(grads, second_ref[...]) * slope).astype(bf16)
    pre_ref[...] = grad_pre
    out = mm(hidden, second_ref[...])
    grad_in = mm_nt(grad_pre, first_ref[...])
    back_ref[...] = jnp.where(own, out, pltpu.roll(grad_in, half, 0)).astype(bf16)


def mix_kernel(
    me_ref, res_ref, h_ref, soft_ref, cot_ref, mask_ref, ex_ref, back_ref, sq_ref,
    out_ref, gres_ref, gb_ref, gbt_ref, small_ref, *, images, seq, tall, experts, groups
):
    small_ref[...] = jnp.zeros_like(small_ref)
    router = ex_ref[2 : 2 + experts, :].astype(bf16)
    gain = ex_ref[1:2, :]
    width = out_ref.shape[2]
    lanes = lax.broadcasted_iota(jnp.int32, (1, width), 1)
    roots = jnp.zeros((1, width), f32)
    for b in range(images):
        at = pl.ds(b * tall, tall)
        length = length_of(mask_ref, me_ref, b, images)
        resid, h_two = res_ref[at, :], h_ref[at, :]
        dispatch, combine = soft_ref[0, b], soft_ref[1, b]
        dispatch_low, combine_low = dispatch.astype(bf16), combine.astype(bf16)
        returned, grad_slots = back_ref[0, b], back_ref[1, b]
        cot = padded(cot_ref[b], tall - seq)
        mixed = mm_tn(combine_low, returned)
        stream = resid + mixed
        out_ref[b] = stream[:seq].astype(bf16)
        column = seen_column(length, tall)
        sums = []
        for value in (stream, mixed):
            squares = jnp.sum(value * value, axis=1, keepdims=True)
            sums.append(jnp.sum(jnp.where(column, squares, 0.0), axis=0, keepdims=True))
        sums.insert(1, sq_ref[b, :, 0:1])
        for k, value in enumerate(sums):
            root = jnp.sqrt(value / (length * width))
            mine = lanes == k * (groups * images) + me_ref[2] * images + b
            roots += jnp.where(mine, root, 0.0)
        grad_c = mm_nt(returned, cot)
        grad_c = combine * (grad_c - jnp.sum(grad_c * combine, axis=0, keepdims=True))
        grad_d = mm_nt(grad_slots, h_two)
        grad_d = dispatch * (grad_d - jnp.sum(grad_d * dispatch, axis=1, keepdims=True))
        grad_logits = (grad_d + grad_c).astype(bf16)
        grad_h = mm_tn(dispatch_low, grad_slots) + mm_tn(grad_logits, router)
        small_ref[0:experts, :] += mm(grad_logits, h_two)
        unit, inverse = unit_of(resid)
        small_ref[experts + 1 : experts + 2, :] += jnp.sum(grad_h * unit, axis=0, keepdims=True)
        scaled = grad_h * gain
        mean_grad = jnp.mean(scaled, axis=-1, keepdims=True)
        mean_proj = jnp.mean(scaled * unit, axis=-1, keepdims=True)
        gres_ref[at, :] = cot.astype(f32) + inverse * (scaled - mean_grad - unit * mean_proj)
    small_ref[experts + 2 : experts + 3, :] = roots
    gb_ref[...] = gres_ref[...].astype(bf16)
    gbt_ref[...] = gres_ref[...].T.astype(bf16)


def back_kernel(
    me_ref, gb_ref, gbt_ref, ht_ref, qkv_a, p_a, ho_a, w_a, qkv_b, p_b, ho_b, w_b, *refs,
    images, tall, x, flip
):
    gw_ref, gh_ref, gj_ref, dho_ref = refs[-4:]
    j = x + 2 * jnp.bitwise_xor(me_ref[1], flip)
    scale = HEAD_DIM ** (-0.5)
    low = low_lanes(tall)
    dho_ref[...] = mm(gb_ref[...], w_b[j, :, 128:])
    for b in range(images):
        at = pl.ds(b * tall, tall)
        joined, joined_last = qkv_a[j, at, :], qkv_b[j, at, :]
        q_pair, k_pair, v_pair = joined[:, :128], joined[:, 128:256], joined[:, 256:384]
        qk_last, v_last = joined_last[:, :128], joined_last[:, 128:256]
        grad = dho_ref[at, :].astype(bf16).astype(f32)
        pair = grad[:, 128:] * ho_a[j, at, :].astype(f32)
        single = grad[:, :128] * ho_b[j, at, :].astype(f32)
        dots = (
            jnp.sum(jnp.where(low, pair, 0.0), axis=1, keepdims=True),
            jnp.sum(jnp.where(low, 0.0, pair), axis=1, keepdims=True),
            jnp.sum(single, axis=1, keepdims=True),
        )
        grad_pair = grad[:, 128:]
        grad_last = jnp.where(low, pltpu.roll(grad[:, :128], HEAD_DIM, 1), 0.0).astype(bf16)
        gq, gk, gv = [], [], []
        for head, (probs, g, v, q, k) in enumerate(
            (
                (p_a[j, b, 0], jnp.where(low, grad_pair, 0.0).astype(bf16), v_pair, q_pair, k_pair),
                (p_a[j, b, 1], jnp.where(low, 0.0, grad_pair).astype(bf16), v_pair, q_pair, k_pair),
                (p_b[j, b], grad_last, v_last, qk_last, qk_last),
            )
        ):
            grad_p = mm_nt(g, v)
            grad_s = (probs.astype(f32) * (grad_p - dots[head])).astype(bf16)
            gq.append(mm(grad_s, k))
            gk.append(mm_tn(grad_s, q))
            gv.append(mm_tn(probs, g))
        last = pltpu.roll(jnp.where(low, gk[2], gq[2]), HEAD_DIM, 1)
        gj_ref[at, :] = jnp.concatenate(
            [
                jnp.where(low, gq[0], gq[1]) * scale,
                jnp.where(low, gk[0], gk[1]) * scale,
                gv[0] + gv[1],
                last * scale,
                gv[2],
            ],
            1,
        ).astype(bf16)
    grad_out = mm(gbt_ref[...], jnp.concatenate([ho_b[j], ho_a[j]], 1))
    grad_in = mm(ht_ref[...], gj_ref[...])
    halves, blocks, rows = gw_ref.shape[:3]
    for d in range(halves * blocks):
        r = jnp.bitwise_xor(me_ref[0], d) if halves > 1 else 0
        entry = (jnp.bitwise_and(r, 1), jnp.right_shift(r, 1)) if halves > 1 else (0, 0)
        at = slice(d * rows, (d + 1) * rows)
        gw_ref[entry + (slice(None), slice(0, 512))] = grad_in[at, :512].astype(bf16)
        gw_ref[entry + (slice(None), slice(512, 640))] = (
            grad_in[at, 512:] + grad_out[at, :128]
        ).astype(bf16)
        gw_ref[entry + (slice(None), slice(640, 768))] = grad_out[at, 128:].astype(bf16)
    into = mm_nt(gj_ref[:, :384], w_a[j]) + mm_nt(gj_ref[:, 384:], w_b[j, :, :256])
    gh_ref[...] = into + refs[0][...] if len(refs) > 4 else into


def last_kernel(
    x_ref, gres_ref, gh_ref, ex_ref, part_ref, gt_ref, small_ref, *, images, seq, tall, experts
):
    total = jnp.zeros((1, x_ref.shape[2]), f32)
    gain = ex_ref[0:1, :]
    for b in range(images):
        at = pl.ds(b * tall, seq)
        unit, inverse = unit_of(x_ref[b].astype(f32))
        grad_h = gh_ref[at, :]
        total += jnp.sum(grad_h * unit, axis=0, keepdims=True)
        scaled = grad_h * gain
        mean_grad = jnp.mean(scaled, axis=-1, keepdims=True)
        mean_proj = jnp.mean(scaled * unit, axis=-1, keepdims=True)
        gt_ref[b] = gres_ref[at, :] + inverse * (scaled - mean_grad - unit * mean_proj)
    small_ref[...] = part_ref[...]
    small_ref[experts : experts + 1, :] = total


def cost(microseconds):
    return int(microseconds * 1.1e9)


def call(kernel, outs, args, scratch=(), flops=0, name=None, scalars=1, grant=16, **static):
    spec = pl.BlockSpec(memory_space=pltpu.VMEM)
    word = pl.BlockSpec(memory_space=pltpu.SMEM)
    moved = sum(math.prod(a.shape) * a.dtype.itemsize for a in args)
    return pl.pallas_call(
        functools.partial(kernel, **static),
        out_shape=[jax.ShapeDtypeStruct(s, d) for s, d in outs],
        in_specs=[word] * scalars + [spec] * (len(args) - scalars),
        out_specs=[spec] * len(outs),
        scratch_shapes=list(scratch),
        compiler_params=pltpu.CompilerParams(vmem_limit_bytes=grant << 20),
        cost_estimate=pl.CostEstimate(flops=flops, bytes_accessed=moved, transcendentals=0),
        name=name,
    )(*args)


def make(mesh):
    dp, mp = mesh.shape["dp"], mesh.shape["mp"]

    def per_device(
        tokens, token_mask, gain_one, w_qkv, w_out, gain_two, router, w_in, w_back, cotangent
    ):
        rows, width = tokens.shape
        seq = token_mask.shape[1]
        tall = -(-seq // 16) * 16
        images = rows // seq
        experts = router.shape[1]
        d_rows, _, part = w_qkv.shape
        count = images * tall
        high = dp // 2
        heads = part // HEAD_DIM
        ready = d_rows % 16 != 0
        each = 2 * (1 << (images - 1).bit_length())
        me = lax.axis_index("dp")
        at_mp = lax.axis_index("mp")
        core = at_mp & 1
        words = jnp.stack([me, core, at_mp]).astype(jnp.int32)
        static = {"images": images, "tall": tall}
        exact = {"images": images, "seq": seq, "tall": tall}

        columns = experts + 2
        packed, extra = call(
            pack_kernel,
            [((d_rows, 4 * part), bf16), ((d_rows, columns + -columns % 128), bf16)],
            (w_qkv.transpose(1, 0, 2), w_out, gain_one[None], gain_two[None], router.T),
            flops=cost(1),
            name="pack",
            scalars=0,
            grant=4,
        )

        half = 2 * part
        first, second, held_extra = packed[:, :half], packed[:, half:], extra
        for depth, bit in enumerate(bits_of(dp)[:-1]):
            other, other_extra = lax.optimization_barrier(
                (swap(first, "dp", dp, bit), swap(held_extra, "dp", dp, bit))
            )
            first = jnp.stack([first, other], depth)
            held_extra = jnp.stack([held_extra, other_extra], depth)
            second = jnp.stack([second, swap(second, "dp", dp, bit)], depth)
        first = first.reshape((high, d_rows, half))
        second = second.reshape((high, d_rows, half))
        other, other_extra = lax.optimization_barrier(
            (swap_both(first, dp, mp, (1, 0), (0, 2)), swap(held_extra, "dp", dp, 1))
        )
        held_extra = jnp.stack([held_extra, other_extra], len(bits_of(dp)) - 1)
        held_extra = held_extra.reshape((dp,) + extra.shape)
        near = jnp.stack([first, other])
        far = swap_both(near, dp, mp, (0, 2), (1, 0))
        first = (near, far, swap(near, "mp", mp, 1), swap(far, "mp", mp, 1))
        near = jnp.stack([second, swap_both(second, dp, mp, (1, 0), (0, 2))])
        second_near, second_far = near, swap_both(near, dp, mp, (0, 2), (1, 0))
        second_near_other = swap(second_near, "mp", mp, 1)

        def whole(x, of_core, near, far, other_near, other_far):
            mine = core == of_core
            low = jnp.where(mine, near, other_near)
            high_part = jnp.where(mine, far, other_far)
            blocks = jnp.stack([low[x], high_part[x]]) if of_core else (high_part if x else low)
            blocks = blocks.transpose(1, 0, 2, 3).reshape((dp, d_rows, half))
            return reorder(blocks, me).reshape(width, half)

        def weights_of(parts):
            if ready:
                return tuple(whole(j & 1, j >> 1, *parts) for j in range(4))
            return parts

        if ready:
            held_extra = reorder(held_extra, me).reshape(1, width, -1)

        x3 = tokens.reshape(images, seq, width)
        cot3 = cotangent.reshape(images, seq, width)
        h_one, h_turned, ex = call(
            prep_kernel,
            [((count, width), bf16), ((width, count), bf16), ((held_extra.shape[2], width), f32)],
            (words, x3, held_extra),
            flops=cost(2),
            name="prep",
            grant=4,
            **exact,
        )

        def saved(columns, probs):
            return [
                ((mp, width, half), bf16),
                ((mp, count, columns), bf16),
                ((mp, images) + probs + (tall, tall), bf16),
                ((mp, count, 128), bf16),
            ]

        pair = call(
            front_pair_kernel,
            saved(384, (2,)),
            (words, h_one, token_mask) + weights_of(first),
            flops=cost(10),
            name="front_pair",
            grant=10,
            ready=ready,
            **static,
        )
        w_a, qkv_a, p_a, ho_a = pair
        second_far, ho_a = lax.optimization_barrier((second_far, ho_a))
        second = (second_near, second_far, second_near_other, swap(second_far, "mp", mp, 1))
        w_b, qkv_b, p_b, ho_b, branch = call(
            front_last_kernel,
            saved(256, ()) + [((count, width), f32)],
            (words, h_one, token_mask, ho_a) + weights_of(second),
            flops=cost(7),
            name="front_last",
            grant=10,
            ready=ready,
            **static,
        )
        resid, h_two, soft, sent, sq_branch = call(
            route_kernel,
            [
                ((count, width), f32),
                ((count, width), bf16),
                ((2, images, experts, tall), f32),
                ((experts * each, width), bf16),
                ((images, 1, 128), f32),
            ],
            (words, x3, branch, cot3, token_mask, ex),
            flops=cost(2),
            name="route",
            grant=6,
            experts=experts,
            **exact,
        )
        got = sent.reshape(dp, each, width)
        got = lax.all_to_all(got, "dp", split_axis=0, concat_axis=0, tiled=True)
        got = gather_mp(got, mp).reshape(-1, width)
        everyone = got.shape[0]
        hidden, grad_pre, grad_expert, back = call(
            expert_kernel,
            [
                ((everyone, w_in.shape[2]), bf16),
                ((everyone, w_in.shape[2]), bf16),
                ((everyone, width), bf16),
                ((everyone, width), bf16),
            ],
            (got, w_in[0], w_back[0]),
            flops=cost(2),
            name="expert",
            scalars=0,
            grant=12 if dp <= 8 else 56,
            each=each,
        )
        back = back.reshape(mp, dp, each, width)
        back = scatter(back, "mp", mp, [1, 2])
        back = lax.all_to_all(back, "dp", split_axis=0, concat_axis=0, tiled=True)
        back = back.reshape(dp, 2, each // 2, width)[:, :, :images].transpose(1, 2, 0, 3)
        grad_w_back = mm_tn(hidden, grad_expert)
        grad_w_in = mm_tn(got, grad_pre)

        out_rows, grad_resid, grad_low, grad_turned, small = call(
            mix_kernel,
            [
                ((images, seq, width), bf16),
                ((count, width), f32),
                ((count, width), bf16),
                ((width, count), bf16),
                ((experts + 3, width), f32),
            ],
            (words, resid, h_two, soft, cot3, token_mask, ex, back, sq_branch),
            flops=cost(5),
            name="mix",
            grant=8,
            experts=experts,
            groups=mp,
            **exact,
        )
        shape = (1, 1, width, 4 * part) if ready else (2, high, d_rows, 4 * part)

        def back_of(x, flip, *so_far):
            grads, total = call(
                back_kernel,
                [(shape, bf16), ((count, width), f32)],
                (words, grad_low, grad_turned, h_turned)
                + (qkv_a, p_a, ho_a, w_a, qkv_b, p_b, ho_b, w_b)
                + so_far,
                [pltpu.VMEM((count, JOINED), bf16), pltpu.VMEM((count, 256), f32)],
                flops=cost(6),
                name="back",
                grant=10,
                x=x,
                flip=flip,
                **static,
            )
            if ready:
                grads = reorder(grads.reshape(dp, d_rows, 4 * part), me)
                grads = grads.reshape(high, 2, d_rows, 4 * part).transpose(1, 0, 2, 3)
            return grads, total

        sent_grads, grad_h = back_of(1, 1)
        other = swap(sent_grads, "mp", mp, 1)
        kept_grads, grad_h = back_of(1, 0, grad_h)
        far_sum = plus(kept_grads, other)
        far_sum, grad_h = lax.optimization_barrier((far_sum, grad_h))
        early = swap_both(far_sum[1], dp, mp, (0, 2), (1, 0))
        sent_grads, grad_h = back_of(0, 1, grad_h)
        early, grad_h = lax.optimization_barrier((early, grad_h))
        other = swap(sent_grads, "mp", mp, 1)
        kept_grads, grad_h = back_of(0, 0, grad_h)
        near_sum = plus(kept_grads, other)
        grad_tokens, small = call(
            last_kernel,
            [((images, seq, width), f32), ((experts + 3, width), f32)],
            (x3, grad_resid, grad_h, ex, small),
            flops=cost(3),
            name="last",
            scalars=0,
            grant=6,
            experts=experts,
            **exact,
        )
        second = jnp.where(core == 0, far_sum[0], near_sum[1])
        third = plus(jnp.where(core == 0, near_sum[1], far_sum[0]), early)
        second = swap_both(second, dp, mp, (0, 2), (1, 0))
        third = swap_both(third, dp, mp, (1, 0), (0, 2))
        summed = plus(near_sum[0], second, third)
        own, other = scatter_open(summed, "dp", dp, bits_of(high), 2)
        grad_qkv, grad_out = call(
            unpack_kernel,
            [((3, d_rows, part), f32), ((part, d_rows), f32)],
            (own, other),
            flops=cost(1),
            name="unpack",
            scalars=0,
            grant=6,
        )

        for bit in bits_of(mp)[::-1]:
            small = small + swap(small, "mp", mp, bit)
        root_squares = small[-1, : 3 * mp * images].reshape(3, mp * images)
        for bit in bits_of(dp)[::-1]:
            small = small + swap(small, "dp", dp, bit)
        small = lax.dynamic_slice_in_dim(small, me * d_rows, d_rows, 1)
        return (
            out_rows.reshape(rows, width),
            grad_tokens.reshape(rows, width),
            small[experts],
            grad_qkv.transpose(1, 0, 2),
            grad_out,
            small[experts + 1],
            small[:experts].T,
            grad_w_in[None],
            grad_w_back[None],
            root_squares,
        )

    return per_device


def solution(mesh):
    in_specs = (
        P(("dp", "mp"), None),
        P("dp", None),
        P("dp"),
        P("dp", None, "mp"),
        P("mp", "dp"),
        P("dp"),
        P("dp", None),
        P("dp", None, "mp"),
        P("dp", "mp", None),
        P(("dp", "mp"), None),
    )
    out_specs = (
        P(("dp", "mp"), None),
        P(("dp", "mp"), None),
        P("dp"),
        P("dp", None, "mp"),
        P("mp", "dp"),
        P("dp"),
        P("dp", None),
        P("dp", None, "mp"),
        P("dp", "mp", None),
        P(None, "dp"),
    )
    return jax.shard_map(
        make(mesh), mesh=mesh, in_specs=in_specs, out_specs=out_specs, check_vma=False
    )
```

```python
import functools
import math

import jax
import jax.numpy as jnp
from jax import lax
from jax.experimental import pallas as pl
from jax.experimental.pallas import tpu as pltpu
from jax.sharding import PartitionSpec as P

HEAD_DIM = 64


epsilon = 1e-06
bf16 = jnp.bfloat16
f32 = jnp.float32


def bits_of(size):
    return [1 << k for k in reversed(range(size.bit_length() - 1))]


def swap(array_in, axis_name, size, bit):
    return lax.ppermute(array_in, axis_name, [(i, i ^ bit) for i in range(size)])


def swap_both(array_in, dp, mp, even, odd):
    pairs = []
    for d in range(dp):
        for m in range(mp):
            flip = odd if m & 1 else even
            pairs.append((d * mp + m, (d ^ flip[0]) * mp + (m ^ flip[1])))
    return lax.ppermute(array_in, ("dp", "mp"), pairs)


def gather_mp(block, mp):
    held = block[None]
    for bit in bits_of(mp):
        other = swap(held, "mp", mp, bit)
        held = jnp.stack([held, other], 1).reshape((-1,) + block.shape)
    return held


def scatter(held, axis_name, size, bits, unit=1):
    left = sorted(bits)
    for bit in bits:
        inner = 1 << left.index(bit)
        left.remove(bit)
        pairs = held.reshape((held.shape[0] // (2 * inner), 2, inner) + held.shape[1:])
        other = swap(pairs[:, 1], axis_name, size, bit * unit)
        held = pairs[:, 0].astype(f32) + other.astype(f32)
        held = held.astype(bf16).reshape((-1,) + held.shape[2:])
    return held[0]


def mirrored(index, size):
    bits = size.bit_length() - 1
    return sum(((index >> k) & 1) << (bits - 1 - k) for k in range(bits)) if bits else index


def unmirrored(blocks):
    size = blocks.shape[0]
    bits = size.bit_length() - 1
    split = blocks.reshape((2,) * bits + blocks.shape[1:])
    turn = tuple(range(bits))[::-1] + tuple(range(bits, split.ndim))
    return split.transpose(turn).reshape(blocks.shape)


def reorder(blocks, me):
    size = blocks.shape[0]
    for bit in bits_of(size):
        pairs = blocks.reshape((size // (2 * bit), 2, bit) + blocks.shape[1:])
        blocks = jnp.where((me & bit) > 0, pairs[:, ::-1], pairs).reshape(blocks.shape)
    return blocks


def mm(a, b):
    return lax.dot_general(a, b, (((1,), (0,)), ((), ())), preferred_element_type=f32)


def mm_nt(a, b):
    return lax.dot_general(a, b, (((1,), (1,)), ((), ())), preferred_element_type=f32)


def mm_tn(a, b):
    return lax.dot_general(a, b, (((0,), (0,)), ((), ())), preferred_element_type=f32)


def unit_of(rows_f):
    mean_row = jnp.mean(rows_f, axis=-1, keepdims=True)
    centered = rows_f - mean_row
    variance = jnp.mean(centered * centered, axis=-1, keepdims=True)
    inverse = lax.rsqrt(variance + epsilon)
    return centered * inverse, inverse


def padded(value, pad):
    return jnp.concatenate([value, jnp.zeros((pad, value.shape[1]), value.dtype)], 0)


def low_lanes(rows):
    return lax.broadcasted_iota(jnp.int32, (rows, 128), 1) < HEAD_DIM


JOINED = 640


def pack_kernel(
    me_ref, qkv_hbm, out_hbm, one_hbm, two_hbm, router_hbm, first_ref, second_ref, extra_ref,
    qkv_ref, out_ref, one_ref, two_ref, router_ref, sems
):
    del me_ref
    pairs = (
        (qkv_hbm, qkv_ref), (out_hbm, out_ref), (one_hbm, one_ref), (two_hbm, two_ref), (router_hbm, router_ref),
    )
    copies = [pltpu.make_async_copy(a, b, sems.at[k]) for k, (a, b) in enumerate(pairs)]
    for copy in copies:
        copy.start()
    for copy in copies:
        copy.wait()
    low, mid = 2 * HEAD_DIM, qkv_ref.shape[2]
    out = out_ref[...].astype(f32).T.astype(bf16)
    first_ref[...] = jnp.concatenate([qkv_ref[c, :, :low] for c in range(3)], axis=1)
    second_ref[...] = jnp.concatenate(
        [qkv_ref[c, :, low:mid] for c in range(3)] + [out[:, low:mid], out[:, :low]], axis=1
    )
    rows = one_ref.shape[1]
    columns = [one_ref[...], two_ref[...], router_ref[...]]
    columns = [value.astype(f32) for value in columns]
    filled = sum(value.shape[0] for value in columns)
    columns.append(jnp.zeros((extra_ref.shape[1] - filled, rows), f32))
    extra_ref[...] = jnp.concatenate(columns, 0).T.astype(bf16)


def fold_kernel(*refs, halves):
    terms, (kept_ref, left_ref) = refs[:-2], refs[-2:]
    size = terms[0].shape[0]
    for k in range(size):
        total = terms[0][k].astype(f32)
        for term in terms[1:]:
            total = total + term[k].astype(f32)
        at, odd = (k % (size // 2), k >= size // 2) if halves else (k // 2, k % 2 == 1)
        (left_ref if odd else kept_ref)[at] = total.astype(bf16)


def blend_kernel(me_ref, far_ref, kept_ref, other_ref, early_ref, near_ref, second_ref, third_ref):
    near = [kept_ref[k].astype(f32) + other_ref[k].astype(f32) for k in (0, 1)]
    near_ref[...] = near[0].astype(bf16)
    first_core = me_ref[1] == 0

    @pl.when(first_core)
    def _():
        second_ref[...] = far_ref[...]
        third_ref[...] = (near[1] + early_ref[...].astype(f32)).astype(bf16)

    @pl.when(jnp.logical_not(first_core))
    def _():
        second_ref[...] = near[1].astype(bf16)
        third_ref[...] = (far_ref[...].astype(f32) + early_ref[...].astype(f32)).astype(bf16)


def finish_kernel(me_ref, own_ref, other_ref, one_ref, two_ref, router_ref, root_ref):
    experts, rows = router_ref.shape
    total = own_ref[...] + other_ref[...]
    width = total.shape[1]
    mine = pltpu.roll(total, lax.rem(width - me_ref[0] * rows, width), 1)
    one_ref[...] = mine[experts : experts + 1, :rows]
    two_ref[...] = mine[experts + 1 : experts + 2, :rows]
    router_ref[...] = mine[:experts, :rows]
    images = root_ref.shape[1]
    mine = pltpu.roll(total, lax.rem(width - me_ref[0] * images, width), 1)
    root_ref[...] = mine[experts + 2 : experts + 5, :images]


def unpack_kernel(own_ref, other_ref, qkv_ref, out_ref):
    low, mid = 2 * HEAD_DIM, qkv_ref.shape[2]
    summed = own_ref[...].astype(f32) + other_ref[...].astype(f32)
    for c in range(3):
        qkv_ref[c, :, :low] = summed[:, c * low : (c + 1) * low]
        start = 3 * low + c * HEAD_DIM
        qkv_ref[c, :, low:mid] = summed[:, start : start + HEAD_DIM]
    out_ref[...] = jnp.concatenate([summed[:, 640:], summed[:, 576:640]], axis=1).T


def length_of(mask_ref, me_ref, b, images):
    row = mask_ref[pl.ds(me_ref[2] * images + b, 1), :]
    return jnp.sum(row.astype(f32), axis=1, keepdims=True)


def seen_row(length, tall):
    return lax.broadcasted_iota(jnp.int32, (1, tall), 1).astype(f32) < length


def seen_column(length, tall):
    return lax.broadcasted_iota(jnp.int32, (tall, 1), 0).astype(f32) < length


def prep_kernel(me_ref, x_ref, extra_ref, h_ref, ht_ref, small_ref, *, images, seq, tall):
    blocks = extra_ref.shape[0]
    me = me_ref[0]
    parts = [extra_ref[mirrored(me ^ d, blocks) if blocks > 1 else 0] for d in range(blocks)]
    small_ref[...] = jnp.concatenate(parts, 0).astype(f32).T
    gain = small_ref[0:1, :]
    for b in range(images):
        unit, _ = unit_of(x_ref[b].astype(f32))
        h_ref[pl.ds(b * tall, tall), :] = padded((unit * gain).astype(bf16), tall - seq)
    ht_ref[...] = h_ref[...].T


def fetch_group(me_ref, w_ref, slot, x, core, near, far, other_near, other_far):
    me, at_core = me_ref[0], me_ref[1]
    rows = near.shape[2]
    blocks = 2 * near.shape[1]

    def block(d, carry):
        r = jnp.bitwise_xor(me, d)
        low, high = jnp.bitwise_and(r, 1), mirrored(jnp.right_shift(r, 1), near.shape[1])
        at = pl.ds(pl.multiple_of(d * rows, 16), rows)
        for mine, first, second in ((True, near, far), (False, other_near, other_far)):
            ours = at_core == core if mine else at_core != core
            if core == 0:

                @pl.when(ours)
                def _(first=first, second=second):
                    w_ref[slot, at, :] = (second if x else first)[low, high]

            else:

                @pl.when(jnp.logical_and(ours, low == 0))
                def _(first=first):
                    w_ref[slot, at, :] = first[x, high]

                @pl.when(jnp.logical_and(ours, low == 1))
                def _(second=second):
                    w_ref[slot, at, :] = second[x, high]

        return carry

    lax.fori_loop(0, blocks, block, 0)


def attend(q, k, v, bias):
    scores = mm_nt(q, k) * HEAD_DIM ** (-0.5) + bias
    terms = jnp.exp(scores - jnp.max(scores, axis=-1, keepdims=True))
    probs = (terms * (1.0 / jnp.sum(terms, axis=-1, keepdims=True))).astype(bf16)
    return probs, mm(probs, v)


def bias_of(mask_ref, me_ref, b, images, tall):
    return jnp.where(seen_row(length_of(mask_ref, me_ref, b, images), tall), 0.0, -1e30)


def fetch_all(me_ref, w_ref, refs, ready):
    for slot in range(w_ref.shape[0]):
        if ready:
            w_ref[slot] = refs[slot][...]
        else:
            fetch_group(me_ref, w_ref, slot, slot & 1, slot >> 1, *refs)


def front_pair_kernel(me_ref, h_ref, mask_ref, *refs, images, tall, ready):
    w_ref, qkv_ref, p_ref, ho_ref = refs[4:]
    fetch_all(me_ref, w_ref, refs[:4], ready)
    low = low_lanes(tall)

    def group(j, carry):
        qkv_ref[j] = mm(h_ref[...], w_ref[j]).astype(bf16)
        for b in range(images):
            at = pl.ds(b * tall, tall)
            joined = qkv_ref[j, at, :]
            q, k, v = joined[:, :128], joined[:, 128:256], joined[:, 256:384]
            none = jnp.zeros_like(q)
            bias = bias_of(mask_ref, me_ref, b, images, tall)
            p_ref[j, b, 0], first = attend(jnp.where(low, q, none), k, v, bias)
            p_ref[j, b, 1], second = attend(jnp.where(low, none, q), k, v, bias)
            ho_ref[j, at, :] = jnp.where(low, first, second).astype(bf16)
        return carry

    lax.fori_loop(0, w_ref.shape[0], group, 0)


def front_last_kernel(me_ref, h_ref, mask_ref, pair_ref, *refs, images, tall, ready):
    w_ref, qkv_ref, p_ref, ho_ref, wo_ref, br_ref = refs[4:]
    fetch_all(me_ref, w_ref, refs[:4], ready)
    low = low_lanes(tall)
    groups = w_ref.shape[0]
    for j in range(groups):
        wo_ref[:, j * 256 : (j + 1) * 256] = w_ref[j, :, 128:]

    def two(i, carry):
        for j in (2 * i, 2 * i + 1):
            qkv_ref[j] = mm(h_ref[...], w_ref[j, :, :256]).astype(bf16)
            start = pl.multiple_of(j * 256, 256)
            for b in range(images):
                at = pl.ds(b * tall, tall)
                joined = qkv_ref[j, at, :]
                qk, v = joined[:, :128], joined[:, 128:256]
                k = pltpu.roll(qk.astype(f32), HEAD_DIM, 1).astype(bf16)
                bias = bias_of(mask_ref, me_ref, b, images, tall)
                p_ref[j, b], out = attend(jnp.where(low, qk, jnp.zeros_like(qk)), k, v, bias)
                out = jnp.where(low, 0.0, pltpu.roll(out, HEAD_DIM, 1)).astype(bf16)
                ho_ref[at, pl.ds(start, 128)] = out
                ho_ref[at, pl.ds(start + 128, 128)] = pair_ref[j, at, :]
        return carry

    lax.fori_loop(0, groups // 2, two, 0)
    br_ref[...] = mm_nt(ho_ref[...], wo_ref[...])


def spot(rows, b, start, experts):
    each = rows // experts
    at_row = lax.broadcasted_iota(jnp.int32, (rows, experts), 0)
    at_column = lax.broadcasted_iota(jnp.int32, (rows, experts), 1)
    return jnp.where(at_row == at_column * each + (start + b), 1.0, 0.0).astype(bf16)


def route_kernel(
    me_ref, x_ref, br_ref, cot_ref, mask_ref, ex_ref,
    res_ref, h_ref, soft_ref, sent_ref, sq_ref, *, images, seq, tall, experts
):
    rows = sent_ref.shape[0]
    half = rows // experts // 2
    router = ex_ref[2 : 2 + experts, :].astype(bf16)
    gain = ex_ref[1:2, :]
    total = jnp.zeros(sent_ref.shape, f32)
    for b in range(images):
        at = pl.ds(b * tall, tall)
        length = length_of(mask_ref, me_ref, b, images)
        branch = br_ref[at, :]
        resid = padded(x_ref[b].astype(f32), tall - seq) + branch
        res_ref[at, :] = resid
        unit, _ = unit_of(resid)
        h_two = (unit * gain).astype(bf16)
        h_ref[at, :] = h_two
        logits = mm_nt(router, h_two)
        held = jnp.where(seen_row(length, tall), logits, -1e30)
        terms = jnp.exp(held - jnp.max(held, axis=1, keepdims=True))
        dispatch = terms / jnp.sum(terms, axis=1, keepdims=True)
        terms = jnp.exp(logits - jnp.max(logits, axis=0, keepdims=True))
        combine = terms / jnp.sum(terms, axis=0, keepdims=True)
        soft_ref[0, b] = dispatch
        soft_ref[1, b] = combine
        cot = padded(cot_ref[b], tall - seq)
        wide_d = mm(spot(rows, b, 0, experts), dispatch.astype(bf16)).astype(bf16)
        wide_c = mm(spot(rows, b, half, experts), combine.astype(bf16)).astype(bf16)
        total += mm(wide_d, h_two) + mm(wide_c, cot)
        squares = jnp.sum(branch * branch, axis=1, keepdims=True)
        squares = jnp.sum(jnp.where(seen_column(length, tall), squares, 0.0), axis=0, keepdims=True)
        sq_ref[b] = jnp.broadcast_to(squares, (1, 128))
    sent_ref[...] = total.astype(bf16)


def expert_kernel(got_ref, first_ref, second_ref, hid_ref, pre_ref, grad_ref, back_ref, *, each):
    rows = got_ref.shape[0]
    half = each // 2
    got = got_ref[...]
    own = jnp.bitwise_and(lax.broadcasted_iota(jnp.int32, (rows, 1), 0), each - 1) < half
    grads = jnp.where(own, pltpu.roll(got.astype(f32), rows - half, 0), 0.0).astype(bf16)
    grad_ref[...] = grads
    u = mm(got, first_ref[...])
    cubic = 0.7978845608028654 * (u + 0.044715 * u * u * u)
    t = jnp.tanh(cubic)
    hidden = jnp.where(own, 0.5 * u * (1.0 + t), 0.0).astype(bf16)
    hid_ref[...] = hidden
    slope = 0.5 * (1.0 + t) + 0.5 * u * (1.0 - t * t) * 0.7978845608028654 * (
        1.0 + 3.0 * 0.044715 * u * u
    )
    grad_pre = (mm_nt(grads, second_ref[...]) * slope).astype(bf16)
    pre_ref[...] = grad_pre
    out = mm(hidden, second_ref[...])
    grad_in = mm_nt(grad_pre, first_ref[...])
    back_ref[...] = jnp.where(own, out, pltpu.roll(grad_in, half, 0)).astype(bf16)


def mix_kernel(
    me_ref, res_ref, h_ref, soft_ref, cot_ref, mask_ref, ex_ref, back_ref, sq_ref,
    out_ref, gres_ref, gb_ref, gbt_ref, small_ref, *, images, seq, tall, experts, groups
):
    small_ref[...] = jnp.zeros_like(small_ref)
    router = ex_ref[2 : 2 + experts, :].astype(bf16)
    gain = ex_ref[1:2, :]
    width = out_ref.shape[2]
    lanes = lax.broadcasted_iota(jnp.int32, (1, width), 1)
    roots = [jnp.zeros((1, width), f32) for _ in range(3)]
    for b in range(images):
        at = pl.ds(b * tall, tall)
        length = length_of(mask_ref, me_ref, b, images)
        resid, h_two = res_ref[at, :], h_ref[at, :]
        dispatch, combine = soft_ref[0, b], soft_ref[1, b]
        dispatch_low, combine_low = dispatch.astype(bf16), combine.astype(bf16)
        returned, grad_slots = back_ref[0, b], back_ref[1, b]
        cot = padded(cot_ref[b], tall - seq)
        mixed = mm_tn(combine_low, returned)
        stream = resid + mixed
        out_ref[b] = stream[:seq].astype(bf16)
        column = seen_column(length, tall)
        sums = []
        for value in (stream, mixed):
            squares = jnp.sum(value * value, axis=1, keepdims=True)
            sums.append(jnp.sum(jnp.where(column, squares, 0.0), axis=0, keepdims=True))
        sums.insert(1, sq_ref[b, :, 0:1])
        for k, value in enumerate(sums):
            root = jnp.sqrt(value / (length * width))
            mine = lanes == (me_ref[0] * groups + me_ref[2]) * images + b
            roots[k] += jnp.where(mine, root, 0.0)
        grad_c = mm_nt(returned, cot)
        grad_c = combine * (grad_c - jnp.sum(grad_c * combine, axis=0, keepdims=True))
        grad_d = mm_nt(grad_slots, h_two)
        grad_d = dispatch * (grad_d - jnp.sum(grad_d * dispatch, axis=1, keepdims=True))
        grad_logits = (grad_d + grad_c).astype(bf16)
        grad_h = mm_tn(dispatch_low, grad_slots) + mm_tn(grad_logits, router)
        small_ref[0:experts, :] += mm(grad_logits, h_two)
        unit, inverse = unit_of(resid)
        small_ref[experts + 1 : experts + 2, :] += jnp.sum(grad_h * unit, axis=0, keepdims=True)
        scaled = grad_h * gain
        mean_grad = jnp.mean(scaled, axis=-1, keepdims=True)
        mean_proj = jnp.mean(scaled * unit, axis=-1, keepdims=True)
        gres_ref[at, :] = cot.astype(f32) + inverse * (scaled - mean_grad - unit * mean_proj)
    for k in range(3):
        small_ref[experts + 2 + k : experts + 3 + k, :] = roots[k]
    gb_ref[...] = gres_ref[...].astype(bf16)
    gbt_ref[...] = gres_ref[...].T.astype(bf16)


def back_kernel(
    me_ref, gb_ref, gbt_ref, ht_ref, qkv_a, p_a, qkv_b, p_b, ho_ref, wo_ref,
    gw_ref, gj_ref, dho_ref, *, images, tall, x, flip
):
    j = x + 2 * jnp.bitwise_xor(me_ref[1], flip)
    own = pl.ds(pl.multiple_of(j * 256, 256), 256)
    scale = HEAD_DIM ** (-0.5)
    low = low_lanes(tall)
    dho_ref[...] = mm(gb_ref[...], wo_ref[:, own])
    for b in range(images):
        at = pl.ds(b * tall, tall)
        joined, joined_last = qkv_a[j, at, :], qkv_b[j, at, :]
        q_pair, k_pair, v_pair = joined[:, :128], joined[:, 128:256], joined[:, 256:384]
        qk_last, v_last = joined_last[:, :128], joined_last[:, 128:256]
        grad = dho_ref[at, :].astype(bf16).astype(f32)
        product = grad * ho_ref[at, own].astype(f32)
        single, pair = product[:, :128], product[:, 128:]
        dots = (
            jnp.sum(jnp.where(low, pair, 0.0), axis=1, keepdims=True),
            jnp.sum(jnp.where(low, 0.0, pair), axis=1, keepdims=True),
            jnp.sum(single, axis=1, keepdims=True),
        )
        grad_pair = grad[:, 128:]
        grad_last = jnp.where(low, pltpu.roll(grad[:, :128], HEAD_DIM, 1), 0.0).astype(bf16)
        gq, gk, gv = [], [], []
        for head, (probs, g, v, q, k) in enumerate(
            (
                (p_a[j, b, 0], jnp.where(low, grad_pair, 0.0).astype(bf16), v_pair, q_pair, k_pair),
                (p_a[j, b, 1], jnp.where(low, 0.0, grad_pair).astype(bf16), v_pair, q_pair, k_pair),
                (p_b[j, b], grad_last, v_last, qk_last, qk_last),
            )
        ):
            grad_p = mm_nt(g, v)
            grad_s = (probs.astype(f32) * (grad_p - dots[head])).astype(bf16)
            gq.append(mm(grad_s, k))
            gk.append(mm_tn(grad_s, q))
            gv.append(mm_tn(probs, g))
        last = pltpu.roll(jnp.where(low, gk[2], gq[2]), HEAD_DIM, 1)
        gj_ref[at, :] = jnp.concatenate(
            [
                jnp.where(low, gq[0], gq[1]) * scale,
                jnp.where(low, gk[0], gk[1]) * scale,
                gv[0] + gv[1],
                last * scale,
                gv[2],
            ],
            1,
        ).astype(bf16)
    grad_out = mm(gbt_ref[...], ho_ref[:, own])
    grad_in = mm(ht_ref[...], gj_ref[...])
    halves, blocks, rows = gw_ref.shape[:3]
    for d in range(halves * blocks):
        r = jnp.bitwise_xor(me_ref[0], d) if halves > 1 else 0
        entry = (jnp.bitwise_and(r, 1), jnp.right_shift(r, 1)) if halves > 1 else (0, 0)
        at = slice(d * rows, (d + 1) * rows)
        gw_ref[entry + (slice(None), slice(0, 512))] = grad_in[at, :512].astype(bf16)
        gw_ref[entry + (slice(None), slice(512, 640))] = (
            grad_in[at, 512:] + grad_out[at, :128]
        ).astype(bf16)
        gw_ref[entry + (slice(None), slice(640, 768))] = grad_out[at, 128:].astype(bf16)


def last_kernel(
    me_ref, x_ref, gres_ref, ex_ref, part_ref, w_a, w_b, *refs, images, seq, tall, experts, order
):
    grads, (gt_ref, small_ref, gh_ref) = refs[:-3], refs[-3:]
    total = jnp.zeros((1, x_ref.shape[2]), f32)
    gain = ex_ref[0:1, :]
    for k, (ref, (x, flip)) in enumerate(zip(grads, order)):
        j = x + 2 * jnp.bitwise_xor(me_ref[1], flip)
        into = mm_nt(ref[:, :384], w_a[j]) + mm_nt(ref[:, 384:], w_b[j, :, :256])
        if k == 0:
            gh_ref[...] = into
        else:
            gh_ref[...] += into
    for b in range(images):
        at = pl.ds(b * tall, seq)
        unit, inverse = unit_of(x_ref[b].astype(f32))
        grad_h = gh_ref[at, :]
        total += jnp.sum(grad_h * unit, axis=0, keepdims=True)
        scaled = grad_h * gain
        mean_grad = jnp.mean(scaled, axis=-1, keepdims=True)
        mean_proj = jnp.mean(scaled * unit, axis=-1, keepdims=True)
        gt_ref[b] = gres_ref[at, :] + inverse * (scaled - mean_grad - unit * mean_proj)
    small_ref[...] = part_ref[...]
    small_ref[experts : experts + 1, :] = total


def cost(microseconds):
    return int(microseconds * 1.1e9)


def call(kernel, outs, args, scratch=(), flops=0, name=None, scalars=1, grant=16, **static):
    spec = pl.BlockSpec(memory_space=pltpu.VMEM)
    word = pl.BlockSpec(memory_space=pltpu.SMEM)
    moved = sum(math.prod(a.shape) * a.dtype.itemsize for a in args)
    return pl.pallas_call(
        functools.partial(kernel, **static),
        out_shape=[jax.ShapeDtypeStruct(s, d) for s, d in outs],
        in_specs=[word] * scalars + [spec] * (len(args) - scalars),
        out_specs=[spec] * len(outs),
        scratch_shapes=list(scratch),
        compiler_params=pltpu.CompilerParams(vmem_limit_bytes=grant << 20),
        cost_estimate=pl.CostEstimate(flops=flops, bytes_accessed=moved, transcendentals=0),
        name=name,
    )(*args)


def make(mesh):
    dp, mp = mesh.shape["dp"], mesh.shape["mp"]

    def per_device(
        tokens, token_mask, gain_one, w_qkv, w_out, gain_two, router, w_in, w_back, cotangent
    ):
        rows, width = tokens.shape
        seq = token_mask.shape[1]
        tall = -(-seq // 16) * 16
        images = rows // seq
        experts = router.shape[1]
        d_rows, _, part = w_qkv.shape
        count = images * tall
        high = dp // 2
        heads = part // HEAD_DIM
        ready = d_rows % 16 != 0
        each = 2 * (1 << (images - 1).bit_length())
        me = lax.axis_index("dp")
        at_mp = lax.axis_index("mp")
        core = at_mp & 1
        words = jnp.stack([me, core, at_mp]).astype(jnp.int32)
        static = {"images": images, "tall": tall}
        exact = {"images": images, "seq": seq, "tall": tall}

        columns = experts + 2
        half = 2 * part
        hbm = pl.BlockSpec(memory_space=pltpu.HBM)
        vmem = pl.BlockSpec(memory_space=pltpu.VMEM)
        word = pl.BlockSpec(memory_space=pltpu.SMEM)
        wide = columns + -columns % 128
        shapes = [(3, d_rows, part), (part, d_rows), (1, d_rows), (1, d_rows), (experts, d_rows)]
        first, second, extra = pl.pallas_call(
            pack_kernel,
            out_shape=[jax.ShapeDtypeStruct((d_rows, n), bf16) for n in (half, half, wide)],
            in_specs=[word] + [hbm] * 5,
            out_specs=[vmem] * 3,
            scratch_shapes=[pltpu.VMEM(shape, bf16) for shape in shapes] + [pltpu.SemaphoreType.DMA((5,))],
            compiler_params=pltpu.CompilerParams(vmem_limit_bytes=67_000_000),
            name="pack",
        )(words, w_qkv.transpose(1, 0, 2), w_out, gain_one[None], gain_two[None], router.T)

        first, second, held_extra = first[None], second[None], extra[None]
        for bit in bits_of(dp)[:-1]:
            other, other_extra = lax.optimization_barrier(
                (swap(first, "dp", dp, bit), swap(held_extra, "dp", dp, bit))
            )
            first = jnp.concatenate([first, other])
            held_extra = jnp.concatenate([held_extra, other_extra])
            second = jnp.concatenate([second, swap(second, "dp", dp, bit)])
        other, other_extra = lax.optimization_barrier(
            (swap_both(first, dp, mp, (1, 0), (0, 2)), swap(held_extra, "dp", dp, 1))
        )
        held_extra = jnp.concatenate([held_extra, other_extra])
        near = jnp.stack([first, other])
        far = swap_both(near, dp, mp, (0, 2), (1, 0))
        first = (near, far, swap(near, "mp", mp, 1), swap(far, "mp", mp, 1))
        near = jnp.stack([second, swap_both(second, dp, mp, (1, 0), (0, 2))])
        second_near, second_far = near, swap_both(near, dp, mp, (0, 2), (1, 0))
        second_near_other = swap(second_near, "mp", mp, 1)

        def whole(x, of_core, near, far, other_near, other_far):
            mine = core == of_core
            low = jnp.where(mine, near, other_near)
            high_part = jnp.where(mine, far, other_far)
            blocks = jnp.stack([low[x], high_part[x]]) if of_core else (high_part if x else low)
            blocks = blocks.reshape((dp, d_rows, half))
            blocks = unmirrored(blocks)
            return reorder(blocks, me).reshape(width, half)

        def weights_of(parts):
            if ready:
                return tuple(whole(j & 1, j >> 1, *parts) for j in range(4))
            return parts

        if ready:
            held_extra = reorder(unmirrored(held_extra), me).reshape(1, width, -1)

        x3 = tokens.reshape(images, seq, width)
        cot3 = cotangent.reshape(images, seq, width)
        h_one, h_turned, ex = call(
            prep_kernel,
            [((count, width), bf16), ((width, count), bf16), ((held_extra.shape[2], width), f32)],
            (words, x3, held_extra),
            flops=cost(2),
            name="prep",
            grant=4,
            **exact,
        )

        def saved(columns, probs):
            return [
                ((mp, width, half), bf16),
                ((mp, count, columns), bf16),
                ((mp, images) + probs + (tall, tall), bf16),
                ((mp, count, 128), bf16),
            ]

        pair = call(
            front_pair_kernel,
            saved(384, (2,)),
            (words, h_one, token_mask) + weights_of(first),
            flops=cost(10),
            name="front_pair",
            grant=10,
            ready=ready,
            **static,
        )
        w_a, qkv_a, p_a, ho_a = pair
        second_far, ho_a = lax.optimization_barrier((second_far, ho_a))
        second = (second_near, second_far, second_near_other, swap(second_far, "mp", mp, 1))
        w_b, qkv_b, p_b, heads_out, w_heads, branch = call(
            front_last_kernel,
            saved(256, ())[:3]
            + [
                ((count, 256 * mp), bf16),
                ((width, 256 * mp), bf16),
                ((count, width), f32),
            ],
            (words, h_one, token_mask, ho_a) + weights_of(second),
            flops=cost(7),
            name="front_last",
            grant=10,
            ready=ready,
            **static,
        )
        resid, h_two, soft, sent, sq_branch = call(
            route_kernel,
            [
                ((count, width), f32),
                ((count, width), bf16),
                ((2, images, experts, tall), f32),
                ((experts * each, width), bf16),
                ((images, 1, 128), f32),
            ],
            (words, x3, branch, cot3, token_mask, ex),
            flops=cost(2),
            name="route",
            grant=6,
            experts=experts,
            **exact,
        )
        got = sent.reshape(dp, each, width)
        got = lax.all_to_all(got, "dp", split_axis=0, concat_axis=0, tiled=True)
        got = gather_mp(got, mp).reshape(-1, width)
        everyone = got.shape[0]
        hidden, grad_pre, grad_expert, back = call(
            expert_kernel,
            [
                ((everyone, w_in.shape[2]), bf16),
                ((everyone, w_in.shape[2]), bf16),
                ((everyone, width), bf16),
                ((everyone, width), bf16),
            ],
            (got, w_in[0], w_back[0]),
            flops=cost(2),
            name="expert",
            scalars=0,
            grant=12 if dp <= 8 else 56,
            each=each,
        )
        back = back.reshape(mp, dp, each, width)
        back = scatter(back, "mp", mp, [1, 2])
        back = lax.all_to_all(back, "dp", split_axis=0, concat_axis=0, tiled=True)
        back = back.reshape(dp, 2, each // 2, width)[:, :, :images].transpose(1, 2, 0, 3)
        grad_w_back = mm_tn(hidden, grad_expert)
        grad_w_in = mm_tn(got, grad_pre)

        out_rows, grad_resid, grad_low, grad_turned, small = call(
            mix_kernel,
            [
                ((images, seq, width), bf16),
                ((count, width), f32),
                ((count, width), bf16),
                ((width, count), bf16),
                ((experts + 5, width), f32),
            ],
            (words, resid, h_two, soft, cot3, token_mask, ex, back, sq_branch),
            flops=cost(5),
            name="mix",
            grant=8,
            experts=experts,
            groups=mp,
            **exact,
        )
        shape = (1, 1, width, 4 * part) if ready else (2, high, d_rows, 4 * part)

        def back_of(x, flip, grad_in):
            grads, joined = call(
                back_kernel,
                [(shape, bf16), ((count, JOINED), bf16)],
                (words, grad_in, grad_turned, h_turned, qkv_a, p_a, qkv_b, p_b, heads_out, w_heads),
                [pltpu.VMEM((count, 256), f32)],
                flops=cost(8),
                name="back",
                grant=10,
                x=x,
                flip=flip,
                **static,
            )
            if ready:
                grads = reorder(grads.reshape(dp, d_rows, 4 * part), me)
                grads = grads.reshape(high, 2, d_rows, 4 * part).transpose(1, 0, 2, 3)
            return grads, joined

        def fold(terms, halves):
            size = terms[0].shape
            kept = ((size[0] // 2,) + size[1:], bf16)
            return call(
                fold_kernel,
                [kept, kept],
                terms,
                flops=cost(1),
                name="fold",
                scalars=0,
                grant=6,
                halves=halves,
            )

        order = ((1, 1), (1, 0), (0, 1), (0, 0))
        sent_grads, joined_a = back_of(1, 1, grad_low)
        other = swap(sent_grads, "mp", mp, 1)
        grad_low, joined_a = lax.optimization_barrier((grad_low, joined_a))
        kept_grads, joined_b = back_of(1, 0, grad_low)
        far_kept, far_left = fold((kept_grads, other), True)
        far_left, grad_low, joined_b = lax.optimization_barrier((far_left, grad_low, joined_b))
        early = swap_both(far_left[0], dp, mp, (0, 2), (1, 0))
        sent_grads, joined_c = back_of(0, 1, grad_low)
        early, grad_low, joined_c = lax.optimization_barrier((early, grad_low, joined_c))
        other = swap(sent_grads, "mp", mp, 1)
        kept_grads, joined_d = back_of(0, 0, grad_low)
        part_shape = ((high, d_rows, 4 * part), bf16)
        near_sum, second, third = call(
            blend_kernel,
            [part_shape] * 3,
            (words, far_kept[0], kept_grads, other, early),
            flops=cost(1),
            name="blend",
            grant=8,
        )
        second = swap_both(second, dp, mp, (0, 2), (1, 0))
        third = swap_both(third, dp, mp, (1, 0), (0, 2))
        grad_tokens, small, _ = call(
            last_kernel,
            [((images, seq, width), f32), ((experts + 5, width), f32), ((count, width), f32)],
            (words, x3, grad_resid, ex, small, w_a, w_b, joined_a, joined_b, joined_c, joined_d),
            flops=cost(6),
            name="last",
            grant=8,
            experts=experts,
            order=order,
            **exact,
        )
        for bit in bits_of(dp)[:-1]:
            small = small + swap(small, "dp", dp, bit)
        kept, left = fold((near_sum, second, third), False)
        left, small = lax.optimization_barrier((left, small))
        for bit in bits_of(high)[:0:-1]:
            kept, left = fold((kept, swap(left, "dp", dp, 2 * bit)), False)
        own, other = kept[0], swap(left[0], "dp", dp, 2 * bits_of(high)[0])
        grad_qkv, grad_out = call(
            unpack_kernel,
            [((3, d_rows, part), f32), ((part, d_rows), f32)],
            (own, other),
            flops=cost(1),
            name="unpack",
            scalars=0,
            grant=6,
        )
        small = small + swap(small, "dp", dp, 1)
        small = small + swap(small, "mp", mp, 2)
        grad_one, grad_two, grad_router, root_squares = call(
            finish_kernel,
            [
                ((1, d_rows), f32),
                ((1, d_rows), f32),
                ((experts, d_rows), f32),
                ((3, mp * images), f32),
            ],
            (words, small, swap(small, "mp", mp, 1)),
            flops=cost(1),
            name="finish",
            grant=4,
        )
        return (
            out_rows.reshape(rows, width),
            grad_tokens.reshape(rows, width),
            grad_one[0],
            grad_qkv.transpose(1, 0, 2),
            grad_out,
            grad_two[0],
            grad_router.T,
            grad_w_in[None],
            grad_w_back[None],
            root_squares,
        )

    return per_device


def solution(mesh):
    in_specs = (
        P(("dp", "mp"), None),
        P("dp", None),
        P("dp"),
        P("dp", None, "mp"),
        P("mp", "dp"),
        P("dp"),
        P("dp", None),
        P("dp", None, "mp"),
        P("dp", "mp", None),
        P(("dp", "mp"), None),
    )
    out_specs = (
        P(("dp", "mp"), None),
        P(("dp", "mp"), None),
        P("dp"),
        P("dp", None, "mp"),
        P("mp", "dp"),
        P("dp"),
        P("dp", None),
        P("dp", None, "mp"),
        P("dp", "mp", None),
        P(None, "dp"),
    )
    return jax.shard_map(
        make(mesh), mesh=mesh, in_specs=in_specs, out_specs=out_specs, check_vma=False
    )
```

```python
import functools
import math

import jax
import jax.numpy as jnp
from jax import lax
from jax.experimental import pallas as pl
from jax.experimental.pallas import tpu as pltpu
from jax.sharding import PartitionSpec as P

HEAD_DIM = 64


epsilon = 1e-06
bf16 = jnp.bfloat16
f32 = jnp.float32


def bits_of(size):
    return [1 << k for k in reversed(range(size.bit_length() - 1))]


def swap(array_in, axis_name, size, bit):
    return lax.ppermute(array_in, axis_name, [(i, i ^ bit) for i in range(size)])


def swap_both(array_in, dp, mp, even, odd):
    pairs = []
    for d in range(dp):
        for m in range(mp):
            flip = odd if m & 1 else even
            pairs.append((d * mp + m, (d ^ flip[0]) * mp + (m ^ flip[1])))
    return lax.ppermute(array_in, ("dp", "mp"), pairs)


def gather_mp(block, mp):
    held = block[None]
    for bit in bits_of(mp):
        other = swap(held, "mp", mp, bit)
        held = jnp.stack([held, other], 1).reshape((-1,) + block.shape)
    return held


def scatter(held, axis_name, size, bits, unit=1):
    left = sorted(bits)
    for bit in bits:
        inner = 1 << left.index(bit)
        left.remove(bit)
        pairs = held.reshape((held.shape[0] // (2 * inner), 2, inner) + held.shape[1:])
        other = swap(pairs[:, 1], axis_name, size, bit * unit)
        held = pairs[:, 0].astype(f32) + other.astype(f32)
        held = held.astype(bf16).reshape((-1,) + held.shape[2:])
    return held[0]


def mirrored(index, size):
    bits = size.bit_length() - 1
    return sum(((index >> k) & 1) << (bits - 1 - k) for k in range(bits)) if bits else index


def unmirrored(blocks):
    size = blocks.shape[0]
    bits = size.bit_length() - 1
    split = blocks.reshape((2,) * bits + blocks.shape[1:])
    turn = tuple(range(bits))[::-1] + tuple(range(bits, split.ndim))
    return split.transpose(turn).reshape(blocks.shape)


def reorder(blocks, me):
    size = blocks.shape[0]
    for bit in bits_of(size):
        pairs = blocks.reshape((size // (2 * bit), 2, bit) + blocks.shape[1:])
        blocks = jnp.where((me & bit) > 0, pairs[:, ::-1], pairs).reshape(blocks.shape)
    return blocks


def mm(a, b):
    return lax.dot_general(a, b, (((1,), (0,)), ((), ())), preferred_element_type=f32)


def mm_nt(a, b):
    return lax.dot_general(a, b, (((1,), (1,)), ((), ())), preferred_element_type=f32)


def mm_tn(a, b):
    return lax.dot_general(a, b, (((0,), (0,)), ((), ())), preferred_element_type=f32)


def unit_of(rows_f):
    mean_row = jnp.mean(rows_f, axis=-1, keepdims=True)
    centered = rows_f - mean_row
    variance = jnp.mean(centered * centered, axis=-1, keepdims=True)
    inverse = lax.rsqrt(variance + epsilon)
    return centered * inverse, inverse


def padded(value, pad):
    return jnp.concatenate([value, jnp.zeros((pad, value.shape[1]), value.dtype)], 0)


def low_lanes(rows):
    return lax.broadcasted_iota(jnp.int32, (rows, 128), 1) < HEAD_DIM


JOINED = 640


def pack_kernel(
    me_ref, qkv_hbm, out_hbm, one_hbm, two_hbm, router_hbm, first_ref, second_ref, extra_ref,
    qkv_ref, out_ref, one_ref, two_ref, router_ref, sems
):
    del me_ref
    pairs = (
        (qkv_hbm, qkv_ref), (out_hbm, out_ref), (one_hbm, one_ref), (two_hbm, two_ref), (router_hbm, router_ref),
    )
    copies = [pltpu.make_async_copy(a, b, sems.at[k]) for k, (a, b) in enumerate(pairs)]
    for copy in copies:
        copy.start()
    for copy in copies:
        copy.wait()
    low, mid = 2 * HEAD_DIM, qkv_ref.shape[2]
    out = out_ref[...].astype(f32).T.astype(bf16)
    first_ref[...] = jnp.concatenate([qkv_ref[c, :, :low] for c in range(3)], axis=1)
    second_ref[...] = jnp.concatenate(
        [qkv_ref[c, :, low:mid] for c in range(3)] + [out[:, low:mid], out[:, :low]], axis=1
    )
    rows = one_ref.shape[1]
    columns = [one_ref[...], two_ref[...], router_ref[...]]
    columns = [value.astype(f32) for value in columns]
    filled = sum(value.shape[0] for value in columns)
    columns.append(jnp.zeros((extra_ref.shape[1] - filled, rows), f32))
    extra_ref[...] = jnp.concatenate(columns, 0).T.astype(bf16)


def fold_kernel(*refs, halves):
    terms, (kept_ref, left_ref) = refs[:-2], refs[-2:]
    size = terms[0].shape[0]
    for k in range(size):
        total = terms[0][k].astype(f32)
        for term in terms[1:]:
            total = total + term[k].astype(f32)
        at, odd = (k % (size // 2), k >= size // 2) if halves else (k // 2, k % 2 == 1)
        (left_ref if odd else kept_ref)[at] = total.astype(bf16)


def blend_kernel(me_ref, far_ref, kept_ref, other_ref, early_ref, near_ref, second_ref, third_ref):
    near = [kept_ref[k].astype(f32) + other_ref[k].astype(f32) for k in (0, 1)]
    near_ref[...] = near[0].astype(bf16)
    first_core = me_ref[1] == 0

    @pl.when(first_core)
    def _():
        second_ref[...] = far_ref[...]
        third_ref[...] = (near[1] + early_ref[...].astype(f32)).astype(bf16)

    @pl.when(jnp.logical_not(first_core))
    def _():
        second_ref[...] = near[1].astype(bf16)
        third_ref[...] = (far_ref[...].astype(f32) + early_ref[...].astype(f32)).astype(bf16)


def finish_kernel(me_ref, own_ref, other_ref, one_ref, two_ref, router_ref, root_ref):
    experts, rows = router_ref.shape
    total = own_ref[...] + other_ref[...]
    width = total.shape[1]
    mine = pltpu.roll(total, lax.rem(width - me_ref[0] * rows, width), 1)
    one_ref[...] = mine[experts : experts + 1, :rows]
    two_ref[...] = mine[experts + 1 : experts + 2, :rows]
    router_ref[...] = mine[:experts, :rows]
    images = root_ref.shape[1]
    mine = pltpu.roll(total, lax.rem(width - me_ref[0] * images, width), 1)
    root_ref[...] = mine[experts + 2 : experts + 5, :images]


def unpack_kernel(own_ref, other_ref, qkv_ref, out_ref):
    low, mid = 2 * HEAD_DIM, qkv_ref.shape[2]
    summed = own_ref[...].astype(f32) + other_ref[...].astype(f32)
    for c in range(3):
        qkv_ref[c, :, :low] = summed[:, c * low : (c + 1) * low]
        start = 3 * low + c * HEAD_DIM
        qkv_ref[c, :, low:mid] = summed[:, start : start + HEAD_DIM]
    out_ref[...] = jnp.concatenate([summed[:, 640:], summed[:, 576:640]], axis=1).T


def length_of(mask_ref, me_ref, b, images):
    row = mask_ref[pl.ds(me_ref[2] * images + b, 1), :]
    return jnp.sum(row.astype(f32), axis=1, keepdims=True)


def seen_row(length, tall):
    return lax.broadcasted_iota(jnp.int32, (1, tall), 1).astype(f32) < length


def seen_column(length, tall):
    return lax.broadcasted_iota(jnp.int32, (tall, 1), 0).astype(f32) < length


def prep_kernel(me_ref, x_ref, extra_ref, h_ref, ht_ref, small_ref, *, images, seq, tall):
    blocks = extra_ref.shape[0]
    me = me_ref[0]
    parts = [extra_ref[mirrored(me ^ d, blocks) if blocks > 1 else 0] for d in range(blocks)]
    small_ref[...] = jnp.concatenate(parts, 0).astype(f32).T
    gain = small_ref[0:1, :]
    for b in range(images):
        unit, _ = unit_of(x_ref[b].astype(f32))
        h_ref[pl.ds(b * tall, tall), :] = padded((unit * gain).astype(bf16), tall - seq)
    ht_ref[...] = h_ref[...].T


def fetch_all(me_ref, refs, put):
    rows, high_size = refs[0].shape[2], refs[0].shape[1]
    for core in (0, 1):

        @pl.when(me_ref[1] == core)
        def _(core=core):
            for slot in range(4):
                x, of_core = slot & 1, slot >> 1
                first, second = refs[:2] if of_core == core else refs[2:4]
                for r in range(2 * high_size):
                    low, high = r & 1, mirrored(r >> 1, high_size)
                    if of_core == 0:
                        block = (second if x else first)[low, high]
                    else:
                        block = (second if low else first)[x, high]
                    d = jnp.bitwise_xor(me_ref[0], r)
                    put(slot, pl.ds(pl.multiple_of(d * rows, 16), rows), block)


def attend(triples):
    scores = [mm_nt(q, k) * HEAD_DIM ** (-0.5) + bias for q, k, _, bias in triples]
    terms = [jnp.exp(value - jnp.max(value, axis=-1, keepdims=True)) for value in scores]
    probs = [
        (value * (1.0 / jnp.sum(value, axis=-1, keepdims=True))).astype(bf16) for value in terms
    ]
    return probs, [mm(value, v) for value, (_, _, v, _) in zip(probs, triples)]


def bias_of(mask_ref, me_ref, b, images, tall):
    return jnp.where(seen_row(length_of(mask_ref, me_ref, b, images), tall), 0.0, -1e30)


def front_pair_kernel(me_ref, h_ref, mask_ref, *refs, images, tall, ready):
    w_ref, qkv_ref, p_ref, ho_ref = refs[4:]

    def put(slot, at, block):
        w_ref[slot, at, :] = block

    if ready:
        for slot in range(4):
            put(slot, slice(None), refs[slot][...])
    else:
        fetch_all(me_ref, refs[:4], put)
    low = low_lanes(tall)

    def group(j, carry):
        qkv_ref[j] = mm(h_ref[...], w_ref[j]).astype(bf16)
        triples = []
        for b in range(images):
            joined = qkv_ref[j, pl.ds(b * tall, tall), :]
            q, k, v = joined[:, :128], joined[:, 128:256], joined[:, 256:384]
            none = jnp.zeros_like(q)
            bias = bias_of(mask_ref, me_ref, b, images, tall)
            triples.append((jnp.where(low, q, none), k, v, bias))
            triples.append((jnp.where(low, none, q), k, v, bias))
        probs, outs = attend(triples)
        for b in range(images):
            p_ref[j, b, 0], p_ref[j, b, 1] = probs[2 * b], probs[2 * b + 1]
            pair = jnp.where(low, outs[2 * b], outs[2 * b + 1])
            ho_ref[j, pl.ds(b * tall, tall), :] = pair.astype(bf16)
        return carry

    lax.fori_loop(0, w_ref.shape[0], group, 0)


def front_last_kernel(me_ref, h_ref, mask_ref, pair_ref, *refs, images, tall, ready):
    w_ref, qkv_ref, p_ref, ho_ref, wo_ref, br_ref = refs[4:]

    def put(slot, at, block):
        w_ref[slot, at, :] = block[:, :256]
        wo_ref[at, slot * 256 : (slot + 1) * 256] = block[:, 128:]

    if ready:
        for slot in range(4):
            put(slot, slice(None), refs[slot][...])
    else:
        fetch_all(me_ref, refs[:4], put)
    low = low_lanes(tall)

    def two(i, carry):
        places = [(2 * i + k, b) for k in (0, 1) for b in range(images)]
        for j in (2 * i, 2 * i + 1):
            qkv_ref[j] = mm(h_ref[...], w_ref[j]).astype(bf16)
        triples = []
        for j, b in places:
            joined = qkv_ref[j, pl.ds(b * tall, tall), :]
            qk, v = joined[:, :128], joined[:, 128:256]
            k = pltpu.roll(qk.astype(f32), HEAD_DIM, 1).astype(bf16)
            bias = bias_of(mask_ref, me_ref, b, images, tall)
            triples.append((jnp.where(low, qk, jnp.zeros_like(qk)), k, v, bias))
        probs, outs = attend(triples)
        for (j, b), prob, out in zip(places, probs, outs):
            at, start = pl.ds(b * tall, tall), pl.multiple_of(j * 256, 256)
            p_ref[j, b] = prob
            ho_ref[at, pl.ds(start, 128)] = jnp.where(low, 0.0, pltpu.roll(out, HEAD_DIM, 1)).astype(bf16)
            ho_ref[at, pl.ds(start + 128, 128)] = pair_ref[j, at, :]
        return carry

    lax.fori_loop(0, w_ref.shape[0] // 2, two, 0)
    br_ref[...] = mm_nt(ho_ref[...], wo_ref[...])


def spot(rows, b, start, experts):
    each = rows // experts
    at_row = lax.broadcasted_iota(jnp.int32, (rows, experts), 0)
    at_column = lax.broadcasted_iota(jnp.int32, (rows, experts), 1)
    return jnp.where(at_row == at_column * each + (start + b), 1.0, 0.0).astype(bf16)


def route_kernel(
    me_ref, x_ref, br_ref, cot_ref, mask_ref, ex_ref,
    res_ref, h_ref, soft_ref, sent_ref, sq_ref, *, images, seq, tall, experts
):
    rows = sent_ref.shape[0]
    half = rows // experts // 2
    router = ex_ref[2 : 2 + experts, :].astype(bf16)
    gain = ex_ref[1:2, :]
    total = jnp.zeros(sent_ref.shape, f32)
    for b in range(images):
        at = pl.ds(b * tall, tall)
        length = length_of(mask_ref, me_ref, b, images)
        branch = br_ref[at, :]
        resid = padded(x_ref[b].astype(f32), tall - seq) + branch
        res_ref[at, :] = resid
        unit, _ = unit_of(resid)
        h_two = (unit * gain).astype(bf16)
        h_ref[at, :] = h_two
        logits = mm_nt(router, h_two)
        held = jnp.where(seen_row(length, tall), logits, -1e30)
        terms = jnp.exp(held - jnp.max(held, axis=1, keepdims=True))
        dispatch = terms / jnp.sum(terms, axis=1, keepdims=True)
        terms = jnp.exp(logits - jnp.max(logits, axis=0, keepdims=True))
        combine = terms / jnp.sum(terms, axis=0, keepdims=True)
        soft_ref[0, b] = dispatch
        soft_ref[1, b] = combine
        cot = padded(cot_ref[b], tall - seq)
        wide_d = mm(spot(rows, b, 0, experts), dispatch.astype(bf16)).astype(bf16)
        wide_c = mm(spot(rows, b, half, experts), combine.astype(bf16)).astype(bf16)
        total += mm(wide_d, h_two) + mm(wide_c, cot)
        squares = jnp.sum(branch * branch, axis=1, keepdims=True)
        squares = jnp.sum(jnp.where(seen_column(length, tall), squares, 0.0), axis=0, keepdims=True)
        sq_ref[b] = jnp.broadcast_to(squares, (1, 128))
    sent_ref[...] = total.astype(bf16)


def expert_kernel(got_ref, first_ref, second_ref, hid_ref, pre_ref, grad_ref, back_ref, *, each):
    rows = got_ref.shape[0]
    half = each // 2
    got = got_ref[...]
    own = jnp.bitwise_and(lax.broadcasted_iota(jnp.int32, (rows, 1), 0), each - 1) < half
    grads = jnp.where(own, pltpu.roll(got.astype(f32), rows - half, 0), 0.0).astype(bf16)
    grad_ref[...] = grads
    u = mm(got, first_ref[...])
    cubic = 0.7978845608028654 * (u + 0.044715 * u * u * u)
    t = jnp.tanh(cubic)
    hidden = jnp.where(own, 0.5 * u * (1.0 + t), 0.0).astype(bf16)
    hid_ref[...] = hidden
    slope = 0.5 * (1.0 + t) + 0.5 * u * (1.0 - t * t) * 0.7978845608028654 * (
        1.0 + 3.0 * 0.044715 * u * u
    )
    grad_pre = (mm_nt(grads, second_ref[...]) * slope).astype(bf16)
    pre_ref[...] = grad_pre
    out = mm(hidden, second_ref[...])
    grad_in = mm_nt(grad_pre, first_ref[...])
    back_ref[...] = jnp.where(own, out, pltpu.roll(grad_in, half, 0)).astype(bf16)


def mix_kernel(
    me_ref, res_ref, h_ref, soft_ref, cot_ref, mask_ref, ex_ref, back_ref, sq_ref,
    out_ref, gres_ref, gb_ref, gbt_ref, small_ref, *, images, seq, tall, experts, groups
):
    small_ref[...] = jnp.zeros_like(small_ref)
    router = ex_ref[2 : 2 + experts, :].astype(bf16)
    gain = ex_ref[1:2, :]
    width = out_ref.shape[2]
    lanes = lax.broadcasted_iota(jnp.int32, (1, width), 1)
    roots = [jnp.zeros((1, width), f32) for _ in range(3)]
    for b in range(images):
        at = pl.ds(b * tall, tall)
        length = length_of(mask_ref, me_ref, b, images)
        resid, h_two = res_ref[at, :], h_ref[at, :]
        dispatch, combine = soft_ref[0, b], soft_ref[1, b]
        dispatch_low, combine_low = dispatch.astype(bf16), combine.astype(bf16)
        returned, grad_slots = back_ref[0, b], back_ref[1, b]
        cot = padded(cot_ref[b], tall - seq)
        mixed = mm_tn(combine_low, returned)
        stream = resid + mixed
        out_ref[b] = stream[:seq].astype(bf16)
        column = seen_column(length, tall)
        sums = []
        for value in (stream, mixed):
            squares = jnp.sum(value * value, axis=1, keepdims=True)
            sums.append(jnp.sum(jnp.where(column, squares, 0.0), axis=0, keepdims=True))
        sums.insert(1, sq_ref[b, :, 0:1])
        for k, value in enumerate(sums):
            root = jnp.sqrt(value / (length * width))
            mine = lanes == (me_ref[0] * groups + me_ref[2]) * images + b
            roots[k] += jnp.where(mine, root, 0.0)
        grad_c = mm_nt(returned, cot)
        grad_c = combine * (grad_c - jnp.sum(grad_c * combine, axis=0, keepdims=True))
        grad_d = mm_nt(grad_slots, h_two)
        grad_d = dispatch * (grad_d - jnp.sum(grad_d * dispatch, axis=1, keepdims=True))
        grad_logits = (grad_d + grad_c).astype(bf16)
        grad_h = mm_tn(dispatch_low, grad_slots) + mm_tn(grad_logits, router)
        small_ref[0:experts, :] += mm(grad_logits, h_two)
        unit, inverse = unit_of(resid)
        small_ref[experts + 1 : experts + 2, :] += jnp.sum(grad_h * unit, axis=0, keepdims=True)
        scaled = grad_h * gain
        mean_grad = jnp.mean(scaled, axis=-1, keepdims=True)
        mean_proj = jnp.mean(scaled * unit, axis=-1, keepdims=True)
        gres_ref[at, :] = cot.astype(f32) + inverse * (scaled - mean_grad - unit * mean_proj)
    for k in range(3):
        small_ref[experts + 2 + k : experts + 3 + k, :] = roots[k]
    gb_ref[...] = gres_ref[...].astype(bf16)
    gbt_ref[...] = gres_ref[...].T.astype(bf16)


def back_kernel(
    me_ref, gb_ref, gbt_ref, ht_ref, qkv_a, p_a, qkv_b, p_b, ho_ref, wo_ref,
    gw_ref, gj_ref, dho_ref, *, images, tall, x, flip
):
    j = x + 2 * jnp.bitwise_xor(me_ref[1], flip)
    own = pl.ds(pl.multiple_of(j * 256, 256), 256)
    scale = HEAD_DIM ** (-0.5)
    low = low_lanes(tall)
    dho_ref[...] = mm(gb_ref[...], wo_ref[:, own])
    heads, dots = [], []
    for b in range(images):
        at = pl.ds(b * tall, tall)
        joined, joined_last = qkv_a[j, at, :], qkv_b[j, at, :]
        q_pair, k_pair, v_pair = joined[:, :128], joined[:, 128:256], joined[:, 256:384]
        qk_last, v_last = joined_last[:, :128], joined_last[:, 128:256]
        grad = dho_ref[at, :].astype(bf16).astype(f32)
        product = grad * ho_ref[at, own].astype(f32)
        single, pair = product[:, :128], product[:, 128:]
        dots += [
            jnp.sum(jnp.where(low, pair, 0.0), axis=1, keepdims=True),
            jnp.sum(jnp.where(low, 0.0, pair), axis=1, keepdims=True),
            jnp.sum(single, axis=1, keepdims=True),
        ]
        grad_pair = grad[:, 128:]
        grad_last = jnp.where(low, pltpu.roll(grad[:, :128], HEAD_DIM, 1), 0.0).astype(bf16)
        heads += [
            (p_a[j, b, 0], jnp.where(low, grad_pair, 0.0).astype(bf16), v_pair, q_pair, k_pair),
            (p_a[j, b, 1], jnp.where(low, 0.0, grad_pair).astype(bf16), v_pair, q_pair, k_pair),
            (p_b[j, b], grad_last, v_last, qk_last, qk_last),
        ]
    grad_p = [mm_nt(g, v) for _, g, v, _, _ in heads]
    grad_s = [
        (probs.astype(f32) * (value - dot)).astype(bf16)
        for (probs, _, _, _, _), value, dot in zip(heads, grad_p, dots)
    ]
    gqs = [mm(value, k) for value, (_, _, _, _, k) in zip(grad_s, heads)]
    gks = [mm_tn(value, q) for value, (_, _, _, q, _) in zip(grad_s, heads)]
    gvs = [mm_tn(probs, g) for probs, g, _, _, _ in heads]
    for b in range(images):
        at = pl.ds(b * tall, tall)
        gq, gk, gv = (value[3 * b : 3 * b + 3] for value in (gqs, gks, gvs))
        last = pltpu.roll(jnp.where(low, gk[2], gq[2]), HEAD_DIM, 1)
        gj_ref[at, :] = jnp.concatenate(
            [
                jnp.where(low, gq[0], gq[1]) * scale,
                jnp.where(low, gk[0], gk[1]) * scale,
                gv[0] + gv[1],
                last * scale,
                gv[2],
            ],
            1,
        ).astype(bf16)
    grad_out = mm(gbt_ref[...], ho_ref[:, own])
    grad_in = mm(ht_ref[...], gj_ref[...])
    halves, blocks, rows = gw_ref.shape[:3]
    for d in range(halves * blocks):
        r = jnp.bitwise_xor(me_ref[0], d) if halves > 1 else 0
        entry = (jnp.bitwise_and(r, 1), jnp.right_shift(r, 1)) if halves > 1 else (0, 0)
        at = slice(d * rows, (d + 1) * rows)
        gw_ref[entry + (slice(None), slice(0, 512))] = grad_in[at, :512].astype(bf16)
        gw_ref[entry + (slice(None), slice(512, 640))] = (
            grad_in[at, 512:] + grad_out[at, :128]
        ).astype(bf16)
        gw_ref[entry + (slice(None), slice(640, 768))] = grad_out[at, 128:].astype(bf16)


def last_kernel(
    me_ref, x_ref, gres_ref, ex_ref, part_ref, w_a, w_b, *refs, images, seq, tall, experts, order
):
    grads, (gt_ref, small_ref, gh_ref) = refs[:-3], refs[-3:]
    total = jnp.zeros((1, x_ref.shape[2]), f32)
    gain = ex_ref[0:1, :]
    for k, (ref, (x, flip)) in enumerate(zip(grads, order)):
        j = x + 2 * jnp.bitwise_xor(me_ref[1], flip)
        into = mm_nt(ref[:, :384], w_a[j]) + mm_nt(ref[:, 384:], w_b[j])
        if k == 0:
            gh_ref[...] = into
        else:
            gh_ref[...] += into
    for b in range(images):
        at = pl.ds(b * tall, seq)
        unit, inverse = unit_of(x_ref[b].astype(f32))
        grad_h = gh_ref[at, :]
        total += jnp.sum(grad_h * unit, axis=0, keepdims=True)
        scaled = grad_h * gain
        mean_grad = jnp.mean(scaled, axis=-1, keepdims=True)
        mean_proj = jnp.mean(scaled * unit, axis=-1, keepdims=True)
        gt_ref[b] = gres_ref[at, :] + inverse * (scaled - mean_grad - unit * mean_proj)
    small_ref[...] = part_ref[...]
    small_ref[experts : experts + 1, :] = total


def cost(microseconds):
    return int(microseconds * 1.1e9)


def call(kernel, outs, args, scratch=(), flops=0, name=None, scalars=1, grant=16, **static):
    spec = pl.BlockSpec(memory_space=pltpu.VMEM)
    word = pl.BlockSpec(memory_space=pltpu.SMEM)
    moved = sum(math.prod(a.shape) * a.dtype.itemsize for a in args)
    return pl.pallas_call(
        functools.partial(kernel, **static),
        out_shape=[jax.ShapeDtypeStruct(s, d) for s, d in outs],
        in_specs=[word] * scalars + [spec] * (len(args) - scalars),
        out_specs=[spec] * len(outs),
        scratch_shapes=list(scratch),
        compiler_params=pltpu.CompilerParams(vmem_limit_bytes=grant << 20),
        cost_estimate=pl.CostEstimate(flops=flops, bytes_accessed=moved, transcendentals=0),
        name=name,
    )(*args)


def make(mesh):
    dp, mp = mesh.shape["dp"], mesh.shape["mp"]

    def per_device(
        tokens, token_mask, gain_one, w_qkv, w_out, gain_two, router, w_in, w_back, cotangent
    ):
        rows, width = tokens.shape
        seq = token_mask.shape[1]
        tall = -(-seq // 16) * 16
        images = rows // seq
        experts = router.shape[1]
        d_rows, _, part = w_qkv.shape
        count = images * tall
        high = dp // 2
        heads = part // HEAD_DIM
        ready = d_rows % 16 != 0
        each = 2 * (1 << (images - 1).bit_length())
        me = lax.axis_index("dp")
        at_mp = lax.axis_index("mp")
        core = at_mp & 1
        words = jnp.stack([me, core, at_mp]).astype(jnp.int32)
        static = {"images": images, "tall": tall}
        exact = {"images": images, "seq": seq, "tall": tall}

        columns = experts + 2
        half = 2 * part
        hbm = pl.BlockSpec(memory_space=pltpu.HBM)
        vmem = pl.BlockSpec(memory_space=pltpu.VMEM)
        word = pl.BlockSpec(memory_space=pltpu.SMEM)
        wide = columns + -columns % 128
        shapes = [(3, d_rows, part), (part, d_rows), (1, d_rows), (1, d_rows), (experts, d_rows)]
        first, second, extra = pl.pallas_call(
            pack_kernel,
            out_shape=[jax.ShapeDtypeStruct((d_rows, n), bf16) for n in (half, half, wide)],
            in_specs=[word] + [hbm] * 5,
            out_specs=[vmem] * 3,
            scratch_shapes=[pltpu.VMEM(shape, bf16) for shape in shapes] + [pltpu.SemaphoreType.DMA((5,))],
            compiler_params=pltpu.CompilerParams(vmem_limit_bytes=67_000_000),
            name="pack",
        )(words, w_qkv.transpose(1, 0, 2), w_out, gain_one[None], gain_two[None], router.T)

        first, second, held_extra = first[None], second[None], extra[None]
        for bit in bits_of(dp)[:-1]:
            first = jnp.concatenate([first, swap(first, "dp", dp, bit)])
            held_extra = jnp.concatenate([held_extra, swap(held_extra, "dp", dp, bit)])
            second = jnp.concatenate([second, swap(second, "dp", dp, bit)])
        other, held_extra = lax.optimization_barrier(
            (swap_both(first, dp, mp, (1, 0), (0, 2)), held_extra)
        )
        held_extra = jnp.concatenate([held_extra, swap(held_extra, "dp", dp, 1)])
        held_extra = held_extra.reshape((dp,) + extra.shape)
        if ready:
            held_extra = reorder(unmirrored(held_extra), me).reshape(1, width, -1)
        x3 = tokens.reshape(images, seq, width)
        cot3 = cotangent.reshape(images, seq, width)
        h_one, h_turned, ex = call(
            prep_kernel,
            [((count, width), bf16), ((width, count), bf16), ((held_extra.shape[2], width), f32)],
            (words, x3, held_extra),
            flops=cost(2),
            name="prep",
            grant=4,
            **exact,
        )
        near = jnp.stack([first, other])
        far = swap_both(near, dp, mp, (0, 2), (1, 0))
        far, h_one = lax.optimization_barrier((far, h_one))
        first = (near, far, swap(near, "mp", mp, 1), swap(far, "mp", mp, 1))
        near = jnp.stack([second, swap_both(second, dp, mp, (1, 0), (0, 2))])
        second_near, second_far = near, swap_both(near, dp, mp, (0, 2), (1, 0))
        second_near_other = swap(second_near, "mp", mp, 1)

        def whole(x, of_core, near, far, other_near, other_far):
            mine = core == of_core
            low = jnp.where(mine, near, other_near)
            high_part = jnp.where(mine, far, other_far)
            blocks = jnp.stack([low[x], high_part[x]]) if of_core else (high_part if x else low)
            blocks = blocks.reshape((dp, d_rows, half))
            blocks = unmirrored(blocks)
            return reorder(blocks, me).reshape(width, half)

        def weights_of(parts):
            if ready:
                return tuple(whole(j & 1, j >> 1, *parts) for j in range(4))
            return parts

        def saved(kept, columns, probs):
            return [
                ((mp, width, kept), bf16),
                ((mp, count, columns), bf16),
                ((mp, images) + probs + (tall, tall), bf16),
                ((mp, count, 128), bf16),
            ]

        pair = call(
            front_pair_kernel,
            saved(half, 384, (2,)),
            (words, h_one, token_mask) + weights_of(first),
            flops=cost(10),
            name="front_pair",
            grant=10,
            ready=ready,
            **static,
        )
        w_a, qkv_a, p_a, ho_a = pair
        second_far, ho_a = lax.optimization_barrier((second_far, ho_a))
        second = (second_near, second_far, second_near_other, swap(second_far, "mp", mp, 1))
        w_b, qkv_b, p_b, heads_out, w_heads, branch = call(
            front_last_kernel,
            saved(256, 256, ())[:3]
            + [
                ((count, 256 * mp), bf16),
                ((width, 256 * mp), bf16),
                ((count, width), f32),
            ],
            (words, h_one, token_mask, ho_a) + weights_of(second),
            flops=cost(7),
            name="front_last",
            grant=10,
            ready=ready,
            **static,
        )
        resid, h_two, soft, sent, sq_branch = call(
            route_kernel,
            [
                ((count, width), f32),
                ((count, width), bf16),
                ((2, images, experts, tall), f32),
                ((experts * each, width), bf16),
                ((images, 1, 128), f32),
            ],
            (words, x3, branch, cot3, token_mask, ex),
            flops=cost(2),
            name="route",
            grant=6,
            experts=experts,
            **exact,
        )
        got = sent.reshape(dp, each, width)
        got = lax.all_to_all(got, "dp", split_axis=0, concat_axis=0, tiled=True)
        got = gather_mp(got, mp).reshape(-1, width)
        everyone = got.shape[0]
        hidden, grad_pre, grad_expert, back = call(
            expert_kernel,
            [
                ((everyone, w_in.shape[2]), bf16),
                ((everyone, w_in.shape[2]), bf16),
                ((everyone, width), bf16),
                ((everyone, width), bf16),
            ],
            (got, w_in[0], w_back[0]),
            flops=cost(2),
            name="expert",
            scalars=0,
            grant=12 if dp <= 8 else 56,
            each=each,
        )
        back = back.reshape(mp, dp, each, width)
        back = scatter(back, "mp", mp, [1, 2])
        back = lax.all_to_all(back, "dp", split_axis=0, concat_axis=0, tiled=True)
        back = back.reshape(dp, 2, each // 2, width)[:, :, :images].transpose(1, 2, 0, 3)
        grad_w_back = mm_tn(hidden, grad_expert)
        grad_w_in = mm_tn(got, grad_pre)

        out_rows, grad_resid, grad_low, grad_turned, small = call(
            mix_kernel,
            [
                ((images, seq, width), bf16),
                ((count, width), f32),
                ((count, width), bf16),
                ((width, count), bf16),
                ((experts + 5, width), f32),
            ],
            (words, resid, h_two, soft, cot3, token_mask, ex, back, sq_branch),
            flops=cost(5),
            name="mix",
            grant=8,
            experts=experts,
            groups=mp,
            **exact,
        )
        shape = (1, 1, width, 4 * part) if ready else (2, high, d_rows, 4 * part)

        def back_of(x, flip, grad_in):
            grads, joined = call(
                back_kernel,
                [(shape, bf16), ((count, JOINED), bf16)],
                (words, grad_in, grad_turned, h_turned, qkv_a, p_a, qkv_b, p_b, heads_out, w_heads),
                [pltpu.VMEM((count, 256), f32)],
                flops=cost(8),
                name="back",
                grant=10,
                x=x,
                flip=flip,
                **static,
            )
            if ready:
                grads = reorder(grads.reshape(dp, d_rows, 4 * part), me)
                grads = grads.reshape(high, 2, d_rows, 4 * part).transpose(1, 0, 2, 3)
            return grads, joined

        def fold(terms, halves):
            size = terms[0].shape
            kept = ((size[0] // 2,) + size[1:], bf16)
            return call(
                fold_kernel,
                [kept, kept],
                terms,
                flops=cost(1),
                name="fold",
                scalars=0,
                grant=6,
                halves=halves,
            )

        order = ((1, 1), (1, 0), (0, 1), (0, 0))
        sent_grads, joined_a = back_of(1, 1, grad_low)
        other = swap(sent_grads, "mp", mp, 1)
        grad_low, joined_a = lax.optimization_barrier((grad_low, joined_a))
        kept_grads, joined_b = back_of(1, 0, grad_low)
        far_kept, far_left = fold((kept_grads, other), True)
        far_left, grad_low, joined_b = lax.optimization_barrier((far_left, grad_low, joined_b))
        early = swap_both(far_left[0], dp, mp, (0, 2), (1, 0))
        sent_grads, joined_c = back_of(0, 1, grad_low)
        grad_low, joined_c = lax.optimization_barrier((grad_low, joined_c))
        other = swap(sent_grads, "mp", mp, 1)
        kept_grads, joined_d = back_of(0, 0, grad_low)
        part_shape = ((high, d_rows, 4 * part), bf16)
        near_sum, second, third = call(
            blend_kernel,
            [part_shape] * 3,
            (words, far_kept[0], kept_grads, other, early),
            flops=cost(1),
            name="blend",
            grant=8,
        )
        second = swap_both(second, dp, mp, (0, 2), (1, 0))
        third = swap_both(third, dp, mp, (1, 0), (0, 2))
        grad_tokens, small, _ = call(
            last_kernel,
            [((images, seq, width), f32), ((experts + 5, width), f32), ((count, width), f32)],
            (words, x3, grad_resid, ex, small, w_a, w_b, joined_a, joined_b, joined_c, joined_d),
            flops=cost(6),
            name="last",
            grant=8,
            experts=experts,
            order=order,
            **exact,
        )
        for bit in bits_of(dp)[:-1]:
            small = small + swap(small, "dp", dp, bit)
        kept, left = fold((near_sum, second, third), False)
        left, small = lax.optimization_barrier((left, small))
        for bit in bits_of(high)[:0:-1]:
            kept, left = fold((kept, swap(left, "dp", dp, 2 * bit)), False)
        own, other = kept[0], swap(left[0], "dp", dp, 2 * bits_of(high)[0])
        grad_qkv, grad_out = call(
            unpack_kernel,
            [((3, d_rows, part), f32), ((part, d_rows), f32)],
            (own, other),
            flops=cost(1),
            name="unpack",
            scalars=0,
            grant=6,
        )
        small = small + swap(small, "dp", dp, 1)
        small = small + swap(small, "mp", mp, 2)
        grad_one, grad_two, grad_router, root_squares = call(
            finish_kernel,
            [
                ((1, d_rows), f32),
                ((1, d_rows), f32),
                ((experts, d_rows), f32),
                ((3, mp * images), f32),
            ],
            (words, small, swap(small, "mp", mp, 1)),
            flops=cost(1),
            name="finish",
            grant=4,
        )
        return (
            out_rows.reshape(rows, width),
            grad_tokens.reshape(rows, width),
            grad_one[0],
            grad_qkv.transpose(1, 0, 2),
            grad_out,
            grad_two[0],
            grad_router.T,
            grad_w_in[None],
            grad_w_back[None],
            root_squares,
        )

    return per_device


def solution(mesh):
    in_specs = (
        P(("dp", "mp"), None),
        P("dp", None),
        P("dp"),
        P("dp", None, "mp"),
        P("mp", "dp"),
        P("dp"),
        P("dp", None),
        P("dp", None, "mp"),
        P("dp", "mp", None),
        P(("dp", "mp"), None),
    )
    out_specs = (
        P(("dp", "mp"), None),
        P(("dp", "mp"), None),
        P("dp"),
        P("dp", None, "mp"),
        P("mp", "dp"),
        P("dp"),
        P("dp", None),
        P("dp", None, "mp"),
        P("dp", "mp", None),
        P(None, "dp"),
    )
    return jax.shard_map(
        make(mesh), mesh=mesh, in_specs=in_specs, out_specs=out_specs, check_vma=False
    )
```

```python
import functools
import math

import jax
import jax.numpy as jnp
from jax import lax
from jax.experimental import pallas as pl
from jax.experimental.pallas import tpu as pltpu
from jax.sharding import PartitionSpec as P

HEAD_DIM = 64


epsilon = 1e-06
bf16 = jnp.bfloat16
f32 = jnp.float32


def bits_of(size):
    return [1 << k for k in reversed(range(size.bit_length() - 1))]


def swap(array_in, axis_name, size, bit):
    return lax.ppermute(array_in, axis_name, [(i, i ^ bit) for i in range(size)])


def swap_both(array_in, dp, mp, even, odd):
    pairs = []
    for d in range(dp):
        for m in range(mp):
            flip = odd if m & 1 else even
            pairs.append((d * mp + m, (d ^ flip[0]) * mp + (m ^ flip[1])))
    return lax.ppermute(array_in, ("dp", "mp"), pairs)


def gather_mp(block, mp):
    held = block[None]
    for bit in bits_of(mp):
        other = swap(held, "mp", mp, bit)
        held = jnp.stack([held, other], 1).reshape((-1,) + block.shape)
    return held


def scatter(held, axis_name, size, bits, unit=1):
    left = sorted(bits)
    for bit in bits:
        inner = 1 << left.index(bit)
        left.remove(bit)
        pairs = held.reshape((held.shape[0] // (2 * inner), 2, inner) + held.shape[1:])
        other = swap(pairs[:, 1], axis_name, size, bit * unit)
        held = pairs[:, 0].astype(f32) + other.astype(f32)
        held = held.astype(bf16).reshape((-1,) + held.shape[2:])
    return held[0]


def mirrored(index, size):
    bits = size.bit_length() - 1
    return sum(((index >> k) & 1) << (bits - 1 - k) for k in range(bits)) if bits else index


def unmirrored(blocks):
    size = blocks.shape[0]
    bits = size.bit_length() - 1
    split = blocks.reshape((2,) * bits + blocks.shape[1:])
    turn = tuple(range(bits))[::-1] + tuple(range(bits, split.ndim))
    return split.transpose(turn).reshape(blocks.shape)


def reorder(blocks, me):
    size = blocks.shape[0]
    for bit in bits_of(size):
        pairs = blocks.reshape((size // (2 * bit), 2, bit) + blocks.shape[1:])
        blocks = jnp.where((me & bit) > 0, pairs[:, ::-1], pairs).reshape(blocks.shape)
    return blocks


def mm(a, b):
    return lax.dot_general(a, b, (((1,), (0,)), ((), ())), preferred_element_type=f32)


def mm_nt(a, b):
    return lax.dot_general(a, b, (((1,), (1,)), ((), ())), preferred_element_type=f32)


def mm_tn(a, b):
    return lax.dot_general(a, b, (((0,), (0,)), ((), ())), preferred_element_type=f32)


def unit_of(rows_f):
    mean_row = jnp.mean(rows_f, axis=-1, keepdims=True)
    centered = rows_f - mean_row
    variance = jnp.mean(centered * centered, axis=-1, keepdims=True)
    inverse = lax.rsqrt(variance + epsilon)
    return centered * inverse, inverse


def padded(value, pad):
    return jnp.concatenate([value, jnp.zeros((pad, value.shape[1]), value.dtype)], 0)


def low_lanes(rows):
    return lax.broadcasted_iota(jnp.int32, (rows, 128), 1) < HEAD_DIM


JOINED = 640


def pack_kernel(
    me_ref, qkv_hbm, out_hbm, one_hbm, two_hbm, router_hbm, first_ref, second_ref, extra_ref,
    qkv_ref, out_ref, one_ref, two_ref, router_ref, sems
):
    del me_ref
    pairs = (
        (qkv_hbm, qkv_ref), (out_hbm, out_ref), (one_hbm, one_ref), (two_hbm, two_ref), (router_hbm, router_ref),
    )
    copies = [pltpu.make_async_copy(a, b, sems.at[k]) for k, (a, b) in enumerate(pairs)]
    for copy in copies:
        copy.start()
    for copy in copies:
        copy.wait()
    low, mid = 2 * HEAD_DIM, qkv_ref.shape[2]
    out = out_ref[...].astype(f32).T.astype(bf16)
    first_ref[...] = jnp.concatenate([qkv_ref[c, :, :low] for c in range(3)], axis=1)
    second_ref[...] = jnp.concatenate(
        [qkv_ref[c, :, low:mid] for c in range(3)] + [out[:, low:mid], out[:, :low]], axis=1
    )
    rows = one_ref.shape[1]
    columns = [one_ref[...], two_ref[...], router_ref[...]]
    columns = [value.astype(f32) for value in columns]
    filled = sum(value.shape[0] for value in columns)
    columns.append(jnp.zeros((extra_ref.shape[1] - filled, rows), f32))
    extra_ref[...] = jnp.concatenate(columns, 0).T.astype(bf16)


def fold_kernel(*refs, halves, starts):
    terms, (kept_ref, left_ref) = refs[:-2], refs[-2:]
    size, columns = terms[0].shape[0], kept_ref.shape[-1]
    for k in range(size):
        total = None
        for term, start in zip(terms, starts):
            value = term[k][..., start : start + columns].astype(f32)
            total = value if total is None else total + value
        at, odd = (k % (size // 2), k >= size // 2) if halves else (k // 2, k % 2 == 1)
        (left_ref if odd else kept_ref)[at] = total.astype(bf16)


def blend_kernel(me_ref, far_ref, kept_ref, other_ref, near_ref, own_ref, second_ref):
    for k, ref in ((0, near_ref), (1, own_ref)):
        ref[...] = (kept_ref[k].astype(f32) + other_ref[k].astype(f32)).astype(bf16)
    first_core = me_ref[1] == 0

    @pl.when(first_core)
    def _():
        second_ref[...] = far_ref[...]

    @pl.when(jnp.logical_not(first_core))
    def _():
        second_ref[...] = own_ref[...]


def blend_late_kernel(me_ref, far_ref, own_ref, early_ref, *thirds):
    columns = thirds[0].shape[-1]
    for core, ref in ((0, own_ref), (1, far_ref)):

        @pl.when(me_ref[1] == core)
        def _(ref=ref):
            for k, third in enumerate(thirds):
                at = slice(k * columns, (k + 1) * columns)
                total = ref[..., at].astype(f32) + early_ref[..., at].astype(f32)
                third[...] = total.astype(bf16)


def finish_kernel(me_ref, own_ref, other_ref, one_ref, two_ref, router_ref, root_ref):
    experts, rows = router_ref.shape
    total = own_ref[...] + other_ref[...]
    width = total.shape[1]
    mine = pltpu.roll(total, lax.rem(width - me_ref[0] * rows, width), 1)
    one_ref[...] = mine[experts : experts + 1, :rows]
    two_ref[...] = mine[experts + 1 : experts + 2, :rows]
    router_ref[...] = mine[:experts, :rows]
    images = root_ref.shape[1]
    mine = pltpu.roll(total, lax.rem(width - me_ref[0] * images, width), 1)
    root_ref[...] = mine[experts + 2 : experts + 5, :images]


def unpack_kernel(own_a, other_a, own_b, other_b, qkv_ref, out_ref):
    low, mid = 2 * HEAD_DIM, qkv_ref.shape[2]
    pair = own_a[...].astype(f32) + other_a[...].astype(f32)
    rest = own_b[...].astype(f32) + other_b[...].astype(f32)
    for c in range(3):
        qkv_ref[c, :, :low] = pair[:, c * low : (c + 1) * low]
        qkv_ref[c, :, low:mid] = rest[:, c * HEAD_DIM : (c + 1) * HEAD_DIM]
    out_ref[...] = jnp.concatenate([rest[:, 256:], rest[:, 192:256]], axis=1).T


def length_of(mask_ref, me_ref, b, images):
    row = mask_ref[pl.ds(me_ref[2] * images + b, 1), :]
    return jnp.sum(row.astype(f32), axis=1, keepdims=True)


def seen_row(length, tall):
    return lax.broadcasted_iota(jnp.int32, (1, tall), 1).astype(f32) < length


def seen_column(length, tall):
    return lax.broadcasted_iota(jnp.int32, (tall, 1), 0).astype(f32) < length


def prep_kernel(me_ref, x_ref, extra_ref, h_ref, ht_ref, small_ref, *, images, seq, tall):
    blocks = extra_ref.shape[0]
    me = me_ref[0]
    parts = [extra_ref[mirrored(me ^ d, blocks) if blocks > 1 else 0] for d in range(blocks)]
    small_ref[...] = jnp.concatenate(parts, 0).astype(f32).T
    gain = small_ref[0:1, :]
    for b in range(images):
        unit, _ = unit_of(x_ref[b].astype(f32))
        h_ref[pl.ds(b * tall, tall), :] = padded((unit * gain).astype(bf16), tall - seq)
    ht_ref[...] = h_ref[...].T


def fetch_all(me_ref, refs, put):
    rows, high_size = refs[0].shape[2], refs[0].shape[1]
    for core in (0, 1):

        @pl.when(me_ref[1] == core)
        def _(core=core):
            for slot in range(4):
                x, of_core = slot & 1, slot >> 1
                first, second = refs[:2] if of_core == core else refs[2:4]
                for r in range(2 * high_size):
                    low, high = r & 1, mirrored(r >> 1, high_size)
                    if of_core == 0:
                        block = (second if x else first)[low, high]
                    else:
                        block = (second if low else first)[x, high]
                    d = jnp.bitwise_xor(me_ref[0], r)
                    put(slot, pl.ds(pl.multiple_of(d * rows, 16), rows), block)


def attend(triples):
    scores = [mm_nt(q, k) * HEAD_DIM ** (-0.5) + bias for q, k, _, bias in triples]
    terms = [jnp.exp(value - jnp.max(value, axis=-1, keepdims=True)) for value in scores]
    probs = [
        (value * (1.0 / jnp.sum(value, axis=-1, keepdims=True))).astype(bf16) for value in terms
    ]
    return probs, [mm(value, v) for value, (_, _, v, _) in zip(probs, triples)]


def bias_of(mask_ref, me_ref, b, images, tall):
    return jnp.where(seen_row(length_of(mask_ref, me_ref, b, images), tall), 0.0, -1e30)


def front_pair_kernel(me_ref, h_ref, mask_ref, *refs, images, tall, ready):
    w_ref, qkv_ref, p_ref, ho_ref = refs[4:]

    def put(slot, at, block):
        w_ref[slot, at, :] = block

    if ready:
        for slot in range(4):
            put(slot, slice(None), refs[slot][...])
    else:
        fetch_all(me_ref, refs[:4], put)
    low = low_lanes(tall)

    def group(j, carry):
        qkv_ref[j] = mm(h_ref[...], w_ref[j]).astype(bf16)
        triples = []
        for b in range(images):
            joined = qkv_ref[j, pl.ds(b * tall, tall), :]
            q, k, v = joined[:, :128], joined[:, 128:256], joined[:, 256:384]
            none = jnp.zeros_like(q)
            bias = bias_of(mask_ref, me_ref, b, images, tall)
            triples.append((jnp.where(low, q, none), k, v, bias))
            triples.append((jnp.where(low, none, q), k, v, bias))
        probs, outs = attend(triples)
        for b in range(images):
            p_ref[j, b, 0], p_ref[j, b, 1] = probs[2 * b], probs[2 * b + 1]
            pair = jnp.where(low, outs[2 * b], outs[2 * b + 1])
            ho_ref[j, pl.ds(b * tall, tall), :] = pair.astype(bf16)
        return carry

    lax.fori_loop(0, w_ref.shape[0], group, 0)


def front_last_kernel(me_ref, h_ref, mask_ref, pair_ref, *refs, images, tall, ready):
    w_ref, qkv_ref, p_ref, ho_ref, wo_ref, br_ref = refs[4:]

    def put(slot, at, block):
        w_ref[slot, at, :] = block[:, :256]
        wo_ref[at, slot * 256 : (slot + 1) * 256] = block[:, 128:]

    if ready:
        for slot in range(4):
            put(slot, slice(None), refs[slot][...])
    else:
        fetch_all(me_ref, refs[:4], put)
    low = low_lanes(tall)

    def two(i, carry):
        places = [(2 * i + k, b) for k in (0, 1) for b in range(images)]
        for j in (2 * i, 2 * i + 1):
            qkv_ref[j] = mm(h_ref[...], w_ref[j]).astype(bf16)
        triples = []
        for j, b in places:
            joined = qkv_ref[j, pl.ds(b * tall, tall), :]
            qk, v = joined[:, :128], joined[:, 128:256]
            k = pltpu.roll(qk.astype(f32), HEAD_DIM, 1).astype(bf16)
            bias = bias_of(mask_ref, me_ref, b, images, tall)
            triples.append((jnp.where(low, qk, jnp.zeros_like(qk)), k, v, bias))
        probs, outs = attend(triples)
        for (j, b), prob, out in zip(places, probs, outs):
            at, start = pl.ds(b * tall, tall), pl.multiple_of(j * 256, 256)
            p_ref[j, b] = prob
            ho_ref[at, pl.ds(start, 128)] = jnp.where(low, 0.0, pltpu.roll(out, HEAD_DIM, 1)).astype(bf16)
            ho_ref[at, pl.ds(start + 128, 128)] = pair_ref[j, at, :]
        return carry

    lax.fori_loop(0, w_ref.shape[0] // 2, two, 0)
    br_ref[...] = mm_nt(ho_ref[...], wo_ref[...])


def spot(rows, b, start, experts):
    each = rows // experts
    at_row = lax.broadcasted_iota(jnp.int32, (rows, experts), 0)
    at_column = lax.broadcasted_iota(jnp.int32, (rows, experts), 1)
    return jnp.where(at_row == at_column * each + (start + b), 1.0, 0.0).astype(bf16)


def route_kernel(
    me_ref, x_ref, br_ref, cot_ref, mask_ref, ex_ref,
    res_ref, h_ref, soft_ref, sent_ref, sq_ref, *, images, seq, tall, experts
):
    rows = sent_ref.shape[0]
    half = rows // experts // 2
    router = ex_ref[2 : 2 + experts, :].astype(bf16)
    gain = ex_ref[1:2, :]
    total = jnp.zeros(sent_ref.shape, f32)
    for b in range(images):
        at = pl.ds(b * tall, tall)
        length = length_of(mask_ref, me_ref, b, images)
        branch = br_ref[at, :]
        resid = padded(x_ref[b].astype(f32), tall - seq) + branch
        res_ref[at, :] = resid
        unit, _ = unit_of(resid)
        h_two = (unit * gain).astype(bf16)
        h_ref[at, :] = h_two
        logits = mm_nt(router, h_two)
        held = jnp.where(seen_row(length, tall), logits, -1e30)
        terms = jnp.exp(held - jnp.max(held, axis=1, keepdims=True))
        dispatch = terms / jnp.sum(terms, axis=1, keepdims=True)
        terms = jnp.exp(logits - jnp.max(logits, axis=0, keepdims=True))
        combine = terms / jnp.sum(terms, axis=0, keepdims=True)
        soft_ref[0, b] = dispatch
        soft_ref[1, b] = combine
        cot = padded(cot_ref[b], tall - seq)
        wide_d = mm(spot(rows, b, 0, experts), dispatch.astype(bf16)).astype(bf16)
        wide_c = mm(spot(rows, b, half, experts), combine.astype(bf16)).astype(bf16)
        total += mm(wide_d, h_two) + mm(wide_c, cot)
        squares = jnp.sum(branch * branch, axis=1, keepdims=True)
        squares = jnp.sum(jnp.where(seen_column(length, tall), squares, 0.0), axis=0, keepdims=True)
        sq_ref[b] = jnp.broadcast_to(squares, (1, 128))
    sent_ref[...] = total.astype(bf16)


def expert_kernel(got_ref, first_ref, second_ref, hid_ref, pre_ref, grad_ref, back_ref, *, each):
    rows = got_ref.shape[0]
    half = each // 2
    got = got_ref[...]
    own = jnp.bitwise_and(lax.broadcasted_iota(jnp.int32, (rows, 1), 0), each - 1) < half
    grads = jnp.where(own, pltpu.roll(got.astype(f32), rows - half, 0), 0.0).astype(bf16)
    grad_ref[...] = grads
    u = mm(got, first_ref[...])
    cubic = 0.7978845608028654 * (u + 0.044715 * u * u * u)
    t = jnp.tanh(cubic)
    hidden = jnp.where(own, 0.5 * u * (1.0 + t), 0.0).astype(bf16)
    hid_ref[...] = hidden
    slope = 0.5 * (1.0 + t) + 0.5 * u * (1.0 - t * t) * 0.7978845608028654 * (
        1.0 + 3.0 * 0.044715 * u * u
    )
    grad_pre = (mm_nt(grads, second_ref[...]) * slope).astype(bf16)
    pre_ref[...] = grad_pre
    out = mm(hidden, second_ref[...])
    grad_in = mm_nt(grad_pre, first_ref[...])
    back_ref[...] = jnp.where(own, out, pltpu.roll(grad_in, half, 0)).astype(bf16)


def mix_kernel(
    me_ref, res_ref, h_ref, soft_ref, cot_ref, mask_ref, ex_ref, back_ref, sq_ref,
    out_ref, gres_ref, gb_ref, gbt_ref, small_ref, *, images, seq, tall, experts, groups
):
    small_ref[...] = jnp.zeros_like(small_ref)
    router = ex_ref[2 : 2 + experts, :].astype(bf16)
    gain = ex_ref[1:2, :]
    width = out_ref.shape[2]
    lanes = lax.broadcasted_iota(jnp.int32, (1, width), 1)
    roots = [jnp.zeros((1, width), f32) for _ in range(3)]
    for b in range(images):
        at = pl.ds(b * tall, tall)
        length = length_of(mask_ref, me_ref, b, images)
        resid, h_two = res_ref[at, :], h_ref[at, :]
        dispatch, combine = soft_ref[0, b], soft_ref[1, b]
        dispatch_low, combine_low = dispatch.astype(bf16), combine.astype(bf16)
        returned, grad_slots = back_ref[0, b], back_ref[1, b]
        cot = padded(cot_ref[b], tall - seq)
        mixed = mm_tn(combine_low, returned)
        stream = resid + mixed
        out_ref[b] = stream[:seq].astype(bf16)
        column = seen_column(length, tall)
        sums = []
        for value in (stream, mixed):
            squares = jnp.sum(value * value, axis=1, keepdims=True)
            sums.append(jnp.sum(jnp.where(column, squares, 0.0), axis=0, keepdims=True))
        sums.insert(1, sq_ref[b, :, 0:1])
        for k, value in enumerate(sums):
            root = jnp.sqrt(value / (length * width))
            mine = lanes == (me_ref[0] * groups + me_ref[2]) * images + b
            roots[k] += jnp.where(mine, root, 0.0)
        grad_c = mm_nt(returned, cot)
        grad_c = combine * (grad_c - jnp.sum(grad_c * combine, axis=0, keepdims=True))
        grad_d = mm_nt(grad_slots, h_two)
        grad_d = dispatch * (grad_d - jnp.sum(grad_d * dispatch, axis=1, keepdims=True))
        grad_logits = (grad_d + grad_c).astype(bf16)
        grad_h = mm_tn(dispatch_low, grad_slots) + mm_tn(grad_logits, router)
        small_ref[0:experts, :] += mm(grad_logits, h_two)
        unit, inverse = unit_of(resid)
        small_ref[experts + 1 : experts + 2, :] += jnp.sum(grad_h * unit, axis=0, keepdims=True)
        scaled = grad_h * gain
        mean_grad = jnp.mean(scaled, axis=-1, keepdims=True)
        mean_proj = jnp.mean(scaled * unit, axis=-1, keepdims=True)
        gres_ref[at, :] = cot.astype(f32) + inverse * (scaled - mean_grad - unit * mean_proj)
    for k in range(3):
        small_ref[experts + 2 + k : experts + 3 + k, :] = roots[k]
    gb_ref[...] = gres_ref[...].astype(bf16)
    gbt_ref[...] = gres_ref[...].T.astype(bf16)


def back_kernel(
    me_ref, gb_ref, gbt_ref, ht_ref, qkv_a, p_a, qkv_b, p_b, ho_ref, wo_ref,
    gw_ref, gj_ref, dho_ref, *, images, tall, x, flip
):
    j = x + 2 * jnp.bitwise_xor(me_ref[1], flip)
    own = pl.ds(pl.multiple_of(j * 256, 256), 256)
    scale = HEAD_DIM ** (-0.5)
    low = low_lanes(tall)
    dho_ref[...] = mm(gb_ref[...], wo_ref[:, own])
    heads, dots = [], []
    for b in range(images):
        at = pl.ds(b * tall, tall)
        joined, joined_last = qkv_a[j, at, :], qkv_b[j, at, :]
        q_pair, k_pair, v_pair = joined[:, :128], joined[:, 128:256], joined[:, 256:384]
        qk_last, v_last = joined_last[:, :128], joined_last[:, 128:256]
        grad = dho_ref[at, :].astype(bf16).astype(f32)
        product = grad * ho_ref[at, own].astype(f32)
        single, pair = product[:, :128], product[:, 128:]
        dots += [
            jnp.sum(jnp.where(low, pair, 0.0), axis=1, keepdims=True),
            jnp.sum(jnp.where(low, 0.0, pair), axis=1, keepdims=True),
            jnp.sum(single, axis=1, keepdims=True),
        ]
        grad_pair = grad[:, 128:]
        grad_last = jnp.where(low, pltpu.roll(grad[:, :128], HEAD_DIM, 1), 0.0).astype(bf16)
        heads += [
            (p_a[j, b, 0], jnp.where(low, grad_pair, 0.0).astype(bf16), v_pair, q_pair, k_pair),
            (p_a[j, b, 1], jnp.where(low, 0.0, grad_pair).astype(bf16), v_pair, q_pair, k_pair),
            (p_b[j, b], grad_last, v_last, qk_last, qk_last),
        ]
    grad_p = [mm_nt(g, v) for _, g, v, _, _ in heads]
    grad_s = [
        (probs.astype(f32) * (value - dot)).astype(bf16)
        for (probs, _, _, _, _), value, dot in zip(heads, grad_p, dots)
    ]
    gqs = [mm(value, k) for value, (_, _, _, _, k) in zip(grad_s, heads)]
    gks = [mm_tn(value, q) for value, (_, _, _, q, _) in zip(grad_s, heads)]
    gvs = [mm_tn(probs, g) for probs, g, _, _, _ in heads]
    for b in range(images):
        at = pl.ds(b * tall, tall)
        gq, gk, gv = (value[3 * b : 3 * b + 3] for value in (gqs, gks, gvs))
        last = pltpu.roll(jnp.where(low, gk[2], gq[2]), HEAD_DIM, 1)
        gj_ref[at, :] = jnp.concatenate(
            [
                jnp.where(low, gq[0], gq[1]) * scale,
                jnp.where(low, gk[0], gk[1]) * scale,
                gv[0] + gv[1],
                last * scale,
                gv[2],
            ],
            1,
        ).astype(bf16)
    grad_out = mm(gbt_ref[...], ho_ref[:, own])
    grad_in = mm(ht_ref[...], gj_ref[...])
    halves, blocks, rows = gw_ref.shape[:3]
    for d in range(halves * blocks):
        r = jnp.bitwise_xor(me_ref[0], d) if halves > 1 else 0
        entry = (jnp.bitwise_and(r, 1), jnp.right_shift(r, 1)) if halves > 1 else (0, 0)
        at = slice(d * rows, (d + 1) * rows)
        gw_ref[entry + (slice(None), slice(0, 512))] = grad_in[at, :512].astype(bf16)
        gw_ref[entry + (slice(None), slice(512, 640))] = (
            grad_in[at, 512:] + grad_out[at, :128]
        ).astype(bf16)
        gw_ref[entry + (slice(None), slice(640, 768))] = grad_out[at, 128:].astype(bf16)


def last_kernel(
    me_ref, x_ref, gres_ref, ex_ref, part_ref, w_a, w_b, *refs, images, seq, tall, experts, order
):
    grads, (gt_ref, small_ref, gh_ref) = refs[:-3], refs[-3:]
    total = jnp.zeros((1, x_ref.shape[2]), f32)
    gain = ex_ref[0:1, :]
    for k, (ref, (x, flip)) in enumerate(zip(grads, order)):
        j = x + 2 * jnp.bitwise_xor(me_ref[1], flip)
        into = mm_nt(ref[:, :384], w_a[j]) + mm_nt(ref[:, 384:], w_b[j])
        if k == 0:
            gh_ref[...] = into
        else:
            gh_ref[...] += into
    for b in range(images):
        at = pl.ds(b * tall, seq)
        unit, inverse = unit_of(x_ref[b].astype(f32))
        grad_h = gh_ref[at, :]
        total += jnp.sum(grad_h * unit, axis=0, keepdims=True)
        scaled = grad_h * gain
        mean_grad = jnp.mean(scaled, axis=-1, keepdims=True)
        mean_proj = jnp.mean(scaled * unit, axis=-1, keepdims=True)
        gt_ref[b] = gres_ref[at, :] + inverse * (scaled - mean_grad - unit * mean_proj)
    small_ref[...] = part_ref[...]
    small_ref[experts : experts + 1, :] = total


def cost(microseconds):
    return int(microseconds * 1.1e9)


def call(kernel, outs, args, scratch=(), flops=0, name=None, scalars=1, grant=16, **static):
    spec = pl.BlockSpec(memory_space=pltpu.VMEM)
    word = pl.BlockSpec(memory_space=pltpu.SMEM)
    moved = sum(math.prod(a.shape) * a.dtype.itemsize for a in args)
    return pl.pallas_call(
        functools.partial(kernel, **static),
        out_shape=[jax.ShapeDtypeStruct(s, d) for s, d in outs],
        in_specs=[word] * scalars + [spec] * (len(args) - scalars),
        out_specs=[spec] * len(outs),
        scratch_shapes=list(scratch),
        compiler_params=pltpu.CompilerParams(vmem_limit_bytes=grant << 20),
        cost_estimate=pl.CostEstimate(flops=flops, bytes_accessed=moved, transcendentals=0),
        name=name,
    )(*args)


def make(mesh):
    dp, mp = mesh.shape["dp"], mesh.shape["mp"]

    def per_device(
        tokens, token_mask, gain_one, w_qkv, w_out, gain_two, router, w_in, w_back, cotangent
    ):
        rows, width = tokens.shape
        seq = token_mask.shape[1]
        tall = -(-seq // 16) * 16
        images = rows // seq
        experts = router.shape[1]
        d_rows, _, part = w_qkv.shape
        count = images * tall
        high = dp // 2
        heads = part // HEAD_DIM
        ready = d_rows % 16 != 0
        each = 2 * (1 << (images - 1).bit_length())
        me = lax.axis_index("dp")
        at_mp = lax.axis_index("mp")
        core = at_mp & 1
        words = jnp.stack([me, core, at_mp]).astype(jnp.int32)
        static = {"images": images, "tall": tall}
        exact = {"images": images, "seq": seq, "tall": tall}

        columns = experts + 2
        half = 2 * part
        hbm = pl.BlockSpec(memory_space=pltpu.HBM)
        vmem = pl.BlockSpec(memory_space=pltpu.VMEM)
        word = pl.BlockSpec(memory_space=pltpu.SMEM)
        wide = columns + -columns % 128
        shapes = [(3, d_rows, part), (part, d_rows), (1, d_rows), (1, d_rows), (experts, d_rows)]
        first, second, extra = pl.pallas_call(
            pack_kernel,
            out_shape=[jax.ShapeDtypeStruct((d_rows, n), bf16) for n in (half, half, wide)],
            in_specs=[word] + [hbm] * 5,
            out_specs=[vmem] * 3,
            scratch_shapes=[pltpu.VMEM(shape, bf16) for shape in shapes] + [pltpu.SemaphoreType.DMA((5,))],
            compiler_params=pltpu.CompilerParams(vmem_limit_bytes=67_000_000),
            name="pack",
        )(words, w_qkv.transpose(1, 0, 2), w_out, gain_one[None], gain_two[None], router.T)

        first, second, held_extra = first[None], second[None], extra[None]
        for bit in bits_of(dp)[:-1]:
            first = jnp.concatenate([first, swap(first, "dp", dp, bit)])
            held_extra = jnp.concatenate([held_extra, swap(held_extra, "dp", dp, bit)])
        stages = bits_of(dp)[:-1]
        second = jnp.concatenate([second, swap(second, "dp", dp, stages[0])])
        other, held_extra, second = lax.optimization_barrier(
            (swap_both(first, dp, mp, (1, 0), (0, 2)), held_extra, second)
        )
        for bit in stages[1:]:
            second = jnp.concatenate([second, swap(second, "dp", dp, bit)])
        held_extra = jnp.concatenate([held_extra, swap(held_extra, "dp", dp, 1)])
        held_extra = held_extra.reshape((dp,) + extra.shape)
        if ready:
            held_extra = reorder(unmirrored(held_extra), me).reshape(1, width, -1)
        x3 = tokens.reshape(images, seq, width)
        cot3 = cotangent.reshape(images, seq, width)
        h_one, h_turned, ex = call(
            prep_kernel,
            [((count, width), bf16), ((width, count), bf16), ((held_extra.shape[2], width), f32)],
            (words, x3, held_extra),
            flops=cost(2),
            name="prep",
            grant=4,
            **exact,
        )
        near = jnp.stack([first, other])
        far = swap_both(near, dp, mp, (0, 2), (1, 0))
        second = second.reshape((high, d_rows, half))
        other = swap_both(second, dp, mp, (1, 0), (0, 2))
        far, h_one, other = lax.optimization_barrier((far, h_one, other))
        first = (near, far, swap(near, "mp", mp, 1), swap(far, "mp", mp, 1))
        near = jnp.stack([second, other])
        second_near, second_far = near, swap_both(near, dp, mp, (0, 2), (1, 0))
        second_near_other = swap(second_near, "mp", mp, 1)

        def whole(x, of_core, near, far, other_near, other_far):
            mine = core == of_core
            low = jnp.where(mine, near, other_near)
            high_part = jnp.where(mine, far, other_far)
            blocks = jnp.stack([low[x], high_part[x]]) if of_core else (high_part if x else low)
            blocks = blocks.reshape((dp, d_rows, half))
            blocks = unmirrored(blocks)
            return reorder(blocks, me).reshape(width, half)

        def weights_of(parts):
            if ready:
                return tuple(whole(j & 1, j >> 1, *parts) for j in range(4))
            return parts

        def saved(kept, columns, probs):
            return [
                ((mp, width, kept), bf16),
                ((mp, count, columns), bf16),
                ((mp, images) + probs + (tall, tall), bf16),
                ((mp, count, 128), bf16),
            ]

        pair = call(
            front_pair_kernel,
            saved(half, 384, (2,)),
            (words, h_one, token_mask) + weights_of(first),
            flops=cost(10),
            name="front_pair",
            grant=10,
            ready=ready,
            **static,
        )
        w_a, qkv_a, p_a, ho_a = pair
        second_far, ho_a = lax.optimization_barrier((second_far, ho_a))
        second = (second_near, second_far, second_near_other, swap(second_far, "mp", mp, 1))
        w_b, qkv_b, p_b, heads_out, w_heads, branch = call(
            front_last_kernel,
            saved(256, 256, ())[:3]
            + [
                ((count, 256 * mp), bf16),
                ((width, 256 * mp), bf16),
                ((count, width), f32),
            ],
            (words, h_one, token_mask, ho_a) + weights_of(second),
            flops=cost(7),
            name="front_last",
            grant=10,
            ready=ready,
            **static,
        )
        resid, h_two, soft, sent, sq_branch = call(
            route_kernel,
            [
                ((count, width), f32),
                ((count, width), bf16),
                ((2, images, experts, tall), f32),
                ((experts * each, width), bf16),
                ((images, 1, 128), f32),
            ],
            (words, x3, branch, cot3, token_mask, ex),
            flops=cost(2),
            name="route",
            grant=6,
            experts=experts,
            **exact,
        )
        got = sent.reshape(dp, each, width)
        got = lax.all_to_all(got, "dp", split_axis=0, concat_axis=0, tiled=True)
        got = gather_mp(got, mp).reshape(-1, width)
        everyone = got.shape[0]
        hidden, grad_pre, grad_expert, back = call(
            expert_kernel,
            [
                ((everyone, w_in.shape[2]), bf16),
                ((everyone, w_in.shape[2]), bf16),
                ((everyone, width), bf16),
                ((everyone, width), bf16),
            ],
            (got, w_in[0], w_back[0]),
            flops=cost(2),
            name="expert",
            scalars=0,
            grant=12 if dp <= 8 else 56,
            each=each,
        )
        back = back.reshape(mp, dp, each, width)
        back = scatter(back, "mp", mp, [1, 2])
        back = lax.all_to_all(back, "dp", split_axis=0, concat_axis=0, tiled=True)
        back = back.reshape(dp, 2, each // 2, width)[:, :, :images].transpose(1, 2, 0, 3)
        grad_w_back = mm_tn(hidden, grad_expert)
        grad_w_in = mm_tn(got, grad_pre)

        out_rows, grad_resid, grad_low, grad_turned, small = call(
            mix_kernel,
            [
                ((images, seq, width), bf16),
                ((count, width), f32),
                ((count, width), bf16),
                ((width, count), bf16),
                ((experts + 5, width), f32),
            ],
            (words, resid, h_two, soft, cot3, token_mask, ex, back, sq_branch),
            flops=cost(5),
            name="mix",
            grant=8,
            experts=experts,
            groups=mp,
            **exact,
        )
        shape = (1, 1, width, 4 * part) if ready else (2, high, d_rows, 4 * part)

        def back_of(x, flip, grad_in):
            grads, joined = call(
                back_kernel,
                [(shape, bf16), ((count, JOINED), bf16)],
                (words, grad_in, grad_turned, h_turned, qkv_a, p_a, qkv_b, p_b, heads_out, w_heads),
                [pltpu.VMEM((count, 256), f32)],
                flops=cost(8),
                name="back",
                grant=10,
                x=x,
                flip=flip,
                **static,
            )
            if ready:
                grads = reorder(grads.reshape(dp, d_rows, 4 * part), me)
                grads = grads.reshape(high, 2, d_rows, 4 * part).transpose(1, 0, 2, 3)
            return grads, joined

        def fold(terms, halves, starts=None, kept_columns=4 * part):
            size = terms[0].shape
            kept = ((size[0] // 2,) + size[1:-1] + (kept_columns,), bf16)
            return call(
                fold_kernel,
                [kept, kept],
                terms,
                flops=cost(1),
                name="fold",
                scalars=0,
                grant=6,
                halves=halves,
                starts=starts or (0,) * len(terms),
            )

        order = ((1, 1), (1, 0), (0, 1), (0, 0))
        sent_grads, joined_a = back_of(1, 1, grad_low)
        other = swap(sent_grads, "mp", mp, 1)
        grad_low, joined_a = lax.optimization_barrier((grad_low, joined_a))
        kept_grads, joined_b = back_of(1, 0, grad_low)
        far_kept, far_left = fold((kept_grads, other), True)
        far_left, grad_low, joined_b = lax.optimization_barrier((far_left, grad_low, joined_b))
        early = swap_both(far_left[0], dp, mp, (0, 2), (1, 0))
        sent_grads, joined_c = back_of(0, 1, grad_low)
        grad_low, joined_c = lax.optimization_barrier((grad_low, joined_c))
        other = swap(sent_grads, "mp", mp, 1)
        kept_grads, joined_d = back_of(0, 0, grad_low)
        part_shape = ((high, d_rows, 4 * part), bf16)
        near_sum, own_sum, second = call(
            blend_kernel,
            [part_shape] * 3,
            (words, far_kept[0], kept_grads, other),
            flops=cost(1),
            name="blend",
            grant=8,
        )
        second = swap_both(second, dp, mp, (0, 2), (1, 0))
        thirds = call(
            blend_late_kernel,
            [((high, d_rows, half), bf16)] * 2,
            (words, far_kept[0], own_sum, early),
            flops=cost(1),
            name="blend_late",
            grant=8,
        )
        thirds = [swap_both(third, dp, mp, (1, 0), (0, 2)) for third in thirds]
        grad_tokens, small, _ = call(
            last_kernel,
            [((images, seq, width), f32), ((experts + 5, width), f32), ((count, width), f32)],
            (words, x3, grad_resid, ex, small, w_a, w_b, joined_a, joined_b, joined_c, joined_d),
            flops=cost(6),
            name="last",
            grant=8,
            experts=experts,
            order=order,
            **exact,
        )
        for bit in bits_of(dp)[:-1]:
            small = small + swap(small, "dp", dp, bit)
        parts = []
        for k, third in enumerate(thirds):
            starts = (k * half, k * half, 0)
            kept, left = fold((near_sum, second, third), False, starts, half)
            if k == 0:
                left, small = lax.optimization_barrier((left, small))
            for bit in bits_of(high)[:0:-1]:
                kept, left = fold((kept, swap(left, "dp", dp, 2 * bit)), False, None, half)
            parts += [kept[0], swap(left[0], "dp", dp, 2 * bits_of(high)[0])]
        grad_qkv, grad_out = call(
            unpack_kernel,
            [((3, d_rows, part), f32), ((part, d_rows), f32)],
            parts,
            flops=cost(1),
            name="unpack",
            scalars=0,
            grant=6,
        )
        small = small + swap(small, "dp", dp, 1)
        small = small + swap(small, "mp", mp, 2)
        grad_one, grad_two, grad_router, root_squares = call(
            finish_kernel,
            [
                ((1, d_rows), f32),
                ((1, d_rows), f32),
                ((experts, d_rows), f32),
                ((3, mp * images), f32),
            ],
            (words, small, swap(small, "mp", mp, 1)),
            flops=cost(1),
            name="finish",
            grant=4,
        )
        return (
            out_rows.reshape(rows, width),
            grad_tokens.reshape(rows, width),
            grad_one[0],
            grad_qkv.transpose(1, 0, 2),
            grad_out,
            grad_two[0],
            grad_router.T,
            grad_w_in[None],
            grad_w_back[None],
            root_squares,
        )

    return per_device


def solution(mesh):
    in_specs = (
        P(("dp", "mp"), None),
        P("dp", None),
        P("dp"),
        P("dp", None, "mp"),
        P("mp", "dp"),
        P("dp"),
        P("dp", None),
        P("dp", None, "mp"),
        P("dp", "mp", None),
        P(("dp", "mp"), None),
    )
    out_specs = (
        P(("dp", "mp"), None),
        P(("dp", "mp"), None),
        P("dp"),
        P("dp", None, "mp"),
        P("mp", "dp"),
        P("dp"),
        P("dp", None),
        P("dp", None, "mp"),
        P("dp", "mp", None),
        P(None, "dp"),
    )
    return jax.shard_map(
        make(mesh), mesh=mesh, in_specs=in_specs, out_specs=out_specs, check_vma=False
    )
```

```python
import functools
import math

import jax
import jax.numpy as jnp
from jax import lax
from jax.experimental import pallas as pl
from jax.experimental.pallas import tpu as pltpu
from jax.sharding import PartitionSpec as P

HEAD_DIM = 64


epsilon = 1e-06
bf16 = jnp.bfloat16
f32 = jnp.float32


def bits_of(size):
    return [1 << k for k in reversed(range(size.bit_length() - 1))]


def swap(array_in, axis_name, size, bit):
    return lax.ppermute(array_in, axis_name, [(i, i ^ bit) for i in range(size)])


def swap_both(array_in, dp, mp, even, odd):
    pairs = []
    for d in range(dp):
        for m in range(mp):
            flip = odd if m & 1 else even
            pairs.append((d * mp + m, (d ^ flip[0]) * mp + (m ^ flip[1])))
    return lax.ppermute(array_in, ("dp", "mp"), pairs)


def gather_mp(block, mp):
    held = block[None]
    for bit in bits_of(mp):
        other = swap(held, "mp", mp, bit)
        held = jnp.stack([held, other], 1).reshape((-1,) + block.shape)
    return held


def scatter(held, axis_name, size, bits, unit=1):
    left = sorted(bits)
    for bit in bits:
        inner = 1 << left.index(bit)
        left.remove(bit)
        pairs = held.reshape((held.shape[0] // (2 * inner), 2, inner) + held.shape[1:])
        other = swap(pairs[:, 1], axis_name, size, bit * unit)
        held = pairs[:, 0].astype(f32) + other.astype(f32)
        held = held.astype(bf16).reshape((-1,) + held.shape[2:])
    return held[0]


def mirrored(index, size):
    bits = size.bit_length() - 1
    return sum(((index >> k) & 1) << (bits - 1 - k) for k in range(bits)) if bits else index


def unmirrored(blocks):
    size = blocks.shape[0]
    bits = size.bit_length() - 1
    split = blocks.reshape((2,) * bits + blocks.shape[1:])
    turn = tuple(range(bits))[::-1] + tuple(range(bits, split.ndim))
    return split.transpose(turn).reshape(blocks.shape)


def reorder(blocks, me):
    size = blocks.shape[0]
    for bit in bits_of(size):
        pairs = blocks.reshape((size // (2 * bit), 2, bit) + blocks.shape[1:])
        blocks = jnp.where((me & bit) > 0, pairs[:, ::-1], pairs).reshape(blocks.shape)
    return blocks


def mm(a, b):
    return lax.dot_general(a, b, (((1,), (0,)), ((), ())), preferred_element_type=f32)


def mm_nt(a, b):
    return lax.dot_general(a, b, (((1,), (1,)), ((), ())), preferred_element_type=f32)


def mm_tn(a, b):
    return lax.dot_general(a, b, (((0,), (0,)), ((), ())), preferred_element_type=f32)


def unit_of(rows_f):
    mean_row = jnp.mean(rows_f, axis=-1, keepdims=True)
    centered = rows_f - mean_row
    variance = jnp.mean(centered * centered, axis=-1, keepdims=True)
    inverse = lax.rsqrt(variance + epsilon)
    return centered * inverse, inverse


def padded(value, pad):
    return jnp.concatenate([value, jnp.zeros((pad, value.shape[1]), value.dtype)], 0)


def low_lanes(rows):
    return lax.broadcasted_iota(jnp.int32, (rows, 128), 1) < HEAD_DIM


JOINED = 640


def pack_kernel(
    me_ref, qkv_hbm, out_hbm, one_hbm, two_hbm, router_hbm, first_ref, second_ref, extra_ref,
    qkv_ref, out_ref, one_ref, two_ref, router_ref, sems
):
    del me_ref
    pairs = (
        (qkv_hbm, qkv_ref), (out_hbm, out_ref), (one_hbm, one_ref), (two_hbm, two_ref), (router_hbm, router_ref),
    )
    copies = [pltpu.make_async_copy(a, b, sems.at[k]) for k, (a, b) in enumerate(pairs)]
    for copy in copies:
        copy.start()
    for copy in copies:
        copy.wait()
    low, mid = 2 * HEAD_DIM, qkv_ref.shape[2]
    out = out_ref[...].astype(f32).T.astype(bf16)
    first_ref[...] = jnp.concatenate([qkv_ref[c, :, :low] for c in range(3)], axis=1)
    second_ref[...] = jnp.concatenate(
        [qkv_ref[c, :, low:mid] for c in range(3)] + [out[:, low:mid], out[:, :low]], axis=1
    )
    rows = one_ref.shape[1]
    columns = [one_ref[...], two_ref[...], router_ref[...]]
    columns = [value.astype(f32) for value in columns]
    filled = sum(value.shape[0] for value in columns)
    columns.append(jnp.zeros((extra_ref.shape[1] - filled, rows), f32))
    extra_ref[...] = jnp.concatenate(columns, 0).T.astype(bf16)


def fold_kernel(*refs, halves, starts):
    terms, (kept_ref, left_ref) = refs[:-2], refs[-2:]
    size, columns = terms[0].shape[0], kept_ref.shape[-1]
    for k in range(size):
        total = None
        for term, start in zip(terms, starts):
            value = term[k][..., start : start + columns].astype(f32)
            total = value if total is None else total + value
        at, odd = (k % (size // 2), k >= size // 2) if halves else (k // 2, k % 2 == 1)
        (left_ref if odd else kept_ref)[at] = total.astype(bf16)


def blend_kernel(me_ref, far_ref, kept_ref, other_ref, near_ref, own_ref, second_ref):
    for k, ref in ((0, near_ref), (1, own_ref)):
        ref[...] = (kept_ref[k].astype(f32) + other_ref[k].astype(f32)).astype(bf16)
    first_core = me_ref[1] == 0

    @pl.when(first_core)
    def _():
        second_ref[...] = far_ref[...]

    @pl.when(jnp.logical_not(first_core))
    def _():
        second_ref[...] = own_ref[...]


def blend_late_kernel(me_ref, far_ref, own_ref, early_ref, *thirds):
    columns = thirds[0].shape[-1]
    for core, ref in ((0, own_ref), (1, far_ref)):

        @pl.when(me_ref[1] == core)
        def _(ref=ref):
            for k, third in enumerate(thirds):
                at = slice(k * columns, (k + 1) * columns)
                total = ref[..., at].astype(f32) + early_ref[..., at].astype(f32)
                third[...] = total.astype(bf16)


def finish_kernel(me_ref, own_ref, other_ref, one_ref, two_ref, router_ref, root_ref):
    experts, rows = router_ref.shape
    total = own_ref[...] + other_ref[...]
    width = total.shape[1]
    mine = pltpu.roll(total, lax.rem(width - me_ref[0] * rows, width), 1)
    one_ref[...] = mine[experts : experts + 1, :rows]
    two_ref[...] = mine[experts + 1 : experts + 2, :rows]
    router_ref[...] = mine[:experts, :rows]
    images = root_ref.shape[1]
    mine = pltpu.roll(total, lax.rem(width - me_ref[0] * images, width), 1)
    root_ref[...] = mine[experts + 2 : experts + 5, :images]


def unpack_kernel(own_a, other_a, own_b, other_b, qkv_ref, out_ref):
    low, mid = 2 * HEAD_DIM, qkv_ref.shape[2]
    pair = own_a[...].astype(f32) + other_a[...].astype(f32)
    rest = own_b[...].astype(f32) + other_b[...].astype(f32)
    for c in range(3):
        qkv_ref[c, :, :low] = pair[:, c * low : (c + 1) * low]
        qkv_ref[c, :, low:mid] = rest[:, c * HEAD_DIM : (c + 1) * HEAD_DIM]
    out_ref[...] = jnp.concatenate([rest[:, 256:], rest[:, 192:256]], axis=1).T


def length_of(mask_ref, me_ref, b, images):
    row = mask_ref[pl.ds(me_ref[2] * images + b, 1), :]
    return jnp.sum(row.astype(f32), axis=1, keepdims=True)


def seen_row(length, tall):
    return lax.broadcasted_iota(jnp.int32, (1, tall), 1).astype(f32) < length


def seen_column(length, tall):
    return lax.broadcasted_iota(jnp.int32, (tall, 1), 0).astype(f32) < length


def prep_kernel(me_ref, x_ref, extra_ref, h_ref, ht_ref, small_ref, *, images, seq, tall):
    blocks = extra_ref.shape[0]
    me = me_ref[0]
    parts = [extra_ref[mirrored(me ^ d, blocks) if blocks > 1 else 0] for d in range(blocks)]
    small_ref[...] = jnp.concatenate(parts, 0).astype(f32).T
    gain = small_ref[0:1, :]
    for b in range(images):
        unit, _ = unit_of(x_ref[b].astype(f32))
        h_ref[pl.ds(b * tall, tall), :] = padded((unit * gain).astype(bf16), tall - seq)
    ht_ref[...] = h_ref[...].T


def fetch_all(me_ref, refs, put):
    rows, high_size = refs[0].shape[2], refs[0].shape[1]
    for core in (0, 1):

        @pl.when(me_ref[1] == core)
        def _(core=core):
            for slot in range(4):
                x, of_core = slot & 1, slot >> 1
                first, second = refs[:2] if of_core == core else refs[2:4]
                for r in range(2 * high_size):
                    low, high = r & 1, mirrored(r >> 1, high_size)
                    if of_core == 0:
                        block = (second if x else first)[low, high]
                    else:
                        block = (second if low else first)[x, high]
                    d = jnp.bitwise_xor(me_ref[0], r)
                    put(slot, pl.ds(pl.multiple_of(d * rows, 16), rows), block)


def attend(triples):
    scores = [mm_nt(q, k) * HEAD_DIM ** (-0.5) + bias for q, k, _, bias in triples]
    terms = [jnp.exp(value - jnp.max(value, axis=-1, keepdims=True)) for value in scores]
    probs = [
        (value * (1.0 / jnp.sum(value, axis=-1, keepdims=True))).astype(bf16) for value in terms
    ]
    return probs, [mm(value, v) for value, (_, _, v, _) in zip(probs, triples)]


def bias_of(mask_ref, me_ref, b, images, tall):
    return jnp.where(seen_row(length_of(mask_ref, me_ref, b, images), tall), 0.0, -1e30)


def front_pair_kernel(me_ref, h_ref, mask_ref, *refs, images, tall, ready):
    w_ref, qkv_ref, p_ref, ho_ref = refs[4:]

    def put(slot, at, block):
        w_ref[slot, at, :] = block

    if ready:
        for slot in range(4):
            put(slot, slice(None), refs[slot][...])
    else:
        fetch_all(me_ref, refs[:4], put)
    low = low_lanes(tall)

    def group(j, carry):
        qkv_ref[j] = mm(h_ref[...], w_ref[j]).astype(bf16)
        triples = []
        for b in range(images):
            joined = qkv_ref[j, pl.ds(b * tall, tall), :]
            q, k, v = joined[:, :128], joined[:, 128:256], joined[:, 256:384]
            none = jnp.zeros_like(q)
            bias = bias_of(mask_ref, me_ref, b, images, tall)
            triples.append((jnp.where(low, q, none), k, v, bias))
            triples.append((jnp.where(low, none, q), k, v, bias))
        probs, outs = attend(triples)
        for b in range(images):
            p_ref[j, b, 0], p_ref[j, b, 1] = probs[2 * b], probs[2 * b + 1]
            pair = jnp.where(low, outs[2 * b], outs[2 * b + 1])
            ho_ref[j, pl.ds(b * tall, tall), :] = pair.astype(bf16)
        return carry

    lax.fori_loop(0, w_ref.shape[0], group, 0)


def front_last_kernel(me_ref, h_ref, mask_ref, pair_ref, *refs, images, tall, ready):
    w_ref, qkv_ref, p_ref, ho_ref, wo_ref, br_ref = refs[4:]

    def put(slot, at, block):
        w_ref[slot, at, :] = block[:, :256]
        wo_ref[at, slot * 256 : (slot + 1) * 256] = block[:, 128:]

    if ready:
        for slot in range(4):
            put(slot, slice(None), refs[slot][...])
    else:
        fetch_all(me_ref, refs[:4], put)
    low = low_lanes(tall)

    def two(i, carry):
        places = [(2 * i + k, b) for k in (0, 1) for b in range(images)]
        for j in (2 * i, 2 * i + 1):
            qkv_ref[j] = mm(h_ref[...], w_ref[j]).astype(bf16)
        triples = []
        for j, b in places:
            joined = qkv_ref[j, pl.ds(b * tall, tall), :]
            qk, v = joined[:, :128], joined[:, 128:256]
            k = pltpu.roll(qk.astype(f32), HEAD_DIM, 1).astype(bf16)
            bias = bias_of(mask_ref, me_ref, b, images, tall)
            triples.append((jnp.where(low, qk, jnp.zeros_like(qk)), k, v, bias))
        probs, outs = attend(triples)
        for (j, b), prob, out in zip(places, probs, outs):
            at, start = pl.ds(b * tall, tall), pl.multiple_of(j * 256, 256)
            p_ref[j, b] = prob
            ho_ref[at, pl.ds(start, 128)] = jnp.where(low, 0.0, pltpu.roll(out, HEAD_DIM, 1)).astype(bf16)
            ho_ref[at, pl.ds(start + 128, 128)] = pair_ref[j, at, :]
        return carry

    lax.fori_loop(0, w_ref.shape[0] // 2, two, 0)
    br_ref[...] = mm_nt(ho_ref[...], wo_ref[...])


def spot(rows, b, start, experts):
    each = rows // experts
    at_row = lax.broadcasted_iota(jnp.int32, (rows, experts), 0)
    at_column = lax.broadcasted_iota(jnp.int32, (rows, experts), 1)
    return jnp.where(at_row == at_column * each + (start + b), 1.0, 0.0).astype(bf16)


def route_kernel(
    me_ref, x_ref, br_ref, cot_ref, mask_ref, ex_ref,
    res_ref, h_ref, soft_ref, sent_ref, sq_ref, *, images, seq, tall, experts
):
    rows = sent_ref.shape[0]
    half = rows // experts // 2
    router = ex_ref[2 : 2 + experts, :].astype(bf16)
    gain = ex_ref[1:2, :]
    total = jnp.zeros(sent_ref.shape, f32)
    for b in range(images):
        at = pl.ds(b * tall, tall)
        length = length_of(mask_ref, me_ref, b, images)
        branch = br_ref[at, :]
        resid = padded(x_ref[b].astype(f32), tall - seq) + branch
        res_ref[at, :] = resid
        unit, _ = unit_of(resid)
        h_two = (unit * gain).astype(bf16)
        h_ref[at, :] = h_two
        logits = mm_nt(router, h_two)
        held = jnp.where(seen_row(length, tall), logits, -1e30)
        terms = jnp.exp(held - jnp.max(held, axis=1, keepdims=True))
        dispatch = terms / jnp.sum(terms, axis=1, keepdims=True)
        terms = jnp.exp(logits - jnp.max(logits, axis=0, keepdims=True))
        combine = terms / jnp.sum(terms, axis=0, keepdims=True)
        soft_ref[0, b] = dispatch
        soft_ref[1, b] = combine
        cot = padded(cot_ref[b], tall - seq)
        wide_d = mm(spot(rows, b, 0, experts), dispatch.astype(bf16)).astype(bf16)
        wide_c = mm(spot(rows, b, half, experts), combine.astype(bf16)).astype(bf16)
        total += mm(wide_d, h_two) + mm(wide_c, cot)
        squares = jnp.sum(branch * branch, axis=1, keepdims=True)
        squares = jnp.sum(jnp.where(seen_column(length, tall), squares, 0.0), axis=0, keepdims=True)
        sq_ref[b] = jnp.broadcast_to(squares, (1, 128))
    sent_ref[...] = total.astype(bf16)


def expert_kernel(got_ref, first_ref, second_ref, hid_ref, pre_ref, grad_ref, back_ref, *, each):
    rows = got_ref.shape[0]
    half = each // 2
    got = got_ref[...]
    own = jnp.bitwise_and(lax.broadcasted_iota(jnp.int32, (rows, 1), 0), each - 1) < half
    grads = jnp.where(own, pltpu.roll(got.astype(f32), rows - half, 0), 0.0).astype(bf16)
    grad_ref[...] = grads
    u = mm(got, first_ref[...])
    cubic = 0.7978845608028654 * (u + 0.044715 * u * u * u)
    t = jnp.tanh(cubic)
    hidden = jnp.where(own, 0.5 * u * (1.0 + t), 0.0).astype(bf16)
    hid_ref[...] = hidden
    slope = 0.5 * (1.0 + t) + 0.5 * u * (1.0 - t * t) * 0.7978845608028654 * (
        1.0 + 3.0 * 0.044715 * u * u
    )
    grad_pre = (mm_nt(grads, second_ref[...]) * slope).astype(bf16)
    pre_ref[...] = grad_pre
    out = mm(hidden, second_ref[...])
    grad_in = mm_nt(grad_pre, first_ref[...])
    back_ref[...] = jnp.where(own, out, pltpu.roll(grad_in, half, 0)).astype(bf16)


def mix_kernel(
    me_ref, res_ref, h_ref, soft_ref, cot_ref, mask_ref, ex_ref, back_ref, sq_ref,
    out_ref, gres_ref, gb_ref, gbt_ref, small_ref, *, images, seq, tall, experts, groups
):
    small_ref[...] = jnp.zeros_like(small_ref)
    router = ex_ref[2 : 2 + experts, :].astype(bf16)
    gain = ex_ref[1:2, :]
    width = out_ref.shape[2]
    lanes = lax.broadcasted_iota(jnp.int32, (1, width), 1)
    roots = [jnp.zeros((1, width), f32) for _ in range(3)]
    for b in range(images):
        at = pl.ds(b * tall, tall)
        length = length_of(mask_ref, me_ref, b, images)
        resid, h_two = res_ref[at, :], h_ref[at, :]
        dispatch, combine = soft_ref[0, b], soft_ref[1, b]
        dispatch_low, combine_low = dispatch.astype(bf16), combine.astype(bf16)
        returned, grad_slots = back_ref[0, b], back_ref[1, b]
        cot = padded(cot_ref[b], tall - seq)
        mixed = mm_tn(combine_low, returned)
        stream = resid + mixed
        out_ref[b] = stream[:seq].astype(bf16)
        column = seen_column(length, tall)
        sums = []
        for value in (stream, mixed):
            squares = jnp.sum(value * value, axis=1, keepdims=True)
            sums.append(jnp.sum(jnp.where(column, squares, 0.0), axis=0, keepdims=True))
        sums.insert(1, sq_ref[b, :, 0:1])
        for k, value in enumerate(sums):
            root = jnp.sqrt(value / (length * width))
            mine = lanes == (me_ref[0] * groups + me_ref[2]) * images + b
            roots[k] += jnp.where(mine, root, 0.0)
        grad_c = mm_nt(returned, cot)
        grad_c = combine * (grad_c - jnp.sum(grad_c * combine, axis=0, keepdims=True))
        grad_d = mm_nt(grad_slots, h_two)
        grad_d = dispatch * (grad_d - jnp.sum(grad_d * dispatch, axis=1, keepdims=True))
        grad_logits = (grad_d + grad_c).astype(bf16)
        grad_h = mm_tn(dispatch_low, grad_slots) + mm_tn(grad_logits, router)
        small_ref[0:experts, :] += mm(grad_logits, h_two)
        unit, inverse = unit_of(resid)
        small_ref[experts + 1 : experts + 2, :] += jnp.sum(grad_h * unit, axis=0, keepdims=True)
        scaled = grad_h * gain
        mean_grad = jnp.mean(scaled, axis=-1, keepdims=True)
        mean_proj = jnp.mean(scaled * unit, axis=-1, keepdims=True)
        gres_ref[at, :] = cot.astype(f32) + inverse * (scaled - mean_grad - unit * mean_proj)
    for k in range(3):
        small_ref[experts + 2 + k : experts + 3 + k, :] = roots[k]
    gb_ref[...] = gres_ref[...].astype(bf16)
    gbt_ref[...] = gres_ref[...].T.astype(bf16)


def back_kernel(
    me_ref, gb_ref, gbt_ref, ht_ref, qkv_a, p_a, qkv_b, p_b, ho_ref, wo_ref,
    gw_ref, gj_ref, dho_ref, *, images, tall, x, flip
):
    j = x + 2 * jnp.bitwise_xor(me_ref[1], flip)
    own = pl.ds(pl.multiple_of(j * 256, 256), 256)
    scale = HEAD_DIM ** (-0.5)
    low = low_lanes(tall)
    dho_ref[...] = mm(gb_ref[...], wo_ref[:, own])
    heads, dots = [], []
    for b in range(images):
        at = pl.ds(b * tall, tall)
        joined, joined_last = qkv_a[j, at, :], qkv_b[j, at, :]
        q_pair, k_pair, v_pair = joined[:, :128], joined[:, 128:256], joined[:, 256:384]
        qk_last, v_last = joined_last[:, :128], joined_last[:, 128:256]
        grad = dho_ref[at, :].astype(bf16).astype(f32)
        product = grad * ho_ref[at, own].astype(f32)
        single, pair = product[:, :128], product[:, 128:]
        dots += [
            jnp.sum(jnp.where(low, pair, 0.0), axis=1, keepdims=True),
            jnp.sum(jnp.where(low, 0.0, pair), axis=1, keepdims=True),
            jnp.sum(single, axis=1, keepdims=True),
        ]
        grad_pair = grad[:, 128:]
        grad_last = jnp.where(low, pltpu.roll(grad[:, :128], HEAD_DIM, 1), 0.0).astype(bf16)
        heads += [
            (p_a[j, b, 0], jnp.where(low, grad_pair, 0.0).astype(bf16), v_pair, q_pair, k_pair),
            (p_a[j, b, 1], jnp.where(low, 0.0, grad_pair).astype(bf16), v_pair, q_pair, k_pair),
            (p_b[j, b], grad_last, v_last, qk_last, qk_last),
        ]
    grad_p = [mm_nt(g, v) for _, g, v, _, _ in heads]
    grad_s = [
        (probs.astype(f32) * (value - dot)).astype(bf16)
        for (probs, _, _, _, _), value, dot in zip(heads, grad_p, dots)
    ]
    gqs = [mm(value, k) for value, (_, _, _, _, k) in zip(grad_s, heads)]
    gks = [mm_tn(value, q) for value, (_, _, _, q, _) in zip(grad_s, heads)]
    gvs = [mm_tn(probs, g) for probs, g, _, _, _ in heads]
    for b in range(images):
        at = pl.ds(b * tall, tall)
        gq, gk, gv = (value[3 * b : 3 * b + 3] for value in (gqs, gks, gvs))
        last = pltpu.roll(jnp.where(low, gk[2], gq[2]), HEAD_DIM, 1)
        gj_ref[at, :] = jnp.concatenate(
            [
                jnp.where(low, gq[0], gq[1]) * scale,
                jnp.where(low, gk[0], gk[1]) * scale,
                gv[0] + gv[1],
                last * scale,
                gv[2],
            ],
            1,
        ).astype(bf16)
    grad_out = mm(gbt_ref[...], ho_ref[:, own])
    grad_in = mm(ht_ref[...], gj_ref[...])
    halves, blocks, rows = gw_ref.shape[:3]
    for d in range(halves * blocks):
        r = jnp.bitwise_xor(me_ref[0], d) if halves > 1 else 0
        entry = (jnp.bitwise_and(r, 1), jnp.right_shift(r, 1)) if halves > 1 else (0, 0)
        at = slice(d * rows, (d + 1) * rows)
        gw_ref[entry + (slice(None), slice(0, 512))] = grad_in[at, :512].astype(bf16)
        gw_ref[entry + (slice(None), slice(512, 640))] = (
            grad_in[at, 512:] + grad_out[at, :128]
        ).astype(bf16)
        gw_ref[entry + (slice(None), slice(640, 768))] = grad_out[at, 128:].astype(bf16)


def input_kernel(me_ref, w_a, w_b, *refs, order):
    grads, gh_ref = refs[:-1], refs[-1]
    for k, (ref, (x, flip)) in enumerate(zip(grads, order)):
        j = x + 2 * jnp.bitwise_xor(me_ref[1], flip)
        into = mm_nt(ref[:, :384], w_a[j]) + mm_nt(ref[:, 384:], w_b[j])
        if k == 0:
            gh_ref[...] = into
        else:
            gh_ref[...] += into


def last_kernel(x_ref, gres_ref, gh_ref, ex_ref, part_ref, gt_ref, small_ref, *, images, seq, tall, experts):
    total = jnp.zeros((1, x_ref.shape[2]), f32)
    gain = ex_ref[0:1, :]
    for b in range(images):
        at = pl.ds(b * tall, seq)
        unit, inverse = unit_of(x_ref[b].astype(f32))
        grad_h = gh_ref[at, :]
        total += jnp.sum(grad_h * unit, axis=0, keepdims=True)
        scaled = grad_h * gain
        mean_grad = jnp.mean(scaled, axis=-1, keepdims=True)
        mean_proj = jnp.mean(scaled * unit, axis=-1, keepdims=True)
        gt_ref[b] = gres_ref[at, :] + inverse * (scaled - mean_grad - unit * mean_proj)
    small_ref[...] = part_ref[...]
    small_ref[experts : experts + 1, :] = total


def cost(microseconds):
    return int(microseconds * 1.1e9)


def call(kernel, outs, args, scratch=(), flops=0, name=None, scalars=1, grant=16, **static):
    spec = pl.BlockSpec(memory_space=pltpu.VMEM)
    word = pl.BlockSpec(memory_space=pltpu.SMEM)
    moved = sum(math.prod(a.shape) * a.dtype.itemsize for a in args)
    return pl.pallas_call(
        functools.partial(kernel, **static),
        out_shape=[jax.ShapeDtypeStruct(s, d) for s, d in outs],
        in_specs=[word] * scalars + [spec] * (len(args) - scalars),
        out_specs=[spec] * len(outs),
        scratch_shapes=list(scratch),
        compiler_params=pltpu.CompilerParams(vmem_limit_bytes=grant << 20),
        cost_estimate=pl.CostEstimate(flops=flops, bytes_accessed=moved, transcendentals=0),
        name=name,
    )(*args)


def make(mesh):
    dp, mp = mesh.shape["dp"], mesh.shape["mp"]

    def per_device(
        tokens, token_mask, gain_one, w_qkv, w_out, gain_two, router, w_in, w_back, cotangent
    ):
        rows, width = tokens.shape
        seq = token_mask.shape[1]
        tall = -(-seq // 16) * 16
        images = rows // seq
        experts = router.shape[1]
        d_rows, _, part = w_qkv.shape
        count = images * tall
        high = dp // 2
        heads = part // HEAD_DIM
        ready = d_rows % 16 != 0
        each = 2 * (1 << (images - 1).bit_length())
        me = lax.axis_index("dp")
        at_mp = lax.axis_index("mp")
        core = at_mp & 1
        words = jnp.stack([me, core, at_mp]).astype(jnp.int32)
        static = {"images": images, "tall": tall}
        exact = {"images": images, "seq": seq, "tall": tall}

        columns = experts + 2
        half = 2 * part
        hbm = pl.BlockSpec(memory_space=pltpu.HBM)
        vmem = pl.BlockSpec(memory_space=pltpu.VMEM)
        word = pl.BlockSpec(memory_space=pltpu.SMEM)
        wide = columns + -columns % 128
        shapes = [(3, d_rows, part), (part, d_rows), (1, d_rows), (1, d_rows), (experts, d_rows)]
        first, second, extra = pl.pallas_call(
            pack_kernel,
            out_shape=[jax.ShapeDtypeStruct((d_rows, n), bf16) for n in (half, half, wide)],
            in_specs=[word] + [hbm] * 5,
            out_specs=[vmem] * 3,
            scratch_shapes=[pltpu.VMEM(shape, bf16) for shape in shapes] + [pltpu.SemaphoreType.DMA((5,))],
            compiler_params=pltpu.CompilerParams(vmem_limit_bytes=67_000_000),
            name="pack",
        )(words, w_qkv.transpose(1, 0, 2), w_out, gain_one[None], gain_two[None], router.T)

        first, second, held_extra = first[None], second[None], extra[None]
        for bit in bits_of(dp)[:-1]:
            first = jnp.concatenate([first, swap(first, "dp", dp, bit)])
            held_extra = jnp.concatenate([held_extra, swap(held_extra, "dp", dp, bit)])
        stages = bits_of(dp)[:-1]
        second = jnp.concatenate([second, swap(second, "dp", dp, stages[0])])
        other, held_extra, second = lax.optimization_barrier(
            (swap_both(first, dp, mp, (1, 0), (0, 2)), held_extra, second)
        )
        for bit in stages[1:]:
            second = jnp.concatenate([second, swap(second, "dp", dp, bit)])
        held_extra = jnp.concatenate([held_extra, swap(held_extra, "dp", dp, 1)])
        held_extra = held_extra.reshape((dp,) + extra.shape)
        if ready:
            held_extra = reorder(unmirrored(held_extra), me).reshape(1, width, -1)
        x3 = tokens.reshape(images, seq, width)
        cot3 = cotangent.reshape(images, seq, width)
        h_one, h_turned, ex = call(
            prep_kernel,
            [((count, width), bf16), ((width, count), bf16), ((held_extra.shape[2], width), f32)],
            (words, x3, held_extra),
            flops=cost(2),
            name="prep",
            grant=4,
            **exact,
        )
        near = jnp.stack([first, other])
        far = swap_both(near, dp, mp, (0, 2), (1, 0))
        second = second.reshape((high, d_rows, half))
        other = swap_both(second, dp, mp, (1, 0), (0, 2))
        far, h_one, other = lax.optimization_barrier((far, h_one, other))
        first = (near, far, swap(near, "mp", mp, 1), swap(far, "mp", mp, 1))
        near = jnp.stack([second, other])
        second_near, second_far = near, swap_both(near, dp, mp, (0, 2), (1, 0))
        second_near_other = swap(second_near, "mp", mp, 1)

        def whole(x, of_core, near, far, other_near, other_far):
            mine = core == of_core
            low = jnp.where(mine, near, other_near)
            high_part = jnp.where(mine, far, other_far)
            blocks = jnp.stack([low[x], high_part[x]]) if of_core else (high_part if x else low)
            blocks = blocks.reshape((dp, d_rows, half))
            blocks = unmirrored(blocks)
            return reorder(blocks, me).reshape(width, half)

        def weights_of(parts):
            if ready:
                return tuple(whole(j & 1, j >> 1, *parts) for j in range(4))
            return parts

        def saved(kept, columns, probs):
            return [
                ((mp, width, kept), bf16),
                ((mp, count, columns), bf16),
                ((mp, images) + probs + (tall, tall), bf16),
                ((mp, count, 128), bf16),
            ]

        pair = call(
            front_pair_kernel,
            saved(half, 384, (2,)),
            (words, h_one, token_mask) + weights_of(first),
            flops=cost(10),
            name="front_pair",
            grant=10,
            ready=ready,
            **static,
        )
        w_a, qkv_a, p_a, ho_a = pair
        second_far, ho_a = lax.optimization_barrier((second_far, ho_a))
        second = (second_near, second_far, second_near_other, swap(second_far, "mp", mp, 1))
        w_b, qkv_b, p_b, heads_out, w_heads, branch = call(
            front_last_kernel,
            saved(256, 256, ())[:3]
            + [
                ((count, 256 * mp), bf16),
                ((width, 256 * mp), bf16),
                ((count, width), f32),
            ],
            (words, h_one, token_mask, ho_a) + weights_of(second),
            flops=cost(7),
            name="front_last",
            grant=10,
            ready=ready,
            **static,
        )
        resid, h_two, soft, sent, sq_branch = call(
            route_kernel,
            [
                ((count, width), f32),
                ((count, width), bf16),
                ((2, images, experts, tall), f32),
                ((experts * each, width), bf16),
                ((images, 1, 128), f32),
            ],
            (words, x3, branch, cot3, token_mask, ex),
            flops=cost(2),
            name="route",
            grant=6,
            experts=experts,
            **exact,
        )
        got = sent.reshape(dp, each, width)
        got = lax.all_to_all(got, "dp", split_axis=0, concat_axis=0, tiled=True)
        got = gather_mp(got, mp).reshape(-1, width)
        everyone = got.shape[0]
        hidden, grad_pre, grad_expert, back = call(
            expert_kernel,
            [
                ((everyone, w_in.shape[2]), bf16),
                ((everyone, w_in.shape[2]), bf16),
                ((everyone, width), bf16),
                ((everyone, width), bf16),
            ],
            (got, w_in[0], w_back[0]),
            flops=cost(2),
            name="expert",
            scalars=0,
            grant=12 if dp <= 8 else 56,
            each=each,
        )
        back = back.reshape(mp, dp, each, width)
        back = scatter(back, "mp", mp, [1, 2])
        back = lax.all_to_all(back, "dp", split_axis=0, concat_axis=0, tiled=True)
        back = back.reshape(dp, 2, each // 2, width)[:, :, :images].transpose(1, 2, 0, 3)
        grad_w_back = mm_tn(hidden, grad_expert)
        grad_w_in = mm_tn(got, grad_pre)

        out_rows, grad_resid, grad_low, grad_turned, small = call(
            mix_kernel,
            [
                ((images, seq, width), bf16),
                ((count, width), f32),
                ((count, width), bf16),
                ((width, count), bf16),
                ((experts + 5, width), f32),
            ],
            (words, resid, h_two, soft, cot3, token_mask, ex, back, sq_branch),
            flops=cost(5),
            name="mix",
            grant=8,
            experts=experts,
            groups=mp,
            **exact,
        )
        shape = (1, 1, width, 4 * part) if ready else (2, high, d_rows, 4 * part)

        def back_of(x, flip, grad_in):
            grads, joined = call(
                back_kernel,
                [(shape, bf16), ((count, JOINED), bf16)],
                (words, grad_in, grad_turned, h_turned, qkv_a, p_a, qkv_b, p_b, heads_out, w_heads),
                [pltpu.VMEM((count, 256), f32)],
                flops=cost(8),
                name="back",
                grant=10,
                x=x,
                flip=flip,
                **static,
            )
            if ready:
                grads = reorder(grads.reshape(dp, d_rows, 4 * part), me)
                grads = grads.reshape(high, 2, d_rows, 4 * part).transpose(1, 0, 2, 3)
            return grads, joined

        def fold(terms, halves, starts=None, kept_columns=4 * part):
            size = terms[0].shape
            kept = ((size[0] // 2,) + size[1:-1] + (kept_columns,), bf16)
            return call(
                fold_kernel,
                [kept, kept],
                terms,
                flops=cost(1),
                name="fold",
                scalars=0,
                grant=6,
                halves=halves,
                starts=starts or (0,) * len(terms),
            )

        order = ((1, 1), (1, 0), (0, 1), (0, 0))
        sent_grads, joined_a = back_of(1, 1, grad_low)
        other = swap(sent_grads, "mp", mp, 1)
        grad_low, joined_a = lax.optimization_barrier((grad_low, joined_a))
        kept_grads, joined_b = back_of(1, 0, grad_low)
        far_kept, far_left = fold((kept_grads, other), True)
        far_left, grad_low, joined_b = lax.optimization_barrier((far_left, grad_low, joined_b))
        early = swap_both(far_left[0], dp, mp, (0, 2), (1, 0))
        sent_grads, joined_c = back_of(0, 1, grad_low)
        grad_low, joined_c = lax.optimization_barrier((grad_low, joined_c))
        other = swap(sent_grads, "mp", mp, 1)
        kept_grads, joined_d = back_of(0, 0, grad_low)
        part_shape = ((high, d_rows, 4 * part), bf16)
        near_sum, own_sum, second = call(
            blend_kernel,
            [part_shape] * 3,
            (words, far_kept[0], kept_grads, other),
            flops=cost(1),
            name="blend",
            grant=8,
        )
        second = swap_both(second, dp, mp, (0, 2), (1, 0))
        thirds = call(
            blend_late_kernel,
            [((high, d_rows, half), bf16)] * 2,
            (words, far_kept[0], own_sum, early),
            flops=cost(1),
            name="blend_late",
            grant=8,
        )
        thirds = [swap_both(third, dp, mp, (1, 0), (0, 2)) for third in thirds]
        grad_h = call(
            input_kernel,
            [((count, width), f32)],
            (words, w_a, w_b, joined_a, joined_b, joined_c, joined_d),
            flops=cost(4),
            name="input",
            grant=8,
            order=order,
        )[0]
        pieces = [
            list(fold((near_sum, second, third), False, (k * half, k * half, 0), half))
            for k, third in enumerate(thirds)
        ]
        pieces[0][1], grad_h = lax.optimization_barrier((pieces[0][1], grad_h))
        grad_tokens, small = call(
            last_kernel,
            [((images, seq, width), f32), ((experts + 5, width), f32)],
            (x3, grad_resid, grad_h, ex, small),
            flops=cost(0.1),
            name="last",
            scalars=0,
            grant=8,
            experts=experts,
            **exact,
        )
        for bit in bits_of(mp)[::-1]:
            small = small + swap(small, "mp", mp, bit)
        parts = []
        for k, (kept, left) in enumerate(pieces):
            for bit in bits_of(high)[:0:-1]:
                other = swap(left, "dp", dp, 2 * bit)
                if k == 0:
                    other, small = lax.optimization_barrier((other, small))
                kept, left = fold((kept, other), False, None, half)
            parts += [kept[0], swap(left[0], "dp", dp, 2 * bits_of(high)[0])]
        grad_qkv, grad_out = call(
            unpack_kernel,
            [((3, d_rows, part), f32), ((part, d_rows), f32)],
            parts,
            flops=cost(1),
            name="unpack",
            scalars=0,
            grant=6,
        )
        for bit in bits_of(dp)[:0:-1]:
            small = small + swap(small, "dp", dp, bit)
        grad_one, grad_two, grad_router, root_squares = call(
            finish_kernel,
            [
                ((1, d_rows), f32),
                ((1, d_rows), f32),
                ((experts, d_rows), f32),
                ((3, mp * images), f32),
            ],
            (words, small, swap(small, "dp", dp, bits_of(dp)[0])),
            flops=cost(1),
            name="finish",
            grant=4,
        )
        return (
            out_rows.reshape(rows, width),
            grad_tokens.reshape(rows, width),
            grad_one[0],
            grad_qkv.transpose(1, 0, 2),
            grad_out,
            grad_two[0],
            grad_router.T,
            grad_w_in[None],
            grad_w_back[None],
            root_squares,
        )

    return per_device


def solution(mesh):
    in_specs = (
        P(("dp", "mp"), None),
        P("dp", None),
        P("dp"),
        P("dp", None, "mp"),
        P("mp", "dp"),
        P("dp"),
        P("dp", None),
        P("dp", None, "mp"),
        P("dp", "mp", None),
        P(("dp", "mp"), None),
    )
    out_specs = (
        P(("dp", "mp"), None),
        P(("dp", "mp"), None),
        P("dp"),
        P("dp", None, "mp"),
        P("mp", "dp"),
        P("dp"),
        P("dp", None),
        P("dp", None, "mp"),
        P("dp", "mp", None),
        P(None, "dp"),
    )
    return jax.shard_map(
        make(mesh), mesh=mesh, in_specs=in_specs, out_specs=out_specs, check_vma=False
    )
```

```python
import functools
import math

import jax
import jax.numpy as jnp
from jax import lax
from jax.experimental import pallas as pl
from jax.experimental.pallas import tpu as pltpu
from jax.sharding import PartitionSpec as P

HEAD_DIM = 64


epsilon = 1e-06
bf16 = jnp.bfloat16
f32 = jnp.float32


def bits_of(size):
    return [1 << k for k in reversed(range(size.bit_length() - 1))]


def swap(array_in, axis_name, size, bit):
    return lax.ppermute(array_in, axis_name, [(i, i ^ bit) for i in range(size)])


def swap_both(array_in, dp, mp, even, odd):
    pairs = []
    for d in range(dp):
        for m in range(mp):
            flip = odd if m & 1 else even
            pairs.append((d * mp + m, (d ^ flip[0]) * mp + (m ^ flip[1])))
    return lax.ppermute(array_in, ("dp", "mp"), pairs)


def gather_mp(block, mp):
    held = block[None]
    for bit in bits_of(mp):
        other = swap(held, "mp", mp, bit)
        held = jnp.stack([held, other], 1).reshape((-1,) + block.shape)
    return held


def scatter(held, axis_name, size, bits, unit=1):
    left = sorted(bits)
    for bit in bits:
        inner = 1 << left.index(bit)
        left.remove(bit)
        pairs = held.reshape((held.shape[0] // (2 * inner), 2, inner) + held.shape[1:])
        other = swap(pairs[:, 1], axis_name, size, bit * unit)
        held = pairs[:, 0].astype(f32) + other.astype(f32)
        held = held.astype(bf16).reshape((-1,) + held.shape[2:])
    return held[0]


def mirrored(index, size):
    bits = size.bit_length() - 1
    return sum(((index >> k) & 1) << (bits - 1 - k) for k in range(bits)) if bits else index


def unmirrored(blocks):
    size = blocks.shape[0]
    bits = size.bit_length() - 1
    split = blocks.reshape((2,) * bits + blocks.shape[1:])
    turn = tuple(range(bits))[::-1] + tuple(range(bits, split.ndim))
    return split.transpose(turn).reshape(blocks.shape)


def reorder(blocks, me):
    size = blocks.shape[0]
    for bit in bits_of(size):
        pairs = blocks.reshape((size // (2 * bit), 2, bit) + blocks.shape[1:])
        blocks = jnp.where((me & bit) > 0, pairs[:, ::-1], pairs).reshape(blocks.shape)
    return blocks


def mm(a, b):
    return lax.dot_general(a, b, (((1,), (0,)), ((), ())), preferred_element_type=f32)


def mm_nt(a, b):
    return lax.dot_general(a, b, (((1,), (1,)), ((), ())), preferred_element_type=f32)


def mm_tn(a, b):
    return lax.dot_general(a, b, (((0,), (0,)), ((), ())), preferred_element_type=f32)


def unit_of(rows_f):
    mean_row = jnp.mean(rows_f, axis=-1, keepdims=True)
    centered = rows_f - mean_row
    variance = jnp.mean(centered * centered, axis=-1, keepdims=True)
    inverse = lax.rsqrt(variance + epsilon)
    return centered * inverse, inverse


def padded(value, pad):
    return jnp.concatenate([value, jnp.zeros((pad, value.shape[1]), value.dtype)], 0)


def low_lanes(rows):
    return lax.broadcasted_iota(jnp.int32, (rows, 128), 1) < HEAD_DIM


JOINED = 640


def pack_kernel(
    me_ref, qkv_hbm, out_hbm, one_hbm, two_hbm, router_hbm, first_ref, second_ref, extra_ref,
    qkv_ref, out_ref, one_ref, two_ref, router_ref, sems
):
    del me_ref
    pairs = (
        (qkv_hbm, qkv_ref), (out_hbm, out_ref), (one_hbm, one_ref), (two_hbm, two_ref), (router_hbm, router_ref),
    )
    copies = [pltpu.make_async_copy(a, b, sems.at[k]) for k, (a, b) in enumerate(pairs)]
    for copy in copies:
        copy.start()
    for copy in copies:
        copy.wait()
    low, mid = 2 * HEAD_DIM, qkv_ref.shape[2]
    out = out_ref[...].astype(f32).T.astype(bf16)
    first_ref[...] = jnp.concatenate([qkv_ref[c, :, :low] for c in range(3)], axis=1)
    second_ref[...] = jnp.concatenate(
        [qkv_ref[c, :, low:mid] for c in range(3)] + [out[:, low:mid], out[:, :low]], axis=1
    )
    rows = one_ref.shape[1]
    columns = [one_ref[...], two_ref[...], router_ref[...]]
    columns = [value.astype(f32) for value in columns]
    filled = sum(value.shape[0] for value in columns)
    columns.append(jnp.zeros((extra_ref.shape[1] - filled, rows), f32))
    extra_ref[...] = jnp.concatenate(columns, 0).T.astype(bf16)


def fold_kernel(*refs, halves, starts):
    terms, (kept_ref, left_ref) = refs[:-2], refs[-2:]
    size, columns = terms[0].shape[0], kept_ref.shape[-1]
    for k in range(size):
        total = None
        for term, start in zip(terms, starts):
            value = term[k][..., start : start + columns].astype(f32)
            total = value if total is None else total + value
        at, odd = (k % (size // 2), k >= size // 2) if halves else (k // 2, k % 2 == 1)
        (left_ref if odd else kept_ref)[at] = total.astype(bf16)


def blend_kernel(me_ref, far_ref, kept_ref, other_ref, near_ref, own_ref, second_ref):
    for k, ref in ((0, near_ref), (1, own_ref)):
        ref[...] = (kept_ref[k].astype(f32) + other_ref[k].astype(f32)).astype(bf16)
    first_core = me_ref[1] == 0

    @pl.when(first_core)
    def _():
        second_ref[...] = far_ref[...]

    @pl.when(jnp.logical_not(first_core))
    def _():
        second_ref[...] = own_ref[...]


def blend_late_kernel(me_ref, far_ref, own_ref, early_ref, *thirds):
    columns = thirds[0].shape[-1]
    for core, ref in ((0, own_ref), (1, far_ref)):

        @pl.when(me_ref[1] == core)
        def _(ref=ref):
            for k, third in enumerate(thirds):
                at = slice(k * columns, (k + 1) * columns)
                total = ref[..., at].astype(f32) + early_ref[..., at].astype(f32)
                third[...] = total.astype(bf16)


def finish_kernel(me_ref, own_ref, other_ref, one_ref, two_ref, router_ref, root_ref):
    experts, rows = router_ref.shape
    total = own_ref[...] + other_ref[...]
    width = total.shape[1]
    mine = pltpu.roll(total, lax.rem(width - me_ref[0] * rows, width), 1)
    one_ref[...] = mine[experts : experts + 1, :rows]
    two_ref[...] = mine[experts + 1 : experts + 2, :rows]
    router_ref[...] = mine[:experts, :rows]
    images = root_ref.shape[1]
    mine = pltpu.roll(total, lax.rem(width - me_ref[0] * images, width), 1)
    root_ref[...] = mine[experts + 2 : experts + 5, :images]


def unpack_kernel(own_a, other_a, own_b, other_b, qkv_ref, out_ref):
    low, mid = 2 * HEAD_DIM, qkv_ref.shape[2]
    pair = own_a[...].astype(f32) + other_a[...].astype(f32)
    rest = own_b[...].astype(f32) + other_b[...].astype(f32)
    for c in range(3):
        qkv_ref[c, :, :low] = pair[:, c * low : (c + 1) * low]
        qkv_ref[c, :, low:mid] = rest[:, c * HEAD_DIM : (c + 1) * HEAD_DIM]
    out_ref[...] = jnp.concatenate([rest[:, 256:], rest[:, 192:256]], axis=1).T


def length_of(mask_ref, me_ref, b, images):
    row = mask_ref[pl.ds(me_ref[2] * images + b, 1), :]
    return jnp.sum(row.astype(f32), axis=1, keepdims=True)


def seen_row(length, tall):
    return lax.broadcasted_iota(jnp.int32, (1, tall), 1).astype(f32) < length


def seen_column(length, tall):
    return lax.broadcasted_iota(jnp.int32, (tall, 1), 0).astype(f32) < length


def prep_kernel(me_ref, x_ref, extra_ref, h_ref, ht_ref, small_ref, *, images, seq, tall):
    blocks = extra_ref.shape[0]
    me = me_ref[0]
    parts = [extra_ref[mirrored(me ^ d, blocks) if blocks > 1 else 0] for d in range(blocks)]
    small_ref[...] = jnp.concatenate(parts, 0).astype(f32).T
    gain = small_ref[0:1, :]
    for b in range(images):
        unit, _ = unit_of(x_ref[b].astype(f32))
        h_ref[pl.ds(b * tall, tall), :] = padded((unit * gain).astype(bf16), tall - seq)
    ht_ref[...] = h_ref[...].T


def fetch_all(me_ref, refs, put):
    rows, high_size = refs[0].shape[2], refs[0].shape[1]
    for core in (0, 1):

        @pl.when(me_ref[1] == core)
        def _(core=core):
            for slot in range(4):
                x, of_core = slot & 1, slot >> 1
                first, second = refs[:2] if of_core == core else refs[2:4]
                for r in range(2 * high_size):
                    low, high = r & 1, mirrored(r >> 1, high_size)
                    if of_core == 0:
                        block = (second if x else first)[low, high]
                    else:
                        block = (second if low else first)[x, high]
                    d = jnp.bitwise_xor(me_ref[0], r)
                    put(slot, pl.ds(pl.multiple_of(d * rows, 16), rows), block)


def attend(triples):
    scores = [mm_nt(q, k) * HEAD_DIM ** (-0.5) + bias for q, k, _, bias in triples]
    terms = [jnp.exp(value - jnp.max(value, axis=-1, keepdims=True)) for value in scores]
    probs = [
        (value * (1.0 / jnp.sum(value, axis=-1, keepdims=True))).astype(bf16) for value in terms
    ]
    return probs, [mm(value, v) for value, (_, _, v, _) in zip(probs, triples)]


def bias_of(mask_ref, me_ref, b, images, tall):
    return jnp.where(seen_row(length_of(mask_ref, me_ref, b, images), tall), 0.0, -1e30)


def front_pair_kernel(me_ref, h_ref, mask_ref, *refs, images, tall, ready):
    w_ref, qkv_ref, p_ref, ho_ref = refs[4:]

    def put(slot, at, block):
        w_ref[slot, at, :] = block

    if ready:
        for slot in range(4):
            put(slot, slice(None), refs[slot][...])
    else:
        fetch_all(me_ref, refs[:4], put)
    low = low_lanes(tall)

    def group(j, carry):
        qkv_ref[j] = mm(h_ref[...], w_ref[j]).astype(bf16)
        triples = []
        for b in range(images):
            joined = qkv_ref[j, pl.ds(b * tall, tall), :]
            q, k, v = joined[:, :128], joined[:, 128:256], joined[:, 256:384]
            none = jnp.zeros_like(q)
            bias = bias_of(mask_ref, me_ref, b, images, tall)
            triples.append((jnp.where(low, q, none), k, v, bias))
            triples.append((jnp.where(low, none, q), k, v, bias))
        probs, outs = attend(triples)
        for b in range(images):
            p_ref[j, b, 0], p_ref[j, b, 1] = probs[2 * b], probs[2 * b + 1]
            pair = jnp.where(low, outs[2 * b], outs[2 * b + 1])
            ho_ref[j, pl.ds(b * tall, tall), :] = pair.astype(bf16)
        return carry

    lax.fori_loop(0, w_ref.shape[0], group, 0)


def front_last_kernel(me_ref, h_ref, mask_ref, pair_ref, *refs, images, tall, ready):
    w_ref, qkv_ref, p_ref, ho_ref, wo_ref, br_ref = refs[4:]

    def put(slot, at, block):
        w_ref[slot, at, :] = block[:, :256]
        wo_ref[at, slot * 256 : (slot + 1) * 256] = block[:, 128:]

    if ready:
        for slot in range(4):
            put(slot, slice(None), refs[slot][...])
    else:
        fetch_all(me_ref, refs[:4], put)
    low = low_lanes(tall)

    def two(i, carry):
        places = [(2 * i + k, b) for k in (0, 1) for b in range(images)]
        for j in (2 * i, 2 * i + 1):
            qkv_ref[j] = mm(h_ref[...], w_ref[j]).astype(bf16)
        triples = []
        for j, b in places:
            joined = qkv_ref[j, pl.ds(b * tall, tall), :]
            qk, v = joined[:, :128], joined[:, 128:256]
            k = pltpu.roll(qk.astype(f32), HEAD_DIM, 1).astype(bf16)
            bias = bias_of(mask_ref, me_ref, b, images, tall)
            triples.append((jnp.where(low, qk, jnp.zeros_like(qk)), k, v, bias))
        probs, outs = attend(triples)
        for (j, b), prob, out in zip(places, probs, outs):
            at, start = pl.ds(b * tall, tall), pl.multiple_of(j * 256, 256)
            p_ref[j, b] = prob
            ho_ref[at, pl.ds(start, 128)] = jnp.where(low, 0.0, pltpu.roll(out, HEAD_DIM, 1)).astype(bf16)
            ho_ref[at, pl.ds(start + 128, 128)] = pair_ref[j, at, :]
        return carry

    lax.fori_loop(0, w_ref.shape[0] // 2, two, 0)
    br_ref[...] = mm_nt(ho_ref[...], wo_ref[...])


def spot(rows, b, start, experts):
    each = rows // experts
    at_row = lax.broadcasted_iota(jnp.int32, (rows, experts), 0)
    at_column = lax.broadcasted_iota(jnp.int32, (rows, experts), 1)
    return jnp.where(at_row == at_column * each + (start + b), 1.0, 0.0).astype(bf16)


def route_kernel(
    me_ref, x_ref, br_ref, cot_ref, mask_ref, ex_ref,
    res_ref, h_ref, soft_ref, sent_ref, sq_ref, *, images, seq, tall, experts
):
    rows = sent_ref.shape[0]
    half = rows // experts // 2
    router = ex_ref[2 : 2 + experts, :].astype(bf16)
    gain = ex_ref[1:2, :]
    total = jnp.zeros(sent_ref.shape, f32)
    for b in range(images):
        at = pl.ds(b * tall, tall)
        length = length_of(mask_ref, me_ref, b, images)
        branch = br_ref[at, :]
        resid = padded(x_ref[b].astype(f32), tall - seq) + branch
        res_ref[at, :] = resid
        unit, _ = unit_of(resid)
        h_two = (unit * gain).astype(bf16)
        h_ref[at, :] = h_two
        logits = mm_nt(router, h_two)
        held = jnp.where(seen_row(length, tall), logits, -1e30)
        terms = jnp.exp(held - jnp.max(held, axis=1, keepdims=True))
        dispatch = terms / jnp.sum(terms, axis=1, keepdims=True)
        terms = jnp.exp(logits - jnp.max(logits, axis=0, keepdims=True))
        combine = terms / jnp.sum(terms, axis=0, keepdims=True)
        soft_ref[0, b] = dispatch
        soft_ref[1, b] = combine
        cot = padded(cot_ref[b], tall - seq)
        wide_d = mm(spot(rows, b, 0, experts), dispatch.astype(bf16)).astype(bf16)
        wide_c = mm(spot(rows, b, half, experts), combine.astype(bf16)).astype(bf16)
        total += mm(wide_d, h_two) + mm(wide_c, cot)
        squares = jnp.sum(branch * branch, axis=1, keepdims=True)
        squares = jnp.sum(jnp.where(seen_column(length, tall), squares, 0.0), axis=0, keepdims=True)
        sq_ref[b] = jnp.broadcast_to(squares, (1, 128))
    sent_ref[...] = total.astype(bf16)


def expert_kernel(got_ref, first_ref, second_ref, hid_ref, pre_ref, grad_ref, back_ref, *, each):
    rows = got_ref.shape[0]
    half = each // 2
    got = got_ref[...]
    own = jnp.bitwise_and(lax.broadcasted_iota(jnp.int32, (rows, 1), 0), each - 1) < half
    grads = jnp.where(own, pltpu.roll(got.astype(f32), rows - half, 0), 0.0).astype(bf16)
    grad_ref[...] = grads
    u = mm(got, first_ref[...])
    cubic = 0.7978845608028654 * (u + 0.044715 * u * u * u)
    t = jnp.tanh(cubic)
    hidden = jnp.where(own, 0.5 * u * (1.0 + t), 0.0).astype(bf16)
    hid_ref[...] = hidden
    slope = 0.5 * (1.0 + t) + 0.5 * u * (1.0 - t * t) * 0.7978845608028654 * (
        1.0 + 3.0 * 0.044715 * u * u
    )
    grad_pre = (mm_nt(grads, second_ref[...]) * slope).astype(bf16)
    pre_ref[...] = grad_pre
    out = mm(hidden, second_ref[...])
    grad_in = mm_nt(grad_pre, first_ref[...])
    back_ref[...] = jnp.where(own, out, pltpu.roll(grad_in, half, 0)).astype(bf16)


def mix_kernel(
    me_ref, res_ref, h_ref, soft_ref, cot_ref, mask_ref, ex_ref, back_ref, sq_ref,
    out_ref, gres_ref, gb_ref, gbt_ref, small_ref, *, images, seq, tall, experts, groups
):
    small_ref[...] = jnp.zeros_like(small_ref)
    router = ex_ref[2 : 2 + experts, :].astype(bf16)
    gain = ex_ref[1:2, :]
    width = out_ref.shape[2]
    lanes = lax.broadcasted_iota(jnp.int32, (1, width), 1)
    roots = [jnp.zeros((1, width), f32) for _ in range(3)]
    for b in range(images):
        at = pl.ds(b * tall, tall)
        length = length_of(mask_ref, me_ref, b, images)
        resid, h_two = res_ref[at, :], h_ref[at, :]
        dispatch, combine = soft_ref[0, b], soft_ref[1, b]
        dispatch_low, combine_low = dispatch.astype(bf16), combine.astype(bf16)
        returned, grad_slots = back_ref[0, b], back_ref[1, b]
        cot = padded(cot_ref[b], tall - seq)
        mixed = mm_tn(combine_low, returned)
        stream = resid + mixed
        out_ref[b] = stream[:seq].astype(bf16)
        column = seen_column(length, tall)
        sums = []
        for value in (stream, mixed):
            squares = jnp.sum(value * value, axis=1, keepdims=True)
            sums.append(jnp.sum(jnp.where(column, squares, 0.0), axis=0, keepdims=True))
        sums.insert(1, sq_ref[b, :, 0:1])
        for k, value in enumerate(sums):
            root = jnp.sqrt(value / (length * width))
            mine = lanes == (me_ref[0] * groups + me_ref[2]) * images + b
            roots[k] += jnp.where(mine, root, 0.0)
        grad_c = mm_nt(returned, cot)
        grad_c = combine * (grad_c - jnp.sum(grad_c * combine, axis=0, keepdims=True))
        grad_d = mm_nt(grad_slots, h_two)
        grad_d = dispatch * (grad_d - jnp.sum(grad_d * dispatch, axis=1, keepdims=True))
        grad_logits = (grad_d + grad_c).astype(bf16)
        grad_h = mm_tn(dispatch_low, grad_slots) + mm_tn(grad_logits, router)
        small_ref[0:experts, :] += mm(grad_logits, h_two)
        unit, inverse = unit_of(resid)
        small_ref[experts + 1 : experts + 2, :] += jnp.sum(grad_h * unit, axis=0, keepdims=True)
        scaled = grad_h * gain
        mean_grad = jnp.mean(scaled, axis=-1, keepdims=True)
        mean_proj = jnp.mean(scaled * unit, axis=-1, keepdims=True)
        gres_ref[at, :] = cot.astype(f32) + inverse * (scaled - mean_grad - unit * mean_proj)
    for k in range(3):
        small_ref[experts + 2 + k : experts + 3 + k, :] = roots[k]
    gb_ref[...] = gres_ref[...].astype(bf16)
    gbt_ref[...] = gres_ref[...].T.astype(bf16)


def back_kernel(
    me_ref, gb_ref, gbt_ref, ht_ref, qkv_a, p_a, qkv_b, p_b, ho_ref, wo_ref,
    gw_ref, gj_ref, dho_ref, *, images, tall, x, flip
):
    j = x + 2 * jnp.bitwise_xor(me_ref[1], flip)
    own = pl.ds(pl.multiple_of(j * 256, 256), 256)
    scale = HEAD_DIM ** (-0.5)
    low = low_lanes(tall)
    dho_ref[...] = mm(gb_ref[...], wo_ref[:, own])
    heads, dots = [], []
    for b in range(images):
        at = pl.ds(b * tall, tall)
        joined, joined_last = qkv_a[j, at, :], qkv_b[j, at, :]
        q_pair, k_pair, v_pair = joined[:, :128], joined[:, 128:256], joined[:, 256:384]
        qk_last, v_last = joined_last[:, :128], joined_last[:, 128:256]
        grad = dho_ref[at, :].astype(bf16).astype(f32)
        product = grad * ho_ref[at, own].astype(f32)
        single, pair = product[:, :128], product[:, 128:]
        dots += [
            jnp.sum(jnp.where(low, pair, 0.0), axis=1, keepdims=True),
            jnp.sum(jnp.where(low, 0.0, pair), axis=1, keepdims=True),
            jnp.sum(single, axis=1, keepdims=True),
        ]
        grad_pair = grad[:, 128:]
        grad_last = jnp.where(low, pltpu.roll(grad[:, :128], HEAD_DIM, 1), 0.0).astype(bf16)
        heads += [
            (p_a[j, b, 0], jnp.where(low, grad_pair, 0.0).astype(bf16), v_pair, q_pair, k_pair),
            (p_a[j, b, 1], jnp.where(low, 0.0, grad_pair).astype(bf16), v_pair, q_pair, k_pair),
            (p_b[j, b], grad_last, v_last, qk_last, qk_last),
        ]
    grad_p = [mm_nt(g, v) for _, g, v, _, _ in heads]
    grad_s = [
        (probs.astype(f32) * (value - dot)).astype(bf16)
        for (probs, _, _, _, _), value, dot in zip(heads, grad_p, dots)
    ]
    gqs = [mm(value, k) for value, (_, _, _, _, k) in zip(grad_s, heads)]
    gks = [mm_tn(value, q) for value, (_, _, _, q, _) in zip(grad_s, heads)]
    gvs = [mm_tn(probs, g) for probs, g, _, _, _ in heads]
    for b in range(images):
        at = pl.ds(b * tall, tall)
        gq, gk, gv = (value[3 * b : 3 * b + 3] for value in (gqs, gks, gvs))
        last = pltpu.roll(jnp.where(low, gk[2], gq[2]), HEAD_DIM, 1)
        gj_ref[at, :] = jnp.concatenate(
            [
                jnp.where(low, gq[0], gq[1]) * scale,
                jnp.where(low, gk[0], gk[1]) * scale,
                gv[0] + gv[1],
                last * scale,
                gv[2],
            ],
            1,
        ).astype(bf16)
    grad_out = mm(gbt_ref[...], ho_ref[:, own])
    grad_in = mm(ht_ref[...], gj_ref[...])
    halves, blocks, rows = gw_ref.shape[:3]
    for d in range(halves * blocks):
        r = jnp.bitwise_xor(me_ref[0], d) if halves > 1 else 0
        entry = (jnp.bitwise_and(r, 1), jnp.right_shift(r, 1)) if halves > 1 else (0, 0)
        at = slice(d * rows, (d + 1) * rows)
        gw_ref[entry + (slice(None), slice(0, 512))] = grad_in[at, :512].astype(bf16)
        gw_ref[entry + (slice(None), slice(512, 640))] = (
            grad_in[at, 512:] + grad_out[at, :128]
        ).astype(bf16)
        gw_ref[entry + (slice(None), slice(640, 768))] = grad_out[at, 128:].astype(bf16)


def input_kernel(me_ref, w_a, w_b, *refs, order):
    grads, gh_ref = refs[:-1], refs[-1]
    for k, (ref, (x, flip)) in enumerate(zip(grads, order)):
        j = x + 2 * jnp.bitwise_xor(me_ref[1], flip)
        into = mm_nt(ref[:, :384], w_a[j]) + mm_nt(ref[:, 384:], w_b[j])
        if k == 0:
            gh_ref[...] = into
        else:
            gh_ref[...] += into


def last_kernel(x_ref, gres_ref, gh_ref, ex_ref, part_ref, gt_ref, small_ref, *, images, seq, tall, experts):
    total = jnp.zeros((1, x_ref.shape[2]), f32)
    gain = ex_ref[0:1, :]
    for b in range(images):
        at = pl.ds(b * tall, seq)
        unit, inverse = unit_of(x_ref[b].astype(f32))
        grad_h = gh_ref[at, :]
        total += jnp.sum(grad_h * unit, axis=0, keepdims=True)
        scaled = grad_h * gain
        mean_grad = jnp.mean(scaled, axis=-1, keepdims=True)
        mean_proj = jnp.mean(scaled * unit, axis=-1, keepdims=True)
        gt_ref[b] = gres_ref[at, :] + inverse * (scaled - mean_grad - unit * mean_proj)
    small_ref[...] = part_ref[...]
    small_ref[experts : experts + 1, :] = total


def cost(microseconds):
    return int(microseconds * 1.1e9)


def call(kernel, outs, args, scratch=(), flops=0, name=None, scalars=1, grant=16, **static):
    spec = pl.BlockSpec(memory_space=pltpu.VMEM)
    word = pl.BlockSpec(memory_space=pltpu.SMEM)
    moved = sum(math.prod(a.shape) * a.dtype.itemsize for a in args)
    return pl.pallas_call(
        functools.partial(kernel, **static),
        out_shape=[jax.ShapeDtypeStruct(s, d) for s, d in outs],
        in_specs=[word] * scalars + [spec] * (len(args) - scalars),
        out_specs=[spec] * len(outs),
        scratch_shapes=list(scratch),
        compiler_params=pltpu.CompilerParams(vmem_limit_bytes=grant << 20),
        cost_estimate=pl.CostEstimate(flops=flops, bytes_accessed=moved, transcendentals=0),
        name=name,
    )(*args)


def make(mesh):
    dp, mp = mesh.shape["dp"], mesh.shape["mp"]

    def per_device(
        tokens, token_mask, gain_one, w_qkv, w_out, gain_two, router, w_in, w_back, cotangent
    ):
        rows, width = tokens.shape
        seq = token_mask.shape[1]
        tall = -(-seq // 16) * 16
        images = rows // seq
        experts = router.shape[1]
        d_rows, _, part = w_qkv.shape
        count = images * tall
        high = dp // 2
        heads = part // HEAD_DIM
        ready = d_rows % 16 != 0
        each = 2 * (1 << (images - 1).bit_length())
        me = lax.axis_index("dp")
        at_mp = lax.axis_index("mp")
        core = at_mp & 1
        words = jnp.stack([me, core, at_mp]).astype(jnp.int32)
        static = {"images": images, "tall": tall}
        exact = {"images": images, "seq": seq, "tall": tall}

        columns = experts + 2
        half = 2 * part
        hbm = pl.BlockSpec(memory_space=pltpu.HBM)
        vmem = pl.BlockSpec(memory_space=pltpu.VMEM)
        word = pl.BlockSpec(memory_space=pltpu.SMEM)
        wide = columns + -columns % 128
        shapes = [(3, d_rows, part), (part, d_rows), (1, d_rows), (1, d_rows), (experts, d_rows)]
        first, second, extra = pl.pallas_call(
            pack_kernel,
            out_shape=[jax.ShapeDtypeStruct((d_rows, n), bf16) for n in (half, half, wide)],
            in_specs=[word] + [hbm] * 5,
            out_specs=[vmem] * 3,
            scratch_shapes=[pltpu.VMEM(shape, bf16) for shape in shapes] + [pltpu.SemaphoreType.DMA((5,))],
            compiler_params=pltpu.CompilerParams(vmem_limit_bytes=67_000_000),
            name="pack",
        )(words, w_qkv.transpose(1, 0, 2), w_out, gain_one[None], gain_two[None], router.T)

        first, second, held_extra = first[None], second[None], extra[None]
        for bit in bits_of(dp)[:-1]:
            first = jnp.concatenate([first, swap(first, "dp", dp, bit)])
            held_extra = jnp.concatenate([held_extra, swap(held_extra, "dp", dp, bit)])
        stages = bits_of(dp)[:-1]
        second = jnp.concatenate([second, swap(second, "dp", dp, stages[0])])
        other, held_extra, second = lax.optimization_barrier(
            (swap_both(first, dp, mp, (1, 0), (0, 2)), held_extra, second)
        )
        for bit in stages[1:]:
            second = jnp.concatenate([second, swap(second, "dp", dp, bit)])
        held_extra = jnp.concatenate([held_extra, swap(held_extra, "dp", dp, 1)])
        held_extra = held_extra.reshape((dp,) + extra.shape)
        if ready:
            held_extra = reorder(unmirrored(held_extra), me).reshape(1, width, -1)
        x3 = tokens.reshape(images, seq, width)
        cot3 = cotangent.reshape(images, seq, width)
        h_one, h_turned, ex = call(
            prep_kernel,
            [((count, width), bf16), ((width, count), bf16), ((held_extra.shape[2], width), f32)],
            (words, x3, held_extra),
            flops=cost(2),
            name="prep",
            grant=4,
            **exact,
        )
        near = jnp.stack([first, other])
        far = swap_both(near, dp, mp, (0, 2), (1, 0))
        second = second.reshape((high, d_rows, half))
        other = swap_both(second, dp, mp, (1, 0), (0, 2))
        far, h_one, other = lax.optimization_barrier((far, h_one, other))
        first = (near, far, swap(near, "mp", mp, 1), swap(far, "mp", mp, 1))
        near = jnp.stack([second, other])
        second_near, second_far = near, swap_both(near, dp, mp, (0, 2), (1, 0))
        second_near_other = swap(second_near, "mp", mp, 1)

        def whole(x, of_core, near, far, other_near, other_far):
            mine = core == of_core
            low = jnp.where(mine, near, other_near)
            high_part = jnp.where(mine, far, other_far)
            blocks = jnp.stack([low[x], high_part[x]]) if of_core else (high_part if x else low)
            blocks = blocks.reshape((dp, d_rows, half))
            blocks = unmirrored(blocks)
            return reorder(blocks, me).reshape(width, half)

        def weights_of(parts):
            if ready:
                return tuple(whole(j & 1, j >> 1, *parts) for j in range(4))
            return parts

        def saved(kept, columns, probs):
            return [
                ((mp, width, kept), bf16),
                ((mp, count, columns), bf16),
                ((mp, images) + probs + (tall, tall), bf16),
                ((mp, count, 128), bf16),
            ]

        pair = call(
            front_pair_kernel,
            saved(half, 384, (2,)),
            (words, h_one, token_mask) + weights_of(first),
            flops=cost(10),
            name="front_pair",
            grant=10,
            ready=ready,
            **static,
        )
        w_a, qkv_a, p_a, ho_a = pair
        second_far, ho_a = lax.optimization_barrier((second_far, ho_a))
        second = (second_near, second_far, second_near_other, swap(second_far, "mp", mp, 1))
        w_b, qkv_b, p_b, heads_out, w_heads, branch = call(
            front_last_kernel,
            saved(256, 256, ())[:3]
            + [
                ((count, 256 * mp), bf16),
                ((width, 256 * mp), bf16),
                ((count, width), f32),
            ],
            (words, h_one, token_mask, ho_a) + weights_of(second),
            flops=cost(7),
            name="front_last",
            grant=10,
            ready=ready,
            **static,
        )
        resid, h_two, soft, sent, sq_branch = call(
            route_kernel,
            [
                ((count, width), f32),
                ((count, width), bf16),
                ((2, images, experts, tall), f32),
                ((experts * each, width), bf16),
                ((images, 1, 128), f32),
            ],
            (words, x3, branch, cot3, token_mask, ex),
            flops=cost(2),
            name="route",
            grant=6,
            experts=experts,
            **exact,
        )
        got = sent.reshape(dp, each, width)
        got = lax.all_to_all(got, "dp", split_axis=0, concat_axis=0, tiled=True)
        got = gather_mp(got, mp).reshape(-1, width)
        everyone = got.shape[0]
        hidden, grad_pre, grad_expert, back = call(
            expert_kernel,
            [
                ((everyone, w_in.shape[2]), bf16),
                ((everyone, w_in.shape[2]), bf16),
                ((everyone, width), bf16),
                ((everyone, width), bf16),
            ],
            (got, w_in[0], w_back[0]),
            flops=cost(2),
            name="expert",
            scalars=0,
            grant=12 if dp <= 8 else 56,
            each=each,
        )
        back = back.reshape(mp, dp, each, width)
        back = scatter(back, "mp", mp, [1, 2])
        back = lax.all_to_all(back, "dp", split_axis=0, concat_axis=0, tiled=True)
        back = back.reshape(dp, 2, each // 2, width)[:, :, :images].transpose(1, 2, 0, 3)
        grad_w_back = mm_tn(hidden, grad_expert)
        grad_w_in = mm_tn(got, grad_pre)

        out_rows, grad_resid, grad_low, grad_turned, small = call(
            mix_kernel,
            [
                ((images, seq, width), bf16),
                ((count, width), f32),
                ((count, width), bf16),
                ((width, count), bf16),
                ((experts + 5, width), f32),
            ],
            (words, resid, h_two, soft, cot3, token_mask, ex, back, sq_branch),
            flops=cost(5),
            name="mix",
            grant=8,
            experts=experts,
            groups=mp,
            **exact,
        )
        shape = (1, 1, width, 4 * part) if ready else (2, high, d_rows, 4 * part)

        def back_of(x, flip, grad_in):
            grads, joined = call(
                back_kernel,
                [(shape, bf16), ((count, JOINED), bf16)],
                (words, grad_in, grad_turned, h_turned, qkv_a, p_a, qkv_b, p_b, heads_out, w_heads),
                [pltpu.VMEM((count, 256), f32)],
                flops=cost(8),
                name="back",
                grant=10,
                x=x,
                flip=flip,
                **static,
            )
            if ready:
                grads = reorder(grads.reshape(dp, d_rows, 4 * part), me)
                grads = grads.reshape(high, 2, d_rows, 4 * part).transpose(1, 0, 2, 3)
            return grads, joined

        def fold(terms, halves, starts=None, kept_columns=4 * part):
            size = terms[0].shape
            kept = ((size[0] // 2,) + size[1:-1] + (kept_columns,), bf16)
            return call(
                fold_kernel,
                [kept, kept],
                terms,
                flops=cost(1),
                name="fold",
                scalars=0,
                grant=6,
                halves=halves,
                starts=starts or (0,) * len(terms),
            )

        order = ((1, 1), (1, 0), (0, 1), (0, 0))
        sent_grads, joined_a = back_of(1, 1, grad_low)
        other = swap(sent_grads, "mp", mp, 1)
        grad_low, joined_a = lax.optimization_barrier((grad_low, joined_a))
        kept_grads, joined_b = back_of(1, 0, grad_low)
        far_kept, far_left = fold((kept_grads, other), True)
        far_left, grad_low, joined_b = lax.optimization_barrier((far_left, grad_low, joined_b))
        early = swap_both(far_left[0], dp, mp, (0, 2), (1, 0))
        sent_grads, joined_c = back_of(0, 1, grad_low)
        grad_low, joined_c = lax.optimization_barrier((grad_low, joined_c))
        other = swap(sent_grads, "mp", mp, 1)
        kept_grads, joined_d = back_of(0, 0, grad_low)
        part_shape = ((high, d_rows, 4 * part), bf16)
        near_sum, own_sum, second = call(
            blend_kernel,
            [part_shape] * 3,
            (words, far_kept[0], kept_grads, other),
            flops=cost(1),
            name="blend",
            grant=8,
        )
        second = swap_both(second, dp, mp, (0, 2), (1, 0))
        grad_h = call(
            input_kernel,
            [((count, width), f32)],
            (words, w_a, w_b, joined_a, joined_b, joined_c, joined_d),
            flops=cost(4),
            name="input",
            grant=8,
            order=order,
        )[0]
        early, grad_h = lax.optimization_barrier((early, grad_h))
        thirds = call(
            blend_late_kernel,
            [((high, d_rows, half), bf16)] * 2,
            (words, far_kept[0], own_sum, early),
            flops=cost(1),
            name="blend_late",
            grant=8,
        )
        thirds = [swap_both(third, dp, mp, (1, 0), (0, 2)) for third in thirds]
        pieces = [
            list(fold((near_sum, second, third), False, (k * half, k * half, 0), half))
            for k, third in enumerate(thirds)
        ]
        grad_tokens, small = call(
            last_kernel,
            [((images, seq, width), f32), ((experts + 5, width), f32)],
            (x3, grad_resid, grad_h, ex, small),
            flops=cost(0.1),
            name="last",
            scalars=0,
            grant=8,
            experts=experts,
            **exact,
        )
        for bit in bits_of(dp)[:-1]:
            small = small + swap(small, "dp", dp, bit)
        parts = []
        for k, (kept, left) in enumerate(pieces):
            for bit in bits_of(high)[:0:-1]:
                other = swap(left, "dp", dp, 2 * bit)
                if k == 0:
                    other, small = lax.optimization_barrier((other, small))
                kept, left = fold((kept, other), False, None, half)
            parts += [kept[0], swap(left[0], "dp", dp, 2 * bits_of(high)[0])]
        grad_qkv, grad_out = call(
            unpack_kernel,
            [((3, d_rows, part), f32), ((part, d_rows), f32)],
            parts,
            flops=cost(1),
            name="unpack",
            scalars=0,
            grant=6,
        )
        small = small + swap(small, "dp", dp, 1)
        small = small + swap(small, "mp", mp, 2)
        grad_one, grad_two, grad_router, root_squares = call(
            finish_kernel,
            [
                ((1, d_rows), f32),
                ((1, d_rows), f32),
                ((experts, d_rows), f32),
                ((3, mp * images), f32),
            ],
            (words, small, swap(small, "mp", mp, 1)),
            flops=cost(1),
            name="finish",
            grant=4,
        )
        return (
            out_rows.reshape(rows, width),
            grad_tokens.reshape(rows, width),
            grad_one[0],
            grad_qkv.transpose(1, 0, 2),
            grad_out,
            grad_two[0],
            grad_router.T,
            grad_w_in[None],
            grad_w_back[None],
            root_squares,
        )

    return per_device


def solution(mesh):
    in_specs = (
        P(("dp", "mp"), None),
        P("dp", None),
        P("dp"),
        P("dp", None, "mp"),
        P("mp", "dp"),
        P("dp"),
        P("dp", None),
        P("dp", None, "mp"),
        P("dp", "mp", None),
        P(("dp", "mp"), None),
    )
    out_specs = (
        P(("dp", "mp"), None),
        P(("dp", "mp"), None),
        P("dp"),
        P("dp", None, "mp"),
        P("mp", "dp"),
        P("dp"),
        P("dp", None),
        P("dp", None, "mp"),
        P("dp", "mp", None),
        P(None, "dp"),
    )
    return jax.shard_map(
        make(mesh), mesh=mesh, in_specs=in_specs, out_specs=out_specs, check_vma=False
    )
```

```python
import functools
import math

import jax
import jax.numpy as jnp
from jax import lax
from jax.experimental import pallas as pl
from jax.experimental.pallas import tpu as pltpu
from jax.sharding import PartitionSpec as P

HEAD_DIM = 64


epsilon = 1e-06
bf16 = jnp.bfloat16
f32 = jnp.float32


def bits_of(size):
    return [1 << k for k in reversed(range(size.bit_length() - 1))]


def swap(array_in, axis_name, size, bit):
    return lax.ppermute(array_in, axis_name, [(i, i ^ bit) for i in range(size)])


def swap_both(array_in, dp, mp, even, odd):
    pairs = []
    for d in range(dp):
        for m in range(mp):
            flip = odd if m & 1 else even
            pairs.append((d * mp + m, (d ^ flip[0]) * mp + (m ^ flip[1])))
    return lax.ppermute(array_in, ("dp", "mp"), pairs)


def gather_mp(block, mp):
    held = block[None]
    for bit in bits_of(mp):
        other = swap(held, "mp", mp, bit)
        held = jnp.stack([held, other], 1).reshape((-1,) + block.shape)
    return held


def scatter(held, axis_name, size, bits, unit=1):
    left = sorted(bits)
    for bit in bits:
        inner = 1 << left.index(bit)
        left.remove(bit)
        pairs = held.reshape((held.shape[0] // (2 * inner), 2, inner) + held.shape[1:])
        other = swap(pairs[:, 1], axis_name, size, bit * unit)
        held = pairs[:, 0].astype(f32) + other.astype(f32)
        held = held.astype(bf16).reshape((-1,) + held.shape[2:])
    return held[0]


def mirrored(index, size):
    bits = size.bit_length() - 1
    return sum(((index >> k) & 1) << (bits - 1 - k) for k in range(bits)) if bits else index


def unmirrored(blocks):
    size = blocks.shape[0]
    bits = size.bit_length() - 1
    split = blocks.reshape((2,) * bits + blocks.shape[1:])
    turn = tuple(range(bits))[::-1] + tuple(range(bits, split.ndim))
    return split.transpose(turn).reshape(blocks.shape)


def reorder(blocks, me):
    size = blocks.shape[0]
    for bit in bits_of(size):
        pairs = blocks.reshape((size // (2 * bit), 2, bit) + blocks.shape[1:])
        blocks = jnp.where((me & bit) > 0, pairs[:, ::-1], pairs).reshape(blocks.shape)
    return blocks


def mm(a, b):
    return lax.dot_general(a, b, (((1,), (0,)), ((), ())), preferred_element_type=f32)


def mm_nt(a, b):
    return lax.dot_general(a, b, (((1,), (1,)), ((), ())), preferred_element_type=f32)


def mm_tn(a, b):
    return lax.dot_general(a, b, (((0,), (0,)), ((), ())), preferred_element_type=f32)


def unit_of(rows_f):
    mean_row = jnp.mean(rows_f, axis=-1, keepdims=True)
    centered = rows_f - mean_row
    variance = jnp.mean(centered * centered, axis=-1, keepdims=True)
    inverse = lax.rsqrt(variance + epsilon)
    return centered * inverse, inverse


def padded(value, pad):
    return jnp.concatenate([value, jnp.zeros((pad, value.shape[1]), value.dtype)], 0)


def low_lanes(rows):
    return lax.broadcasted_iota(jnp.int32, (rows, 128), 1) < HEAD_DIM


JOINED = 640


def pack_kernel(
    me_ref, qkv_hbm, out_hbm, one_hbm, two_hbm, router_hbm, first_ref, second_ref, extra_ref,
    qkv_ref, out_ref, one_ref, two_ref, router_ref, sems
):
    del me_ref
    pairs = (
        (qkv_hbm, qkv_ref), (out_hbm, out_ref), (one_hbm, one_ref), (two_hbm, two_ref), (router_hbm, router_ref),
    )
    copies = [pltpu.make_async_copy(a, b, sems.at[k]) for k, (a, b) in enumerate(pairs)]
    for copy in copies:
        copy.start()
    for copy in copies:
        copy.wait()
    low, mid = 2 * HEAD_DIM, qkv_ref.shape[2]
    out = out_ref[...].astype(f32).T.astype(bf16)
    first_ref[...] = jnp.concatenate([qkv_ref[c, :, :low] for c in range(3)], axis=1)
    second_ref[...] = jnp.concatenate(
        [qkv_ref[c, :, low:mid] for c in range(3)] + [out[:, low:mid], out[:, :low]], axis=1
    )
    rows = one_ref.shape[1]
    columns = [one_ref[...], two_ref[...], router_ref[...]]
    columns = [value.astype(f32) for value in columns]
    filled = sum(value.shape[0] for value in columns)
    columns.append(jnp.zeros((extra_ref.shape[1] - filled, rows), f32))
    extra_ref[...] = jnp.concatenate(columns, 0).T.astype(bf16)


def join_kernel(a_ref, b_ref, out_ref):
    size = a_ref.shape[0]
    out_ref[:size] = a_ref[...]
    out_ref[size:] = b_ref[...]


def join(a, b):
    shape = (a.shape[0] + b.shape[0],) + a.shape[1:]
    return call(join_kernel, [(shape, a.dtype)], (a, b), flops=1000, name="join", scalars=0, grant=4)[0]


def fold_kernel(*refs, halves, starts):
    terms, (kept_ref, left_ref) = refs[:-2], refs[-2:]
    size, columns = terms[0].shape[0], kept_ref.shape[-1]
    for k in range(size):
        total = None
        for term, start in zip(terms, starts):
            value = term[k][..., start : start + columns].astype(f32)
            total = value if total is None else total + value
        at, odd = (k % (size // 2), k >= size // 2) if halves else (k // 2, k % 2 == 1)
        (left_ref if odd else kept_ref)[at] = total.astype(bf16)


def blend_kernel(me_ref, far_ref, kept_ref, other_ref, near_ref, own_ref, second_ref):
    for k, ref in ((0, near_ref), (1, own_ref)):
        ref[...] = (kept_ref[k].astype(f32) + other_ref[k].astype(f32)).astype(bf16)
    first_core = me_ref[1] == 0

    @pl.when(first_core)
    def _():
        second_ref[...] = far_ref[...]

    @pl.when(jnp.logical_not(first_core))
    def _():
        second_ref[...] = own_ref[...]


def blend_late_kernel(me_ref, far_ref, own_ref, early_ref, *thirds):
    columns = thirds[0].shape[-1]
    for core, ref in ((0, own_ref), (1, far_ref)):

        @pl.when(me_ref[1] == core)
        def _(ref=ref):
            for k, third in enumerate(thirds):
                at = slice(k * columns, (k + 1) * columns)
                total = ref[..., at].astype(f32) + early_ref[..., at].astype(f32)
                third[...] = total.astype(bf16)


def finish_kernel(me_ref, own_ref, other_ref, one_ref, two_ref, router_ref, root_ref):
    experts, rows = router_ref.shape
    total = own_ref[...] + other_ref[...]
    width = total.shape[1]
    mine = pltpu.roll(total, lax.rem(width - me_ref[0] * rows, width), 1)
    one_ref[...] = mine[experts : experts + 1, :rows]
    two_ref[...] = mine[experts + 1 : experts + 2, :rows]
    router_ref[...] = mine[:experts, :rows]
    images = root_ref.shape[1]
    mine = pltpu.roll(total, lax.rem(width - me_ref[0] * images, width), 1)
    root_ref[...] = mine[experts + 2 : experts + 5, :images]


def unpack_kernel(own_a, other_a, own_b, other_b, qkv_ref, out_ref):
    low, mid = 2 * HEAD_DIM, qkv_ref.shape[2]
    pair = own_a[...].astype(f32) + other_a[...].astype(f32)
    rest = own_b[...].astype(f32) + other_b[...].astype(f32)
    for c in range(3):
        qkv_ref[c, :, :low] = pair[:, c * low : (c + 1) * low]
        qkv_ref[c, :, low:mid] = rest[:, c * HEAD_DIM : (c + 1) * HEAD_DIM]
    out_ref[...] = jnp.concatenate([rest[:, 256:], rest[:, 192:256]], axis=1).T


def length_of(mask_ref, me_ref, b, images):
    row = mask_ref[pl.ds(me_ref[2] * images + b, 1), :]
    return jnp.sum(row.astype(f32), axis=1, keepdims=True)


def seen_row(length, tall):
    return lax.broadcasted_iota(jnp.int32, (1, tall), 1).astype(f32) < length


def seen_column(length, tall):
    return lax.broadcasted_iota(jnp.int32, (tall, 1), 0).astype(f32) < length


def prep_kernel(me_ref, x_ref, extra_ref, h_ref, ht_ref, small_ref, *, images, seq, tall):
    blocks = extra_ref.shape[0]
    me = me_ref[0]
    parts = [extra_ref[mirrored(me ^ d, blocks) if blocks > 1 else 0] for d in range(blocks)]
    small_ref[...] = jnp.concatenate(parts, 0).astype(f32).T
    gain = small_ref[0:1, :]
    for b in range(images):
        unit, _ = unit_of(x_ref[b].astype(f32))
        h_ref[pl.ds(b * tall, tall), :] = padded((unit * gain).astype(bf16), tall - seq)
    ht_ref[...] = h_ref[...].T


def fetch_all(me_ref, refs, put):
    rows, high_size = refs[0].shape[2], refs[0].shape[1]
    for core in (0, 1):

        @pl.when(me_ref[1] == core)
        def _(core=core):
            for slot in range(4):
                x, of_core = slot & 1, slot >> 1
                first, second = refs[:2] if of_core == core else refs[2:4]
                for r in range(2 * high_size):
                    low, high = r & 1, mirrored(r >> 1, high_size)
                    if of_core == 0:
                        block = (second if x else first)[low, high]
                    else:
                        block = (second if low else first)[x, high]
                    d = jnp.bitwise_xor(me_ref[0], r)
                    put(slot, pl.ds(pl.multiple_of(d * rows, 16), rows), block)


def attend(triples):
    scores = [mm_nt(q, k) * HEAD_DIM ** (-0.5) + bias for q, k, _, bias in triples]
    terms = [jnp.exp(value - jnp.max(value, axis=-1, keepdims=True)) for value in scores]
    probs = [
        (value * (1.0 / jnp.sum(value, axis=-1, keepdims=True))).astype(bf16) for value in terms
    ]
    return probs, [mm(value, v) for value, (_, _, v, _) in zip(probs, triples)]


def bias_of(mask_ref, me_ref, b, images, tall):
    return jnp.where(seen_row(length_of(mask_ref, me_ref, b, images), tall), 0.0, -1e30)


def front_pair_kernel(me_ref, h_ref, mask_ref, *refs, images, tall, ready):
    w_ref, qkv_ref, p_ref, ho_ref = refs[4:]

    def put(slot, at, block):
        w_ref[slot, at, :] = block

    if ready:
        for slot in range(4):
            put(slot, slice(None), refs[slot][...])
    else:
        fetch_all(me_ref, refs[:4], put)
    low = low_lanes(tall)

    def group(j, carry):
        qkv_ref[j] = mm(h_ref[...], w_ref[j]).astype(bf16)
        triples = []
        for b in range(images):
            joined = qkv_ref[j, pl.ds(b * tall, tall), :]
            q, k, v = joined[:, :128], joined[:, 128:256], joined[:, 256:384]
            none = jnp.zeros_like(q)
            bias = bias_of(mask_ref, me_ref, b, images, tall)
            triples.append((jnp.where(low, q, none), k, v, bias))
            triples.append((jnp.where(low, none, q), k, v, bias))
        probs, outs = attend(triples)
        for b in range(images):
            p_ref[j, b, 0], p_ref[j, b, 1] = probs[2 * b], probs[2 * b + 1]
            pair = jnp.where(low, outs[2 * b], outs[2 * b + 1])
            ho_ref[j, pl.ds(b * tall, tall), :] = pair.astype(bf16)
        return carry

    lax.fori_loop(0, w_ref.shape[0], group, 0)


def front_last_kernel(me_ref, h_ref, mask_ref, pair_ref, *refs, images, tall, ready):
    w_ref, qkv_ref, p_ref, ho_ref, wo_ref, br_ref = refs[4:]

    def put(slot, at, block):
        w_ref[slot, at, :] = block[:, :256]
        wo_ref[at, slot * 256 : (slot + 1) * 256] = block[:, 128:]

    if ready:
        for slot in range(4):
            put(slot, slice(None), refs[slot][...])
    else:
        fetch_all(me_ref, refs[:4], put)
    low = low_lanes(tall)

    def two(i, carry):
        places = [(2 * i + k, b) for k in (0, 1) for b in range(images)]
        for j in (2 * i, 2 * i + 1):
            qkv_ref[j] = mm(h_ref[...], w_ref[j]).astype(bf16)
        triples = []
        for j, b in places:
            joined = qkv_ref[j, pl.ds(b * tall, tall), :]
            qk, v = joined[:, :128], joined[:, 128:256]
            k = pltpu.roll(qk.astype(f32), HEAD_DIM, 1).astype(bf16)
            bias = bias_of(mask_ref, me_ref, b, images, tall)
            triples.append((jnp.where(low, qk, jnp.zeros_like(qk)), k, v, bias))
        probs, outs = attend(triples)
        for (j, b), prob, out in zip(places, probs, outs):
            at, start = pl.ds(b * tall, tall), pl.multiple_of(j * 256, 256)
            p_ref[j, b] = prob
            ho_ref[at, pl.ds(start, 128)] = jnp.where(low, 0.0, pltpu.roll(out, HEAD_DIM, 1)).astype(bf16)
            ho_ref[at, pl.ds(start + 128, 128)] = pair_ref[j, at, :]
        return carry

    lax.fori_loop(0, w_ref.shape[0] // 2, two, 0)
    br_ref[...] = mm_nt(ho_ref[...], wo_ref[...])


def spot(rows, b, start, experts):
    each = rows // experts
    at_row = lax.broadcasted_iota(jnp.int32, (rows, experts), 0)
    at_column = lax.broadcasted_iota(jnp.int32, (rows, experts), 1)
    return jnp.where(at_row == at_column * each + (start + b), 1.0, 0.0).astype(bf16)


def route_kernel(
    me_ref, x_ref, br_ref, cot_ref, mask_ref, ex_ref,
    res_ref, h_ref, soft_ref, sent_ref, sq_ref, *, images, seq, tall, experts
):
    rows = sent_ref.shape[0]
    half = rows // experts // 2
    router = ex_ref[2 : 2 + experts, :].astype(bf16)
    gain = ex_ref[1:2, :]
    total = jnp.zeros(sent_ref.shape, f32)
    for b in range(images):
        at = pl.ds(b * tall, tall)
        length = length_of(mask_ref, me_ref, b, images)
        branch = br_ref[at, :]
        resid = padded(x_ref[b].astype(f32), tall - seq) + branch
        res_ref[at, :] = resid
        unit, _ = unit_of(resid)
        h_two = (unit * gain).astype(bf16)
        h_ref[at, :] = h_two
        logits = mm_nt(router, h_two)
        held = jnp.where(seen_row(length, tall), logits, -1e30)
        terms = jnp.exp(held - jnp.max(held, axis=1, keepdims=True))
        dispatch = terms / jnp.sum(terms, axis=1, keepdims=True)
        terms = jnp.exp(logits - jnp.max(logits, axis=0, keepdims=True))
        combine = terms / jnp.sum(terms, axis=0, keepdims=True)
        soft_ref[0, b] = dispatch
        soft_ref[1, b] = combine
        cot = padded(cot_ref[b], tall - seq)
        wide_d = mm(spot(rows, b, 0, experts), dispatch.astype(bf16)).astype(bf16)
        wide_c = mm(spot(rows, b, half, experts), combine.astype(bf16)).astype(bf16)
        total += mm(wide_d, h_two) + mm(wide_c, cot)
        squares = jnp.sum(branch * branch, axis=1, keepdims=True)
        squares = jnp.sum(jnp.where(seen_column(length, tall), squares, 0.0), axis=0, keepdims=True)
        sq_ref[b] = jnp.broadcast_to(squares, (1, 128))
    sent_ref[...] = total.astype(bf16)


def expert_kernel(got_ref, first_ref, second_ref, hid_ref, pre_ref, grad_ref, back_ref, *, each):
    rows = got_ref.shape[0]
    half = each // 2
    got = got_ref[...]
    own = jnp.bitwise_and(lax.broadcasted_iota(jnp.int32, (rows, 1), 0), each - 1) < half
    grads = jnp.where(own, pltpu.roll(got.astype(f32), rows - half, 0), 0.0).astype(bf16)
    grad_ref[...] = grads
    u = mm(got, first_ref[...])
    cubic = 0.7978845608028654 * (u + 0.044715 * u * u * u)
    t = jnp.tanh(cubic)
    hidden = jnp.where(own, 0.5 * u * (1.0 + t), 0.0).astype(bf16)
    hid_ref[...] = hidden
    slope = 0.5 * (1.0 + t) + 0.5 * u * (1.0 - t * t) * 0.7978845608028654 * (
        1.0 + 3.0 * 0.044715 * u * u
    )
    grad_pre = (mm_nt(grads, second_ref[...]) * slope).astype(bf16)
    pre_ref[...] = grad_pre
    out = mm(hidden, second_ref[...])
    grad_in = mm_nt(grad_pre, first_ref[...])
    back_ref[...] = jnp.where(own, out, pltpu.roll(grad_in, half, 0)).astype(bf16)


def mix_kernel(
    me_ref, res_ref, h_ref, soft_ref, cot_ref, mask_ref, ex_ref, back_ref, sq_ref,
    out_ref, gres_ref, gb_ref, gbt_ref, small_ref, *, images, seq, tall, experts, groups
):
    small_ref[...] = jnp.zeros_like(small_ref)
    router = ex_ref[2 : 2 + experts, :].astype(bf16)
    gain = ex_ref[1:2, :]
    width = out_ref.shape[2]
    lanes = lax.broadcasted_iota(jnp.int32, (1, width), 1)
    roots = [jnp.zeros((1, width), f32) for _ in range(3)]
    for b in range(images):
        at = pl.ds(b * tall, tall)
        length = length_of(mask_ref, me_ref, b, images)
        resid, h_two = res_ref[at, :], h_ref[at, :]
        dispatch, combine = soft_ref[0, b], soft_ref[1, b]
        dispatch_low, combine_low = dispatch.astype(bf16), combine.astype(bf16)
        returned, grad_slots = back_ref[0, b], back_ref[1, b]
        cot = padded(cot_ref[b], tall - seq)
        mixed = mm_tn(combine_low, returned)
        stream = resid + mixed
        out_ref[b] = stream[:seq].astype(bf16)
        column = seen_column(length, tall)
        sums = []
        for value in (stream, mixed):
            squares = jnp.sum(value * value, axis=1, keepdims=True)
            sums.append(jnp.sum(jnp.where(column, squares, 0.0), axis=0, keepdims=True))
        sums.insert(1, sq_ref[b, :, 0:1])
        for k, value in enumerate(sums):
            root = jnp.sqrt(value / (length * width))
            mine = lanes == (me_ref[0] * groups + me_ref[2]) * images + b
            roots[k] += jnp.where(mine, root, 0.0)
        grad_c = mm_nt(returned, cot)
        grad_c = combine * (grad_c - jnp.sum(grad_c * combine, axis=0, keepdims=True))
        grad_d = mm_nt(grad_slots, h_two)
        grad_d = dispatch * (grad_d - jnp.sum(grad_d * dispatch, axis=1, keepdims=True))
        grad_logits = (grad_d + grad_c).astype(bf16)
        grad_h = mm_tn(dispatch_low, grad_slots) + mm_tn(grad_logits, router)
        small_ref[0:experts, :] += mm(grad_logits, h_two)
        unit, inverse = unit_of(resid)
        small_ref[experts + 1 : experts + 2, :] += jnp.sum(grad_h * unit, axis=0, keepdims=True)
        scaled = grad_h * gain
        mean_grad = jnp.mean(scaled, axis=-1, keepdims=True)
        mean_proj = jnp.mean(scaled * unit, axis=-1, keepdims=True)
        gres_ref[at, :] = cot.astype(f32) + inverse * (scaled - mean_grad - unit * mean_proj)
    for k in range(3):
        small_ref[experts + 2 + k : experts + 3 + k, :] = roots[k]
    gb_ref[...] = gres_ref[...].astype(bf16)
    gbt_ref[...] = gres_ref[...].T.astype(bf16)


def back_kernel(
    me_ref, gb_ref, gbt_ref, ht_ref, qkv_a, p_a, qkv_b, p_b, ho_ref, wo_ref,
    gw_ref, gj_ref, dho_ref, *, images, tall, x, flip
):
    j = x + 2 * jnp.bitwise_xor(me_ref[1], flip)
    own = pl.ds(pl.multiple_of(j * 256, 256), 256)
    scale = HEAD_DIM ** (-0.5)
    low = low_lanes(tall)
    dho_ref[...] = mm(gb_ref[...], wo_ref[:, own])
    heads, dots = [], []
    for b in range(images):
        at = pl.ds(b * tall, tall)
        joined, joined_last = qkv_a[j, at, :], qkv_b[j, at, :]
        q_pair, k_pair, v_pair = joined[:, :128], joined[:, 128:256], joined[:, 256:384]
        qk_last, v_last = joined_last[:, :128], joined_last[:, 128:256]
        grad = dho_ref[at, :].astype(bf16).astype(f32)
        product = grad * ho_ref[at, own].astype(f32)
        single, pair = product[:, :128], product[:, 128:]
        dots += [
            jnp.sum(jnp.where(low, pair, 0.0), axis=1, keepdims=True),
            jnp.sum(jnp.where(low, 0.0, pair), axis=1, keepdims=True),
            jnp.sum(single, axis=1, keepdims=True),
        ]
        grad_pair = grad[:, 128:]
        grad_last = jnp.where(low, pltpu.roll(grad[:, :128], HEAD_DIM, 1), 0.0).astype(bf16)
        heads += [
            (p_a[j, b, 0], jnp.where(low, grad_pair, 0.0).astype(bf16), v_pair, q_pair, k_pair),
            (p_a[j, b, 1], jnp.where(low, 0.0, grad_pair).astype(bf16), v_pair, q_pair, k_pair),
            (p_b[j, b], grad_last, v_last, qk_last, qk_last),
        ]
    grad_p = [mm_nt(g, v) for _, g, v, _, _ in heads]
    grad_s = [
        (probs.astype(f32) * (value - dot)).astype(bf16)
        for (probs, _, _, _, _), value, dot in zip(heads, grad_p, dots)
    ]
    gqs = [mm(value, k) for value, (_, _, _, _, k) in zip(grad_s, heads)]
    gks = [mm_tn(value, q) for value, (_, _, _, q, _) in zip(grad_s, heads)]
    gvs = [mm_tn(probs, g) for probs, g, _, _, _ in heads]
    for b in range(images):
        at = pl.ds(b * tall, tall)
        gq, gk, gv = (value[3 * b : 3 * b + 3] for value in (gqs, gks, gvs))
        last = pltpu.roll(jnp.where(low, gk[2], gq[2]), HEAD_DIM, 1)
        gj_ref[at, :] = jnp.concatenate(
            [
                jnp.where(low, gq[0], gq[1]) * scale,
                jnp.where(low, gk[0], gk[1]) * scale,
                gv[0] + gv[1],
                last * scale,
                gv[2],
            ],
            1,
        ).astype(bf16)
    grad_out = mm(gbt_ref[...], ho_ref[:, own])
    grad_in = mm(ht_ref[...], gj_ref[...])
    halves, blocks, rows = gw_ref.shape[:3]
    for d in range(halves * blocks):
        r = jnp.bitwise_xor(me_ref[0], d) if halves > 1 else 0
        entry = (jnp.bitwise_and(r, 1), jnp.right_shift(r, 1)) if halves > 1 else (0, 0)
        at = slice(d * rows, (d + 1) * rows)
        gw_ref[entry + (slice(None), slice(0, 512))] = grad_in[at, :512].astype(bf16)
        gw_ref[entry + (slice(None), slice(512, 640))] = (
            grad_in[at, 512:] + grad_out[at, :128]
        ).astype(bf16)
        gw_ref[entry + (slice(None), slice(640, 768))] = grad_out[at, 128:].astype(bf16)


def input_kernel(me_ref, w_a, w_b, *refs, order):
    grads, gh_ref = refs[:-1], refs[-1]
    for k, (ref, (x, flip)) in enumerate(zip(grads, order)):
        j = x + 2 * jnp.bitwise_xor(me_ref[1], flip)
        into = mm_nt(ref[:, :384], w_a[j]) + mm_nt(ref[:, 384:], w_b[j])
        if k == 0:
            gh_ref[...] = into
        else:
            gh_ref[...] += into


def last_kernel(x_ref, gres_ref, gh_ref, ex_ref, part_ref, gt_ref, small_ref, *, images, seq, tall, experts):
    total = jnp.zeros((1, x_ref.shape[2]), f32)
    gain = ex_ref[0:1, :]
    for b in range(images):
        at = pl.ds(b * tall, seq)
        unit, inverse = unit_of(x_ref[b].astype(f32))
        grad_h = gh_ref[at, :]
        total += jnp.sum(grad_h * unit, axis=0, keepdims=True)
        scaled = grad_h * gain
        mean_grad = jnp.mean(scaled, axis=-1, keepdims=True)
        mean_proj = jnp.mean(scaled * unit, axis=-1, keepdims=True)
        gt_ref[b] = gres_ref[at, :] + inverse * (scaled - mean_grad - unit * mean_proj)
    small_ref[...] = part_ref[...]
    small_ref[experts : experts + 1, :] = total


def cost(microseconds):
    return int(microseconds * 1.1e9)


def call(kernel, outs, args, scratch=(), flops=0, name=None, scalars=1, grant=16, **static):
    spec = pl.BlockSpec(memory_space=pltpu.VMEM)
    word = pl.BlockSpec(memory_space=pltpu.SMEM)
    moved = sum(math.prod(a.shape) * a.dtype.itemsize for a in args)
    return pl.pallas_call(
        functools.partial(kernel, **static),
        out_shape=[jax.ShapeDtypeStruct(s, d) for s, d in outs],
        in_specs=[word] * scalars + [spec] * (len(args) - scalars),
        out_specs=[spec] * len(outs),
        scratch_shapes=list(scratch),
        compiler_params=pltpu.CompilerParams(vmem_limit_bytes=grant << 20),
        cost_estimate=pl.CostEstimate(flops=flops, bytes_accessed=moved, transcendentals=0),
        name=name,
    )(*args)


def make(mesh):
    dp, mp = mesh.shape["dp"], mesh.shape["mp"]

    def per_device(
        tokens, token_mask, gain_one, w_qkv, w_out, gain_two, router, w_in, w_back, cotangent
    ):
        rows, width = tokens.shape
        seq = token_mask.shape[1]
        tall = -(-seq // 16) * 16
        images = rows // seq
        experts = router.shape[1]
        d_rows, _, part = w_qkv.shape
        count = images * tall
        high = dp // 2
        heads = part // HEAD_DIM
        ready = d_rows % 16 != 0
        each = 2 * (1 << (images - 1).bit_length())
        me = lax.axis_index("dp")
        at_mp = lax.axis_index("mp")
        core = at_mp & 1
        words = jnp.stack([me, core, at_mp]).astype(jnp.int32)
        static = {"images": images, "tall": tall}
        exact = {"images": images, "seq": seq, "tall": tall}

        columns = experts + 2
        half = 2 * part
        hbm = pl.BlockSpec(memory_space=pltpu.HBM)
        vmem = pl.BlockSpec(memory_space=pltpu.VMEM)
        word = pl.BlockSpec(memory_space=pltpu.SMEM)
        wide = columns + -columns % 128
        shapes = [(3, d_rows, part), (part, d_rows), (1, d_rows), (1, d_rows), (experts, d_rows)]
        first, second, extra = pl.pallas_call(
            pack_kernel,
            out_shape=[jax.ShapeDtypeStruct((d_rows, n), bf16) for n in (half, half, wide)],
            in_specs=[word] + [hbm] * 5,
            out_specs=[vmem] * 3,
            scratch_shapes=[pltpu.VMEM(shape, bf16) for shape in shapes] + [pltpu.SemaphoreType.DMA((5,))],
            compiler_params=pltpu.CompilerParams(vmem_limit_bytes=67_000_000),
            name="pack",
        )(words, w_qkv.transpose(1, 0, 2), w_out, gain_one[None], gain_two[None], router.T)

        first, second, held_extra = first[None], second[None], extra[None]
        stages = bits_of(dp)[:-1]
        for bit in stages:
            others = swap(first, "dp", dp, bit), swap(second, "dp", dp, bit)
            if bit != stages[-1]:
                others = lax.optimization_barrier(others)
            put = jnp.concatenate if bit == stages[0] else lambda pair: join(*pair)
            first = put([first, others[0]])
            held_extra = put([held_extra, swap(held_extra, "dp", dp, bit)])
            if bit != stages[-1]:
                second = put([second, others[1]])
        other, held_extra, late = lax.optimization_barrier(
            (swap_both(first, dp, mp, (1, 0), (0, 2)), held_extra, others[1])
        )
        second = join(second, late)
        held_extra = join(held_extra, swap(held_extra, "dp", dp, 1))
        held_extra = held_extra.reshape((dp,) + extra.shape)
        if ready:
            held_extra = reorder(unmirrored(held_extra), me).reshape(1, width, -1)
        x3 = tokens.reshape(images, seq, width)
        cot3 = cotangent.reshape(images, seq, width)
        h_one, h_turned, ex = call(
            prep_kernel,
            [((count, width), bf16), ((width, count), bf16), ((held_extra.shape[2], width), f32)],
            (words, x3, held_extra),
            flops=cost(2),
            name="prep",
            grant=4,
            **exact,
        )
        near = join(first, other).reshape((2, high, d_rows, half))
        far = swap_both(near, dp, mp, (0, 2), (1, 0))
        second = second.reshape((high, d_rows, half))
        other = swap_both(second, dp, mp, (1, 0), (0, 2))
        far, h_one, other = lax.optimization_barrier((far, h_one, other))
        first = (near, far, swap(near, "mp", mp, 1), swap(far, "mp", mp, 1))
        near = join(second, other).reshape((2, high, d_rows, half))
        second_near, second_far = near, swap_both(near, dp, mp, (0, 2), (1, 0))
        second_near_other = swap(second_near, "mp", mp, 1)

        def whole(x, of_core, near, far, other_near, other_far):
            mine = core == of_core
            low = jnp.where(mine, near, other_near)
            high_part = jnp.where(mine, far, other_far)
            blocks = jnp.stack([low[x], high_part[x]]) if of_core else (high_part if x else low)
            blocks = blocks.reshape((dp, d_rows, half))
            blocks = unmirrored(blocks)
            return reorder(blocks, me).reshape(width, half)

        def weights_of(parts):
            if ready:
                return tuple(whole(j & 1, j >> 1, *parts) for j in range(4))
            return parts

        def saved(kept, columns, probs):
            return [
                ((mp, width, kept), bf16),
                ((mp, count, columns), bf16),
                ((mp, images) + probs + (tall, tall), bf16),
                ((mp, count, 128), bf16),
            ]

        pair = call(
            front_pair_kernel,
            saved(half, 384, (2,)),
            (words, h_one, token_mask) + weights_of(first),
            flops=cost(10),
            name="front_pair",
            grant=10,
            ready=ready,
            **static,
        )
        w_a, qkv_a, p_a, ho_a = pair
        second_far, ho_a = lax.optimization_barrier((second_far, ho_a))
        second = (second_near, second_far, second_near_other, swap(second_far, "mp", mp, 1))
        w_b, qkv_b, p_b, heads_out, w_heads, branch = call(
            front_last_kernel,
            saved(256, 256, ())[:3]
            + [
                ((count, 256 * mp), bf16),
                ((width, 256 * mp), bf16),
                ((count, width), f32),
            ],
            (words, h_one, token_mask, ho_a) + weights_of(second),
            flops=cost(7),
            name="front_last",
            grant=10,
            ready=ready,
            **static,
        )
        resid, h_two, soft, sent, sq_branch = call(
            route_kernel,
            [
                ((count, width), f32),
                ((count, width), bf16),
                ((2, images, experts, tall), f32),
                ((experts * each, width), bf16),
                ((images, 1, 128), f32),
            ],
            (words, x3, branch, cot3, token_mask, ex),
            flops=cost(2),
            name="route",
            grant=6,
            experts=experts,
            **exact,
        )
        got = sent.reshape(dp, each, width)
        got = lax.all_to_all(got, "dp", split_axis=0, concat_axis=0, tiled=True)
        got = gather_mp(got, mp).reshape(-1, width)
        everyone = got.shape[0]
        hidden, grad_pre, grad_expert, back = call(
            expert_kernel,
            [
                ((everyone, w_in.shape[2]), bf16),
                ((everyone, w_in.shape[2]), bf16),
                ((everyone, width), bf16),
                ((everyone, width), bf16),
            ],
            (got, w_in[0], w_back[0]),
            flops=cost(2),
            name="expert",
            scalars=0,
            grant=12 if dp <= 8 else 56,
            each=each,
        )
        back = back.reshape(mp, dp, each, width)
        back = scatter(back, "mp", mp, [1, 2])
        back = lax.all_to_all(back, "dp", split_axis=0, concat_axis=0, tiled=True)
        back = back.reshape(dp, 2, each // 2, width)[:, :, :images].transpose(1, 2, 0, 3)
        grad_w_back = mm_tn(hidden, grad_expert)
        grad_w_in = mm_tn(got, grad_pre)

        out_rows, grad_resid, grad_low, grad_turned, small = call(
            mix_kernel,
            [
                ((images, seq, width), bf16),
                ((count, width), f32),
                ((count, width), bf16),
                ((width, count), bf16),
                ((experts + 5, width), f32),
            ],
            (words, resid, h_two, soft, cot3, token_mask, ex, back, sq_branch),
            flops=cost(5),
            name="mix",
            grant=8,
            experts=experts,
            groups=mp,
            **exact,
        )
        shape = (1, 1, width, 4 * part) if ready else (2, high, d_rows, 4 * part)

        def back_of(x, flip, grad_in):
            grads, joined = call(
                back_kernel,
                [(shape, bf16), ((count, JOINED), bf16)],
                (words, grad_in, grad_turned, h_turned, qkv_a, p_a, qkv_b, p_b, heads_out, w_heads),
                [pltpu.VMEM((count, 256), f32)],
                flops=cost(8),
                name="back",
                grant=10,
                x=x,
                flip=flip,
                **static,
            )
            if ready:
                grads = reorder(grads.reshape(dp, d_rows, 4 * part), me)
                grads = grads.reshape(high, 2, d_rows, 4 * part).transpose(1, 0, 2, 3)
            return grads, joined

        def fold(terms, halves, starts=None, kept_columns=4 * part):
            size = terms[0].shape
            kept = ((size[0] // 2,) + size[1:-1] + (kept_columns,), bf16)
            return call(
                fold_kernel,
                [kept, kept],
                terms,
                flops=cost(1),
                name="fold",
                scalars=0,
                grant=6,
                halves=halves,
                starts=starts or (0,) * len(terms),
            )

        order = ((1, 1), (1, 0), (0, 1), (0, 0))
        sent_grads, joined_a = back_of(1, 1, grad_low)
        other = swap(sent_grads, "mp", mp, 1)
        grad_low, joined_a = lax.optimization_barrier((grad_low, joined_a))
        kept_grads, joined_b = back_of(1, 0, grad_low)
        far_kept, far_left = fold((kept_grads, other), True)
        far_left, grad_low, joined_b = lax.optimization_barrier((far_left, grad_low, joined_b))
        early = swap_both(far_left[0], dp, mp, (0, 2), (1, 0))
        sent_grads, joined_c = back_of(0, 1, grad_low)
        grad_low, joined_c = lax.optimization_barrier((grad_low, joined_c))
        other = swap(sent_grads, "mp", mp, 1)
        kept_grads, joined_d = back_of(0, 0, grad_low)
        part_shape = ((high, d_rows, 4 * part), bf16)
        near_sum, own_sum, second = call(
            blend_kernel,
            [part_shape] * 3,
            (words, far_kept[0], kept_grads, other),
            flops=cost(1),
            name="blend",
            grant=8,
        )
        second = swap_both(second, dp, mp, (0, 2), (1, 0))
        grad_h = call(
            input_kernel,
            [((count, width), f32)],
            (words, w_a, w_b, joined_a, joined_b, joined_c, joined_d),
            flops=cost(4),
            name="input",
            grant=8,
            order=order,
        )[0]
        early, grad_h = lax.optimization_barrier((early, grad_h))
        thirds = call(
            blend_late_kernel,
            [((high, d_rows, half), bf16)] * 2,
            (words, far_kept[0], own_sum, early),
            flops=cost(1),
            name="blend_late",
            grant=8,
        )
        thirds = [swap_both(third, dp, mp, (1, 0), (0, 2)) for third in thirds]
        pieces = [
            list(fold((near_sum, second, third), False, (k * half, k * half, 0), half))
            for k, third in enumerate(thirds)
        ]
        grad_tokens, small = call(
            last_kernel,
            [((images, seq, width), f32), ((experts + 5, width), f32)],
            (x3, grad_resid, grad_h, ex, small),
            flops=cost(0.1),
            name="last",
            scalars=0,
            grant=8,
            experts=experts,
            **exact,
        )
        for bit in bits_of(dp)[:-1]:
            small = small + swap(small, "dp", dp, bit)
        parts = []
        for k, (kept, left) in enumerate(pieces):
            for bit in bits_of(high)[:0:-1]:
                other = swap(left, "dp", dp, 2 * bit)
                if k == 0:
                    other, small = lax.optimization_barrier((other, small))
                kept, left = fold((kept, other), False, None, half)
            parts += [kept[0], swap(left[0], "dp", dp, 2 * bits_of(high)[0])]
        grad_qkv, grad_out = call(
            unpack_kernel,
            [((3, d_rows, part), f32), ((part, d_rows), f32)],
            parts,
            flops=cost(1),
            name="unpack",
            scalars=0,
            grant=6,
        )
        small = small + swap(small, "dp", dp, 1)
        small = small + swap(small, "mp", mp, 2)
        grad_one, grad_two, grad_router, root_squares = call(
            finish_kernel,
            [
                ((1, d_rows), f32),
                ((1, d_rows), f32),
                ((experts, d_rows), f32),
                ((3, mp * images), f32),
            ],
            (words, small, swap(small, "mp", mp, 1)),
            flops=cost(1),
            name="finish",
            grant=4,
        )
        return (
            out_rows.reshape(rows, width),
            grad_tokens.reshape(rows, width),
            grad_one[0],
            grad_qkv.transpose(1, 0, 2),
            grad_out,
            grad_two[0],
            grad_router.T,
            grad_w_in[None],
            grad_w_back[None],
            root_squares,
        )

    return per_device


def solution(mesh):
    in_specs = (
        P(("dp", "mp"), None),
        P("dp", None),
        P("dp"),
        P("dp", None, "mp"),
        P("mp", "dp"),
        P("dp"),
        P("dp", None),
        P("dp", None, "mp"),
        P("dp", "mp", None),
        P(("dp", "mp"), None),
    )
    out_specs = (
        P(("dp", "mp"), None),
        P(("dp", "mp"), None),
        P("dp"),
        P("dp", None, "mp"),
        P("mp", "dp"),
        P("dp"),
        P("dp", None),
        P("dp", None, "mp"),
        P("dp", "mp", None),
        P(None, "dp"),
    )
    return jax.shard_map(
        make(mesh), mesh=mesh, in_specs=in_specs, out_specs=out_specs, check_vma=False
    )
```

```python
import functools
import math

import jax
import jax.numpy as jnp
from jax import lax
from jax.experimental import pallas as pl
from jax.experimental.pallas import tpu as pltpu
from jax.sharding import PartitionSpec as P

HEAD_DIM = 64


epsilon = 1e-06
bf16 = jnp.bfloat16
f32 = jnp.float32


def bits_of(size):
    return [1 << k for k in reversed(range(size.bit_length() - 1))]


def swap(array_in, axis_name, size, bit):
    return lax.ppermute(array_in, axis_name, [(i, i ^ bit) for i in range(size)])


def swap_both(array_in, dp, mp, even, odd):
    pairs = []
    for d in range(dp):
        for m in range(mp):
            flip = odd if m & 1 else even
            pairs.append((d * mp + m, (d ^ flip[0]) * mp + (m ^ flip[1])))
    return lax.ppermute(array_in, ("dp", "mp"), pairs)


def gather_mp(block, mp):
    held = block[None]
    for bit in bits_of(mp):
        other = swap(held, "mp", mp, bit)
        held = jnp.stack([held, other], 1).reshape((-1,) + block.shape)
    return held


def scatter(held, axis_name, size, bits, unit=1):
    left = sorted(bits)
    for bit in bits:
        inner = 1 << left.index(bit)
        left.remove(bit)
        pairs = held.reshape((held.shape[0] // (2 * inner), 2, inner) + held.shape[1:])
        other = swap(pairs[:, 1], axis_name, size, bit * unit)
        held = pairs[:, 0].astype(f32) + other.astype(f32)
        held = held.astype(bf16).reshape((-1,) + held.shape[2:])
    return held[0]


def mirrored(index, size):
    bits = size.bit_length() - 1
    return sum(((index >> k) & 1) << (bits - 1 - k) for k in range(bits)) if bits else index


def unmirrored(blocks):
    size = blocks.shape[0]
    bits = size.bit_length() - 1
    split = blocks.reshape((2,) * bits + blocks.shape[1:])
    turn = tuple(range(bits))[::-1] + tuple(range(bits, split.ndim))
    return split.transpose(turn).reshape(blocks.shape)


def reorder(blocks, me):
    size = blocks.shape[0]
    for bit in bits_of(size):
        pairs = blocks.reshape((size // (2 * bit), 2, bit) + blocks.shape[1:])
        blocks = jnp.where((me & bit) > 0, pairs[:, ::-1], pairs).reshape(blocks.shape)
    return blocks


def mm(a, b):
    return lax.dot_general(a, b, (((1,), (0,)), ((), ())), preferred_element_type=f32)


def mm_nt(a, b):
    return lax.dot_general(a, b, (((1,), (1,)), ((), ())), preferred_element_type=f32)


def mm_tn(a, b):
    return lax.dot_general(a, b, (((0,), (0,)), ((), ())), preferred_element_type=f32)


def unit_of(rows_f):
    mean_row = jnp.mean(rows_f, axis=-1, keepdims=True)
    centered = rows_f - mean_row
    variance = jnp.mean(centered * centered, axis=-1, keepdims=True)
    inverse = lax.rsqrt(variance + epsilon)
    return centered * inverse, inverse


def padded(value, pad):
    return jnp.concatenate([value, jnp.zeros((pad, value.shape[1]), value.dtype)], 0)


def low_lanes(rows):
    return lax.broadcasted_iota(jnp.int32, (rows, 128), 1) < HEAD_DIM


JOINED = 640


def pack_kernel(
    me_ref, qkv_hbm, out_hbm, one_hbm, two_hbm, router_hbm, first_ref, second_ref, extra_ref,
    qkv_ref, out_ref, one_ref, two_ref, router_ref, sems
):
    del me_ref
    pairs = (
        (qkv_hbm, qkv_ref), (out_hbm, out_ref), (one_hbm, one_ref), (two_hbm, two_ref), (router_hbm, router_ref),
    )
    copies = [pltpu.make_async_copy(a, b, sems.at[k]) for k, (a, b) in enumerate(pairs)]
    for copy in copies:
        copy.start()
    low, mid = 2 * HEAD_DIM, qkv_ref.shape[2]
    copies[0].wait()
    first_ref[...] = jnp.concatenate([qkv_ref[c, :, :low] for c in range(3)], axis=1)
    for copy in copies[1:]:
        copy.wait()
    out = out_ref[...].astype(f32).T.astype(bf16)
    second_ref[...] = jnp.concatenate(
        [qkv_ref[c, :, low:mid] for c in range(3)] + [out[:, low:mid], out[:, :low]], axis=1
    )
    rows = one_ref.shape[1]
    columns = [one_ref[...], two_ref[...], router_ref[...]]
    columns = [value.astype(f32) for value in columns]
    filled = sum(value.shape[0] for value in columns)
    columns.append(jnp.zeros((extra_ref.shape[1] - filled, rows), f32))
    extra_ref[...] = jnp.concatenate(columns, 0).T.astype(bf16)


def join_kernel(a_ref, b_ref, out_ref):
    size = a_ref.shape[0]
    out_ref[:size] = a_ref[...]
    out_ref[size:] = b_ref[...]


def join(a, b):
    shape = (a.shape[0] + b.shape[0],) + a.shape[1:]
    return call(join_kernel, [(shape, a.dtype)], (a, b), flops=1000, name="join", scalars=0, grant=4)[0]


def fold_kernel(*refs, halves, starts):
    terms, (kept_ref, left_ref) = refs[:-2], refs[-2:]
    size, columns = terms[0].shape[0], kept_ref.shape[-1]
    for k in range(size):
        total = None
        for term, start in zip(terms, starts):
            value = term[k][..., start : start + columns].astype(f32)
            total = value if total is None else total + value
        at, odd = (k % (size // 2), k >= size // 2) if halves else (k // 2, k % 2 == 1)
        (left_ref if odd else kept_ref)[at] = total.astype(bf16)


def blend_kernel(me_ref, far_ref, kept_ref, other_ref, near_ref, own_ref, second_ref):
    for k, ref in ((0, near_ref), (1, own_ref)):
        ref[...] = (kept_ref[k].astype(f32) + other_ref[k].astype(f32)).astype(bf16)
    first_core = me_ref[1] == 0

    @pl.when(first_core)
    def _():
        second_ref[...] = far_ref[...]

    @pl.when(jnp.logical_not(first_core))
    def _():
        second_ref[...] = own_ref[...]


def blend_late_kernel(me_ref, far_ref, own_ref, early_ref, *thirds):
    columns = thirds[0].shape[-1]
    for core, ref in ((0, own_ref), (1, far_ref)):

        @pl.when(me_ref[1] == core)
        def _(ref=ref):
            for k, third in enumerate(thirds):
                at = slice(k * columns, (k + 1) * columns)
                total = ref[..., at].astype(f32) + early_ref[..., at].astype(f32)
                third[...] = total.astype(bf16)


def finish_kernel(me_ref, own_ref, other_ref, one_ref, two_ref, router_ref, root_ref):
    experts, rows = router_ref.shape
    total = own_ref[...] + other_ref[...]
    width = total.shape[1]
    mine = pltpu.roll(total, lax.rem(width - me_ref[0] * rows, width), 1)
    one_ref[...] = mine[experts : experts + 1, :rows]
    two_ref[...] = mine[experts + 1 : experts + 2, :rows]
    router_ref[...] = mine[:experts, :rows]
    images = root_ref.shape[1]
    mine = pltpu.roll(total, lax.rem(width - me_ref[0] * images, width), 1)
    root_ref[...] = mine[experts + 2 : experts + 5, :images]


def unpack_kernel(own_a, other_a, own_b, other_b, qkv_ref, out_ref):
    low, mid = 2 * HEAD_DIM, qkv_ref.shape[2]
    pair = own_a[...].astype(f32) + other_a[...].astype(f32)
    rest = own_b[...].astype(f32) + other_b[...].astype(f32)
    for c in range(3):
        qkv_ref[c, :, :low] = pair[:, c * low : (c + 1) * low]
        qkv_ref[c, :, low:mid] = rest[:, c * HEAD_DIM : (c + 1) * HEAD_DIM]
    out_ref[...] = jnp.concatenate([rest[:, 256:], rest[:, 192:256]], axis=1).T


def length_of(mask_ref, me_ref, b, images):
    row = mask_ref[pl.ds(me_ref[2] * images + b, 1), :]
    return jnp.sum(row.astype(f32), axis=1, keepdims=True)


def seen_row(length, tall):
    return lax.broadcasted_iota(jnp.int32, (1, tall), 1).astype(f32) < length


def seen_column(length, tall):
    return lax.broadcasted_iota(jnp.int32, (tall, 1), 0).astype(f32) < length


def prep_kernel(me_ref, x_ref, extra_ref, h_ref, ht_ref, small_ref, *, images, seq, tall):
    blocks = extra_ref.shape[0]
    me = me_ref[0]
    parts = [extra_ref[mirrored(me ^ d, blocks) if blocks > 1 else 0] for d in range(blocks)]
    small_ref[...] = jnp.concatenate(parts, 0).astype(f32).T
    gain = small_ref[0:1, :]
    for b in range(images):
        unit, _ = unit_of(x_ref[b].astype(f32))
        h_ref[pl.ds(b * tall, tall), :] = padded((unit * gain).astype(bf16), tall - seq)
    ht_ref[...] = h_ref[...].T


def fetch_all(me_ref, refs, put):
    rows, high_size = refs[0].shape[2], refs[0].shape[1]
    for core in (0, 1):

        @pl.when(me_ref[1] == core)
        def _(core=core):
            for slot in range(4):
                x, of_core = slot & 1, slot >> 1
                first, second = refs[:2] if of_core == core else refs[2:4]
                for r in range(2 * high_size):
                    low, high = r & 1, mirrored(r >> 1, high_size)
                    if of_core == 0:
                        block = (second if x else first)[low, high]
                    else:
                        block = (second if low else first)[x, high]
                    d = jnp.bitwise_xor(me_ref[0], r)
                    put(slot, pl.ds(pl.multiple_of(d * rows, 16), rows), block)


def attend(triples):
    scores = [mm_nt(q, k) * HEAD_DIM ** (-0.5) + bias for q, k, _, bias in triples]
    terms = [jnp.exp(value - jnp.max(value, axis=-1, keepdims=True)) for value in scores]
    probs = [
        (value * (1.0 / jnp.sum(value, axis=-1, keepdims=True))).astype(bf16) for value in terms
    ]
    return probs, [mm(value, v) for value, (_, _, v, _) in zip(probs, triples)]


def bias_of(mask_ref, me_ref, b, images, tall):
    return jnp.where(seen_row(length_of(mask_ref, me_ref, b, images), tall), 0.0, -1e30)


def front_pair_kernel(me_ref, h_ref, mask_ref, *refs, images, tall, ready):
    w_ref, qkv_ref, p_ref, ho_ref = refs[4:]

    def put(slot, at, block):
        w_ref[slot, at, :] = block

    if ready:
        for slot in range(4):
            put(slot, slice(None), refs[slot][...])
    else:
        fetch_all(me_ref, refs[:4], put)
    low = low_lanes(tall)

    def group(j, carry):
        qkv_ref[j] = mm(h_ref[...], w_ref[j]).astype(bf16)
        triples = []
        for b in range(images):
            joined = qkv_ref[j, pl.ds(b * tall, tall), :]
            q, k, v = joined[:, :128], joined[:, 128:256], joined[:, 256:384]
            none = jnp.zeros_like(q)
            bias = bias_of(mask_ref, me_ref, b, images, tall)
            triples.append((jnp.where(low, q, none), k, v, bias))
            triples.append((jnp.where(low, none, q), k, v, bias))
        probs, outs = attend(triples)
        for b in range(images):
            p_ref[j, b, 0], p_ref[j, b, 1] = probs[2 * b], probs[2 * b + 1]
            pair = jnp.where(low, outs[2 * b], outs[2 * b + 1])
            ho_ref[j, pl.ds(b * tall, tall), :] = pair.astype(bf16)
        return carry

    lax.fori_loop(0, w_ref.shape[0], group, 0)


def front_last_kernel(me_ref, h_ref, mask_ref, pair_ref, *refs, images, tall, ready):
    w_ref, qkv_ref, p_ref, ho_ref, wo_ref, br_ref = refs[4:]

    def put(slot, at, block):
        w_ref[slot, at, :] = block[:, :256]
        wo_ref[at, slot * 256 : (slot + 1) * 256] = block[:, 128:]

    if ready:
        for slot in range(4):
            put(slot, slice(None), refs[slot][...])
    else:
        fetch_all(me_ref, refs[:4], put)
    low = low_lanes(tall)

    def two(i, carry):
        places = [(2 * i + k, b) for k in (0, 1) for b in range(images)]
        for j in (2 * i, 2 * i + 1):
            qkv_ref[j] = mm(h_ref[...], w_ref[j]).astype(bf16)
        triples = []
        for j, b in places:
            joined = qkv_ref[j, pl.ds(b * tall, tall), :]
            qk, v = joined[:, :128], joined[:, 128:256]
            k = pltpu.roll(qk.astype(f32), HEAD_DIM, 1).astype(bf16)
            bias = bias_of(mask_ref, me_ref, b, images, tall)
            triples.append((jnp.where(low, qk, jnp.zeros_like(qk)), k, v, bias))
        probs, outs = attend(triples)
        for (j, b), prob, out in zip(places, probs, outs):
            at, start = pl.ds(b * tall, tall), pl.multiple_of(j * 256, 256)
            p_ref[j, b] = prob
            ho_ref[at, pl.ds(start, 128)] = jnp.where(low, 0.0, pltpu.roll(out, HEAD_DIM, 1)).astype(bf16)
            ho_ref[at, pl.ds(start + 128, 128)] = pair_ref[j, at, :]
        return carry

    lax.fori_loop(0, w_ref.shape[0] // 2, two, 0)
    br_ref[...] = mm_nt(ho_ref[...], wo_ref[...])


def spot(rows, b, start, experts):
    each = rows // experts
    at_row = lax.broadcasted_iota(jnp.int32, (rows, experts), 0)
    at_column = lax.broadcasted_iota(jnp.int32, (rows, experts), 1)
    return jnp.where(at_row == at_column * each + (start + b), 1.0, 0.0).astype(bf16)


def route_kernel(
    me_ref, x_ref, br_ref, cot_ref, mask_ref, ex_ref,
    res_ref, h_ref, soft_ref, sent_ref, sq_ref, *, images, seq, tall, experts
):
    rows = sent_ref.shape[0]
    half = rows // experts // 2
    router = ex_ref[2 : 2 + experts, :].astype(bf16)
    gain = ex_ref[1:2, :]
    total = jnp.zeros(sent_ref.shape, f32)
    for b in range(images):
        at = pl.ds(b * tall, tall)
        length = length_of(mask_ref, me_ref, b, images)
        branch = br_ref[at, :]
        resid = padded(x_ref[b].astype(f32), tall - seq) + branch
        res_ref[at, :] = resid
        unit, _ = unit_of(resid)
        h_two = (unit * gain).astype(bf16)
        h_ref[at, :] = h_two
        logits = mm_nt(router, h_two)
        held = jnp.where(seen_row(length, tall), logits, -1e30)
        terms = jnp.exp(held - jnp.max(held, axis=1, keepdims=True))
        dispatch = terms / jnp.sum(terms, axis=1, keepdims=True)
        terms = jnp.exp(logits - jnp.max(logits, axis=0, keepdims=True))
        combine = terms / jnp.sum(terms, axis=0, keepdims=True)
        soft_ref[0, b] = dispatch
        soft_ref[1, b] = combine
        cot = padded(cot_ref[b], tall - seq)
        wide_d = mm(spot(rows, b, 0, experts), dispatch.astype(bf16)).astype(bf16)
        wide_c = mm(spot(rows, b, half, experts), combine.astype(bf16)).astype(bf16)
        total += mm(wide_d, h_two) + mm(wide_c, cot)
        squares = jnp.sum(branch * branch, axis=1, keepdims=True)
        squares = jnp.sum(jnp.where(seen_column(length, tall), squares, 0.0), axis=0, keepdims=True)
        sq_ref[b] = jnp.broadcast_to(squares, (1, 128))
    sent_ref[...] = total.astype(bf16)


def expert_kernel(got_ref, first_ref, second_ref, hid_ref, pre_ref, grad_ref, back_ref, *, each):
    rows = got_ref.shape[0]
    half = each // 2
    got = got_ref[...]
    own = jnp.bitwise_and(lax.broadcasted_iota(jnp.int32, (rows, 1), 0), each - 1) < half
    grads = jnp.where(own, pltpu.roll(got.astype(f32), rows - half, 0), 0.0).astype(bf16)
    grad_ref[...] = grads
    u = mm(got, first_ref[...])
    cubic = 0.7978845608028654 * (u + 0.044715 * u * u * u)
    t = jnp.tanh(cubic)
    hidden = jnp.where(own, 0.5 * u * (1.0 + t), 0.0).astype(bf16)
    hid_ref[...] = hidden
    slope = 0.5 * (1.0 + t) + 0.5 * u * (1.0 - t * t) * 0.7978845608028654 * (
        1.0 + 3.0 * 0.044715 * u * u
    )
    grad_pre = (mm_nt(grads, second_ref[...]) * slope).astype(bf16)
    pre_ref[...] = grad_pre
    out = mm(hidden, second_ref[...])
    grad_in = mm_nt(grad_pre, first_ref[...])
    back_ref[...] = jnp.where(own, out, pltpu.roll(grad_in, half, 0)).astype(bf16)


def mix_kernel(
    me_ref, res_ref, h_ref, soft_ref, cot_ref, mask_ref, ex_ref, back_ref, sq_ref,
    out_ref, gres_ref, gb_ref, gbt_ref, small_ref, *, images, seq, tall, experts, groups
):
    small_ref[...] = jnp.zeros_like(small_ref)
    router = ex_ref[2 : 2 + experts, :].astype(bf16)
    gain = ex_ref[1:2, :]
    width = out_ref.shape[2]
    lanes = lax.broadcasted_iota(jnp.int32, (1, width), 1)
    roots = [jnp.zeros((1, width), f32) for _ in range(3)]
    for b in range(images):
        at = pl.ds(b * tall, tall)
        length = length_of(mask_ref, me_ref, b, images)
        resid, h_two = res_ref[at, :], h_ref[at, :]
        dispatch, combine = soft_ref[0, b], soft_ref[1, b]
        dispatch_low, combine_low = dispatch.astype(bf16), combine.astype(bf16)
        returned, grad_slots = back_ref[0, b], back_ref[1, b]
        cot = padded(cot_ref[b], tall - seq)
        mixed = mm_tn(combine_low, returned)
        stream = resid + mixed
        out_ref[b] = stream[:seq].astype(bf16)
        column = seen_column(length, tall)
        sums = []
        for value in (stream, mixed):
            squares = jnp.sum(value * value, axis=1, keepdims=True)
            sums.append(jnp.sum(jnp.where(column, squares, 0.0), axis=0, keepdims=True))
        sums.insert(1, sq_ref[b, :, 0:1])
        for k, value in enumerate(sums):
            root = jnp.sqrt(value / (length * width))
            mine = lanes == (me_ref[0] * groups + me_ref[2]) * images + b
            roots[k] += jnp.where(mine, root, 0.0)
        grad_c = mm_nt(returned, cot)
        grad_c = combine * (grad_c - jnp.sum(grad_c * combine, axis=0, keepdims=True))
        grad_d = mm_nt(grad_slots, h_two)
        grad_d = dispatch * (grad_d - jnp.sum(grad_d * dispatch, axis=1, keepdims=True))
        grad_logits = (grad_d + grad_c).astype(bf16)
        grad_h = mm_tn(dispatch_low, grad_slots) + mm_tn(grad_logits, router)
        small_ref[0:experts, :] += mm(grad_logits, h_two)
        unit, inverse = unit_of(resid)
        small_ref[experts + 1 : experts + 2, :] += jnp.sum(grad_h * unit, axis=0, keepdims=True)
        scaled = grad_h * gain
        mean_grad = jnp.mean(scaled, axis=-1, keepdims=True)
        mean_proj = jnp.mean(scaled * unit, axis=-1, keepdims=True)
        gres_ref[at, :] = cot.astype(f32) + inverse * (scaled - mean_grad - unit * mean_proj)
    for k in range(3):
        small_ref[experts + 2 + k : experts + 3 + k, :] = roots[k]
    gb_ref[...] = gres_ref[...].astype(bf16)
    gbt_ref[...] = gres_ref[...].T.astype(bf16)


def back_kernel(
    me_ref, gb_ref, gbt_ref, ht_ref, qkv_a, p_a, qkv_b, p_b, ho_ref, wo_ref,
    gw_ref, gj_ref, dho_ref, *, images, tall, x, flip
):
    j = x + 2 * jnp.bitwise_xor(me_ref[1], flip)
    own = pl.ds(pl.multiple_of(j * 256, 256), 256)
    scale = HEAD_DIM ** (-0.5)
    low = low_lanes(tall)
    dho_ref[...] = mm(gb_ref[...], wo_ref[:, own])
    heads, dots = [], []
    for b in range(images):
        at = pl.ds(b * tall, tall)
        joined, joined_last = qkv_a[j, at, :], qkv_b[j, at, :]
        q_pair, k_pair, v_pair = joined[:, :128], joined[:, 128:256], joined[:, 256:384]
        qk_last, v_last = joined_last[:, :128], joined_last[:, 128:256]
        grad = dho_ref[at, :].astype(bf16).astype(f32)
        product = grad * ho_ref[at, own].astype(f32)
        single, pair = product[:, :128], product[:, 128:]
        dots += [
            jnp.sum(jnp.where(low, pair, 0.0), axis=1, keepdims=True),
            jnp.sum(jnp.where(low, 0.0, pair), axis=1, keepdims=True),
            jnp.sum(single, axis=1, keepdims=True),
        ]
        grad_pair = grad[:, 128:]
        grad_last = jnp.where(low, pltpu.roll(grad[:, :128], HEAD_DIM, 1), 0.0).astype(bf16)
        heads += [
            (p_a[j, b, 0], jnp.where(low, grad_pair, 0.0).astype(bf16), v_pair, q_pair, k_pair),
            (p_a[j, b, 1], jnp.where(low, 0.0, grad_pair).astype(bf16), v_pair, q_pair, k_pair),
            (p_b[j, b], grad_last, v_last, qk_last, qk_last),
        ]
    grad_p = [mm_nt(g, v) for _, g, v, _, _ in heads]
    grad_s = [
        (probs.astype(f32) * (value - dot)).astype(bf16)
        for (probs, _, _, _, _), value, dot in zip(heads, grad_p, dots)
    ]
    gqs = [mm(value, k) for value, (_, _, _, _, k) in zip(grad_s, heads)]
    gks = [mm_tn(value, q) for value, (_, _, _, q, _) in zip(grad_s, heads)]
    gvs = [mm_tn(probs, g) for probs, g, _, _, _ in heads]
    for b in range(images):
        at = pl.ds(b * tall, tall)
        gq, gk, gv = (value[3 * b : 3 * b + 3] for value in (gqs, gks, gvs))
        last = pltpu.roll(jnp.where(low, gk[2], gq[2]), HEAD_DIM, 1)
        gj_ref[at, :] = jnp.concatenate(
            [
                jnp.where(low, gq[0], gq[1]) * scale,
                jnp.where(low, gk[0], gk[1]) * scale,
                gv[0] + gv[1],
                last * scale,
                gv[2],
            ],
            1,
        ).astype(bf16)
    grad_out = mm(gbt_ref[...], ho_ref[:, own])
    grad_in = mm(ht_ref[...], gj_ref[...])
    halves, blocks, rows = gw_ref.shape[:3]
    for d in range(halves * blocks):
        r = jnp.bitwise_xor(me_ref[0], d) if halves > 1 else 0
        entry = (jnp.bitwise_and(r, 1), jnp.right_shift(r, 1)) if halves > 1 else (0, 0)
        at = slice(d * rows, (d + 1) * rows)
        gw_ref[entry + (slice(None), slice(0, 512))] = grad_in[at, :512].astype(bf16)
        gw_ref[entry + (slice(None), slice(512, 640))] = (
            grad_in[at, 512:] + grad_out[at, :128]
        ).astype(bf16)
        gw_ref[entry + (slice(None), slice(640, 768))] = grad_out[at, 128:].astype(bf16)


def input_kernel(me_ref, w_a, w_b, *refs, order):
    grads, gh_ref = refs[:-1], refs[-1]
    for k, (ref, (x, flip)) in enumerate(zip(grads, order)):
        j = x + 2 * jnp.bitwise_xor(me_ref[1], flip)
        into = mm_nt(ref[:, :384], w_a[j]) + mm_nt(ref[:, 384:], w_b[j])
        if k == 0:
            gh_ref[...] = into
        else:
            gh_ref[...] += into


def last_kernel(x_ref, gres_ref, gh_ref, ex_ref, part_ref, gt_ref, small_ref, *, images, seq, tall, experts):
    total = jnp.zeros((1, x_ref.shape[2]), f32)
    gain = ex_ref[0:1, :]
    for b in range(images):
        at = pl.ds(b * tall, seq)
        unit, inverse = unit_of(x_ref[b].astype(f32))
        grad_h = gh_ref[at, :]
        total += jnp.sum(grad_h * unit, axis=0, keepdims=True)
        scaled = grad_h * gain
        mean_grad = jnp.mean(scaled, axis=-1, keepdims=True)
        mean_proj = jnp.mean(scaled * unit, axis=-1, keepdims=True)
        gt_ref[b] = gres_ref[at, :] + inverse * (scaled - mean_grad - unit * mean_proj)
    small_ref[...] = part_ref[...]
    small_ref[experts : experts + 1, :] = total


def cost(microseconds):
    return int(microseconds * 1.1e9)


def call(kernel, outs, args, scratch=(), flops=0, name=None, scalars=1, grant=16, **static):
    spec = pl.BlockSpec(memory_space=pltpu.VMEM)
    word = pl.BlockSpec(memory_space=pltpu.SMEM)
    moved = sum(math.prod(a.shape) * a.dtype.itemsize for a in args)
    return pl.pallas_call(
        functools.partial(kernel, **static),
        out_shape=[jax.ShapeDtypeStruct(s, d) for s, d in outs],
        in_specs=[word] * scalars + [spec] * (len(args) - scalars),
        out_specs=[spec] * len(outs),
        scratch_shapes=list(scratch),
        compiler_params=pltpu.CompilerParams(vmem_limit_bytes=grant << 20),
        cost_estimate=pl.CostEstimate(flops=flops, bytes_accessed=moved, transcendentals=0),
        name=name,
    )(*args)


def make(mesh):
    dp, mp = mesh.shape["dp"], mesh.shape["mp"]

    def per_device(
        tokens, token_mask, gain_one, w_qkv, w_out, gain_two, router, w_in, w_back, cotangent
    ):
        rows, width = tokens.shape
        seq = token_mask.shape[1]
        tall = -(-seq // 16) * 16
        images = rows // seq
        experts = router.shape[1]
        d_rows, _, part = w_qkv.shape
        count = images * tall
        high = dp // 2
        heads = part // HEAD_DIM
        ready = d_rows % 16 != 0
        each = 2 * (1 << (images - 1).bit_length())
        me = lax.axis_index("dp")
        at_mp = lax.axis_index("mp")
        core = at_mp & 1
        words = jnp.stack([me, core, at_mp]).astype(jnp.int32)
        static = {"images": images, "tall": tall}
        exact = {"images": images, "seq": seq, "tall": tall}

        columns = experts + 2
        half = 2 * part
        hbm = pl.BlockSpec(memory_space=pltpu.HBM)
        vmem = pl.BlockSpec(memory_space=pltpu.VMEM)
        word = pl.BlockSpec(memory_space=pltpu.SMEM)
        wide = columns + -columns % 128
        shapes = [(3, d_rows, part), (part, d_rows), (1, d_rows), (1, d_rows), (experts, d_rows)]
        first, second, extra = pl.pallas_call(
            pack_kernel,
            out_shape=[jax.ShapeDtypeStruct((d_rows, n), bf16) for n in (half, half, wide)],
            in_specs=[word] + [hbm] * 5,
            out_specs=[vmem] * 3,
            scratch_shapes=[pltpu.VMEM(shape, bf16) for shape in shapes] + [pltpu.SemaphoreType.DMA((5,))],
            compiler_params=pltpu.CompilerParams(vmem_limit_bytes=67_000_000),
            name="pack",
        )(words, w_qkv.transpose(1, 0, 2), w_out, gain_one[None], gain_two[None], router.T)

        first, second, held_extra = first[None], second[None], extra[None]
        stages = bits_of(dp)[:-1]
        for bit in stages:
            put = jnp.concatenate if bit == stages[0] else lambda pair: join(*pair)
            first = put([first, swap(first, "dp", dp, bit)])
        held_extra = jnp.concatenate([held_extra, swap(held_extra, "dp", dp, stages[0])])
        other, held_extra, late = lax.optimization_barrier(
            (swap_both(first, dp, mp, (1, 0), (0, 2)), held_extra, swap(second, "dp", dp, stages[0]))
        )
        second = jnp.concatenate([second, late])
        for bit in stages[1:]:
            second = join(second, swap(second, "dp", dp, bit))
            held_extra = join(held_extra, swap(held_extra, "dp", dp, bit))
        held_extra = join(held_extra, swap(held_extra, "dp", dp, 1))
        held_extra = held_extra.reshape((dp,) + extra.shape)
        if ready:
            held_extra = reorder(unmirrored(held_extra), me).reshape(1, width, -1)
        x3 = tokens.reshape(images, seq, width)
        cot3 = cotangent.reshape(images, seq, width)
        h_one, h_turned, ex = call(
            prep_kernel,
            [((count, width), bf16), ((width, count), bf16), ((held_extra.shape[2], width), f32)],
            (words, x3, held_extra),
            flops=cost(2),
            name="prep",
            grant=4,
            **exact,
        )
        near = join(first, other).reshape((2, high, d_rows, half))
        far = swap_both(near, dp, mp, (0, 2), (1, 0))
        second = second.reshape((high, d_rows, half))
        other = swap_both(second, dp, mp, (1, 0), (0, 2))
        far, h_one, other = lax.optimization_barrier((far, h_one, other))
        first = (near, far, swap(near, "mp", mp, 1), swap(far, "mp", mp, 1))
        near = join(second, other).reshape((2, high, d_rows, half))
        second_near, second_far = near, swap_both(near, dp, mp, (0, 2), (1, 0))
        second_near_other = swap(second_near, "mp", mp, 1)

        def whole(x, of_core, near, far, other_near, other_far):
            mine = core == of_core
            low = jnp.where(mine, near, other_near)
            high_part = jnp.where(mine, far, other_far)
            blocks = jnp.stack([low[x], high_part[x]]) if of_core else (high_part if x else low)
            blocks = blocks.reshape((dp, d_rows, half))
            blocks = unmirrored(blocks)
            return reorder(blocks, me).reshape(width, half)

        def weights_of(parts):
            if ready:
                return tuple(whole(j & 1, j >> 1, *parts) for j in range(4))
            return parts

        def saved(kept, columns, probs):
            return [
                ((mp, width, kept), bf16),
                ((mp, count, columns), bf16),
                ((mp, images) + probs + (tall, tall), bf16),
                ((mp, count, 128), bf16),
            ]

        pair = call(
            front_pair_kernel,
            saved(half, 384, (2,)),
            (words, h_one, token_mask) + weights_of(first),
            flops=cost(10),
            name="front_pair",
            grant=10,
            ready=ready,
            **static,
        )
        w_a, qkv_a, p_a, ho_a = pair
        second_far, ho_a = lax.optimization_barrier((second_far, ho_a))
        second = (second_near, second_far, second_near_other, swap(second_far, "mp", mp, 1))
        w_b, qkv_b, p_b, heads_out, w_heads, branch = call(
            front_last_kernel,
            saved(256, 256, ())[:3]
            + [
                ((count, 256 * mp), bf16),
                ((width, 256 * mp), bf16),
                ((count, width), f32),
            ],
            (words, h_one, token_mask, ho_a) + weights_of(second),
            flops=cost(7),
            name="front_last",
            grant=10,
            ready=ready,
            **static,
        )
        resid, h_two, soft, sent, sq_branch = call(
            route_kernel,
            [
                ((count, width), f32),
                ((count, width), bf16),
                ((2, images, experts, tall), f32),
                ((experts * each, width), bf16),
                ((images, 1, 128), f32),
            ],
            (words, x3, branch, cot3, token_mask, ex),
            flops=cost(2),
            name="route",
            grant=6,
            experts=experts,
            **exact,
        )
        got = sent.reshape(dp, each, width)
        got = lax.all_to_all(got, "dp", split_axis=0, concat_axis=0, tiled=True)
        got = gather_mp(got, mp).reshape(-1, width)
        everyone = got.shape[0]
        hidden, grad_pre, grad_expert, back = call(
            expert_kernel,
            [
                ((everyone, w_in.shape[2]), bf16),
                ((everyone, w_in.shape[2]), bf16),
                ((everyone, width), bf16),
                ((everyone, width), bf16),
            ],
            (got, w_in[0], w_back[0]),
            flops=cost(2),
            name="expert",
            scalars=0,
            grant=12 if dp <= 8 else 56,
            each=each,
        )
        back = back.reshape(mp, dp, each, width)
        back = scatter(back, "mp", mp, [1, 2])
        back = lax.all_to_all(back, "dp", split_axis=0, concat_axis=0, tiled=True)
        back = back.reshape(dp, 2, each // 2, width)[:, :, :images].transpose(1, 2, 0, 3)
        grad_w_back = mm_tn(hidden, grad_expert)
        grad_w_in = mm_tn(got, grad_pre)

        out_rows, grad_resid, grad_low, grad_turned, small = call(
            mix_kernel,
            [
                ((images, seq, width), bf16),
                ((count, width), f32),
                ((count, width), bf16),
                ((width, count), bf16),
                ((experts + 5, width), f32),
            ],
            (words, resid, h_two, soft, cot3, token_mask, ex, back, sq_branch),
            flops=cost(5),
            name="mix",
            grant=8,
            experts=experts,
            groups=mp,
            **exact,
        )
        shape = (1, 1, width, 4 * part) if ready else (2, high, d_rows, 4 * part)

        def back_of(x, flip, grad_in):
            grads, joined = call(
                back_kernel,
                [(shape, bf16), ((count, JOINED), bf16)],
                (words, grad_in, grad_turned, h_turned, qkv_a, p_a, qkv_b, p_b, heads_out, w_heads),
                [pltpu.VMEM((count, 256), f32)],
                flops=cost(8),
                name="back",
                grant=10,
                x=x,
                flip=flip,
                **static,
            )
            if ready:
                grads = reorder(grads.reshape(dp, d_rows, 4 * part), me)
                grads = grads.reshape(high, 2, d_rows, 4 * part).transpose(1, 0, 2, 3)
            return grads, joined

        def fold(terms, halves, starts=None, kept_columns=4 * part):
            size = terms[0].shape
            kept = ((size[0] // 2,) + size[1:-1] + (kept_columns,), bf16)
            return call(
                fold_kernel,
                [kept, kept],
                terms,
                flops=cost(1),
                name="fold",
                scalars=0,
                grant=6,
                halves=halves,
                starts=starts or (0,) * len(terms),
            )

        order = ((1, 1), (1, 0), (0, 1), (0, 0))
        sent_grads, joined_a = back_of(1, 1, grad_low)
        other = swap(sent_grads, "mp", mp, 1)
        grad_low, joined_a = lax.optimization_barrier((grad_low, joined_a))
        kept_grads, joined_b = back_of(1, 0, grad_low)
        far_kept, far_left = fold((kept_grads, other), True)
        far_left, grad_low, joined_b = lax.optimization_barrier((far_left, grad_low, joined_b))
        early = swap_both(far_left[0], dp, mp, (0, 2), (1, 0))
        sent_grads, joined_c = back_of(0, 1, grad_low)
        grad_low, joined_c = lax.optimization_barrier((grad_low, joined_c))
        other = swap(sent_grads, "mp", mp, 1)
        kept_grads, joined_d = back_of(0, 0, grad_low)
        part_shape = ((high, d_rows, 4 * part), bf16)
        near_sum, own_sum, second = call(
            blend_kernel,
            [part_shape] * 3,
            (words, far_kept[0], kept_grads, other),
            flops=cost(1),
            name="blend",
            grant=8,
        )
        second = swap_both(second, dp, mp, (0, 2), (1, 0))
        grad_h = call(
            input_kernel,
            [((count, width), f32)],
            (words, w_a, w_b, joined_a, joined_b, joined_c, joined_d),
            flops=cost(4),
            name="input",
            grant=8,
            order=order,
        )[0]
        early, grad_h = lax.optimization_barrier((early, grad_h))
        thirds = call(
            blend_late_kernel,
            [((high, d_rows, half), bf16)] * 2,
            (words, far_kept[0], own_sum, early),
            flops=cost(1),
            name="blend_late",
            grant=8,
        )
        thirds = [swap_both(third, dp, mp, (1, 0), (0, 2)) for third in thirds]
        pieces = [
            list(fold((near_sum, second, third), False, (k * half, k * half, 0), half))
            for k, third in enumerate(thirds)
        ]
        grad_tokens, small = call(
            last_kernel,
            [((images, seq, width), f32), ((experts + 5, width), f32)],
            (x3, grad_resid, grad_h, ex, small),
            flops=cost(0.1),
            name="last",
            scalars=0,
            grant=8,
            experts=experts,
            **exact,
        )
        for bit in bits_of(dp)[:-1]:
            small = small + swap(small, "dp", dp, bit)
        parts = []
        for k, (kept, left) in enumerate(pieces):
            for bit in bits_of(high)[:0:-1]:
                other = swap(left, "dp", dp, 2 * bit)
                if k == 0:
                    other, small = lax.optimization_barrier((other, small))
                kept, left = fold((kept, other), False, None, half)
            parts += [kept[0], swap(left[0], "dp", dp, 2 * bits_of(high)[0])]
        grad_qkv, grad_out = call(
            unpack_kernel,
            [((3, d_rows, part), f32), ((part, d_rows), f32)],
            parts,
            flops=cost(1),
            name="unpack",
            scalars=0,
            grant=6,
        )
        small = small + swap(small, "dp", dp, 1)
        small = small + swap(small, "mp", mp, 2)
        grad_one, grad_two, grad_router, root_squares = call(
            finish_kernel,
            [
                ((1, d_rows), f32),
                ((1, d_rows), f32),
                ((experts, d_rows), f32),
                ((3, mp * images), f32),
            ],
            (words, small, swap(small, "mp", mp, 1)),
            flops=cost(1),
            name="finish",
            grant=4,
        )
        return (
            out_rows.reshape(rows, width),
            grad_tokens.reshape(rows, width),
            grad_one[0],
            grad_qkv.transpose(1, 0, 2),
            grad_out,
            grad_two[0],
            grad_router.T,
            grad_w_in[None],
            grad_w_back[None],
            root_squares,
        )

    return per_device


def solution(mesh):
    in_specs = (
        P(("dp", "mp"), None),
        P("dp", None),
        P("dp"),
        P("dp", None, "mp"),
        P("mp", "dp"),
        P("dp"),
        P("dp", None),
        P("dp", None, "mp"),
        P("dp", "mp", None),
        P(("dp", "mp"), None),
    )
    out_specs = (
        P(("dp", "mp"), None),
        P(("dp", "mp"), None),
        P("dp"),
        P("dp", None, "mp"),
        P("mp", "dp"),
        P("dp"),
        P("dp", None),
        P("dp", None, "mp"),
        P("dp", "mp", None),
        P(None, "dp"),
    )
    return jax.shard_map(
        make(mesh), mesh=mesh, in_specs=in_specs, out_specs=out_specs, check_vma=False
    )
```

```python
import functools
import math

import jax
import jax.numpy as jnp
from jax import lax
from jax.experimental import pallas as pl
from jax.experimental.pallas import tpu as pltpu
from jax.sharding import PartitionSpec as P

HEAD_DIM = 64


epsilon = 1e-06
bf16 = jnp.bfloat16
f32 = jnp.float32


def bits_of(size):
    return [1 << k for k in reversed(range(size.bit_length() - 1))]


def swap(array_in, axis_name, size, bit):
    return lax.ppermute(array_in, axis_name, [(i, i ^ bit) for i in range(size)])


def swap_both(array_in, dp, mp, even, odd):
    pairs = []
    for d in range(dp):
        for m in range(mp):
            flip = odd if m & 1 else even
            pairs.append((d * mp + m, (d ^ flip[0]) * mp + (m ^ flip[1])))
    return lax.ppermute(array_in, ("dp", "mp"), pairs)


def gather_mp(block, mp):
    held = block[None]
    for bit in bits_of(mp):
        other = swap(held, "mp", mp, bit)
        held = jnp.stack([held, other], 1).reshape((-1,) + block.shape)
    return held


def scatter(held, axis_name, size, bits, unit=1):
    left = sorted(bits)
    for bit in bits:
        inner = 1 << left.index(bit)
        left.remove(bit)
        pairs = held.reshape((held.shape[0] // (2 * inner), 2, inner) + held.shape[1:])
        other = swap(pairs[:, 1], axis_name, size, bit * unit)
        held = pairs[:, 0].astype(f32) + other.astype(f32)
        held = held.astype(bf16).reshape((-1,) + held.shape[2:])
    return held[0]


def mirrored(index, size):
    bits = size.bit_length() - 1
    return sum(((index >> k) & 1) << (bits - 1 - k) for k in range(bits)) if bits else index


def unmirrored(blocks):
    size = blocks.shape[0]
    bits = size.bit_length() - 1
    split = blocks.reshape((2,) * bits + blocks.shape[1:])
    turn = tuple(range(bits))[::-1] + tuple(range(bits, split.ndim))
    return split.transpose(turn).reshape(blocks.shape)


def reorder(blocks, me):
    size = blocks.shape[0]
    for bit in bits_of(size):
        pairs = blocks.reshape((size // (2 * bit), 2, bit) + blocks.shape[1:])
        blocks = jnp.where((me & bit) > 0, pairs[:, ::-1], pairs).reshape(blocks.shape)
    return blocks


def mm(a, b):
    return lax.dot_general(a, b, (((1,), (0,)), ((), ())), preferred_element_type=f32)


def mm_nt(a, b):
    return lax.dot_general(a, b, (((1,), (1,)), ((), ())), preferred_element_type=f32)


def mm_tn(a, b):
    return lax.dot_general(a, b, (((0,), (0,)), ((), ())), preferred_element_type=f32)


def unit_of(rows_f):
    mean_row = jnp.mean(rows_f, axis=-1, keepdims=True)
    centered = rows_f - mean_row
    variance = jnp.mean(centered * centered, axis=-1, keepdims=True)
    inverse = lax.rsqrt(variance + epsilon)
    return centered * inverse, inverse


def padded(value, pad):
    return jnp.concatenate([value, jnp.zeros((pad, value.shape[1]), value.dtype)], 0)


def low_lanes(rows):
    return lax.broadcasted_iota(jnp.int32, (rows, 128), 1) < HEAD_DIM


JOINED = 640


def pack_kernel(
    me_ref, qkv_hbm, out_hbm, one_hbm, two_hbm, router_hbm, second_ref, extra_ref,
    qkv_ref, out_ref, one_ref, two_ref, router_ref, sems
):
    del me_ref
    pairs = (
        (qkv_hbm, qkv_ref), (out_hbm, out_ref), (one_hbm, one_ref), (two_hbm, two_ref), (router_hbm, router_ref),
    )
    copies = [pltpu.make_async_copy(a, b, sems.at[k]) for k, (a, b) in enumerate(pairs)]
    for copy in copies:
        copy.start()
    low, mid = 2 * HEAD_DIM, qkv_ref.shape[2]
    for copy in copies:
        copy.wait()
    out = out_ref[...].astype(f32).T.astype(bf16)
    second_ref[...] = jnp.concatenate(
        [qkv_ref[c, :, low:mid] for c in range(3)] + [out[:, low:mid], out[:, :low]], axis=1
    )
    rows = one_ref.shape[1]
    columns = [one_ref[...], two_ref[...], router_ref[...]]
    columns = [value.astype(f32) for value in columns]
    filled = sum(value.shape[0] for value in columns)
    columns.append(jnp.zeros((extra_ref.shape[1] - filled, rows), f32))
    extra_ref[...] = jnp.concatenate(columns, 0).T.astype(bf16)


def join_kernel(a_ref, b_ref, out_ref):
    size = a_ref.shape[0]
    out_ref[:size] = a_ref[...]
    out_ref[size:] = b_ref[...]


def join(a, b):
    shape = (a.shape[0] + b.shape[0],) + a.shape[1:]
    return call(join_kernel, [(shape, a.dtype)], (a, b), flops=1000, name="join", scalars=0, grant=4)[0]


def fold_kernel(*refs, halves, starts):
    terms, (kept_ref, left_ref) = refs[:-2], refs[-2:]
    size, columns = terms[0].shape[0], kept_ref.shape[-1]
    for k in range(size):
        total = None
        for term, start in zip(terms, starts):
            value = term[k][..., start : start + columns].astype(f32)
            total = value if total is None else total + value
        at, odd = (k % (size // 2), k >= size // 2) if halves else (k // 2, k % 2 == 1)
        (left_ref if odd else kept_ref)[at] = total.astype(bf16)


def blend_kernel(me_ref, far_ref, kept_ref, other_ref, near_ref, own_ref, second_ref):
    for k, ref in ((0, near_ref), (1, own_ref)):
        ref[...] = (kept_ref[k].astype(f32) + other_ref[k].astype(f32)).astype(bf16)
    first_core = me_ref[1] == 0

    @pl.when(first_core)
    def _():
        second_ref[...] = far_ref[...]

    @pl.when(jnp.logical_not(first_core))
    def _():
        second_ref[...] = own_ref[...]


def blend_late_kernel(me_ref, far_ref, own_ref, early_ref, *thirds):
    columns = thirds[0].shape[-1]
    for core, ref in ((0, own_ref), (1, far_ref)):

        @pl.when(me_ref[1] == core)
        def _(ref=ref):
            for k, third in enumerate(thirds):
                at = slice(k * columns, (k + 1) * columns)
                total = ref[..., at].astype(f32) + early_ref[..., at].astype(f32)
                third[...] = total.astype(bf16)


def finish_kernel(me_ref, own_ref, other_ref, one_ref, two_ref, router_ref, root_ref):
    experts, rows = router_ref.shape
    total = own_ref[...] + other_ref[...]
    width = total.shape[1]
    mine = pltpu.roll(total, lax.rem(width - me_ref[0] * rows, width), 1)
    one_ref[...] = mine[experts : experts + 1, :rows]
    two_ref[...] = mine[experts + 1 : experts + 2, :rows]
    router_ref[...] = mine[:experts, :rows]
    images = root_ref.shape[1]
    mine = pltpu.roll(total, lax.rem(width - me_ref[0] * images, width), 1)
    root_ref[...] = mine[experts + 2 : experts + 5, :images]


def unpack_kernel(own_a, other_a, own_b, other_b, qkv_ref, out_ref):
    low, mid = 2 * HEAD_DIM, qkv_ref.shape[2]
    pair = own_a[...].astype(f32) + other_a[...].astype(f32)
    rest = own_b[...].astype(f32) + other_b[...].astype(f32)
    for c in range(3):
        qkv_ref[c, :, :low] = pair[:, c * low : (c + 1) * low]
        qkv_ref[c, :, low:mid] = rest[:, c * HEAD_DIM : (c + 1) * HEAD_DIM]
    out_ref[...] = jnp.concatenate([rest[:, 256:], rest[:, 192:256]], axis=1).T


def length_of(mask_ref, me_ref, b, images):
    row = mask_ref[pl.ds(me_ref[2] * images + b, 1), :]
    return jnp.sum(row.astype(f32), axis=1, keepdims=True)


def seen_row(length, tall):
    return lax.broadcasted_iota(jnp.int32, (1, tall), 1).astype(f32) < length


def seen_column(length, tall):
    return lax.broadcasted_iota(jnp.int32, (tall, 1), 0).astype(f32) < length


def prep_kernel(me_ref, x_ref, extra_ref, h_ref, ht_ref, small_ref, *, images, seq, tall):
    blocks = extra_ref.shape[0]
    me = me_ref[0]
    parts = [extra_ref[mirrored(me ^ d, blocks) if blocks > 1 else 0] for d in range(blocks)]
    small_ref[...] = jnp.concatenate(parts, 0).astype(f32).T
    gain = small_ref[0:1, :]
    for b in range(images):
        unit, _ = unit_of(x_ref[b].astype(f32))
        h_ref[pl.ds(b * tall, tall), :] = padded((unit * gain).astype(bf16), tall - seq)
    ht_ref[...] = h_ref[...].T


def fetch_all(me_ref, refs, put):
    rows, high_size = refs[0].shape[-2], refs[0].shape[1]
    for core in (0, 1):

        @pl.when(me_ref[1] == core)
        def _(core=core):
            for slot in range(4):
                x, of_core = slot & 1, slot >> 1
                first, second = refs[:2] if of_core == core else refs[2:4]
                for r in range(2 * high_size):
                    low, high = r & 1, mirrored(r >> 1, high_size)
                    if of_core == 0:
                        block = (second if x else first)[low, high]
                    else:
                        block = (second if low else first)[x, high]
                    d = jnp.bitwise_xor(me_ref[0], r)
                    put(slot, pl.ds(pl.multiple_of(d * rows, 16), rows), block)


def attend(triples):
    scores = [mm_nt(q, k) * HEAD_DIM ** (-0.5) + bias for q, k, _, bias in triples]
    terms = [jnp.exp(value - jnp.max(value, axis=-1, keepdims=True)) for value in scores]
    probs = [
        (value * (1.0 / jnp.sum(value, axis=-1, keepdims=True))).astype(bf16) for value in terms
    ]
    return probs, [mm(value, v) for value, (_, _, v, _) in zip(probs, triples)]


def bias_of(mask_ref, me_ref, b, images, tall):
    return jnp.where(seen_row(length_of(mask_ref, me_ref, b, images), tall), 0.0, -1e30)


def front_pair_kernel(me_ref, h_ref, mask_ref, *refs, images, tall, ready):
    w_ref, qkv_ref, p_ref, ho_ref = refs[4:]

    def put(slot, at, block):
        for c in range(3):
            w_ref[slot, at, c * 128 : (c + 1) * 128] = block[c]

    if ready:
        for slot in range(4):
            w_ref[slot] = refs[slot][...]
    else:
        fetch_all(me_ref, refs[:4], put)
    low = low_lanes(tall)

    def group(j, carry):
        qkv_ref[j] = mm(h_ref[...], w_ref[j]).astype(bf16)
        triples = []
        for b in range(images):
            joined = qkv_ref[j, pl.ds(b * tall, tall), :]
            q, k, v = joined[:, :128], joined[:, 128:256], joined[:, 256:384]
            none = jnp.zeros_like(q)
            bias = bias_of(mask_ref, me_ref, b, images, tall)
            triples.append((jnp.where(low, q, none), k, v, bias))
            triples.append((jnp.where(low, none, q), k, v, bias))
        probs, outs = attend(triples)
        for b in range(images):
            p_ref[j, b, 0], p_ref[j, b, 1] = probs[2 * b], probs[2 * b + 1]
            pair = jnp.where(low, outs[2 * b], outs[2 * b + 1])
            ho_ref[j, pl.ds(b * tall, tall), :] = pair.astype(bf16)
        return carry

    lax.fori_loop(0, w_ref.shape[0], group, 0)


def front_last_kernel(me_ref, h_ref, mask_ref, pair_ref, *refs, images, tall, ready):
    w_ref, qkv_ref, p_ref, ho_ref, wo_ref, br_ref = refs[4:]

    def put(slot, at, block):
        w_ref[slot, at, :] = block[:, :256]
        wo_ref[at, slot * 256 : (slot + 1) * 256] = block[:, 128:]

    if ready:
        for slot in range(4):
            put(slot, slice(None), refs[slot][...])
    else:
        fetch_all(me_ref, refs[:4], put)
    low = low_lanes(tall)

    def two(i, carry):
        places = [(2 * i + k, b) for k in (0, 1) for b in range(images)]
        for j in (2 * i, 2 * i + 1):
            qkv_ref[j] = mm(h_ref[...], w_ref[j]).astype(bf16)
        triples = []
        for j, b in places:
            joined = qkv_ref[j, pl.ds(b * tall, tall), :]
            qk, v = joined[:, :128], joined[:, 128:256]
            k = pltpu.roll(qk.astype(f32), HEAD_DIM, 1).astype(bf16)
            bias = bias_of(mask_ref, me_ref, b, images, tall)
            triples.append((jnp.where(low, qk, jnp.zeros_like(qk)), k, v, bias))
        probs, outs = attend(triples)
        for (j, b), prob, out in zip(places, probs, outs):
            at, start = pl.ds(b * tall, tall), pl.multiple_of(j * 256, 256)
            p_ref[j, b] = prob
            ho_ref[at, pl.ds(start, 128)] = jnp.where(low, 0.0, pltpu.roll(out, HEAD_DIM, 1)).astype(bf16)
            ho_ref[at, pl.ds(start + 128, 128)] = pair_ref[j, at, :]
        return carry

    lax.fori_loop(0, w_ref.shape[0] // 2, two, 0)
    br_ref[...] = mm_nt(ho_ref[...], wo_ref[...])


def spot(rows, b, start, experts):
    each = rows // experts
    at_row = lax.broadcasted_iota(jnp.int32, (rows, experts), 0)
    at_column = lax.broadcasted_iota(jnp.int32, (rows, experts), 1)
    return jnp.where(at_row == at_column * each + (start + b), 1.0, 0.0).astype(bf16)


def route_kernel(
    me_ref, x_ref, br_ref, cot_ref, mask_ref, ex_ref,
    res_ref, h_ref, soft_ref, sent_ref, sq_ref, *, images, seq, tall, experts
):
    rows = sent_ref.shape[0]
    half = rows // experts // 2
    router = ex_ref[2 : 2 + experts, :].astype(bf16)
    gain = ex_ref[1:2, :]
    total = jnp.zeros(sent_ref.shape, f32)
    for b in range(images):
        at = pl.ds(b * tall, tall)
        length = length_of(mask_ref, me_ref, b, images)
        branch = br_ref[at, :]
        resid = padded(x_ref[b].astype(f32), tall - seq) + branch
        res_ref[at, :] = resid
        unit, _ = unit_of(resid)
        h_two = (unit * gain).astype(bf16)
        h_ref[at, :] = h_two
        logits = mm_nt(router, h_two)
        held = jnp.where(seen_row(length, tall), logits, -1e30)
        terms = jnp.exp(held - jnp.max(held, axis=1, keepdims=True))
        dispatch = terms / jnp.sum(terms, axis=1, keepdims=True)
        terms = jnp.exp(logits - jnp.max(logits, axis=0, keepdims=True))
        combine = terms / jnp.sum(terms, axis=0, keepdims=True)
        soft_ref[0, b] = dispatch
        soft_ref[1, b] = combine
        cot = padded(cot_ref[b], tall - seq)
        wide_d = mm(spot(rows, b, 0, experts), dispatch.astype(bf16)).astype(bf16)
        wide_c = mm(spot(rows, b, half, experts), combine.astype(bf16)).astype(bf16)
        total += mm(wide_d, h_two) + mm(wide_c, cot)
        squares = jnp.sum(branch * branch, axis=1, keepdims=True)
        squares = jnp.sum(jnp.where(seen_column(length, tall), squares, 0.0), axis=0, keepdims=True)
        sq_ref[b] = jnp.broadcast_to(squares, (1, 128))
    sent_ref[...] = total.astype(bf16)


def expert_kernel(got_ref, first_ref, second_ref, hid_ref, pre_ref, grad_ref, back_ref, *, each):
    rows = got_ref.shape[0]
    half = each // 2
    got = got_ref[...]
    own = jnp.bitwise_and(lax.broadcasted_iota(jnp.int32, (rows, 1), 0), each - 1) < half
    grads = jnp.where(own, pltpu.roll(got.astype(f32), rows - half, 0), 0.0).astype(bf16)
    grad_ref[...] = grads
    u = mm(got, first_ref[...])
    cubic = 0.7978845608028654 * (u + 0.044715 * u * u * u)
    t = jnp.tanh(cubic)
    hidden = jnp.where(own, 0.5 * u * (1.0 + t), 0.0).astype(bf16)
    hid_ref[...] = hidden
    slope = 0.5 * (1.0 + t) + 0.5 * u * (1.0 - t * t) * 0.7978845608028654 * (
        1.0 + 3.0 * 0.044715 * u * u
    )
    grad_pre = (mm_nt(grads, second_ref[...]) * slope).astype(bf16)
    pre_ref[...] = grad_pre
    out = mm(hidden, second_ref[...])
    grad_in = mm_nt(grad_pre, first_ref[...])
    back_ref[...] = jnp.where(own, out, pltpu.roll(grad_in, half, 0)).astype(bf16)


def mix_kernel(
    me_ref, res_ref, h_ref, soft_ref, cot_ref, mask_ref, ex_ref, back_ref, sq_ref,
    out_ref, gres_ref, gb_ref, gbt_ref, small_ref, *, images, seq, tall, experts, groups
):
    small_ref[...] = jnp.zeros_like(small_ref)
    router = ex_ref[2 : 2 + experts, :].astype(bf16)
    gain = ex_ref[1:2, :]
    width = out_ref.shape[2]
    lanes = lax.broadcasted_iota(jnp.int32, (1, width), 1)
    roots = [jnp.zeros((1, width), f32) for _ in range(3)]
    for b in range(images):
        at = pl.ds(b * tall, tall)
        length = length_of(mask_ref, me_ref, b, images)
        resid, h_two = res_ref[at, :], h_ref[at, :]
        dispatch, combine = soft_ref[0, b], soft_ref[1, b]
        dispatch_low, combine_low = dispatch.astype(bf16), combine.astype(bf16)
        returned, grad_slots = back_ref[0, b], back_ref[1, b]
        cot = padded(cot_ref[b], tall - seq)
        mixed = mm_tn(combine_low, returned)
        stream = resid + mixed
        out_ref[b] = stream[:seq].astype(bf16)
        column = seen_column(length, tall)
        sums = []
        for value in (stream, mixed):
            squares = jnp.sum(value * value, axis=1, keepdims=True)
            sums.append(jnp.sum(jnp.where(column, squares, 0.0), axis=0, keepdims=True))
        sums.insert(1, sq_ref[b, :, 0:1])
        for k, value in enumerate(sums):
            root = jnp.sqrt(value / (length * width))
            mine = lanes == (me_ref[0] * groups + me_ref[2]) * images + b
            roots[k] += jnp.where(mine, root, 0.0)
        grad_c = mm_nt(returned, cot)
        grad_c = combine * (grad_c - jnp.sum(grad_c * combine, axis=0, keepdims=True))
        grad_d = mm_nt(grad_slots, h_two)
        grad_d = dispatch * (grad_d - jnp.sum(grad_d * dispatch, axis=1, keepdims=True))
        grad_logits = (grad_d + grad_c).astype(bf16)
        grad_h = mm_tn(dispatch_low, grad_slots) + mm_tn(grad_logits, router)
        small_ref[0:experts, :] += mm(grad_logits, h_two)
        unit, inverse = unit_of(resid)
        small_ref[experts + 1 : experts + 2, :] += jnp.sum(grad_h * unit, axis=0, keepdims=True)
        scaled = grad_h * gain
        mean_grad = jnp.mean(scaled, axis=-1, keepdims=True)
        mean_proj = jnp.mean(scaled * unit, axis=-1, keepdims=True)
        gres_ref[at, :] = cot.astype(f32) + inverse * (scaled - mean_grad - unit * mean_proj)
    for k in range(3):
        small_ref[experts + 2 + k : experts + 3 + k, :] = roots[k]
    gb_ref[...] = gres_ref[...].astype(bf16)
    gbt_ref[...] = gres_ref[...].T.astype(bf16)


def back_kernel(
    me_ref, gb_ref, gbt_ref, ht_ref, qkv_a, p_a, qkv_b, p_b, ho_ref, wo_ref,
    gw_ref, gj_ref, dho_ref, *, images, tall, x, flip
):
    j = x + 2 * jnp.bitwise_xor(me_ref[1], flip)
    own = pl.ds(pl.multiple_of(j * 256, 256), 256)
    scale = HEAD_DIM ** (-0.5)
    low = low_lanes(tall)
    dho_ref[...] = mm(gb_ref[...], wo_ref[:, own])
    heads, dots = [], []
    for b in range(images):
        at = pl.ds(b * tall, tall)
        joined, joined_last = qkv_a[j, at, :], qkv_b[j, at, :]
        q_pair, k_pair, v_pair = joined[:, :128], joined[:, 128:256], joined[:, 256:384]
        qk_last, v_last = joined_last[:, :128], joined_last[:, 128:256]
        grad = dho_ref[at, :].astype(bf16).astype(f32)
        product = grad * ho_ref[at, own].astype(f32)
        single, pair = product[:, :128], product[:, 128:]
        dots += [
            jnp.sum(jnp.where(low, pair, 0.0), axis=1, keepdims=True),
            jnp.sum(jnp.where(low, 0.0, pair), axis=1, keepdims=True),
            jnp.sum(single, axis=1, keepdims=True),
        ]
        grad_pair = grad[:, 128:]
        grad_last = jnp.where(low, pltpu.roll(grad[:, :128], HEAD_DIM, 1), 0.0).astype(bf16)
        heads += [
            (p_a[j, b, 0], jnp.where(low, grad_pair, 0.0).astype(bf16), v_pair, q_pair, k_pair),
            (p_a[j, b, 1], jnp.where(low, 0.0, grad_pair).astype(bf16), v_pair, q_pair, k_pair),
            (p_b[j, b], grad_last, v_last, qk_last, qk_last),
        ]
    grad_p = [mm_nt(g, v) for _, g, v, _, _ in heads]
    grad_s = [
        (probs.astype(f32) * (value - dot)).astype(bf16)
        for (probs, _, _, _, _), value, dot in zip(heads, grad_p, dots)
    ]
    gqs = [mm(value, k) for value, (_, _, _, _, k) in zip(grad_s, heads)]
    gks = [mm_tn(value, q) for value, (_, _, _, q, _) in zip(grad_s, heads)]
    gvs = [mm_tn(probs, g) for probs, g, _, _, _ in heads]
    for b in range(images):
        at = pl.ds(b * tall, tall)
        gq, gk, gv = (value[3 * b : 3 * b + 3] for value in (gqs, gks, gvs))
        last = pltpu.roll(jnp.where(low, gk[2], gq[2]), HEAD_DIM, 1)
        gj_ref[at, :] = jnp.concatenate(
            [
                jnp.where(low, gq[0], gq[1]) * scale,
                jnp.where(low, gk[0], gk[1]) * scale,
                gv[0] + gv[1],
                last * scale,
                gv[2],
            ],
            1,
        ).astype(bf16)
    grad_out = mm(gbt_ref[...], ho_ref[:, own])
    grad_in = mm(ht_ref[...], gj_ref[...])
    halves, blocks, rows = gw_ref.shape[:3]
    for d in range(halves * blocks):
        r = jnp.bitwise_xor(me_ref[0], d) if halves > 1 else 0
        entry = (jnp.bitwise_and(r, 1), jnp.right_shift(r, 1)) if halves > 1 else (0, 0)
        at = slice(d * rows, (d + 1) * rows)
        gw_ref[entry + (slice(None), slice(0, 512))] = grad_in[at, :512].astype(bf16)
        gw_ref[entry + (slice(None), slice(512, 640))] = (
            grad_in[at, 512:] + grad_out[at, :128]
        ).astype(bf16)
        gw_ref[entry + (slice(None), slice(640, 768))] = grad_out[at, 128:].astype(bf16)


def input_kernel(me_ref, w_a, w_b, *refs, order):
    grads, gh_ref = refs[:-1], refs[-1]
    for k, (ref, (x, flip)) in enumerate(zip(grads, order)):
        j = x + 2 * jnp.bitwise_xor(me_ref[1], flip)
        into = mm_nt(ref[:, :384], w_a[j]) + mm_nt(ref[:, 384:], w_b[j])
        if k == 0:
            gh_ref[...] = into
        else:
            gh_ref[...] += into


def last_kernel(x_ref, gres_ref, gh_ref, ex_ref, part_ref, gt_ref, small_ref, *, images, seq, tall, experts):
    total = jnp.zeros((1, x_ref.shape[2]), f32)
    gain = ex_ref[0:1, :]
    for b in range(images):
        at = pl.ds(b * tall, seq)
        unit, inverse = unit_of(x_ref[b].astype(f32))
        grad_h = gh_ref[at, :]
        total += jnp.sum(grad_h * unit, axis=0, keepdims=True)
        scaled = grad_h * gain
        mean_grad = jnp.mean(scaled, axis=-1, keepdims=True)
        mean_proj = jnp.mean(scaled * unit, axis=-1, keepdims=True)
        gt_ref[b] = gres_ref[at, :] + inverse * (scaled - mean_grad - unit * mean_proj)
    small_ref[...] = part_ref[...]
    small_ref[experts : experts + 1, :] = total


def cost(microseconds):
    return int(microseconds * 1.1e9)


def call(kernel, outs, args, scratch=(), flops=0, name=None, scalars=1, grant=16, **static):
    spec = pl.BlockSpec(memory_space=pltpu.VMEM)
    word = pl.BlockSpec(memory_space=pltpu.SMEM)
    moved = sum(math.prod(a.shape) * a.dtype.itemsize for a in args)
    return pl.pallas_call(
        functools.partial(kernel, **static),
        out_shape=[jax.ShapeDtypeStruct(s, d) for s, d in outs],
        in_specs=[word] * scalars + [spec] * (len(args) - scalars),
        out_specs=[spec] * len(outs),
        scratch_shapes=list(scratch),
        compiler_params=pltpu.CompilerParams(vmem_limit_bytes=grant << 20),
        cost_estimate=pl.CostEstimate(flops=flops, bytes_accessed=moved, transcendentals=0),
        name=name,
    )(*args)


def make(mesh):
    dp, mp = mesh.shape["dp"], mesh.shape["mp"]

    def per_device(
        tokens, token_mask, gain_one, w_qkv, w_out, gain_two, router, w_in, w_back, cotangent
    ):
        rows, width = tokens.shape
        seq = token_mask.shape[1]
        tall = -(-seq // 16) * 16
        images = rows // seq
        experts = router.shape[1]
        d_rows, _, part = w_qkv.shape
        count = images * tall
        high = dp // 2
        heads = part // HEAD_DIM
        ready = d_rows % 16 != 0
        each = 2 * (1 << (images - 1).bit_length())
        me = lax.axis_index("dp")
        at_mp = lax.axis_index("mp")
        core = at_mp & 1
        words = jnp.stack([me, core, at_mp]).astype(jnp.int32)
        static = {"images": images, "tall": tall}
        exact = {"images": images, "seq": seq, "tall": tall}

        columns = experts + 2
        half = 2 * part
        hbm = pl.BlockSpec(memory_space=pltpu.HBM)
        vmem = pl.BlockSpec(memory_space=pltpu.VMEM)
        word = pl.BlockSpec(memory_space=pltpu.SMEM)
        wide = columns + -columns % 128
        shapes = [(3, d_rows, part), (part, d_rows), (1, d_rows), (1, d_rows), (experts, d_rows)]
        qkv = w_qkv.transpose(1, 0, 2)
        qkv, words = lax.optimization_barrier((qkv, words))
        first = qkv[:, :, : 2 * HEAD_DIM]
        second, extra = pl.pallas_call(
            pack_kernel,
            out_shape=[jax.ShapeDtypeStruct((d_rows, n), bf16) for n in (half, wide)],
            in_specs=[word] + [hbm] * 5,
            out_specs=[vmem] * 2,
            scratch_shapes=[pltpu.VMEM(shape, bf16) for shape in shapes] + [pltpu.SemaphoreType.DMA((5,))],
            compiler_params=pltpu.CompilerParams(vmem_limit_bytes=4 << 20),
            cost_estimate=pl.CostEstimate(flops=cost(2), bytes_accessed=300_000, transcendentals=0),
            name="pack",
        )(words, qkv, w_out, gain_one[None], gain_two[None], router.T)

        first, second, held_extra = first[None], second[None], extra[None]
        stages = bits_of(dp)[:-1]
        for bit in stages:
            other = swap(first, "dp", dp, bit)
            if bit == stages[0]:
                other, second, held_extra = lax.optimization_barrier((other, second, held_extra))
            first = join(first, other)
        held_extra = join(held_extra, swap(held_extra, "dp", dp, stages[0]))
        other, held_extra, late = lax.optimization_barrier(
            (swap_both(first, dp, mp, (1, 0), (0, 2)), held_extra, swap(second, "dp", dp, stages[0]))
        )
        second = join(second, late)
        for bit in stages[1:]:
            second = join(second, swap(second, "dp", dp, bit))
            held_extra = join(held_extra, swap(held_extra, "dp", dp, bit))
        held_extra = join(held_extra, swap(held_extra, "dp", dp, 1))
        held_extra = held_extra.reshape((dp,) + extra.shape)
        if ready:
            held_extra = reorder(unmirrored(held_extra), me).reshape(1, width, -1)
        x3 = tokens.reshape(images, seq, width)
        cot3 = cotangent.reshape(images, seq, width)
        h_one, h_turned, ex = call(
            prep_kernel,
            [((count, width), bf16), ((width, count), bf16), ((held_extra.shape[2], width), f32)],
            (words, x3, held_extra),
            flops=cost(2),
            name="prep",
            grant=4,
            **exact,
        )
        near = join(first, other).reshape((2,) + first.shape)
        far = swap_both(near, dp, mp, (0, 2), (1, 0))
        second = second.reshape((high, d_rows, half))
        other = swap_both(second, dp, mp, (1, 0), (0, 2))
        far, h_one, other = lax.optimization_barrier((far, h_one, other))
        first = (near, far, swap(near, "mp", mp, 1), swap(far, "mp", mp, 1))
        near = join(second, other).reshape((2, high, d_rows, half))
        second_near, second_far = near, swap_both(near, dp, mp, (0, 2), (1, 0))
        second_near_other = swap(second_near, "mp", mp, 1)

        def whole(x, of_core, near, far, other_near, other_far):
            mine = core == of_core
            low = jnp.where(mine, near, other_near)
            high_part = jnp.where(mine, far, other_far)
            blocks = jnp.stack([low[x], high_part[x]]) if of_core else (high_part if x else low)
            blocks = blocks.reshape((dp,) + near.shape[2:])
            blocks = reorder(unmirrored(blocks), me)
            if blocks.ndim == 4:
                blocks = blocks.transpose(0, 2, 1, 3)
            return blocks.reshape(width, half)

        def weights_of(parts):
            if ready:
                return tuple(whole(j & 1, j >> 1, *parts) for j in range(4))
            return parts

        def saved(kept, columns, probs):
            return [
                ((mp, width, kept), bf16),
                ((mp, count, columns), bf16),
                ((mp, images) + probs + (tall, tall), bf16),
                ((mp, count, 128), bf16),
            ]

        pair = call(
            front_pair_kernel,
            saved(half, 384, (2,)),
            (words, h_one, token_mask) + weights_of(first),
            flops=cost(10),
            name="front_pair",
            grant=10,
            ready=ready,
            **static,
        )
        w_a, qkv_a, p_a, ho_a = pair
        second_far, ho_a = lax.optimization_barrier((second_far, ho_a))
        second = (second_near, second_far, second_near_other, swap(second_far, "mp", mp, 1))
        w_b, qkv_b, p_b, heads_out, w_heads, branch = call(
            front_last_kernel,
            saved(256, 256, ())[:3]
            + [
                ((count, 256 * mp), bf16),
                ((width, 256 * mp), bf16),
                ((count, width), f32),
            ],
            (words, h_one, token_mask, ho_a) + weights_of(second),
            flops=cost(7),
            name="front_last",
            grant=10,
            ready=ready,
            **static,
        )
        resid, h_two, soft, sent, sq_branch = call(
            route_kernel,
            [
                ((count, width), f32),
                ((count, width), bf16),
                ((2, images, experts, tall), f32),
                ((experts * each, width), bf16),
                ((images, 1, 128), f32),
            ],
            (words, x3, branch, cot3, token_mask, ex),
            flops=cost(2),
            name="route",
            grant=6,
            experts=experts,
            **exact,
        )
        got = sent.reshape(dp, each, width)
        got = lax.all_to_all(got, "dp", split_axis=0, concat_axis=0, tiled=True)
        got = gather_mp(got, mp).reshape(-1, width)
        everyone = got.shape[0]
        hidden, grad_pre, grad_expert, back = call(
            expert_kernel,
            [
                ((everyone, w_in.shape[2]), bf16),
                ((everyone, w_in.shape[2]), bf16),
                ((everyone, width), bf16),
                ((everyone, width), bf16),
            ],
            (got, w_in[0], w_back[0]),
            flops=cost(2),
            name="expert",
            scalars=0,
            grant=12 if dp <= 8 else 56,
            each=each,
        )
        back = back.reshape(mp, dp, each, width)
        back = scatter(back, "mp", mp, [1, 2])
        back = lax.all_to_all(back, "dp", split_axis=0, concat_axis=0, tiled=True)
        back = back.reshape(dp, 2, each // 2, width)[:, :, :images].transpose(1, 2, 0, 3)
        grad_w_back = mm_tn(hidden, grad_expert)
        grad_w_in = mm_tn(got, grad_pre)

        out_rows, grad_resid, grad_low, grad_turned, small = call(
            mix_kernel,
            [
                ((images, seq, width), bf16),
                ((count, width), f32),
                ((count, width), bf16),
                ((width, count), bf16),
                ((experts + 5, width), f32),
            ],
            (words, resid, h_two, soft, cot3, token_mask, ex, back, sq_branch),
            flops=cost(5),
            name="mix",
            grant=8,
            experts=experts,
            groups=mp,
            **exact,
        )
        shape = (1, 1, width, 4 * part) if ready else (2, high, d_rows, 4 * part)

        def back_of(x, flip, grad_in):
            grads, joined = call(
                back_kernel,
                [(shape, bf16), ((count, JOINED), bf16)],
                (words, grad_in, grad_turned, h_turned, qkv_a, p_a, qkv_b, p_b, heads_out, w_heads),
                [pltpu.VMEM((count, 256), f32)],
                flops=cost(8),
                name="back",
                grant=10,
                x=x,
                flip=flip,
                **static,
            )
            if ready:
                grads = reorder(grads.reshape(dp, d_rows, 4 * part), me)
                grads = grads.reshape(high, 2, d_rows, 4 * part).transpose(1, 0, 2, 3)
            return grads, joined

        def fold(terms, halves, starts=None, kept_columns=4 * part):
            size = terms[0].shape
            kept = ((size[0] // 2,) + size[1:-1] + (kept_columns,), bf16)
            return call(
                fold_kernel,
                [kept, kept],
                terms,
                flops=cost(1),
                name="fold",
                scalars=0,
                grant=6,
                halves=halves,
                starts=starts or (0,) * len(terms),
            )

        order = ((1, 1), (1, 0), (0, 1), (0, 0))
        sent_grads, joined_a = back_of(1, 1, grad_low)
        other = swap(sent_grads, "mp", mp, 1)
        grad_low, joined_a = lax.optimization_barrier((grad_low, joined_a))
        kept_grads, joined_b = back_of(1, 0, grad_low)
        far_kept, far_left = fold((kept_grads, other), True)
        far_left, grad_low, joined_b = lax.optimization_barrier((far_left, grad_low, joined_b))
        early = swap_both(far_left[0], dp, mp, (0, 2), (1, 0))
        sent_grads, joined_c = back_of(0, 1, grad_low)
        grad_low, joined_c = lax.optimization_barrier((grad_low, joined_c))
        other = swap(sent_grads, "mp", mp, 1)
        kept_grads, joined_d = back_of(0, 0, grad_low)
        part_shape = ((high, d_rows, 4 * part), bf16)
        near_sum, own_sum, second = call(
            blend_kernel,
            [part_shape] * 3,
            (words, far_kept[0], kept_grads, other),
            flops=cost(1),
            name="blend",
            grant=8,
        )
        second = swap_both(second, dp, mp, (0, 2), (1, 0))
        grad_h = call(
            input_kernel,
            [((count, width), f32)],
            (words, w_a, w_b, joined_a, joined_b, joined_c, joined_d),
            flops=cost(4),
            name="input",
            grant=8,
            order=order,
        )[0]
        early, grad_h = lax.optimization_barrier((early, grad_h))
        thirds = call(
            blend_late_kernel,
            [((high, d_rows, half), bf16)] * 2,
            (words, far_kept[0], own_sum, early),
            flops=cost(1),
            name="blend_late",
            grant=8,
        )
        thirds = [swap_both(third, dp, mp, (1, 0), (0, 2)) for third in thirds]
        pieces = [
            list(fold((near_sum, second, third), False, (k * half, k * half, 0), half))
            for k, third in enumerate(thirds)
        ]
        grad_tokens, small = call(
            last_kernel,
            [((images, seq, width), f32), ((experts + 5, width), f32)],
            (x3, grad_resid, grad_h, ex, small),
            flops=cost(0.1),
            name="last",
            scalars=0,
            grant=8,
            experts=experts,
            **exact,
        )
        for bit in bits_of(dp)[:-1]:
            small = small + swap(small, "dp", dp, bit)
        parts = []
        for k, (kept, left) in enumerate(pieces):
            for bit in bits_of(high)[:0:-1]:
                other = swap(left, "dp", dp, 2 * bit)
                if k == 0:
                    other, small = lax.optimization_barrier((other, small))
                kept, left = fold((kept, other), False, None, half)
            parts += [kept[0], swap(left[0], "dp", dp, 2 * bits_of(high)[0])]
        grad_qkv, grad_out = call(
            unpack_kernel,
            [((3, d_rows, part), f32), ((part, d_rows), f32)],
            parts,
            flops=cost(1),
            name="unpack",
            scalars=0,
            grant=6,
        )
        small = small + swap(small, "dp", dp, 1)
        small = small + swap(small, "mp", mp, 2)
        grad_one, grad_two, grad_router, root_squares = call(
            finish_kernel,
            [
                ((1, d_rows), f32),
                ((1, d_rows), f32),
                ((experts, d_rows), f32),
                ((3, mp * images), f32),
            ],
            (words, small, swap(small, "mp", mp, 1)),
            flops=cost(1),
            name="finish",
            grant=4,
        )
        return (
            out_rows.reshape(rows, width),
            grad_tokens.reshape(rows, width),
            grad_one[0],
            grad_qkv.transpose(1, 0, 2),
            grad_out,
            grad_two[0],
            grad_router.T,
            grad_w_in[None],
            grad_w_back[None],
            root_squares,
        )

    return per_device


def solution(mesh):
    in_specs = (
        P(("dp", "mp"), None),
        P("dp", None),
        P("dp"),
        P("dp", None, "mp"),
        P("mp", "dp"),
        P("dp"),
        P("dp", None),
        P("dp", None, "mp"),
        P("dp", "mp", None),
        P(("dp", "mp"), None),
    )
    out_specs = (
        P(("dp", "mp"), None),
        P(("dp", "mp"), None),
        P("dp"),
        P("dp", None, "mp"),
        P("mp", "dp"),
        P("dp"),
        P("dp", None),
        P("dp", None, "mp"),
        P("dp", "mp", None),
        P(None, "dp"),
    )
    return jax.shard_map(
        make(mesh), mesh=mesh, in_specs=in_specs, out_specs=out_specs, check_vma=False
    )
```

```python
import functools
import math

import jax
import jax.numpy as jnp
from jax import lax
from jax.experimental import pallas as pl
from jax.experimental.pallas import tpu as pltpu
from jax.sharding import PartitionSpec as P

HEAD_DIM = 64


epsilon = 1e-06
bf16 = jnp.bfloat16
f32 = jnp.float32


def bits_of(size):
    return [1 << k for k in reversed(range(size.bit_length() - 1))]


def swap(array_in, axis_name, size, bit):
    return lax.ppermute(array_in, axis_name, [(i, i ^ bit) for i in range(size)])


def swap_both(array_in, dp, mp, even, odd):
    pairs = []
    for d in range(dp):
        for m in range(mp):
            flip = odd if m & 1 else even
            pairs.append((d * mp + m, (d ^ flip[0]) * mp + (m ^ flip[1])))
    return lax.ppermute(array_in, ("dp", "mp"), pairs)


def gather_mp(block, mp):
    held = block[None]
    for bit in bits_of(mp):
        other = swap(held, "mp", mp, bit)
        held = jnp.stack([held, other], 1).reshape((-1,) + block.shape)
    return held


def scatter(held, axis_name, size, bits, unit=1):
    left = sorted(bits)
    for bit in bits:
        inner = 1 << left.index(bit)
        left.remove(bit)
        pairs = held.reshape((held.shape[0] // (2 * inner), 2, inner) + held.shape[1:])
        other = swap(pairs[:, 1], axis_name, size, bit * unit)
        held = pairs[:, 0].astype(f32) + other.astype(f32)
        held = held.astype(bf16).reshape((-1,) + held.shape[2:])
    return held[0]


def mirrored(index, size):
    bits = size.bit_length() - 1
    return sum(((index >> k) & 1) << (bits - 1 - k) for k in range(bits)) if bits else index


def unmirrored(blocks):
    size = blocks.shape[0]
    bits = size.bit_length() - 1
    split = blocks.reshape((2,) * bits + blocks.shape[1:])
    turn = tuple(range(bits))[::-1] + tuple(range(bits, split.ndim))
    return split.transpose(turn).reshape(blocks.shape)


def reorder(blocks, me):
    size = blocks.shape[0]
    for bit in bits_of(size):
        pairs = blocks.reshape((size // (2 * bit), 2, bit) + blocks.shape[1:])
        blocks = jnp.where((me & bit) > 0, pairs[:, ::-1], pairs).reshape(blocks.shape)
    return blocks


def mm(a, b):
    return lax.dot_general(a, b, (((1,), (0,)), ((), ())), preferred_element_type=f32)


def mm_nt(a, b):
    return lax.dot_general(a, b, (((1,), (1,)), ((), ())), preferred_element_type=f32)


def mm_tn(a, b):
    return lax.dot_general(a, b, (((0,), (0,)), ((), ())), preferred_element_type=f32)


def unit_of(rows_f):
    mean_row = jnp.mean(rows_f, axis=-1, keepdims=True)
    centered = rows_f - mean_row
    variance = jnp.mean(centered * centered, axis=-1, keepdims=True)
    inverse = lax.rsqrt(variance + epsilon)
    return centered * inverse, inverse


def padded(value, pad):
    return jnp.concatenate([value, jnp.zeros((pad, value.shape[1]), value.dtype)], 0)


def low_lanes(rows):
    return lax.broadcasted_iota(jnp.int32, (rows, 128), 1) < HEAD_DIM


JOINED = 640


def pack_kernel(
    me_ref, qkv_hbm, out_hbm, one_hbm, two_hbm, router_hbm, second_ref, extra_ref,
    qkv_ref, out_ref, one_ref, two_ref, router_ref, sems
):
    del me_ref
    pairs = (
        (qkv_hbm, qkv_ref), (out_hbm, out_ref), (one_hbm, one_ref), (two_hbm, two_ref), (router_hbm, router_ref),
    )
    copies = [pltpu.make_async_copy(a, b, sems.at[k]) for k, (a, b) in enumerate(pairs)]
    for copy in copies:
        copy.start()
    low, mid = 2 * HEAD_DIM, qkv_ref.shape[2]
    for copy in copies:
        copy.wait()
    out = out_ref[...].astype(f32).T.astype(bf16)
    second_ref[...] = jnp.concatenate(
        [qkv_ref[c, :, low:mid] for c in range(3)] + [out[:, low:mid], out[:, :low]], axis=1
    )
    rows = one_ref.shape[1]
    columns = [one_ref[...], two_ref[...], router_ref[...]]
    columns = [value.astype(f32) for value in columns]
    filled = sum(value.shape[0] for value in columns)
    columns.append(jnp.zeros((extra_ref.shape[1] - filled, rows), f32))
    extra_ref[...] = jnp.concatenate(columns, 0).T.astype(bf16)


def join_kernel(a_ref, b_ref, out_ref):
    size = a_ref.shape[0]
    out_ref[:size] = a_ref[...]
    out_ref[size:] = b_ref[...]


def join(a, b):
    shape = (a.shape[0] + b.shape[0],) + a.shape[1:]
    return call(join_kernel, [(shape, a.dtype)], (a, b), flops=1000, name="join", scalars=0, grant=4)[0]


def fold_kernel(*refs, halves, starts):
    terms, (kept_ref, left_ref) = refs[:-2], refs[-2:]
    size, columns = terms[0].shape[0], kept_ref.shape[-1]
    for k in range(size):
        total = None
        for term, start in zip(terms, starts):
            value = term[k][..., start : start + columns].astype(f32)
            total = value if total is None else total + value
        at, odd = (k % (size // 2), k >= size // 2) if halves else (k // 2, k % 2 == 1)
        (left_ref if odd else kept_ref)[at] = total.astype(bf16)


def blend_kernel(me_ref, far_ref, kept_ref, other_ref, near_ref, own_ref, second_ref):
    for k, ref in ((0, near_ref), (1, own_ref)):
        ref[...] = (kept_ref[k].astype(f32) + other_ref[k].astype(f32)).astype(bf16)
    first_core = me_ref[1] == 0

    @pl.when(first_core)
    def _():
        second_ref[...] = far_ref[...]

    @pl.when(jnp.logical_not(first_core))
    def _():
        second_ref[...] = own_ref[...]


def blend_late_kernel(me_ref, far_ref, own_ref, early_ref, *thirds):
    columns = thirds[0].shape[-1]
    for core, ref in ((0, own_ref), (1, far_ref)):

        @pl.when(me_ref[1] == core)
        def _(ref=ref):
            for k, third in enumerate(thirds):
                at = slice(k * columns, (k + 1) * columns)
                total = ref[..., at].astype(f32) + early_ref[..., at].astype(f32)
                third[...] = total.astype(bf16)


def finish_kernel(me_ref, own_ref, other_ref, one_ref, two_ref, router_ref, root_ref):
    experts, rows = router_ref.shape
    total = own_ref[...] + other_ref[...]
    width = total.shape[1]
    mine = pltpu.roll(total, lax.rem(width - me_ref[0] * rows, width), 1)
    one_ref[...] = mine[experts : experts + 1, :rows]
    two_ref[...] = mine[experts + 1 : experts + 2, :rows]
    router_ref[...] = mine[:experts, :rows]
    images = root_ref.shape[1]
    mine = pltpu.roll(total, lax.rem(width - me_ref[0] * images, width), 1)
    root_ref[...] = mine[experts + 2 : experts + 5, :images]


def unpack_kernel(own_a, other_a, own_b, other_b, qkv_ref, out_ref):
    low, mid = 2 * HEAD_DIM, qkv_ref.shape[2]
    pair = own_a[...].astype(f32) + other_a[...].astype(f32)
    rest = own_b[...].astype(f32) + other_b[...].astype(f32)
    for c in range(3):
        qkv_ref[c, :, :low] = pair[:, c * low : (c + 1) * low]
        qkv_ref[c, :, low:mid] = rest[:, c * HEAD_DIM : (c + 1) * HEAD_DIM]
    out_ref[...] = jnp.concatenate([rest[:, 256:], rest[:, 192:256]], axis=1).T


def length_of(mask_ref, me_ref, b, images):
    row = mask_ref[pl.ds(me_ref[2] * images + b, 1), :]
    return jnp.sum(row.astype(f32), axis=1, keepdims=True)


def seen_row(length, tall):
    return lax.broadcasted_iota(jnp.int32, (1, tall), 1).astype(f32) < length


def seen_column(length, tall):
    return lax.broadcasted_iota(jnp.int32, (tall, 1), 0).astype(f32) < length


def prep_kernel(me_ref, x_ref, extra_ref, h_ref, ht_ref, small_ref, *, images, seq, tall):
    blocks = extra_ref.shape[0]
    me = me_ref[0]
    parts = [extra_ref[mirrored(me ^ d, blocks) if blocks > 1 else 0] for d in range(blocks)]
    small_ref[...] = jnp.concatenate(parts, 0).astype(f32).T
    gain = small_ref[0:1, :]
    for b in range(images):
        unit, _ = unit_of(x_ref[b].astype(f32))
        h_ref[pl.ds(b * tall, tall), :] = padded((unit * gain).astype(bf16), tall - seq)
    ht_ref[...] = h_ref[...].T


def fetch_all(me_ref, refs, put):
    rows, high_size = refs[0].shape[-2], refs[0].shape[1]
    for core in (0, 1):

        @pl.when(me_ref[1] == core)
        def _(core=core):
            for slot in range(4):
                x, of_core = slot & 1, slot >> 1
                first, second = refs[:2] if of_core == core else refs[2:4]
                for r in range(2 * high_size):
                    low, high = r & 1, mirrored(r >> 1, high_size)
                    if of_core == 0:
                        block = (second if x else first)[low, high]
                    else:
                        block = (second if low else first)[x, high]
                    d = jnp.bitwise_xor(me_ref[0], r)
                    put(slot, pl.ds(pl.multiple_of(d * rows, 16), rows), block)


def attend(triples):
    scores = [mm_nt(q, k) * HEAD_DIM ** (-0.5) + bias for q, k, _, bias in triples]
    terms = [jnp.exp(value - jnp.max(value, axis=-1, keepdims=True)) for value in scores]
    probs = [
        (value * (1.0 / jnp.sum(value, axis=-1, keepdims=True))).astype(bf16) for value in terms
    ]
    return probs, [mm(value, v) for value, (_, _, v, _) in zip(probs, triples)]


def bias_of(mask_ref, me_ref, b, images, tall):
    return jnp.where(seen_row(length_of(mask_ref, me_ref, b, images), tall), 0.0, -1e30)


def front_pair_kernel(me_ref, h_ref, mask_ref, *refs, images, tall, ready):
    w_ref, qkv_ref, p_ref, ho_ref = refs[4:]

    def put(slot, at, block):
        for c in range(3):
            w_ref[slot, at, c * 128 : (c + 1) * 128] = block[c]

    if ready:
        for slot in range(4):
            w_ref[slot] = refs[slot][...]
    else:
        fetch_all(me_ref, refs[:4], put)
    low = low_lanes(tall)

    def group(j, carry):
        qkv_ref[j] = mm(h_ref[...], w_ref[j]).astype(bf16)
        triples = []
        for b in range(images):
            joined = qkv_ref[j, pl.ds(b * tall, tall), :]
            q, k, v = joined[:, :128], joined[:, 128:256], joined[:, 256:384]
            none = jnp.zeros_like(q)
            bias = bias_of(mask_ref, me_ref, b, images, tall)
            triples.append((jnp.where(low, q, none), k, v, bias))
            triples.append((jnp.where(low, none, q), k, v, bias))
        probs, outs = attend(triples)
        for b in range(images):
            p_ref[j, b, 0], p_ref[j, b, 1] = probs[2 * b], probs[2 * b + 1]
            pair = jnp.where(low, outs[2 * b], outs[2 * b + 1])
            ho_ref[j, pl.ds(b * tall, tall), :] = pair.astype(bf16)
        return carry

    lax.fori_loop(0, w_ref.shape[0], group, 0)


def front_last_kernel(me_ref, h_ref, mask_ref, pair_ref, *refs, images, tall, ready, flip):
    w_ref, qkv_ref, p_ref, ho_ref, wo_ref, br_ref = refs[-6:]

    def put(slot, at, block):
        w_ref[slot, at, :] = block[:, :256]
        wo_ref[at, slot * 256 : (slot + 1) * 256] = block[:, 128:]

    if ready:
        for slot in range(2):
            put(slot, slice(None), refs[slot][...])
    else:
        near, far = refs[:2]
        rows, high_size = near.shape[-2], near.shape[1]
        for core in (0, 1):

            @pl.when(me_ref[1] == core)
            def _(core=core):
                for x in (0, 1):
                    for r in range(2 * high_size):
                        low, high = r & 1, mirrored(r >> 1, high_size)
                        if core == flip:
                            block = (far if x else near)[low, high]
                        else:
                            block = (far if low else near)[x, high]
                        d = jnp.bitwise_xor(me_ref[0], r)
                        put(x, pl.ds(pl.multiple_of(d * rows, 16), rows), block)

    low = low_lanes(tall)
    places = [(x, b) for x in (0, 1) for b in range(images)]
    for x in (0, 1):
        qkv_ref[x] = mm(h_ref[...], w_ref[x]).astype(bf16)
    triples = []
    for x, b in places:
        joined = qkv_ref[x, pl.ds(b * tall, tall), :]
        qk, v = joined[:, :128], joined[:, 128:256]
        k = pltpu.roll(qk.astype(f32), HEAD_DIM, 1).astype(bf16)
        bias = bias_of(mask_ref, me_ref, b, images, tall)
        triples.append((jnp.where(low, qk, jnp.zeros_like(qk)), k, v, bias))
    probs, outs = attend(triples)
    of_core = jnp.bitwise_xor(me_ref[1], flip)
    for (x, b), prob, out in zip(places, probs, outs):
        at, start = pl.ds(b * tall, tall), x * 256
        p_ref[x, b] = prob
        ho_ref[at, start : start + 128] = jnp.where(low, 0.0, pltpu.roll(out, HEAD_DIM, 1)).astype(bf16)
        ho_ref[at, start + 128 : start + 256] = pair_ref[x + 2 * of_core, at, :]
    branch = mm_nt(ho_ref[...], wo_ref[...])
    br_ref[...] = branch + refs[2][...] if flip else branch


def spot(rows, b, start, experts):
    each = rows // experts
    at_row = lax.broadcasted_iota(jnp.int32, (rows, experts), 0)
    at_column = lax.broadcasted_iota(jnp.int32, (rows, experts), 1)
    return jnp.where(at_row == at_column * each + (start + b), 1.0, 0.0).astype(bf16)


def route_kernel(
    me_ref, x_ref, br_ref, cot_ref, mask_ref, ex_ref,
    res_ref, h_ref, soft_ref, sent_ref, sq_ref, *, images, seq, tall, experts
):
    rows = sent_ref.shape[0]
    half = rows // experts // 2
    router = ex_ref[2 : 2 + experts, :].astype(bf16)
    gain = ex_ref[1:2, :]
    total = jnp.zeros(sent_ref.shape, f32)
    for b in range(images):
        at = pl.ds(b * tall, tall)
        length = length_of(mask_ref, me_ref, b, images)
        branch = br_ref[at, :]
        resid = padded(x_ref[b].astype(f32), tall - seq) + branch
        res_ref[at, :] = resid
        unit, _ = unit_of(resid)
        h_two = (unit * gain).astype(bf16)
        h_ref[at, :] = h_two
        logits = mm_nt(router, h_two)
        held = jnp.where(seen_row(length, tall), logits, -1e30)
        terms = jnp.exp(held - jnp.max(held, axis=1, keepdims=True))
        dispatch = terms / jnp.sum(terms, axis=1, keepdims=True)
        terms = jnp.exp(logits - jnp.max(logits, axis=0, keepdims=True))
        combine = terms / jnp.sum(terms, axis=0, keepdims=True)
        soft_ref[0, b] = dispatch
        soft_ref[1, b] = combine
        cot = padded(cot_ref[b], tall - seq)
        wide_d = mm(spot(rows, b, 0, experts), dispatch.astype(bf16)).astype(bf16)
        wide_c = mm(spot(rows, b, half, experts), combine.astype(bf16)).astype(bf16)
        total += mm(wide_d, h_two) + mm(wide_c, cot)
        squares = jnp.sum(branch * branch, axis=1, keepdims=True)
        squares = jnp.sum(jnp.where(seen_column(length, tall), squares, 0.0), axis=0, keepdims=True)
        sq_ref[b] = jnp.broadcast_to(squares, (1, 128))
    sent_ref[...] = total.astype(bf16)


def expert_kernel(got_ref, first_ref, second_ref, hid_ref, pre_ref, grad_ref, back_ref, *, each):
    rows = got_ref.shape[0]
    half = each // 2
    got = got_ref[...]
    own = jnp.bitwise_and(lax.broadcasted_iota(jnp.int32, (rows, 1), 0), each - 1) < half
    grads = jnp.where(own, pltpu.roll(got.astype(f32), rows - half, 0), 0.0).astype(bf16)
    grad_ref[...] = grads
    u = mm(got, first_ref[...])
    cubic = 0.7978845608028654 * (u + 0.044715 * u * u * u)
    t = jnp.tanh(cubic)
    hidden = jnp.where(own, 0.5 * u * (1.0 + t), 0.0).astype(bf16)
    hid_ref[...] = hidden
    slope = 0.5 * (1.0 + t) + 0.5 * u * (1.0 - t * t) * 0.7978845608028654 * (
        1.0 + 3.0 * 0.044715 * u * u
    )
    grad_pre = (mm_nt(grads, second_ref[...]) * slope).astype(bf16)
    pre_ref[...] = grad_pre
    out = mm(hidden, second_ref[...])
    grad_in = mm_nt(grad_pre, first_ref[...])
    back_ref[...] = jnp.where(own, out, pltpu.roll(grad_in, half, 0)).astype(bf16)


def mix_kernel(
    me_ref, res_ref, h_ref, soft_ref, cot_ref, mask_ref, ex_ref, back_ref, sq_ref,
    out_ref, gres_ref, gb_ref, gbt_ref, small_ref, *, images, seq, tall, experts, groups
):
    small_ref[...] = jnp.zeros_like(small_ref)
    router = ex_ref[2 : 2 + experts, :].astype(bf16)
    gain = ex_ref[1:2, :]
    width = out_ref.shape[2]
    lanes = lax.broadcasted_iota(jnp.int32, (1, width), 1)
    roots = [jnp.zeros((1, width), f32) for _ in range(3)]
    for b in range(images):
        at = pl.ds(b * tall, tall)
        length = length_of(mask_ref, me_ref, b, images)
        resid, h_two = res_ref[at, :], h_ref[at, :]
        dispatch, combine = soft_ref[0, b], soft_ref[1, b]
        dispatch_low, combine_low = dispatch.astype(bf16), combine.astype(bf16)
        returned, grad_slots = back_ref[0, b], back_ref[1, b]
        cot = padded(cot_ref[b], tall - seq)
        mixed = mm_tn(combine_low, returned)
        stream = resid + mixed
        out_ref[b] = stream[:seq].astype(bf16)
        column = seen_column(length, tall)
        sums = []
        for value in (stream, mixed):
            squares = jnp.sum(value * value, axis=1, keepdims=True)
            sums.append(jnp.sum(jnp.where(column, squares, 0.0), axis=0, keepdims=True))
        sums.insert(1, sq_ref[b, :, 0:1])
        for k, value in enumerate(sums):
            root = jnp.sqrt(value / (length * width))
            mine = lanes == (me_ref[0] * groups + me_ref[2]) * images + b
            roots[k] += jnp.where(mine, root, 0.0)
        grad_c = mm_nt(returned, cot)
        grad_c = combine * (grad_c - jnp.sum(grad_c * combine, axis=0, keepdims=True))
        grad_d = mm_nt(grad_slots, h_two)
        grad_d = dispatch * (grad_d - jnp.sum(grad_d * dispatch, axis=1, keepdims=True))
        grad_logits = (grad_d + grad_c).astype(bf16)
        grad_h = mm_tn(dispatch_low, grad_slots) + mm_tn(grad_logits, router)
        small_ref[0:experts, :] += mm(grad_logits, h_two)
        unit, inverse = unit_of(resid)
        small_ref[experts + 1 : experts + 2, :] += jnp.sum(grad_h * unit, axis=0, keepdims=True)
        scaled = grad_h * gain
        mean_grad = jnp.mean(scaled, axis=-1, keepdims=True)
        mean_proj = jnp.mean(scaled * unit, axis=-1, keepdims=True)
        gres_ref[at, :] = cot.astype(f32) + inverse * (scaled - mean_grad - unit * mean_proj)
    for k in range(3):
        small_ref[experts + 2 + k : experts + 3 + k, :] = roots[k]
    gb_ref[...] = gres_ref[...].astype(bf16)
    gbt_ref[...] = gres_ref[...].T.astype(bf16)


def back_kernel(
    me_ref, gb_ref, gbt_ref, ht_ref, qkv_a, p_a, qkv_b, p_b, ho_ref, wo_ref,
    gw_ref, gj_ref, dho_ref, *, images, tall, x, flip
):
    j = x + 2 * jnp.bitwise_xor(me_ref[1], flip)
    own = slice(x * 256, (x + 1) * 256)
    scale = HEAD_DIM ** (-0.5)
    low = low_lanes(tall)
    dho_ref[...] = mm(gb_ref[...], wo_ref[:, own])
    heads, dots = [], []
    for b in range(images):
        at = pl.ds(b * tall, tall)
        joined, joined_last = qkv_a[j, at, :], qkv_b[x, at, :]
        q_pair, k_pair, v_pair = joined[:, :128], joined[:, 128:256], joined[:, 256:384]
        qk_last, v_last = joined_last[:, :128], joined_last[:, 128:256]
        grad = dho_ref[at, :].astype(bf16).astype(f32)
        product = grad * ho_ref[at, own].astype(f32)
        single, pair = product[:, :128], product[:, 128:]
        dots += [
            jnp.sum(jnp.where(low, pair, 0.0), axis=1, keepdims=True),
            jnp.sum(jnp.where(low, 0.0, pair), axis=1, keepdims=True),
            jnp.sum(single, axis=1, keepdims=True),
        ]
        grad_pair = grad[:, 128:]
        grad_last = jnp.where(low, pltpu.roll(grad[:, :128], HEAD_DIM, 1), 0.0).astype(bf16)
        heads += [
            (p_a[j, b, 0], jnp.where(low, grad_pair, 0.0).astype(bf16), v_pair, q_pair, k_pair),
            (p_a[j, b, 1], jnp.where(low, 0.0, grad_pair).astype(bf16), v_pair, q_pair, k_pair),
            (p_b[x, b], grad_last, v_last, qk_last, qk_last),
        ]
    grad_p = [mm_nt(g, v) for _, g, v, _, _ in heads]
    grad_s = [
        (probs.astype(f32) * (value - dot)).astype(bf16)
        for (probs, _, _, _, _), value, dot in zip(heads, grad_p, dots)
    ]
    gqs = [mm(value, k) for value, (_, _, _, _, k) in zip(grad_s, heads)]
    gks = [mm_tn(value, q) for value, (_, _, _, q, _) in zip(grad_s, heads)]
    gvs = [mm_tn(probs, g) for probs, g, _, _, _ in heads]
    for b in range(images):
        at = pl.ds(b * tall, tall)
        gq, gk, gv = (value[3 * b : 3 * b + 3] for value in (gqs, gks, gvs))
        last = pltpu.roll(jnp.where(low, gk[2], gq[2]), HEAD_DIM, 1)
        gj_ref[at, :] = jnp.concatenate(
            [
                jnp.where(low, gq[0], gq[1]) * scale,
                jnp.where(low, gk[0], gk[1]) * scale,
                gv[0] + gv[1],
                last * scale,
                gv[2],
            ],
            1,
        ).astype(bf16)
    grad_out = mm(gbt_ref[...], ho_ref[:, own])
    grad_in = mm(ht_ref[...], gj_ref[...])
    halves, blocks, rows = gw_ref.shape[:3]
    for d in range(halves * blocks):
        r = jnp.bitwise_xor(me_ref[0], d) if halves > 1 else 0
        entry = (jnp.bitwise_and(r, 1), jnp.right_shift(r, 1)) if halves > 1 else (0, 0)
        at = slice(d * rows, (d + 1) * rows)
        gw_ref[entry + (slice(None), slice(0, 512))] = grad_in[at, :512].astype(bf16)
        gw_ref[entry + (slice(None), slice(512, 640))] = (
            grad_in[at, 512:] + grad_out[at, :128]
        ).astype(bf16)
        gw_ref[entry + (slice(None), slice(640, 768))] = grad_out[at, 128:].astype(bf16)


def input_kernel(me_ref, w_a, w_own, w_other, *refs, order):
    grads, gh_ref = refs[:-1], refs[-1]
    for k, (ref, (x, flip)) in enumerate(zip(grads, order)):
        j = x + 2 * jnp.bitwise_xor(me_ref[1], flip)
        into = mm_nt(ref[:, :384], w_a[j]) + mm_nt(ref[:, 384:], (w_own, w_other)[flip][x])
        if k == 0:
            gh_ref[...] = into
        else:
            gh_ref[...] += into


def last_kernel(x_ref, gres_ref, gh_ref, ex_ref, part_ref, gt_ref, small_ref, *, images, seq, tall, experts):
    total = jnp.zeros((1, x_ref.shape[2]), f32)
    gain = ex_ref[0:1, :]
    for b in range(images):
        at = pl.ds(b * tall, seq)
        unit, inverse = unit_of(x_ref[b].astype(f32))
        grad_h = gh_ref[at, :]
        total += jnp.sum(grad_h * unit, axis=0, keepdims=True)
        scaled = grad_h * gain
        mean_grad = jnp.mean(scaled, axis=-1, keepdims=True)
        mean_proj = jnp.mean(scaled * unit, axis=-1, keepdims=True)
        gt_ref[b] = gres_ref[at, :] + inverse * (scaled - mean_grad - unit * mean_proj)
    small_ref[...] = part_ref[...]
    small_ref[experts : experts + 1, :] = total


def cost(microseconds):
    return int(microseconds * 1.1e9)


def call(kernel, outs, args, scratch=(), flops=0, name=None, scalars=1, grant=16, **static):
    spec = pl.BlockSpec(memory_space=pltpu.VMEM)
    word = pl.BlockSpec(memory_space=pltpu.SMEM)
    moved = sum(math.prod(a.shape) * a.dtype.itemsize for a in args)
    return pl.pallas_call(
        functools.partial(kernel, **static),
        out_shape=[jax.ShapeDtypeStruct(s, d) for s, d in outs],
        in_specs=[word] * scalars + [spec] * (len(args) - scalars),
        out_specs=[spec] * len(outs),
        scratch_shapes=list(scratch),
        compiler_params=pltpu.CompilerParams(vmem_limit_bytes=grant << 20),
        cost_estimate=pl.CostEstimate(flops=flops, bytes_accessed=moved, transcendentals=0),
        name=name,
    )(*args)


def make(mesh):
    dp, mp = mesh.shape["dp"], mesh.shape["mp"]

    def per_device(
        tokens, token_mask, gain_one, w_qkv, w_out, gain_two, router, w_in, w_back, cotangent
    ):
        rows, width = tokens.shape
        seq = token_mask.shape[1]
        tall = -(-seq // 16) * 16
        images = rows // seq
        experts = router.shape[1]
        d_rows, _, part = w_qkv.shape
        count = images * tall
        high = dp // 2
        heads = part // HEAD_DIM
        ready = d_rows % 16 != 0
        each = 2 * (1 << (images - 1).bit_length())
        me = lax.axis_index("dp")
        at_mp = lax.axis_index("mp")
        core = at_mp & 1
        words = jnp.stack([me, core, at_mp]).astype(jnp.int32)
        static = {"images": images, "tall": tall}
        exact = {"images": images, "seq": seq, "tall": tall}

        columns = experts + 2
        half = 2 * part
        hbm = pl.BlockSpec(memory_space=pltpu.HBM)
        vmem = pl.BlockSpec(memory_space=pltpu.VMEM)
        word = pl.BlockSpec(memory_space=pltpu.SMEM)
        wide = columns + -columns % 128
        shapes = [(3, d_rows, part), (part, d_rows), (1, d_rows), (1, d_rows), (experts, d_rows)]
        qkv = w_qkv.transpose(1, 0, 2)
        qkv, words = lax.optimization_barrier((qkv, words))
        first = qkv[:, :, : 2 * HEAD_DIM]
        second, extra = pl.pallas_call(
            pack_kernel,
            out_shape=[jax.ShapeDtypeStruct((d_rows, n), bf16) for n in (half, wide)],
            in_specs=[word] + [hbm] * 5,
            out_specs=[vmem] * 2,
            scratch_shapes=[pltpu.VMEM(shape, bf16) for shape in shapes] + [pltpu.SemaphoreType.DMA((5,))],
            compiler_params=pltpu.CompilerParams(vmem_limit_bytes=4 << 20),
            cost_estimate=pl.CostEstimate(flops=cost(2), bytes_accessed=300_000, transcendentals=0),
            name="pack",
        )(words, qkv, w_out, gain_one[None], gain_two[None], router.T)

        first, second, held_extra = first[None], second[None], extra[None]
        stages = bits_of(dp)[:-1]
        for bit in stages:
            other = swap(first, "dp", dp, bit)
            if bit == stages[0]:
                other, second, held_extra = lax.optimization_barrier((other, second, held_extra))
            first = join(first, other)
        held_extra = join(held_extra, swap(held_extra, "dp", dp, stages[0]))
        other, held_extra, late = lax.optimization_barrier(
            (swap_both(first, dp, mp, (1, 0), (0, 2)), held_extra, swap(second, "dp", dp, stages[0]))
        )
        second = join(second, late)
        for bit in stages[1:]:
            second = join(second, swap(second, "dp", dp, bit))
            held_extra = join(held_extra, swap(held_extra, "dp", dp, bit))
        held_extra = join(held_extra, swap(held_extra, "dp", dp, 1))
        held_extra = held_extra.reshape((dp,) + extra.shape)
        if ready:
            held_extra = reorder(unmirrored(held_extra), me).reshape(1, width, -1)
        x3 = tokens.reshape(images, seq, width)
        cot3 = cotangent.reshape(images, seq, width)
        h_one, h_turned, ex = call(
            prep_kernel,
            [((count, width), bf16), ((width, count), bf16), ((held_extra.shape[2], width), f32)],
            (words, x3, held_extra),
            flops=cost(2),
            name="prep",
            grant=4,
            **exact,
        )
        near = join(first, other).reshape((2,) + first.shape)
        far = swap_both(near, dp, mp, (0, 2), (1, 0))
        second = second.reshape((high, d_rows, half))
        other = swap_both(second, dp, mp, (1, 0), (0, 2))
        far, h_one, other = lax.optimization_barrier((far, h_one, other))
        first = (near, far, swap(near, "mp", mp, 1), swap(far, "mp", mp, 1))
        near = join(second, other).reshape((2, high, d_rows, half))
        second_near, second_far = near, swap_both(near, dp, mp, (0, 2), (1, 0))
        second_near_other = swap(second_near, "mp", mp, 1)

        def whole(x, of_core, near, far, other_near, other_far):
            mine = core == of_core
            low = jnp.where(mine, near, other_near)
            high_part = jnp.where(mine, far, other_far)
            blocks = jnp.stack([low[x], high_part[x]]) if of_core else (high_part if x else low)
            blocks = blocks.reshape((dp,) + near.shape[2:])
            blocks = reorder(unmirrored(blocks), me)
            if blocks.ndim == 4:
                blocks = blocks.transpose(0, 2, 1, 3)
            return blocks.reshape(width, half)

        def weights_of(parts):
            if ready:
                return tuple(whole(j & 1, j >> 1, *parts) for j in range(4))
            return parts

        def saved(kept, columns, probs):
            return [
                ((mp, width, kept), bf16),
                ((mp, count, columns), bf16),
                ((mp, images) + probs + (tall, tall), bf16),
                ((mp, count, 128), bf16),
            ]

        pair = call(
            front_pair_kernel,
            saved(half, 384, (2,)),
            (words, h_one, token_mask) + weights_of(first),
            flops=cost(10),
            name="front_pair",
            grant=10,
            ready=ready,
            **static,
        )
        w_a, qkv_a, p_a, ho_a = pair
        second_far, ho_a = lax.optimization_barrier((second_far, ho_a))
        second = (second_near, second_far, second_near_other, swap(second_far, "mp", mp, 1))
        last_parts, branch = [], ()
        for flip in (0, 1):
            if ready:
                sources = tuple(
                    jnp.where(core == flip, whole(x, 0, *second), whole(x, 1, *second)) for x in (0, 1)
                )
            else:
                sources = second[2:] if flip else second[:2]
            outs = call(
                front_last_kernel,
                [
                    ((2, width, 256), bf16),
                    ((2, count, 256), bf16),
                    ((2, images, tall, tall), bf16),
                    ((count, 512), bf16),
                    ((width, 512), bf16),
                    ((count, width), f32),
                ],
                (words, h_one, token_mask, ho_a) + sources + branch,
                flops=cost(3),
                name="front_last",
                grant=10,
                ready=ready,
                flip=flip,
                **static,
            )
            last_parts.append(outs[:5])
            branch = (outs[5],)
        branch = branch[0]
        resid, h_two, soft, sent, sq_branch = call(
            route_kernel,
            [
                ((count, width), f32),
                ((count, width), bf16),
                ((2, images, experts, tall), f32),
                ((experts * each, width), bf16),
                ((images, 1, 128), f32),
            ],
            (words, x3, branch, cot3, token_mask, ex),
            flops=cost(2),
            name="route",
            grant=6,
            experts=experts,
            **exact,
        )
        got = sent.reshape(dp, each, width)
        got = lax.all_to_all(got, "dp", split_axis=0, concat_axis=0, tiled=True)
        got = gather_mp(got, mp).reshape(-1, width)
        everyone = got.shape[0]
        hidden, grad_pre, grad_expert, back = call(
            expert_kernel,
            [
                ((everyone, w_in.shape[2]), bf16),
                ((everyone, w_in.shape[2]), bf16),
                ((everyone, width), bf16),
                ((everyone, width), bf16),
            ],
            (got, w_in[0], w_back[0]),
            flops=cost(2),
            name="expert",
            scalars=0,
            grant=12 if dp <= 8 else 56,
            each=each,
        )
        back = back.reshape(mp, dp, each, width)
        back = scatter(back, "mp", mp, [1, 2])
        back = lax.all_to_all(back, "dp", split_axis=0, concat_axis=0, tiled=True)
        back = back.reshape(dp, 2, each // 2, width)[:, :, :images].transpose(1, 2, 0, 3)
        grad_w_back = mm_tn(hidden, grad_expert)
        grad_w_in = mm_tn(got, grad_pre)

        out_rows, grad_resid, grad_low, grad_turned, small = call(
            mix_kernel,
            [
                ((images, seq, width), bf16),
                ((count, width), f32),
                ((count, width), bf16),
                ((width, count), bf16),
                ((experts + 5, width), f32),
            ],
            (words, resid, h_two, soft, cot3, token_mask, ex, back, sq_branch),
            flops=cost(5),
            name="mix",
            grant=8,
            experts=experts,
            groups=mp,
            **exact,
        )
        shape = (1, 1, width, 4 * part) if ready else (2, high, d_rows, 4 * part)

        def back_of(x, flip, grad_in):
            grads, joined = call(
                back_kernel,
                [(shape, bf16), ((count, JOINED), bf16)],
                (words, grad_in, grad_turned, h_turned, qkv_a, p_a) + tuple(last_parts[flip][1:5]),
                [pltpu.VMEM((count, 256), f32)],
                flops=cost(8),
                name="back",
                grant=10,
                x=x,
                flip=flip,
                **static,
            )
            if ready:
                grads = reorder(grads.reshape(dp, d_rows, 4 * part), me)
                grads = grads.reshape(high, 2, d_rows, 4 * part).transpose(1, 0, 2, 3)
            return grads, joined

        def fold(terms, halves, starts=None, kept_columns=4 * part):
            size = terms[0].shape
            kept = ((size[0] // 2,) + size[1:-1] + (kept_columns,), bf16)
            return call(
                fold_kernel,
                [kept, kept],
                terms,
                flops=cost(1),
                name="fold",
                scalars=0,
                grant=6,
                halves=halves,
                starts=starts or (0,) * len(terms),
            )

        order = ((1, 1), (1, 0), (0, 1), (0, 0))
        sent_grads, joined_a = back_of(1, 1, grad_low)
        other = swap(sent_grads, "mp", mp, 1)
        grad_low, joined_a = lax.optimization_barrier((grad_low, joined_a))
        kept_grads, joined_b = back_of(1, 0, grad_low)
        far_kept, far_left = fold((kept_grads, other), True)
        far_left, grad_low, joined_b = lax.optimization_barrier((far_left, grad_low, joined_b))
        early = swap_both(far_left[0], dp, mp, (0, 2), (1, 0))
        sent_grads, joined_c = back_of(0, 1, grad_low)
        grad_low, joined_c = lax.optimization_barrier((grad_low, joined_c))
        other = swap(sent_grads, "mp", mp, 1)
        kept_grads, joined_d = back_of(0, 0, grad_low)
        part_shape = ((high, d_rows, 4 * part), bf16)
        near_sum, own_sum, second = call(
            blend_kernel,
            [part_shape] * 3,
            (words, far_kept[0], kept_grads, other),
            flops=cost(1),
            name="blend",
            grant=8,
        )
        second = swap_both(second, dp, mp, (0, 2), (1, 0))
        grad_h = call(
            input_kernel,
            [((count, width), f32)],
            (words, w_a, last_parts[0][0], last_parts[1][0], joined_a, joined_b, joined_c, joined_d),
            flops=cost(4),
            name="input",
            grant=8,
            order=order,
        )[0]
        early, grad_h = lax.optimization_barrier((early, grad_h))
        thirds = call(
            blend_late_kernel,
            [((high, d_rows, half), bf16)] * 2,
            (words, far_kept[0], own_sum, early),
            flops=cost(1),
            name="blend_late",
            grant=8,
        )
        thirds = [swap_both(third, dp, mp, (1, 0), (0, 2)) for third in thirds]
        pieces = [
            list(fold((near_sum, second, third), False, (k * half, k * half, 0), half))
            for k, third in enumerate(thirds)
        ]
        grad_tokens, small = call(
            last_kernel,
            [((images, seq, width), f32), ((experts + 5, width), f32)],
            (x3, grad_resid, grad_h, ex, small),
            flops=cost(0.1),
            name="last",
            scalars=0,
            grant=8,
            experts=experts,
            **exact,
        )
        for bit in bits_of(dp)[:-1]:
            small = small + swap(small, "dp", dp, bit)
        parts = []
        for k, (kept, left) in enumerate(pieces):
            for bit in bits_of(high)[:0:-1]:
                other = swap(left, "dp", dp, 2 * bit)
                if k == 0:
                    other, small = lax.optimization_barrier((other, small))
                kept, left = fold((kept, other), False, None, half)
            parts += [kept[0], swap(left[0], "dp", dp, 2 * bits_of(high)[0])]
        grad_qkv, grad_out = call(
            unpack_kernel,
            [((3, d_rows, part), f32), ((part, d_rows), f32)],
            parts,
            flops=cost(1),
            name="unpack",
            scalars=0,
            grant=6,
        )
        small = small + swap(small, "dp", dp, 1)
        small = small + swap(small, "mp", mp, 2)
        grad_one, grad_two, grad_router, root_squares = call(
            finish_kernel,
            [
                ((1, d_rows), f32),
                ((1, d_rows), f32),
                ((experts, d_rows), f32),
                ((3, mp * images), f32),
            ],
            (words, small, swap(small, "mp", mp, 1)),
            flops=cost(1),
            name="finish",
            grant=4,
        )
        return (
            out_rows.reshape(rows, width),
            grad_tokens.reshape(rows, width),
            grad_one[0],
            grad_qkv.transpose(1, 0, 2),
            grad_out,
            grad_two[0],
            grad_router.T,
            grad_w_in[None],
            grad_w_back[None],
            root_squares,
        )

    return per_device


def solution(mesh):
    in_specs = (
        P(("dp", "mp"), None),
        P("dp", None),
        P("dp"),
        P("dp", None, "mp"),
        P("mp", "dp"),
        P("dp"),
        P("dp", None),
        P("dp", None, "mp"),
        P("dp", "mp", None),
        P(("dp", "mp"), None),
    )
    out_specs = (
        P(("dp", "mp"), None),
        P(("dp", "mp"), None),
        P("dp"),
        P("dp", None, "mp"),
        P("mp", "dp"),
        P("dp"),
        P("dp", None),
        P("dp", None, "mp"),
        P("dp", "mp", None),
        P(None, "dp"),
    )
    return jax.shard_map(
        make(mesh), mesh=mesh, in_specs=in_specs, out_specs=out_specs, check_vma=False
    )
```

```python
import functools
import math

import jax
import jax.numpy as jnp
from jax import lax
from jax.experimental import pallas as pl
from jax.experimental.pallas import tpu as pltpu
from jax.sharding import PartitionSpec as P

HEAD_DIM = 64


epsilon = 1e-06
bf16 = jnp.bfloat16
f32 = jnp.float32


def bits_of(size):
    return [1 << k for k in reversed(range(size.bit_length() - 1))]


def swap(array_in, axis_name, size, bit):
    return lax.ppermute(array_in, axis_name, [(i, i ^ bit) for i in range(size)])


def swap_both(array_in, dp, mp, even, odd):
    pairs = []
    for d in range(dp):
        for m in range(mp):
            flip = odd if m & 1 else even
            pairs.append((d * mp + m, (d ^ flip[0]) * mp + (m ^ flip[1])))
    return lax.ppermute(array_in, ("dp", "mp"), pairs)


def gather_mp(block, mp):
    held = block[None]
    for bit in bits_of(mp):
        other = swap(held, "mp", mp, bit)
        held = jnp.stack([held, other], 1).reshape((-1,) + block.shape)
    return held


def scatter(held, axis_name, size, bits, unit=1):
    left = sorted(bits)
    for bit in bits:
        inner = 1 << left.index(bit)
        left.remove(bit)
        pairs = held.reshape((held.shape[0] // (2 * inner), 2, inner) + held.shape[1:])
        other = swap(pairs[:, 1], axis_name, size, bit * unit)
        held = pairs[:, 0].astype(f32) + other.astype(f32)
        held = held.astype(bf16).reshape((-1,) + held.shape[2:])
    return held[0]


def mirrored(index, size):
    bits = size.bit_length() - 1
    return sum(((index >> k) & 1) << (bits - 1 - k) for k in range(bits)) if bits else index


def unmirrored(blocks):
    size = blocks.shape[0]
    bits = size.bit_length() - 1
    split = blocks.reshape((2,) * bits + blocks.shape[1:])
    turn = tuple(range(bits))[::-1] + tuple(range(bits, split.ndim))
    return split.transpose(turn).reshape(blocks.shape)


def reorder(blocks, me):
    size = blocks.shape[0]
    for bit in bits_of(size):
        pairs = blocks.reshape((size // (2 * bit), 2, bit) + blocks.shape[1:])
        blocks = jnp.where((me & bit) > 0, pairs[:, ::-1], pairs).reshape(blocks.shape)
    return blocks


def mm(a, b):
    return lax.dot_general(a, b, (((1,), (0,)), ((), ())), preferred_element_type=f32)


def mm_nt(a, b):
    return lax.dot_general(a, b, (((1,), (1,)), ((), ())), preferred_element_type=f32)


def mm_tn(a, b):
    return lax.dot_general(a, b, (((0,), (0,)), ((), ())), preferred_element_type=f32)


def unit_of(rows_f):
    mean_row = jnp.mean(rows_f, axis=-1, keepdims=True)
    centered = rows_f - mean_row
    variance = jnp.mean(centered * centered, axis=-1, keepdims=True)
    inverse = lax.rsqrt(variance + epsilon)
    return centered * inverse, inverse


def padded(value, pad):
    return jnp.concatenate([value, jnp.zeros((pad, value.shape[1]), value.dtype)], 0)


def low_lanes(rows):
    return lax.broadcasted_iota(jnp.int32, (rows, 128), 1) < HEAD_DIM


JOINED = 640


def pack_kernel(
    me_ref, qkv_hbm, out_hbm, one_hbm, two_hbm, router_hbm, second_ref, extra_ref,
    qkv_ref, out_ref, one_ref, two_ref, router_ref, sems
):
    del me_ref
    pairs = (
        (qkv_hbm, qkv_ref), (out_hbm, out_ref), (one_hbm, one_ref), (two_hbm, two_ref), (router_hbm, router_ref),
    )
    copies = [pltpu.make_async_copy(a, b, sems.at[k]) for k, (a, b) in enumerate(pairs)]
    for copy in copies:
        copy.start()
    low, mid = 2 * HEAD_DIM, qkv_ref.shape[2]
    for copy in copies:
        copy.wait()
    out = out_ref[...].astype(f32).T.astype(bf16)
    second_ref[...] = jnp.concatenate(
        [qkv_ref[c, :, low:mid] for c in range(3)] + [out[:, low:mid], out[:, :low]], axis=1
    )
    rows = one_ref.shape[1]
    columns = [one_ref[...], two_ref[...], router_ref[...]]
    columns = [value.astype(f32) for value in columns]
    filled = sum(value.shape[0] for value in columns)
    columns.append(jnp.zeros((extra_ref.shape[1] - filled, rows), f32))
    extra_ref[...] = jnp.concatenate(columns, 0).T.astype(bf16)


def join_kernel(a_ref, b_ref, out_ref):
    size = a_ref.shape[0]
    out_ref[:size] = a_ref[...]
    out_ref[size:] = b_ref[...]


def join(a, b):
    shape = (a.shape[0] + b.shape[0],) + a.shape[1:]
    return call(join_kernel, [(shape, a.dtype)], (a, b), flops=1000, name="join", scalars=0, grant=4)[0]


def fold_kernel(*refs, halves, starts):
    terms, (kept_ref, left_ref) = refs[:-2], refs[-2:]
    size, columns = terms[0].shape[0], kept_ref.shape[-1]
    for k in range(size):
        total = None
        for term, start in zip(terms, starts):
            value = term[k][..., start : start + columns].astype(f32)
            total = value if total is None else total + value
        at, odd = (k % (size // 2), k >= size // 2) if halves else (k // 2, k % 2 == 1)
        (left_ref if odd else kept_ref)[at] = total.astype(bf16)


def blend_kernel(me_ref, far_ref, kept_ref, other_ref, near_ref, own_ref, second_ref):
    for k, ref in ((0, near_ref), (1, own_ref)):
        ref[...] = (kept_ref[k].astype(f32) + other_ref[k].astype(f32)).astype(bf16)
    first_core = me_ref[1] == 0

    @pl.when(first_core)
    def _():
        second_ref[...] = far_ref[...]

    @pl.when(jnp.logical_not(first_core))
    def _():
        second_ref[...] = own_ref[...]


def blend_late_kernel(me_ref, far_ref, own_ref, early_ref, *thirds):
    columns = thirds[0].shape[-1]
    for core, ref in ((0, own_ref), (1, far_ref)):

        @pl.when(me_ref[1] == core)
        def _(ref=ref):
            for k, third in enumerate(thirds):
                at = slice(k * columns, (k + 1) * columns)
                total = ref[..., at].astype(f32) + early_ref[..., at].astype(f32)
                third[...] = total.astype(bf16)


def finish_kernel(me_ref, own_ref, other_ref, one_ref, two_ref, router_ref, root_ref):
    experts, rows = router_ref.shape
    total = own_ref[...] + other_ref[...]
    width = total.shape[1]
    mine = pltpu.roll(total, lax.rem(width - me_ref[0] * rows, width), 1)
    one_ref[...] = mine[experts : experts + 1, :rows]
    two_ref[...] = mine[experts + 1 : experts + 2, :rows]
    router_ref[...] = mine[:experts, :rows]
    images = root_ref.shape[1]
    mine = pltpu.roll(total, lax.rem(width - me_ref[0] * images, width), 1)
    root_ref[...] = mine[experts + 2 : experts + 5, :images]


def unpack_kernel(own_a, other_a, own_b, other_b, qkv_ref, out_ref):
    low, mid = 2 * HEAD_DIM, qkv_ref.shape[2]
    pair = own_a[...].astype(f32) + other_a[...].astype(f32)
    rest = own_b[...].astype(f32) + other_b[...].astype(f32)
    for c in range(3):
        qkv_ref[c, :, :low] = pair[:, c * low : (c + 1) * low]
        qkv_ref[c, :, low:mid] = rest[:, c * HEAD_DIM : (c + 1) * HEAD_DIM]
    out_ref[...] = jnp.concatenate([rest[:, 256:], rest[:, 192:256]], axis=1).T


def length_of(mask_ref, me_ref, b, images):
    row = mask_ref[pl.ds(me_ref[2] * images + b, 1), :]
    return jnp.sum(row.astype(f32), axis=1, keepdims=True)


def seen_row(length, tall):
    return lax.broadcasted_iota(jnp.int32, (1, tall), 1).astype(f32) < length


def seen_column(length, tall):
    return lax.broadcasted_iota(jnp.int32, (tall, 1), 0).astype(f32) < length


def prep_kernel(me_ref, x_ref, extra_ref, h_ref, ht_ref, small_ref, *, images, seq, tall):
    blocks = extra_ref.shape[0]
    me = me_ref[0]
    parts = [extra_ref[mirrored(me ^ d, blocks) if blocks > 1 else 0] for d in range(blocks)]
    small_ref[...] = jnp.concatenate(parts, 0).astype(f32).T
    gain = small_ref[0:1, :]
    for b in range(images):
        unit, _ = unit_of(x_ref[b].astype(f32))
        h_ref[pl.ds(b * tall, tall), :] = padded((unit * gain).astype(bf16), tall - seq)
    ht_ref[...] = h_ref[...].T


def fetch_all(me_ref, refs, put):
    rows, high_size = refs[0].shape[-2], refs[0].shape[1]
    for core in (0, 1):

        @pl.when(me_ref[1] == core)
        def _(core=core):
            for slot in range(4):
                x, of_core = slot & 1, slot >> 1
                first, second = refs[:2] if of_core == core else refs[2:4]
                for r in range(2 * high_size):
                    low, high = r & 1, mirrored(r >> 1, high_size)
                    if of_core == 0:
                        block = (second if x else first)[low, high]
                    else:
                        block = (second if low else first)[x, high]
                    d = jnp.bitwise_xor(me_ref[0], r)
                    put(slot, pl.ds(pl.multiple_of(d * rows, 16), rows), block)


def attend(triples):
    scores = [mm_nt(q, k) * HEAD_DIM ** (-0.5) + bias for q, k, _, bias in triples]
    terms = [jnp.exp(value - jnp.max(value, axis=-1, keepdims=True)) for value in scores]
    probs = [
        (value * (1.0 / jnp.sum(value, axis=-1, keepdims=True))).astype(bf16) for value in terms
    ]
    return probs, [mm(value, v) for value, (_, _, v, _) in zip(probs, triples)]


def bias_of(mask_ref, me_ref, b, images, tall):
    return jnp.where(seen_row(length_of(mask_ref, me_ref, b, images), tall), 0.0, -1e30)


def front_pair_kernel(me_ref, h_ref, mask_ref, *refs, images, tall, ready):
    w_ref, qkv_ref, p_ref, ho_ref = refs[4:]

    def put(slot, at, block):
        for c in range(3):
            w_ref[slot, at, c * 128 : (c + 1) * 128] = block[c]

    if ready:
        for slot in range(4):
            w_ref[slot] = refs[slot][...]
    else:
        fetch_all(me_ref, refs[:4], put)
    low = low_lanes(tall)

    def group(j, carry):
        qkv_ref[j] = mm(h_ref[...], w_ref[j]).astype(bf16)
        triples = []
        for b in range(images):
            joined = qkv_ref[j, pl.ds(b * tall, tall), :]
            q, k, v = joined[:, :128], joined[:, 128:256], joined[:, 256:384]
            none = jnp.zeros_like(q)
            bias = bias_of(mask_ref, me_ref, b, images, tall)
            triples.append((jnp.where(low, q, none), k, v, bias))
            triples.append((jnp.where(low, none, q), k, v, bias))
        probs, outs = attend(triples)
        for b in range(images):
            p_ref[j, b, 0], p_ref[j, b, 1] = probs[2 * b], probs[2 * b + 1]
            pair = jnp.where(low, outs[2 * b], outs[2 * b + 1])
            ho_ref[j, pl.ds(b * tall, tall), :] = pair.astype(bf16)
        return carry

    lax.fori_loop(0, w_ref.shape[0], group, 0)


def front_last_kernel(me_ref, h_ref, mask_ref, pair_ref, *refs, images, tall, ready, flip):
    w_ref, qkv_ref, p_ref, ho_ref, wo_ref, br_ref = refs[-6:]

    def put(slot, at, block):
        w_ref[slot, at, :] = block[:, :256]
        wo_ref[at, slot * 256 : (slot + 1) * 256] = block[:, 128:]

    if ready:
        for slot in range(2):
            put(slot, slice(None), refs[slot][...])
    else:
        near, far = refs[:2]
        rows, high_size = near.shape[-2], near.shape[1]
        for core in (0, 1):

            @pl.when(me_ref[1] == core)
            def _(core=core):
                for x in (0, 1):
                    for r in range(2 * high_size):
                        low, high = r & 1, mirrored(r >> 1, high_size)
                        if core == flip:
                            block = (far if x else near)[low, high]
                        else:
                            block = (far if low else near)[x, high]
                        d = jnp.bitwise_xor(me_ref[0], r)
                        put(x, pl.ds(pl.multiple_of(d * rows, 16), rows), block)

    low = low_lanes(tall)
    places = [(x, b) for x in (0, 1) for b in range(images)]
    for x in (0, 1):
        qkv_ref[x] = mm(h_ref[...], w_ref[x]).astype(bf16)
    triples = []
    for x, b in places:
        joined = qkv_ref[x, pl.ds(b * tall, tall), :]
        qk, v = joined[:, :128], joined[:, 128:256]
        k = pltpu.roll(qk.astype(f32), HEAD_DIM, 1).astype(bf16)
        bias = bias_of(mask_ref, me_ref, b, images, tall)
        triples.append((jnp.where(low, qk, jnp.zeros_like(qk)), k, v, bias))
    probs, outs = attend(triples)
    of_core = jnp.bitwise_xor(me_ref[1], flip)
    for (x, b), prob, out in zip(places, probs, outs):
        at, start = pl.ds(b * tall, tall), x * 256
        p_ref[x, b] = prob
        ho_ref[at, start : start + 128] = jnp.where(low, 0.0, pltpu.roll(out, HEAD_DIM, 1)).astype(bf16)
        ho_ref[at, start + 128 : start + 256] = pair_ref[x + 2 * of_core, at, :]
    branch = mm_nt(ho_ref[...], wo_ref[...])
    br_ref[...] = branch + refs[2][...] if flip else branch


def spot(rows, b, start, experts):
    each = rows // experts
    at_row = lax.broadcasted_iota(jnp.int32, (rows, experts), 0)
    at_column = lax.broadcasted_iota(jnp.int32, (rows, experts), 1)
    return jnp.where(at_row == at_column * each + (start + b), 1.0, 0.0).astype(bf16)


def route_kernel(
    me_ref, x_ref, br_ref, cot_ref, mask_ref, ex_ref,
    res_ref, h_ref, soft_ref, sent_ref, sq_ref, *, images, seq, tall, experts
):
    rows = sent_ref.shape[0]
    half = rows // experts // 2
    router = ex_ref[2 : 2 + experts, :].astype(bf16)
    gain = ex_ref[1:2, :]
    total = jnp.zeros(sent_ref.shape, f32)
    for b in range(images):
        at = pl.ds(b * tall, tall)
        length = length_of(mask_ref, me_ref, b, images)
        branch = br_ref[at, :]
        resid = padded(x_ref[b].astype(f32), tall - seq) + branch
        res_ref[at, :] = resid
        unit, _ = unit_of(resid)
        h_two = (unit * gain).astype(bf16)
        h_ref[at, :] = h_two
        logits = mm_nt(router, h_two)
        held = jnp.where(seen_row(length, tall), logits, -1e30)
        terms = jnp.exp(held - jnp.max(held, axis=1, keepdims=True))
        dispatch = terms / jnp.sum(terms, axis=1, keepdims=True)
        terms = jnp.exp(logits - jnp.max(logits, axis=0, keepdims=True))
        combine = terms / jnp.sum(terms, axis=0, keepdims=True)
        soft_ref[0, b] = dispatch
        soft_ref[1, b] = combine
        cot = padded(cot_ref[b], tall - seq)
        wide_d = mm(spot(rows, b, 0, experts), dispatch.astype(bf16)).astype(bf16)
        wide_c = mm(spot(rows, b, half, experts), combine.astype(bf16)).astype(bf16)
        total += mm(wide_d, h_two) + mm(wide_c, cot)
        squares = jnp.sum(branch * branch, axis=1, keepdims=True)
        squares = jnp.sum(jnp.where(seen_column(length, tall), squares, 0.0), axis=0, keepdims=True)
        sq_ref[b] = jnp.broadcast_to(squares, (1, 128))
    sent_ref[...] = total.astype(bf16)


def expert_kernel(got_ref, first_ref, second_ref, hid_ref, pre_ref, grad_ref, back_ref, *, each):
    rows = got_ref.shape[0]
    half = each // 2
    got = got_ref[...]
    own = jnp.bitwise_and(lax.broadcasted_iota(jnp.int32, (rows, 1), 0), each - 1) < half
    grads = jnp.where(own, pltpu.roll(got.astype(f32), rows - half, 0), 0.0).astype(bf16)
    grad_ref[...] = grads
    u = mm(got, first_ref[...])
    cubic = 0.7978845608028654 * (u + 0.044715 * u * u * u)
    t = jnp.tanh(cubic)
    hidden = jnp.where(own, 0.5 * u * (1.0 + t), 0.0).astype(bf16)
    hid_ref[...] = hidden
    slope = 0.5 * (1.0 + t) + 0.5 * u * (1.0 - t * t) * 0.7978845608028654 * (
        1.0 + 3.0 * 0.044715 * u * u
    )
    grad_pre = (mm_nt(grads, second_ref[...]) * slope).astype(bf16)
    pre_ref[...] = grad_pre
    out = mm(hidden, second_ref[...])
    grad_in = mm_nt(grad_pre, first_ref[...])
    back_ref[...] = jnp.where(own, out, pltpu.roll(grad_in, half, 0)).astype(bf16)


def mix_kernel(
    me_ref, res_ref, h_ref, soft_ref, cot_ref, mask_ref, ex_ref, back_ref, sq_ref,
    out_ref, gres_ref, gb_ref, gbt_ref, small_ref, *, images, seq, tall, experts, groups
):
    small_ref[...] = jnp.zeros_like(small_ref)
    router = ex_ref[2 : 2 + experts, :].astype(bf16)
    gain = ex_ref[1:2, :]
    width = out_ref.shape[2]
    lanes = lax.broadcasted_iota(jnp.int32, (1, width), 1)
    roots = [jnp.zeros((1, width), f32) for _ in range(3)]
    for b in range(images):
        at = pl.ds(b * tall, tall)
        length = length_of(mask_ref, me_ref, b, images)
        resid, h_two = res_ref[at, :], h_ref[at, :]
        dispatch, combine = soft_ref[0, b], soft_ref[1, b]
        dispatch_low, combine_low = dispatch.astype(bf16), combine.astype(bf16)
        returned, grad_slots = back_ref[0, b], back_ref[1, b]
        cot = padded(cot_ref[b], tall - seq)
        mixed = mm_tn(combine_low, returned)
        stream = resid + mixed
        out_ref[b] = stream[:seq].astype(bf16)
        column = seen_column(length, tall)
        sums = []
        for value in (stream, mixed):
            squares = jnp.sum(value * value, axis=1, keepdims=True)
            sums.append(jnp.sum(jnp.where(column, squares, 0.0), axis=0, keepdims=True))
        sums.insert(1, sq_ref[b, :, 0:1])
        for k, value in enumerate(sums):
            root = jnp.sqrt(value / (length * width))
            mine = lanes == (me_ref[0] * groups + me_ref[2]) * images + b
            roots[k] += jnp.where(mine, root, 0.0)
        grad_c = mm_nt(returned, cot)
        grad_c = combine * (grad_c - jnp.sum(grad_c * combine, axis=0, keepdims=True))
        grad_d = mm_nt(grad_slots, h_two)
        grad_d = dispatch * (grad_d - jnp.sum(grad_d * dispatch, axis=1, keepdims=True))
        grad_logits = (grad_d + grad_c).astype(bf16)
        grad_h = mm_tn(dispatch_low, grad_slots) + mm_tn(grad_logits, router)
        small_ref[0:experts, :] += mm(grad_logits, h_two)
        unit, inverse = unit_of(resid)
        small_ref[experts + 1 : experts + 2, :] += jnp.sum(grad_h * unit, axis=0, keepdims=True)
        scaled = grad_h * gain
        mean_grad = jnp.mean(scaled, axis=-1, keepdims=True)
        mean_proj = jnp.mean(scaled * unit, axis=-1, keepdims=True)
        gres_ref[at, :] = cot.astype(f32) + inverse * (scaled - mean_grad - unit * mean_proj)
    for k in range(3):
        small_ref[experts + 2 + k : experts + 3 + k, :] = roots[k]
    gb_ref[...] = gres_ref[...].astype(bf16)
    gbt_ref[...] = gres_ref[...].T.astype(bf16)


def back_kernel(
    me_ref, gb_ref, gbt_ref, ht_ref, qkv_a, p_a, qkv_b, p_b, ho_ref, wo_ref,
    gw_ref, gj_ref, dho_ref, *, images, tall, x, flip
):
    j = x + 2 * jnp.bitwise_xor(me_ref[1], flip)
    own = slice(x * 256, (x + 1) * 256)
    scale = HEAD_DIM ** (-0.5)
    low = low_lanes(tall)
    dho_ref[...] = mm(gb_ref[...], wo_ref[:, own])
    heads, dots = [], []
    for b in range(images):
        at = pl.ds(b * tall, tall)
        joined, joined_last = qkv_a[j, at, :], qkv_b[x, at, :]
        q_pair, k_pair, v_pair = joined[:, :128], joined[:, 128:256], joined[:, 256:384]
        qk_last, v_last = joined_last[:, :128], joined_last[:, 128:256]
        grad = dho_ref[at, :].astype(bf16).astype(f32)
        product = grad * ho_ref[at, own].astype(f32)
        single, pair = product[:, :128], product[:, 128:]
        dots += [
            jnp.sum(jnp.where(low, pair, 0.0), axis=1, keepdims=True),
            jnp.sum(jnp.where(low, 0.0, pair), axis=1, keepdims=True),
            jnp.sum(single, axis=1, keepdims=True),
        ]
        grad_pair = grad[:, 128:]
        grad_last = jnp.where(low, pltpu.roll(grad[:, :128], HEAD_DIM, 1), 0.0).astype(bf16)
        heads += [
            (p_a[j, b, 0], jnp.where(low, grad_pair, 0.0).astype(bf16), v_pair, q_pair, k_pair),
            (p_a[j, b, 1], jnp.where(low, 0.0, grad_pair).astype(bf16), v_pair, q_pair, k_pair),
            (p_b[x, b], grad_last, v_last, qk_last, qk_last),
        ]
    grad_p = [mm_nt(g, v) for _, g, v, _, _ in heads]
    grad_s = [
        (probs.astype(f32) * (value - dot)).astype(bf16)
        for (probs, _, _, _, _), value, dot in zip(heads, grad_p, dots)
    ]
    gqs = [mm(value, k) for value, (_, _, _, _, k) in zip(grad_s, heads)]
    gks = [mm_tn(value, q) for value, (_, _, _, q, _) in zip(grad_s, heads)]
    gvs = [mm_tn(probs, g) for probs, g, _, _, _ in heads]
    for b in range(images):
        at = pl.ds(b * tall, tall)
        gq, gk, gv = (value[3 * b : 3 * b + 3] for value in (gqs, gks, gvs))
        last = pltpu.roll(jnp.where(low, gk[2], gq[2]), HEAD_DIM, 1)
        gj_ref[at, :] = jnp.concatenate(
            [
                jnp.where(low, gq[0], gq[1]) * scale,
                jnp.where(low, gk[0], gk[1]) * scale,
                gv[0] + gv[1],
                last * scale,
                gv[2],
            ],
            1,
        ).astype(bf16)
    grad_out = mm(gbt_ref[...], ho_ref[:, own])
    grad_in = mm(ht_ref[...], gj_ref[...])
    halves, blocks, rows = gw_ref.shape[:3]
    for d in range(halves * blocks):
        r = jnp.bitwise_xor(me_ref[0], d) if halves > 1 else 0
        entry = (jnp.bitwise_and(r, 1), jnp.right_shift(r, 1)) if halves > 1 else (0, 0)
        at = slice(d * rows, (d + 1) * rows)
        gw_ref[entry + (slice(None), slice(0, 512))] = grad_in[at, :512].astype(bf16)
        gw_ref[entry + (slice(None), slice(512, 640))] = (
            grad_in[at, 512:] + grad_out[at, :128]
        ).astype(bf16)
        gw_ref[entry + (slice(None), slice(640, 768))] = grad_out[at, 128:].astype(bf16)


def input_kernel(me_ref, w_a, w_own, w_other, *refs, order):
    grads, gh_ref = refs[:-1], refs[-1]
    for k, (ref, (x, flip)) in enumerate(zip(grads, order)):
        j = x + 2 * jnp.bitwise_xor(me_ref[1], flip)
        into = mm_nt(ref[:, :384], w_a[j]) + mm_nt(ref[:, 384:], (w_own, w_other)[flip][x])
        if k == 0:
            gh_ref[...] = into
        else:
            gh_ref[...] += into


def last_kernel(x_ref, gres_ref, gh_ref, ex_ref, part_ref, gt_ref, small_ref, *, images, seq, tall, experts):
    total = jnp.zeros((1, x_ref.shape[2]), f32)
    gain = ex_ref[0:1, :]
    for b in range(images):
        at = pl.ds(b * tall, seq)
        unit, inverse = unit_of(x_ref[b].astype(f32))
        grad_h = gh_ref[at, :]
        total += jnp.sum(grad_h * unit, axis=0, keepdims=True)
        scaled = grad_h * gain
        mean_grad = jnp.mean(scaled, axis=-1, keepdims=True)
        mean_proj = jnp.mean(scaled * unit, axis=-1, keepdims=True)
        gt_ref[b] = gres_ref[at, :] + inverse * (scaled - mean_grad - unit * mean_proj)
    small_ref[...] = part_ref[...]
    small_ref[experts : experts + 1, :] = total


def cost(microseconds):
    return int(microseconds * 1.1e9)


def call(kernel, outs, args, scratch=(), flops=0, name=None, scalars=1, grant=16, **static):
    spec = pl.BlockSpec(memory_space=pltpu.VMEM)
    word = pl.BlockSpec(memory_space=pltpu.SMEM)
    moved = sum(math.prod(a.shape) * a.dtype.itemsize for a in args)
    return pl.pallas_call(
        functools.partial(kernel, **static),
        out_shape=[jax.ShapeDtypeStruct(s, d) for s, d in outs],
        in_specs=[word] * scalars + [spec] * (len(args) - scalars),
        out_specs=[spec] * len(outs),
        scratch_shapes=list(scratch),
        compiler_params=pltpu.CompilerParams(vmem_limit_bytes=grant << 20),
        cost_estimate=pl.CostEstimate(flops=flops, bytes_accessed=moved, transcendentals=0),
        name=name,
    )(*args)


def make(mesh):
    dp, mp = mesh.shape["dp"], mesh.shape["mp"]

    def per_device(
        tokens, token_mask, gain_one, w_qkv, w_out, gain_two, router, w_in, w_back, cotangent
    ):
        rows, width = tokens.shape
        seq = token_mask.shape[1]
        tall = -(-seq // 16) * 16
        images = rows // seq
        experts = router.shape[1]
        d_rows, _, part = w_qkv.shape
        count = images * tall
        high = dp // 2
        heads = part // HEAD_DIM
        ready = d_rows % 16 != 0
        each = 2 * (1 << (images - 1).bit_length())
        me = lax.axis_index("dp")
        at_mp = lax.axis_index("mp")
        core = at_mp & 1
        words = jnp.stack([me, core, at_mp]).astype(jnp.int32)
        static = {"images": images, "tall": tall}
        exact = {"images": images, "seq": seq, "tall": tall}

        columns = experts + 2
        half = 2 * part
        hbm = pl.BlockSpec(memory_space=pltpu.HBM)
        vmem = pl.BlockSpec(memory_space=pltpu.VMEM)
        word = pl.BlockSpec(memory_space=pltpu.SMEM)
        wide = columns + -columns % 128
        shapes = [(3, d_rows, part), (part, d_rows), (1, d_rows), (1, d_rows), (experts, d_rows)]
        qkv = w_qkv.transpose(1, 0, 2)
        qkv, words = lax.optimization_barrier((qkv, words))
        first = qkv[:, :, : 2 * HEAD_DIM]
        second, extra = pl.pallas_call(
            pack_kernel,
            out_shape=[jax.ShapeDtypeStruct((d_rows, n), bf16) for n in (half, wide)],
            in_specs=[word] + [hbm] * 5,
            out_specs=[vmem] * 2,
            scratch_shapes=[pltpu.VMEM(shape, bf16) for shape in shapes] + [pltpu.SemaphoreType.DMA((5,))],
            compiler_params=pltpu.CompilerParams(vmem_limit_bytes=4 << 20),
            cost_estimate=pl.CostEstimate(flops=cost(2), bytes_accessed=300_000, transcendentals=0),
            name="pack",
        )(words, qkv, w_out, gain_one[None], gain_two[None], router.T)

        first, second, held_extra = first[None], second[None], extra[None]
        stages = bits_of(dp)[:-1]
        for bit in stages:
            other = swap(first, "dp", dp, bit)
            if bit == stages[0]:
                other, second, held_extra = lax.optimization_barrier((other, second, held_extra))
            else:
                at = stages[stages.index(bit) - 1]
                other, more = lax.optimization_barrier((other, swap(held_extra, "dp", dp, at)))
                held_extra = join(held_extra, more)
            first = join(first, other)
        held_extra = join(held_extra, swap(held_extra, "dp", dp, stages[-1]))
        other, held_extra, late = lax.optimization_barrier(
            (swap_both(first, dp, mp, (1, 0), (0, 2)), held_extra, swap(second, "dp", dp, stages[0]))
        )
        second = join(second, late)
        for bit in stages[1:]:
            second = join(second, swap(second, "dp", dp, bit))
        held_extra = join(held_extra, swap(held_extra, "dp", dp, 1))
        held_extra = held_extra.reshape((dp,) + extra.shape)
        if ready:
            held_extra = reorder(unmirrored(held_extra), me).reshape(1, width, -1)
        x3 = tokens.reshape(images, seq, width)
        cot3 = cotangent.reshape(images, seq, width)
        h_one, h_turned, ex = call(
            prep_kernel,
            [((count, width), bf16), ((width, count), bf16), ((held_extra.shape[2], width), f32)],
            (words, x3, held_extra),
            flops=cost(2),
            name="prep",
            grant=4,
            **exact,
        )
        near = join(first, other).reshape((2,) + first.shape)
        far = swap_both(near, dp, mp, (0, 2), (1, 0))
        second = second.reshape((high, d_rows, half))
        other = swap_both(second, dp, mp, (1, 0), (0, 2))
        far, h_one, other = lax.optimization_barrier((far, h_one, other))
        first = (near, far, swap(near, "mp", mp, 1), swap(far, "mp", mp, 1))
        near = join(second, other).reshape((2, high, d_rows, half))
        second_near, second_far = near, swap_both(near, dp, mp, (0, 2), (1, 0))
        second_near_other = swap(second_near, "mp", mp, 1)

        def whole(x, of_core, near, far, other_near, other_far):
            mine = core == of_core
            low = jnp.where(mine, near, other_near)
            high_part = jnp.where(mine, far, other_far)
            blocks = jnp.stack([low[x], high_part[x]]) if of_core else (high_part if x else low)
            blocks = blocks.reshape((dp,) + near.shape[2:])
            blocks = reorder(unmirrored(blocks), me)
            if blocks.ndim == 4:
                blocks = blocks.transpose(0, 2, 1, 3)
            return blocks.reshape(width, half)

        def weights_of(parts):
            if ready:
                return tuple(whole(j & 1, j >> 1, *parts) for j in range(4))
            return parts

        def saved(kept, columns, probs):
            return [
                ((mp, width, kept), bf16),
                ((mp, count, columns), bf16),
                ((mp, images) + probs + (tall, tall), bf16),
                ((mp, count, 128), bf16),
            ]

        pair = call(
            front_pair_kernel,
            saved(half, 384, (2,)),
            (words, h_one, token_mask) + weights_of(first),
            flops=cost(10),
            name="front_pair",
            grant=10,
            ready=ready,
            **static,
        )
        w_a, qkv_a, p_a, ho_a = pair
        second_far, ho_a = lax.optimization_barrier((second_far, ho_a))
        second = (second_near, second_far, second_near_other, swap(second_far, "mp", mp, 1))
        last_parts, branch = [], ()
        for flip in (0, 1):
            if ready:
                sources = tuple(
                    jnp.where(core == flip, whole(x, 0, *second), whole(x, 1, *second)) for x in (0, 1)
                )
            else:
                sources = second[2:] if flip else second[:2]
            outs = call(
                front_last_kernel,
                [
                    ((2, width, 256), bf16),
                    ((2, count, 256), bf16),
                    ((2, images, tall, tall), bf16),
                    ((count, 512), bf16),
                    ((width, 512), bf16),
                    ((count, width), f32),
                ],
                (words, h_one, token_mask, ho_a) + sources + branch,
                flops=cost(3),
                name="front_last",
                grant=10,
                ready=ready,
                flip=flip,
                **static,
            )
            last_parts.append(outs[:5])
            branch = (outs[5],)
        branch = branch[0]
        resid, h_two, soft, sent, sq_branch = call(
            route_kernel,
            [
                ((count, width), f32),
                ((count, width), bf16),
                ((2, images, experts, tall), f32),
                ((experts * each, width), bf16),
                ((images, 1, 128), f32),
            ],
            (words, x3, branch, cot3, token_mask, ex),
            flops=cost(2),
            name="route",
            grant=6,
            experts=experts,
            **exact,
        )
        got = sent.reshape(dp, each, width)
        got = lax.all_to_all(got, "dp", split_axis=0, concat_axis=0, tiled=True)
        got = gather_mp(got, mp).reshape(-1, width)
        everyone = got.shape[0]
        hidden, grad_pre, grad_expert, back = call(
            expert_kernel,
            [
                ((everyone, w_in.shape[2]), bf16),
                ((everyone, w_in.shape[2]), bf16),
                ((everyone, width), bf16),
                ((everyone, width), bf16),
            ],
            (got, w_in[0], w_back[0]),
            flops=cost(2),
            name="expert",
            scalars=0,
            grant=12 if dp <= 8 else 56,
            each=each,
        )
        back = back.reshape(mp, dp, each, width)
        back = scatter(back, "mp", mp, [1, 2])
        back = lax.all_to_all(back, "dp", split_axis=0, concat_axis=0, tiled=True)
        back = back.reshape(dp, 2, each // 2, width)[:, :, :images].transpose(1, 2, 0, 3)
        grad_w_back = mm_tn(hidden, grad_expert)
        grad_w_in = mm_tn(got, grad_pre)

        out_rows, grad_resid, grad_low, grad_turned, small = call(
            mix_kernel,
            [
                ((images, seq, width), bf16),
                ((count, width), f32),
                ((count, width), bf16),
                ((width, count), bf16),
                ((experts + 5, width), f32),
            ],
            (words, resid, h_two, soft, cot3, token_mask, ex, back, sq_branch),
            flops=cost(5),
            name="mix",
            grant=8,
            experts=experts,
            groups=mp,
            **exact,
        )
        shape = (1, 1, width, 4 * part) if ready else (2, high, d_rows, 4 * part)

        def back_of(x, flip, grad_in):
            grads, joined = call(
                back_kernel,
                [(shape, bf16), ((count, JOINED), bf16)],
                (words, grad_in, grad_turned, h_turned, qkv_a, p_a) + tuple(last_parts[flip][1:5]),
                [pltpu.VMEM((count, 256), f32)],
                flops=cost(8),
                name="back",
                grant=10,
                x=x,
                flip=flip,
                **static,
            )
            if ready:
                grads = reorder(grads.reshape(dp, d_rows, 4 * part), me)
                grads = grads.reshape(high, 2, d_rows, 4 * part).transpose(1, 0, 2, 3)
            return grads, joined

        def fold(terms, halves, starts=None, kept_columns=4 * part):
            size = terms[0].shape
            kept = ((size[0] // 2,) + size[1:-1] + (kept_columns,), bf16)
            return call(
                fold_kernel,
                [kept, kept],
                terms,
                flops=cost(1),
                name="fold",
                scalars=0,
                grant=6,
                halves=halves,
                starts=starts or (0,) * len(terms),
            )

        order = ((1, 1), (1, 0), (0, 1), (0, 0))
        sent_grads, joined_a = back_of(1, 1, grad_low)
        other = swap(sent_grads, "mp", mp, 1)
        grad_low, joined_a = lax.optimization_barrier((grad_low, joined_a))
        kept_grads, joined_b = back_of(1, 0, grad_low)
        far_kept, far_left = fold((kept_grads, other), True)
        far_left, grad_low, joined_b = lax.optimization_barrier((far_left, grad_low, joined_b))
        early = swap_both(far_left[0], dp, mp, (0, 2), (1, 0))
        sent_grads, joined_c = back_of(0, 1, grad_low)
        grad_low, joined_c = lax.optimization_barrier((grad_low, joined_c))
        other = swap(sent_grads, "mp", mp, 1)
        kept_grads, joined_d = back_of(0, 0, grad_low)
        part_shape = ((high, d_rows, 4 * part), bf16)
        near_sum, own_sum, second = call(
            blend_kernel,
            [part_shape] * 3,
            (words, far_kept[0], kept_grads, other),
            flops=cost(1),
            name="blend",
            grant=8,
        )
        second = swap_both(second, dp, mp, (0, 2), (1, 0))
        grad_h = call(
            input_kernel,
            [((count, width), f32)],
            (words, w_a, last_parts[0][0], last_parts[1][0], joined_a, joined_b, joined_c, joined_d),
            flops=cost(4),
            name="input",
            grant=8,
            order=order,
        )[0]
        early, grad_h = lax.optimization_barrier((early, grad_h))
        thirds = call(
            blend_late_kernel,
            [((high, d_rows, half), bf16)] * 2,
            (words, far_kept[0], own_sum, early),
            flops=cost(1),
            name="blend_late",
            grant=8,
        )
        thirds = [swap_both(third, dp, mp, (1, 0), (0, 2)) for third in thirds]
        pieces = [
            list(fold((near_sum, second, third), False, (k * half, k * half, 0), half))
            for k, third in enumerate(thirds)
        ]
        grad_tokens, small = call(
            last_kernel,
            [((images, seq, width), f32), ((experts + 5, width), f32)],
            (x3, grad_resid, grad_h, ex, small),
            flops=cost(0.1),
            name="last",
            scalars=0,
            grant=8,
            experts=experts,
            **exact,
        )
        for bit in bits_of(dp)[:-1]:
            small = small + swap(small, "dp", dp, bit)
        parts = []
        for k, (kept, left) in enumerate(pieces):
            for bit in bits_of(high)[:0:-1]:
                other = swap(left, "dp", dp, 2 * bit)
                if k == 0:
                    other, small = lax.optimization_barrier((other, small))
                kept, left = fold((kept, other), False, None, half)
            parts += [kept[0], swap(left[0], "dp", dp, 2 * bits_of(high)[0])]
        grad_qkv, grad_out = call(
            unpack_kernel,
            [((3, d_rows, part), f32), ((part, d_rows), f32)],
            parts,
            flops=cost(1),
            name="unpack",
            scalars=0,
            grant=6,
        )
        small = small + swap(small, "dp", dp, 1)
        small = small + swap(small, "mp", mp, 2)
        grad_one, grad_two, grad_router, root_squares = call(
            finish_kernel,
            [
                ((1, d_rows), f32),
                ((1, d_rows), f32),
                ((experts, d_rows), f32),
                ((3, mp * images), f32),
            ],
            (words, small, swap(small, "mp", mp, 1)),
            flops=cost(1),
            name="finish",
            grant=4,
        )
        return (
            out_rows.reshape(rows, width),
            grad_tokens.reshape(rows, width),
            grad_one[0],
            grad_qkv.transpose(1, 0, 2),
            grad_out,
            grad_two[0],
            grad_router.T,
            grad_w_in[None],
            grad_w_back[None],
            root_squares,
        )

    return per_device


def solution(mesh):
    in_specs = (
        P(("dp", "mp"), None),
        P("dp", None),
        P("dp"),
        P("dp", None, "mp"),
        P("mp", "dp"),
        P("dp"),
        P("dp", None),
        P("dp", None, "mp"),
        P("dp", "mp", None),
        P(("dp", "mp"), None),
    )
    out_specs = (
        P(("dp", "mp"), None),
        P(("dp", "mp"), None),
        P("dp"),
        P("dp", None, "mp"),
        P("mp", "dp"),
        P("dp"),
        P("dp", None),
        P("dp", None, "mp"),
        P("dp", "mp", None),
        P(None, "dp"),
    )
    return jax.shard_map(
        make(mesh), mesh=mesh, in_specs=in_specs, out_specs=out_specs, check_vma=False
    )
```
